32 devices in a mesh: ulysses: 4 (over y, core), blk: 8 (over z, x).
Axes of the slice: x: 2, y: 2, z: 4, core: 2. Of those that a mesh axis runs over, the one named last changes fastest.
Arguments:
- tokens: bfloat16 [3, 2048, 768], P(None, ('ulysses', 'blk')), may hold values from -6 to 6
- cotangent: bfloat16 [3, 2048, 768], P(None, ('ulysses', 'blk')), may hold values from -6 to 6
- lengths: int32 [3, 32], replicated, may hold values from 1 to 512, 2048 in all within a row
- time_step: int32 [3], replicated, may hold values from 0 to 999
- modulate_weight: bfloat16 [4608, 128], P(('ulysses', 'blk')), may hold values from -0.5 to 0.5
- modulate_bias: bfloat16 [4608], P(('ulysses', 'blk')), may hold values from -3 to 3
- attend_gain: bfloat16 [768], P(('ulysses', 'blk')), may hold values from 0.099609375 to 1.8984375
- input_weight: bfloat16 [768, 2304], P(('ulysses', 'blk')), may hold values from -0.21875 to 0.21875
- output_weight: bfloat16 [768, 768], P(('ulysses', 'blk')), may hold values from -1.75 to 1.75
- feed_gain: bfloat16 [768], P(('ulysses', 'blk')), may hold values from 0.099609375 to 1.8984375
- expand_weight: bfloat16 [768, 3072], P(('ulysses', 'blk')), may hold values from -0.21875 to 0.21875
- expand_bias: bfloat16 [3072], P(('ulysses', 'blk')), may hold values from -3 to 3
- reduce_weight: bfloat16 [3072, 768], P(('ulysses', 'blk')), may hold values from -0.109375 to 0.109375
- reduce_bias: bfloat16 [768], P(('ulysses', 'blk')), may hold values from -3 to 3
Outputs:
- layer_output: bfloat16 [3, 2048, 768], P(None, ('ulysses', 'blk'))
- tokens_grad: bfloat16 [3, 2048, 768], P(None, ('ulysses', 'blk'))
- modulate_weight_grad: float32 [4608, 128], P(('ulysses', 'blk'))
- modulate_bias_grad: float32 [4608], P(('ulysses', 'blk'))
- attend_gain_grad: float32 [768], P(('ulysses', 'blk'))
- input_weight_grad: float32 [768, 2304], P(('ulysses', 'blk'))
- output_weight_grad: float32 [768, 768], P(('ulysses', 'blk'))
- feed_gain_grad: float32 [768], P(('ulysses', 'blk'))
- expand_weight_grad: float32 [768, 3072], P(('ulysses', 'blk'))
- expand_bias_grad: float32 [3072], P(('ulysses', 'blk'))
- reduce_weight_grad: float32 [3072, 768], P(('ulysses', 'blk'))
- reduce_bias_grad: float32 [768], P(('ulysses', 'blk'))
The draws below stay inside these ranges and needn't reach their ends.
Inputs may be any that keep to these rules, and one draw needn't show every extreme that they name: Each row lists the lengths of the 32 documents that fill one sequence of 2048 tokens; the longest is exactly 512.
All inputs are finite; a program needn't handle non-finite values.
Results may differ from the reference program's by a relative error of at most 0.02.
Values may be sent and summed in bfloat16 or wider, within the bound.
No kernel may reach another device: no remote copies, remote signals or barrier semaphores. Data moves between devices by JAX's collectives and lax.ppermute only.
A program may use at most 512 MiB of HBM per device.

```python
import math
import jax
import jax.numpy as jnp
import numpy as np
from jax import lax

D = 768
HEADS = 12
HEAD_DIM = 64
FF = 3072
COND = 128
MICRO = 3
DOCS = 32
SEQ = 2048
MOST = 512


def strengthened(drawn, key, source, target, parts, factor):
    owner, partner = [(jnp.arange(drawn.shape[position]) // (drawn.shape[position] // parts)).reshape([-1 if axis == position else 1 for axis in range(drawn.ndim)]) for position in (source, target)]
    chosen = jax.random.permutation(key, parts)[partner]
    strong = (owner == chosen) | (owner == (partner + parts // 2) % parts)
    return jnp.where(strong, factor * drawn, drawn)


def block_levels(stream_key, shape, pieces, smallest, largest):
    level, own = 1.0, jax.random.fold_in(stream_key, 6)
    for axis_at, blocks in pieces:
        steps = jnp.exp(jax.random.uniform(jax.random.fold_in(own, axis_at), (blocks,), jnp.float32, smallest / len(pieces), largest / len(pieces)))
        level = level * jnp.repeat(steps, shape[axis_at] // blocks).reshape([-1 if axis == axis_at else 1 for axis in range(len(shape))])
    return level


def length_profile(number_of, total, limit, slope):
    portions = [(1 << 20) // math.isqrt(rank ** slope) + 1 for rank in range(2, number_of + 1)]
    rest, counts = total - limit - (number_of - 1), [1] * (number_of - 1)
    while rest > 0:
        free = [i for i in range(number_of - 1) if counts[i] < limit]
        pool, budget = sum([portions[i] for i in free]), rest
        for i in free:
            more = min(limit - counts[i], max(1, budget * portions[i] // pool), rest)
            counts[i] = counts[i] + more
            rest = rest - more
    return np.array([limit] + counts)


def uneven(own_key, number_of, total, reach, lean):
    if number_of == 2:
        one = jax.random.randint(own_key, (), max(1, total - reach), min(reach, total - 1) + 1)
        return jnp.stack([one, total - one])
    sizes = jnp.asarray(length_profile(number_of, total, reach, lean), jnp.int32)
    pairs = (number_of - 1) // 2
    giver, taker = sizes[1:1 + 2 * pairs:2], sizes[2:2 + 2 * pairs:2]
    room = jnp.minimum(giver - 1, reach - taker)
    passed = jax.random.randint(jax.random.fold_in(own_key, 1), (pairs,), 0, 1 << 20) % (room + 1)
    sizes = sizes.at[1:1 + 2 * pairs:2].set(giver - passed).at[2:2 + 2 * pairs:2].set(taker + passed)
    return sizes[jax.random.permutation(jax.random.fold_in(own_key, 2), number_of)]


def scatter_about(key, shape, scale, bound, cuts=(), held_as=jnp.bfloat16):
    values = scale * jax.random.normal(key, shape, jnp.float32)
    if cuts:
        values = values * block_levels(key, shape, cuts, -0.22, 0.18)
    return jnp.clip(values, -bound, bound).astype(held_as)


def bell_draw_with(stream_key, shape, scale, bound, pieces, heavy, kind=jnp.bfloat16):
    values = scale * jax.random.normal(stream_key, shape, jnp.float32)
    if pieces:
        values = values * block_levels(stream_key, shape, pieces, -0.22, 0.18)
    return jnp.clip(strengthened(values, jax.random.fold_in(stream_key, 3), *heavy), -bound, bound).astype(kind)


def setup_inputs(seed: int = 0) -> dict:
    seeds = jax.random.split(jax.random.key(seed), 15)
    return {
        "tokens": bell_draw_with(seeds[0], (MICRO, SEQ, D), 1.0, 6.0, ((1, 32),), (1, 2, 32, 2.75)),
        "cotangent": bell_draw_with(seeds[1], (MICRO, SEQ, D), 1.0, 6.0, ((1, 32),), (1, 2, 32, 2.75)),
        "lengths": jax.vmap(lambda own: uneven(own, DOCS, SEQ, MOST, 2))(jax.random.split(seeds[2], MICRO)).reshape((MICRO, DOCS)).astype(jnp.int32),
        "time_step": jax.random.randint(seeds[3], (MICRO,), 0, 1000).astype(jnp.int32),
        "modulate_weight": scatter_about(seeds[4], (6 * D, COND), COND ** -0.5, 0.5, ((0, 32),)),
        "modulate_bias": scatter_about(seeds[5], (6 * D,), 0.5, 3.0, ((0, 32),)),
        "attend_gain": jnp.clip(1.0 + 0.18 * jax.random.normal(seeds[6], (D,), jnp.float32), 0.099609375, 1.8984375).astype(jnp.bfloat16),
        "input_weight": scatter_about(seeds[7], (D, 3 * D), D ** -0.5, 0.21875, ((0, 32),)),
        "output_weight": scatter_about(seeds[8], (D, D), (D // 64) ** -0.5, 1.75, ((0, 32),)),
        "feed_gain": jnp.clip(1.0 + 0.18 * jax.random.normal(seeds[9], (D,), jnp.float32), 0.099609375, 1.8984375).astype(jnp.bfloat16),
        "expand_weight": scatter_about(seeds[10], (D, FF), D ** -0.5, 0.21875, ((0, 32),)),
        "expand_bias": scatter_about(seeds[11], (FF,), 0.5, 3.0, ((0, 32),)),
        "reduce_weight": scatter_about(seeds[12], (FF, D), FF ** -0.5, 0.109375, ((0, 32),)),
        "reduce_bias": scatter_about(seeds[13], (D,), 0.5, 3.0, ((0, 32),)),
    }


@jax.custom_vjp
def low(v):
    return lax.optimization_barrier(v.astype(jnp.bfloat16)).astype(jnp.float32)

@jax.custom_vjp
def low_back(v):
    return v

def low_keep(v):
    return (low(v), None)

def low_pass(kept, grad):
    return (grad,)

def back_keep(v):
    return (v, None)

def back_low(kept, grad):
    return (low(grad),)
low.defvjp(low_keep, low_pass)
low_back.defvjp(back_keep, back_low)

def time_features(time_step):
    half = COND // 2
    freqs = jnp.exp(-math.log(10000.0) * jnp.arange(half, dtype=jnp.float32) / half)
    angles = time_step.astype(jnp.float32)[:, None] * freqs[None, :]
    return low(jax.nn.silu(jnp.concatenate([jnp.cos(angles), jnp.sin(angles)], 1)))

def doc_layout(index, lengths_row):
    ends = jnp.cumsum(lengths_row).astype(jnp.int32)
    over = index[:, None] >= ends[None, :]
    segment = lax.optimization_barrier(jnp.sum(over.astype(jnp.int32), 1)).astype(jnp.int32)
    place = index - lax.optimization_barrier(jnp.sum(jnp.where(over, lengths_row[None, :], 0), 1)).astype(jnp.int32)
    return (segment, place)

def rotary(values, place, flip):
    half = values.shape[-1] // 2
    freqs = jnp.exp(-math.log(10000.0) * jnp.arange(half, dtype=jnp.float32) / half)
    angles = place.astype(jnp.float32)[:, None] * freqs[None, :]
    cosine = jnp.cos(angles)[:, None, :]
    sine = flip * jnp.sin(angles)[:, None, :]
    first = values[..., :half]
    second = values[..., half:]
    return jnp.concatenate([first * cosine - second * sine, second * cosine + first * sine], -1)

def modulate(values, gain, shift, scale):
    centered = values - lax.optimization_barrier(jnp.mean(values, -1, keepdims=True))
    spread = lax.optimization_barrier(jnp.mean(centered * centered, -1, keepdims=True))
    return centered * lax.rsqrt(spread + 1e-05) * gain * (1.0 + scale) + shift

def attention(queries, keys, values, segment):
    rows = math.gcd(SEQ, 512)

    def block(inputs):
        part, part_segment = inputs
        scores = low_back(jnp.einsum('qhd,khd->hqk', part, keys, precision=lax.Precision.HIGHEST) * 0.125)
        allowed = (part_segment[:, None] == segment[None, :])[None]
        highest = lax.optimization_barrier(jnp.max(jnp.where(allowed, scores, -1e+30), -1, keepdims=True))
        weights = jnp.where(allowed, jnp.exp(scores - highest), 0.0)
        probs = weights / lax.optimization_barrier(jnp.sum(weights, -1, keepdims=True))
        return jnp.einsum('hqk,khd->qhd', low(probs), values, precision=lax.Precision.HIGHEST)
    outputs = lax.map(jax.checkpoint(block), (queries.reshape(SEQ // rows, rows, HEADS, HEAD_DIM), segment.reshape(SEQ // rows, rows)))
    return outputs.reshape(SEQ, HEADS * HEAD_DIM)

def layer(values, cond_row, doc_lengths, mod_weight, mod_bias, gain_one, in_weight, out_weight, gain_two, up_weight, up_bias, down_weight, down_bias):
    mods = jnp.dot(mod_weight, cond_row, precision=lax.Precision.HIGHEST) + mod_bias
    shift1, scale1, gate1, shift2, scale2, gate2 = jnp.split(mods, 6)
    segment, place = doc_layout(jnp.arange(SEQ, dtype=jnp.int32), doc_lengths)
    normed = low(modulate(values, gain_one, shift1, scale1))
    qkv = low_back(jnp.dot(normed, in_weight, precision=lax.Precision.HIGHEST))
    queries = qkv[:, :D].reshape(SEQ, HEADS, HEAD_DIM)
    keys = qkv[:, D:2 * D].reshape(SEQ, HEADS, HEAD_DIM)
    vals = qkv[:, 2 * D:].reshape(SEQ, HEADS, HEAD_DIM)
    queries = low_back(low(rotary(queries, place, 1.0)))
    keys = low_back(low(rotary(keys, place, 1.0)))
    vals = low_back(low(vals))
    attended = low_back(low(attention(queries, keys, vals, segment)))
    attn = low_back(jnp.dot(attended, out_weight, precision=lax.Precision.HIGHEST))
    middle = values + gate1 * attn
    second = low(modulate(middle, gain_two, shift2, scale2))
    hidden = low_back(jnp.dot(second, up_weight, precision=lax.Precision.HIGHEST) + up_bias)
    active = low(jax.nn.gelu(hidden, approximate=True))
    branch = low_back(jnp.dot(active, down_weight, precision=lax.Precision.HIGHEST) + down_bias)
    return middle + gate2 * branch

def reference(tokens, cotangent, lengths, time_step, modulate_weight, modulate_bias, attend_gain, input_weight, output_weight, feed_gain, expand_weight, expand_bias, reduce_weight, reduce_bias):
    weights = tuple((item.astype(jnp.float32) for item in (modulate_weight, modulate_bias, attend_gain, input_weight, output_weight, feed_gain, expand_weight, expand_bias, reduce_weight, reduce_bias)))
    condition = time_features(time_step)

    def micro_step(totals, batch):
        inputs, grads_in, doc_lengths, cond_row = batch

        def forward(values, *params):
            return layer(values, cond_row, doc_lengths, *params)
        result, backward = jax.vjp(forward, inputs.astype(jnp.float32), *weights)
        grads = backward(grads_in.astype(jnp.float32))
        totals = tuple((total + grad for total, grad in zip(totals, grads[1:])))
        return (totals, (result.astype(jnp.bfloat16), grads[0].astype(jnp.bfloat16)))
    zeros = tuple((jnp.zeros(item.shape, jnp.float32) for item in weights))
    totals, (outputs, input_grads) = lax.scan(micro_step, zeros, (tokens, cotangent, lengths, condition))
    return (outputs, input_grads, totals[0], totals[1], totals[2], totals[3], totals[4], totals[5], totals[6], totals[7], totals[8], totals[9])
```

```python
import functools
import math

import jax
import jax.numpy as jnp
from jax import lax
from jax.experimental import pallas as pl
from jax.experimental.pallas import tpu as pltpu
from jax.sharding import PartitionSpec as P

HEADS = 12
ALL = ("ulysses", "blk")
BF = jnp.bfloat16
F32 = jnp.float32
NEG = -1e30


def exchange(x):
    return lax.all_to_all(x, ALL, split_axis=0, concat_axis=0, tiled=True)


def time_features(time_step, half):
    freqs = jnp.exp(-math.log(10000.0) * jnp.arange(half, dtype=F32) / half)
    angles = time_step.astype(F32)[:, None] * freqs[None, :]
    return jax.nn.silu(jnp.concatenate([jnp.cos(angles), jnp.sin(angles)], 1)).astype(BF)


def doc_layout(index, lengths_row):
    ends = jnp.cumsum(lengths_row)
    over = index[:, None] >= ends[None, :]
    segment = jnp.sum(over.astype(jnp.int32), 1)
    place = index - jnp.sum(jnp.where(over, lengths_row[None, :], 0), 1)
    return segment, place


def key_ranges(first, last, lengths_row, block):
    ends = jnp.cumsum(lengths_row)
    start = jnp.sum(jnp.where(first[:, None] >= ends[None, :], lengths_row[None, :], 0), 1)
    stop = jnp.min(jnp.where(ends[None, :] > last[:, None], ends[None, :], 1 << 30), 1)
    return jnp.stack([start // block, (stop + block - 1) // block], 1).reshape(-1)


def whole_vmem():
    return pl.BlockSpec(memory_space=pltpu.VMEM)


def project_body(slots, pairs, heads, extra, a_ref, w_ref, wz_ref, out_ref):
    groups, micro, rows, width = a_ref.shape
    last = a_ref[:, micro - 1].reshape(groups * rows, width)
    for m in range(micro):
        a = a_ref[:, m].reshape(groups * rows, width)
        for h in range(heads):
            slot = m * heads + h
            if slot >= slots:
                continue
            for c in range(0, out_ref.shape[2], 128):
                x = jnp.dot(a, w_ref[h, :, c : c + 128], preferred_element_type=F32)
                if extra and c > 0:
                    x = x + jnp.dot(last, wz_ref[:, c : c + 128], preferred_element_type=F32)
                out_ref[slot, :, c : c + 128] = x.astype(BF)
    for slot in range(pairs, slots):
        out_ref[slot] = jnp.zeros(out_ref.shape[1:], BF)


def turn_tables(cos_ref, sin_ref, extra):
    cos, sin = cos_ref[...], sin_ref[...]
    lane = lax.broadcasted_iota(jnp.int32, cos.shape, 1)
    low = lane < 64
    cos_r, sin_r = pltpu.roll(cos, 64, 1), pltpu.roll(sin, 64, 1)
    tables = [(jnp.where(low, cos, cos_r), jnp.where(low, sin, sin_r))]
    if extra:
        tables.append((jnp.where(low, 1.0, cos), jnp.where(low, 0.0, sin)))
        tables.append((jnp.where(low, cos_r, 1.0), jnp.where(low, sin_r, 0.0)))
    return tables


def turn(x, table):
    lane = lax.broadcasted_iota(jnp.int32, x.shape, 1)
    swapped = jnp.where(lane % 64 < 32, pltpu.roll(x, 96, 1), pltpu.roll(x, 32, 1))
    return x * table[0] + swapped * table[1]


def rotate_in_body(extra, x_ref, cos_ref, sin_ref, *outs):
    blocks, rows, lanes = x_ref.shape
    tables = turn_tables(cos_ref, sin_ref, extra)
    x = x_ref[...].reshape(blocks * rows, lanes)
    x0 = turn(x[:, :128].astype(F32), tables[0])
    outs[0][...] = (x0[:, :64] * 0.125).astype(BF)
    outs[1][...] = x0[:, 64:].astype(BF)
    x1 = x[:, 128:256].astype(F32)
    outs[2][...] = x1[:, :64].astype(BF)
    if extra:
        x1 = turn(x1, tables[1])
        outs[3][...] = (x1[:, 64:] * 0.125).astype(BF)
        x2 = turn(x[:, 256:].astype(F32), tables[2])
        outs[4][...] = x2[:, :64].astype(BF)
        outs[5][...] = x2[:, 64:].astype(BF)


def rotate_out_body(extra, cos_ref, sin_ref, *refs):
    out_ref = refs[-1]
    parts = [ref[...].astype(F32) for ref in refs[:-1]]
    tables = [(c, -s) for c, s in turn_tables(cos_ref, sin_ref, extra)]
    out_ref[:, :128] = turn(jnp.concatenate(parts[:2], 1), tables[0]).astype(BF)
    if extra:
        out_ref[:, 128:256] = turn(jnp.concatenate(parts[2:4], 1), tables[1]).astype(BF)
        out_ref[:, 256:] = turn(jnp.concatenate(parts[4:], 1), tables[2]).astype(BF)
    else:
        out_ref[:, 128:] = jnp.concatenate([parts[2], jnp.zeros_like(parts[2])], 1).astype(BF)


def attend_body(block, range_ref, q_ref, sq_ref, k_ref, v_ref, sk_ref, o_ref, lse_ref):
    i = pl.program_id(0)
    q, sq = q_ref[...], sq_ref[0]
    count, width = q.shape

    def step(j, carry):
        high, total, acc = carry
        at = pl.ds(pl.multiple_of(j * block, block), block)
        k, v, sk = k_ref[at, :], v_ref[at, :], sk_ref[at, :]
        s = lax.dot_general(k, q, (((1,), (1,)), ((), ())), preferred_element_type=F32)
        s = jnp.where(sk == sq, s, NEG)
        new = jnp.maximum(high, jnp.max(s, 0, keepdims=True))
        p = jnp.exp(s - new)
        fix = jnp.exp(high - new)
        total = total * fix + jnp.sum(p, 0, keepdims=True)
        acc = acc * fix + lax.dot_general(
            v, p.astype(BF), (((0,), (0,)), ((), ())), preferred_element_type=F32
        )
        return new, total, acc

    first = (
        jnp.full((1, count), NEG, F32),
        jnp.zeros((1, count), F32),
        jnp.zeros((width, count), F32),
    )
    high, total, acc = lax.fori_loop(range_ref[2 * i], range_ref[2 * i + 1], step, first)
    o_ref[...] = (acc / total).T.astype(BF)
    lse_ref[0] = high + jnp.log(total)


def attend_back_body(
    block, range_ref, q_ref, sq_ref, lse_ref, o_ref, do_ref, k_ref, v_ref, sk_ref,
    dq_ref, dk_ref, dv_ref, dk_sum, dv_sum,
):
    i = pl.program_id(0)

    @pl.when(i == 0)
    def _():
        dk_sum[...] = jnp.zeros_like(dk_sum)
        dv_sum[...] = jnp.zeros_like(dv_sum)

    q, sq, lse, do = q_ref[...], sq_ref[0], lse_ref[0], do_ref[...]
    count, width = q.shape
    delta = jnp.sum((do.astype(F32) * o_ref[...].astype(F32)).T, 0, keepdims=True)

    def step(j, dq):
        at = pl.ds(pl.multiple_of(j * block, block), block)
        k, v, sk = k_ref[at, :], v_ref[at, :], sk_ref[at, :]
        s = lax.dot_general(k, q, (((1,), (1,)), ((), ())), preferred_element_type=F32)
        p = jnp.where(sk == sq, jnp.exp(s - lse), 0.0)
        dp = lax.dot_general(v, do, (((1,), (1,)), ((), ())), preferred_element_type=F32)
        ds = (p * (dp - delta)).astype(BF)
        dv_sum[at, :] += jnp.dot(p.astype(BF), do, preferred_element_type=F32)
        dk_sum[at, :] += jnp.dot(ds, q, preferred_element_type=F32)
        return dq + lax.dot_general(
            k, ds, (((0,), (0,)), ((), ())), preferred_element_type=F32
        )

    dq = lax.fori_loop(
        range_ref[2 * i], range_ref[2 * i + 1], step, jnp.zeros((width, count), F32)
    )
    dq_ref[...] = (dq * 0.125).T.astype(BF)

    @pl.when(i == pl.num_programs(0) - 1)
    def _():
        dk_ref[...] = dk_sum[...].astype(BF)
        dv_ref[...] = dv_sum[...].astype(BF)


def attend(ranges, q, sq, k, v, sk, rows, block):
    count, width = q.shape
    steps = count // rows
    size = k.shape[0]
    by_row = pl.BlockSpec((rows, width), lambda i, r: (i, 0))
    as_row = pl.BlockSpec((1, 1, rows), lambda i, r: (i, 0, 0))
    return pl.pallas_call(
        functools.partial(attend_body, block),
        grid_spec=pltpu.PrefetchScalarGridSpec(
            num_scalar_prefetch=1,
            grid=(steps,),
            in_specs=[by_row, as_row, whole_vmem(), whole_vmem(), whole_vmem()],
            out_specs=[by_row, as_row],
        ),
        out_shape=[
            jax.ShapeDtypeStruct((count, width), BF),
            jax.ShapeDtypeStruct((steps, 1, rows), F32),
        ],
        cost_estimate=pl.CostEstimate(
            flops=count * size * width, transcendentals=count * size // 4, bytes_accessed=4 * size * width
        ),
        name="attend",
    )(ranges, q, sq.reshape(steps, 1, rows), k, v, sk)


def attend_back(ranges, q, sq, lse, o, do, k, v, sk, rows, block):
    count, width = q.shape
    steps = count // rows
    size = k.shape[0]
    by_row = pl.BlockSpec((rows, width), lambda i, r: (i, 0))
    as_row = pl.BlockSpec((1, 1, rows), lambda i, r: (i, 0, 0))
    return pl.pallas_call(
        functools.partial(attend_back_body, block),
        grid_spec=pltpu.PrefetchScalarGridSpec(
            num_scalar_prefetch=1,
            grid=(steps,),
            in_specs=[by_row, as_row, as_row, by_row, by_row, whole_vmem(), whole_vmem(), whole_vmem()],
            out_specs=[by_row, whole_vmem(), whole_vmem()],
            scratch_shapes=[pltpu.VMEM((size, width), F32)] * 2,
        ),
        out_shape=[
            jax.ShapeDtypeStruct((count, width), BF),
            jax.ShapeDtypeStruct((size, width), BF),
            jax.ShapeDtypeStruct((size, width), BF),
        ],
        cost_estimate=pl.CostEstimate(
            flops=3 * count * size * width, transcendentals=count * size // 4, bytes_accessed=8 * size * width
        ),
        name="attend_back",
    )(ranges, q, sq.reshape(steps, 1, rows), lse, o, do, k, v, sk)


def layer_norm(values):
    centered = values - jnp.mean(values, -1, keepdims=True)
    inverse = lax.rsqrt(jnp.mean(centered * centered, -1, keepdims=True) + 1e-05)
    return centered * inverse, inverse


def layer_norm_back(normed, inverse, grad):
    return inverse * (
        grad
        - jnp.mean(grad, -1, keepdims=True)
        - normed * jnp.mean(grad * normed, -1, keepdims=True)
    )


def gelu_tanh(values):
    return jax.nn.gelu(values, approximate=True)


def on_device(
    tokens,
    cotangent,
    lengths,
    time_step,
    modulate_weight,
    modulate_bias,
    attend_gain,
    input_weight,
    output_weight,
    feed_gain,
    expand_weight,
    expand_bias,
    reduce_weight,
    reduce_bias,
):
    groups, blocks = lax.axis_size("ulysses"), lax.axis_size("blk")
    group_id, block_id = lax.axis_index("ulysses"), lax.axis_index("blk")
    devices = groups * blocks
    me = group_id * blocks + block_id
    micro, rows, width = tokens.shape
    own = micro * rows
    size = devices * rows
    head_width = width // HEADS
    heads = HEADS // groups
    pairs = micro * heads
    extra = pairs > blocks
    assert pairs <= blocks + 1 and head_width == 64
    lanes = 384 if extra else 256
    stripe = rows // blocks if extra else 0
    mod_rows = modulate_weight.shape[0]
    gain_rows = attend_gain.shape[0]
    ff_rows = expand_bias.shape[0]
    ff = ff_rows * devices
    folds = ff // width
    pair_micro = jnp.minimum(block_id // heads, micro - 1)

    values = tokens.astype(F32)
    n1, r1 = layer_norm(values)
    weight_pack = jnp.concatenate(
        [
            output_weight,
            expand_weight.reshape(gain_rows, folds, width).transpose(1, 0, 2).reshape(-1, width),
            reduce_weight,
            n1.astype(BF).reshape(own, width),
            cotangent.reshape(own, width),
        ],
        0,
    )
    gathered = lax.all_gather(weight_pack, ALL, axis=0, tiled=False)
    at_expand = gain_rows
    at_reduce = at_expand + folds * gain_rows
    at_n1 = at_reduce + ff_rows
    at_dy = at_n1 + own
    output_full = gathered[:, :gain_rows].reshape(width, width)
    expand_full = (
        gathered[:, at_expand:at_reduce]
        .reshape(devices, folds, gain_rows, width)
        .transpose(0, 2, 1, 3)
        .reshape(width, ff)
    )
    reduce_full = gathered[:, at_reduce:at_n1].reshape(ff, width)

    condition = time_features(time_step, modulate_weight.shape[1] // 2)
    mod_own = jnp.einsum(
        "mc,fc->mf", condition, modulate_weight, preferred_element_type=F32
    ) + modulate_bias.astype(F32)
    small = jnp.concatenate(
        [
            mod_own.reshape(-1),
            attend_gain.astype(F32),
            feed_gain.astype(F32),
            reduce_bias.astype(F32),
            expand_bias.astype(F32),
        ]
    )
    small_size = -(-small.shape[0] // 1024) * 1024
    small = jnp.pad(small, (0, small_size - small.shape[0])).reshape(1, -1, 128)
    small_all = exchange(jnp.broadcast_to(small, (devices,) + small.shape[1:])).reshape(devices, -1)
    at = micro * mod_rows
    mods = small_all[:, :at].reshape(devices, micro, mod_rows).transpose(1, 0, 2).reshape(micro, -1)
    gain1 = small_all[:, at : at + gain_rows].reshape(-1)
    at += gain_rows
    gain2 = small_all[:, at : at + gain_rows].reshape(-1)
    at += gain_rows
    reduce_bias_f = small_all[:, at : at + gain_rows].reshape(-1)
    at += gain_rows
    expand_bias_f = small_all[:, at : at + ff_rows].reshape(-1)
    shift1, scale1, gate1, shift2, scale2, gate2 = [
        part[:, None, :] for part in jnp.split(mods, 6, 1)
    ]

    index = jnp.arange(size, dtype=jnp.int32)
    pair_lengths = lax.dynamic_index_in_dim(lengths, pair_micro, 0, keepdims=False)
    segment, place = doc_layout(index, pair_lengths)
    last_lengths = lengths[micro - 1]
    last_segment, last_place = doc_layout(index, last_lengths)
    half = head_width // 2
    freqs = jnp.exp(-math.log(10000.0) * jnp.arange(half, dtype=F32) / half)
    lane = jnp.arange(128)
    angles = jnp.where(
        (lane < 64)[None, :], place.astype(F32)[:, None], last_place.astype(F32)[:, None]
    ) * jnp.tile(freqs, 4)[None, :]
    cos_table = jnp.cos(angles)
    sin_table = jnp.where((lane % 64 < 32)[None, :], -1.0, 1.0) * jnp.sin(angles)
    query_rows = math.gcd(size, 256)
    key_block = math.gcd(size, 256)
    first = jnp.arange(size // query_rows, dtype=jnp.int32) * query_rows
    ranges = key_ranges(first, first + query_rows - 1, pair_lengths, key_block)
    segment_column = segment[:, None]

    a = (n1 * (gain1 * (1.0 + scale1)) + shift1).astype(BF)
    a_group = lax.all_to_all(
        jnp.broadcast_to(a[None], (groups,) + a.shape), "ulysses", split_axis=0, concat_axis=0, tiled=True
    )
    in_split = (
        input_weight.reshape(gain_rows, 3, groups, heads, head_width)
        .transpose(2, 0, 3, 1, 4)
        .reshape(groups, 1, gain_rows, heads * 3 * head_width)
    )
    in_own = exchange(
        jnp.broadcast_to(in_split, (groups, blocks) + in_split.shape[2:]).reshape(
            (devices,) + in_split.shape[2:]
        )
    ).reshape(width, heads, 3 * head_width)
    in_heads = jnp.pad(
        in_own.transpose(1, 0, 2), ((0, 0), (0, 0), (0, lanes - 3 * head_width))
    )
    in_last = jnp.pad(in_own[:, heads - 1], ((0, 0), (lanes - 3 * head_width, 0)))
    outgoing = pl.pallas_call(
        functools.partial(project_body, blocks, pairs, heads, extra),
        out_shape=jax.ShapeDtypeStruct((blocks, groups * rows, lanes), BF),
        in_specs=[whole_vmem()] * 3,
        out_specs=whole_vmem(),
        cost_estimate=pl.CostEstimate(
            flops=2 * own * groups * width * lanes * heads, transcendentals=0, bytes_accessed=4 * own * groups * width
        ),
        name="project",
    )(a_group, in_heads, in_last)
    incoming = lax.all_to_all(outgoing, "blk", split_axis=0, concat_axis=0, tiled=True)

    span = blocks * rows
    by_span = pl.BlockSpec((span, 64), lambda i: (i, 0))
    table_spec = pl.BlockSpec((span, 128), lambda i: (i, 0))
    parts = 6 if extra else 3
    turned = pl.pallas_call(
        functools.partial(rotate_in_body, extra),
        grid=(groups,),
        in_specs=[pl.BlockSpec((blocks, rows, lanes), lambda i: (0, i, 0)), table_spec, table_spec],
        out_specs=[by_span] * parts,
        out_shape=[jax.ShapeDtypeStruct((size, 64), BF)] * parts,
        name="rotate_in",
    )(incoming, cos_table, sin_table)
    query, key, value = turned[:3]
    attended, lse = attend(
        ranges, query, segment, key, value, segment_column, query_rows, key_block
    )
    message = attended.reshape(devices, rows, head_width)
    if extra:
        striped = lambda x: lax.dynamic_slice_in_dim(
            x.reshape((devices, rows) + x.shape[1:]), block_id * stripe, stripe, 1
        ).reshape((devices * stripe,) + x.shape[1:])
        last_key, last_value = turned[4:]
        last_query = striped(turned[3])
        last_query_segment = striped(last_segment)
        last_rows = math.gcd(devices * stripe, 128)
        chunk = last_rows // stripe
        last_first = jnp.arange(devices // chunk, dtype=jnp.int32) * (chunk * rows) + block_id * stripe
        last_ranges = key_ranges(
            last_first, last_first + (chunk - 1) * rows + stripe - 1, last_lengths, key_block
        )
        last_column = last_segment[:, None]
        last_attended, last_lse = attend(
            last_ranges, last_query, last_query_segment, last_key, last_value, last_column, last_rows, key_block
        )
        message = jnp.concatenate(
            [message, last_attended.reshape(devices, stripe, head_width)], 1
        )
    came = exchange(message)
    own_pairs = min(pairs, blocks)

    def to_heads(x):
        x = x.reshape((groups, blocks) + x.shape[1:])
        y = x[:, :own_pairs, :rows]
        if extra:
            y = jnp.concatenate([y, x[:, :, rows:].reshape(groups, 1, rows, head_width)], 1)
        return (
            y.reshape(groups, micro, heads, rows, head_width)
            .transpose(1, 3, 0, 2, 4)
            .reshape(own, width)
        )

    def from_heads(x):
        y = (
            x.reshape(micro, rows, groups, heads, head_width)
            .transpose(2, 0, 3, 1, 4)
            .reshape(groups, pairs, rows, head_width)
        )
        z = y[:, :own_pairs]
        if own_pairs < blocks:
            z = jnp.pad(z, ((0, 0), (0, blocks - own_pairs), (0, 0), (0, 0)))
        if extra:
            z = jnp.concatenate([z, y[:, own_pairs].reshape(groups, blocks, stripe, head_width)], 2)
        return z.reshape((devices,) + z.shape[2:])

    merged = to_heads(came)
    attn = jnp.dot(merged, output_full, preferred_element_type=F32).reshape(micro, rows, width)
    middle = values + gate1 * attn
    n2, r2 = layer_norm(middle)
    second = (n2 * (gain2 * (1.0 + scale2)) + shift2).astype(BF).reshape(own, width)
    late_pack = jnp.concatenate(
        [second, input_weight.reshape(gain_rows, 3, width).transpose(1, 0, 2).reshape(-1, width)], 0
    )
    late = lax.all_gather(late_pack, ALL, axis=0, tiled=False)

    hidden = jnp.dot(second, expand_full, preferred_element_type=F32) + expand_bias_f
    active, active_back = jax.vjp(gelu_tanh, hidden)
    branch = jnp.dot(active.astype(BF), reduce_full, preferred_element_type=F32) + reduce_bias_f
    branch = branch.reshape(micro, rows, width)
    layer_output = (middle + gate2 * branch).astype(BF)
    grad_out = cotangent.astype(F32)
    d_gate2 = jnp.sum(grad_out * branch, 1)
    grad_branch = (gate2 * grad_out).astype(BF)
    reduce_bias_part = jnp.sum(grad_branch.astype(F32), (0, 1))
    grad_active = lax.dot_general(
        grad_branch.reshape(own, width), reduce_full, (((1,), (1,)), ((), ())), preferred_element_type=F32
    )
    grad_hidden = active_back(grad_active)[0].astype(BF)
    grad_second = lax.dot_general(
        grad_hidden, expand_full, (((1,), (1,)), ((), ())), preferred_element_type=F32
    ).reshape(micro, rows, width)
    d_shift2 = jnp.sum(grad_second, 1)
    p2 = jnp.sum(grad_second * n2, 1)
    grad_middle = grad_out + layer_norm_back(n2, r2, grad_second * ((1.0 + scale2) * gain2))
    d_gate1 = jnp.sum(grad_middle * attn, 1)
    grad_attn = (gate1 * grad_middle).astype(BF).reshape(own, width)
    grad_merged = lax.dot_general(
        grad_attn, output_full, (((1,), (1,)), ((), ())), preferred_element_type=F32
    ).astype(BF)
    do_came = exchange(from_heads(grad_merged))
    output_part = lax.dot_general(
        merged, grad_attn, (((0,), (0,)), ((), ())), preferred_element_type=F32
    ).astype(BF)
    output_came = exchange(output_part.reshape(devices, gain_rows, width))

    do_pair = do_came[:, :rows].reshape(size, head_width)
    grads = list(
        attend_back(
            ranges, query, segment, lse, attended, do_pair, key, value, segment_column, query_rows, key_block
        )
    )
    if extra:
        dq_last, dk_last, dv_last = attend_back(
            last_ranges, last_query, last_query_segment, last_lse, last_attended,
            do_came[:, rows:].reshape(devices * stripe, head_width),
            last_key, last_value, last_column, last_rows, key_block,
        )
        dq_last = lax.dynamic_update_slice_in_dim(
            jnp.zeros((devices, rows, head_width), BF),
            dq_last.reshape(devices, stripe, head_width),
            block_id * stripe,
            1,
        ).reshape(size, head_width)
        grads += [dq_last, dk_last, dv_last]
    grad_heads = pl.pallas_call(
        functools.partial(rotate_out_body, extra),
        grid=(groups,),
        in_specs=[table_spec, table_spec] + [by_span] * parts,
        out_specs=pl.BlockSpec((span, lanes), lambda i: (i, 0)),
        out_shape=jax.ShapeDtypeStruct((size, lanes), BF),
        name="rotate_out",
    )(cos_table, sin_table, *grads)
    back = exchange(grad_heads.reshape(devices, rows, lanes))

    used = 3 * head_width

    def input_part(which, grad):
        normed = lax.dynamic_slice_in_dim(
            gathered[:, at_n1:at_dy], which * rows, rows, 1
        ).reshape(size, width)
        part = lax.dot_general(normed, grad, (((0,), (0,)), ((), ())), preferred_element_type=F32)
        total = jnp.sum(grad.astype(F32), 0)
        pick = lambda x: lax.dynamic_index_in_dim(x, which, 0, keepdims=False)[0]
        return (
            part * (gain1 * (1.0 + pick(scale1)))[:, None] + pick(shift1)[:, None] * total[None, :]
        )

    input_parts = [input_part(pair_micro, grad_heads[:, :used])]
    if extra:
        input_parts.append(input_part(micro - 1, grad_heads[:, used:]))
    input_came = exchange(
        jnp.concatenate(input_parts, 1).astype(BF).reshape(devices, gain_rows, -1)
    ).astype(F32)
    input_came = input_came.reshape(groups, blocks, gain_rows, -1)
    by_pair = input_came[:, :own_pairs, :, :used]
    if extra:
        by_pair = jnp.concatenate(
            [by_pair, jnp.sum(input_came[..., used:], 1, keepdims=True)], 1
        )
    input_grad = (
        jnp.sum(by_pair.reshape(groups, micro, heads, gain_rows, 3, head_width), 1)
        .transpose(2, 3, 0, 1, 4)
        .reshape(gain_rows, 3 * width)
    )

    second_all = late[:, :own].reshape(devices * own, width)
    dy_all = gathered[:, at_dy:].reshape(devices, micro, rows, width)
    dm_all = (dy_all.astype(F32) * gate2[None]).astype(BF).reshape(devices * own, width)
    expand_own = lax.dynamic_slice_in_dim(expand_full, me * ff_rows, ff_rows, 1)
    hidden_own = jnp.dot(second_all, expand_own, preferred_element_type=F32) + expand_bias.astype(F32)
    active_own, active_own_back = jax.vjp(gelu_tanh, hidden_own)
    reduce_grad = lax.dot_general(
        active_own.astype(BF), dm_all, (((0,), (0,)), ((), ())), preferred_element_type=F32
    )
    grad_active_own = lax.dot_general(
        dm_all, reduce_weight, (((1,), (1,)), ((), ())), preferred_element_type=F32
    )
    grad_hidden_own = active_own_back(grad_active_own)[0].astype(BF)
    expand_bias_grad = jnp.sum(grad_hidden_own.astype(F32), 0)
    expand_part = lax.dot_general(
        second_all, grad_hidden_own, (((0,), (0,)), ((), ())), preferred_element_type=F32
    )
    expand_grad = (
        exchange(expand_part.reshape(devices, gain_rows, ff_rows))
        .transpose(1, 0, 2)
        .reshape(gain_rows, ff)
    )

    back = back.reshape(groups, blocks, rows, lanes)
    grad_pairs = back[:, :own_pairs, :, :used]
    if extra:
        last = jnp.sum(back[..., used:].astype(F32), 1, keepdims=True).astype(BF)
        grad_pairs = jnp.concatenate([grad_pairs, last], 1)
    grad_qkv = (
        grad_pairs.reshape(groups, micro, heads, rows, 3, head_width)
        .transpose(4, 1, 3, 0, 2, 5)
        .reshape(3, own, width)
    )
    grad_first = jnp.zeros((own, width), F32)
    for part in range(3):
        weight = late[:, own + part * gain_rows : own + (part + 1) * gain_rows].reshape(width, width)
        grad_first += lax.dot_general(
            grad_qkv[part], weight, (((1,), (1,)), ((), ())), preferred_element_type=F32
        )
    grad_first = grad_first.reshape(micro, rows, width)
    d_shift1 = jnp.sum(grad_first, 1)
    p1 = jnp.sum(grad_first * n1, 1)
    tokens_grad = (
        grad_middle + layer_norm_back(n1, r1, grad_first * ((1.0 + scale1) * gain1))
    ).astype(BF)

    grad_mods = jnp.concatenate(
        [d_shift1, p1 * gain1, d_gate1, d_shift2, p2 * gain2, d_gate2], 1
    )
    gain1_part = jnp.sum((1.0 + scale1[:, 0]) * p1, 0)
    gain2_part = jnp.sum((1.0 + scale2[:, 0]) * p2, 0)
    small_parts = jnp.concatenate(
        [grad_mods.reshape(micro, devices, mod_rows).transpose(1, 0, 2).reshape(devices, -1)]
        + [x.reshape(devices, gain_rows) for x in (gain1_part, gain2_part, reduce_bias_part)],
        1,
    )
    count = small_parts.shape[1]
    padded = -(-count // 1024) * 1024
    small_sum = jnp.sum(
        exchange(
            jnp.pad(small_parts, ((0, 0), (0, padded - count))).reshape(devices, -1, 128)
        ),
        0,
    ).reshape(-1)
    at = micro * mod_rows
    mod_sum = small_sum[:at].reshape(micro, mod_rows)
    modulate_weight_grad = jnp.sum(
        mod_sum[:, :, None] * condition.astype(F32)[:, None, :], 0
    )
    output_grad = jnp.sum(output_came.astype(F32), 0)
    return (
        layer_output,
        tokens_grad,
        modulate_weight_grad,
        jnp.sum(mod_sum, 0),
        small_sum[at : at + gain_rows],
        input_grad,
        output_grad,
        small_sum[at + gain_rows : at + 2 * gain_rows],
        expand_grad,
        expand_bias_grad,
        reduce_grad,
        small_sum[at + 2 * gain_rows : at + 3 * gain_rows],
    )


def solution(mesh):
    both = P(("ulysses", "blk"))
    tall = P(("ulysses", "blk"), None)
    seq = P(None, ("ulysses", "blk"), None)
    in_specs = (
        seq, seq, P(), P(), tall, both, both, tall, tall, both, tall, both, tall, both,
    )
    out_specs = (seq, seq, tall, both, both, tall, tall, both, tall, both, tall, both)
    return jax.shard_map(
        on_device, mesh=mesh, in_specs=in_specs, out_specs=out_specs, check_vma=False
    )
```

```python
import functools
import math

import jax
import jax.numpy as jnp
from jax import lax
from jax.experimental import pallas as pl
from jax.experimental.pallas import tpu as pltpu
from jax.sharding import PartitionSpec as P

HEADS = 12
ALL = ("ulysses", "blk")
BF = jnp.bfloat16
F32 = jnp.float32
NEG = -1e30


def exchange(x):
    return lax.all_to_all(x, ALL, split_axis=0, concat_axis=0, tiled=True)


def time_features(time_step, half):
    freqs = jnp.exp(-math.log(10000.0) * jnp.arange(half, dtype=F32) / half)
    angles = time_step.astype(F32)[:, None] * freqs[None, :]
    return jax.nn.silu(jnp.concatenate([jnp.cos(angles), jnp.sin(angles)], 1)).astype(BF)


def doc_layout(index, lengths_row):
    ends = jnp.cumsum(lengths_row)
    over = index[:, None] >= ends[None, :]
    segment = jnp.sum(over.astype(jnp.int32), 1)
    place = index - jnp.sum(jnp.where(over, lengths_row[None, :], 0), 1)
    return segment, place


def key_ranges(first, last, lengths_row, block):
    ends = jnp.cumsum(lengths_row)
    start = jnp.sum(jnp.where(first[:, None] >= ends[None, :], lengths_row[None, :], 0), 1)
    stop = jnp.min(jnp.where(ends[None, :] > last[:, None], ends[None, :], 1 << 30), 1)
    return jnp.stack([start // block, (stop + block - 1) // block], 1).reshape(-1)


def whole_vmem():
    return pl.BlockSpec(memory_space=pltpu.VMEM)


def swap(blocks, axis):
    size = lax.axis_size(axis)
    return [
        x if k == 0 else lax.ppermute(x, axis, [(i, i ^ k) for i in range(size)])
        for k, x in enumerate(blocks)
    ]


def project_body(blocks, pairs, heads, extra, place_ref, c_ref, shift_ref, w_ref, *refs):
    groups = len(refs) - blocks - 1
    tokens, outs, kept = refs[:groups], refs[groups:-1], refs[-1]
    micro, rows, width = tokens[0].shape
    two = 128 * heads
    weights = [w_ref[:, c : min(c + 128, w_ref.shape[1])] for c in range(0, w_ref.shape[1], 128)]
    order = list(range(micro))[::-1]
    z_qk = z_v = None
    for m in order:
        a = jnp.concatenate(
            [(x[m].astype(F32) * c_ref[m][None] + shift_ref[m][None]).astype(BF) for x in tokens], 0
        )
        parts = [jnp.dot(a, w, preferred_element_type=F32).astype(BF) for w in weights]
        v = jnp.concatenate(parts[heads:], 1)
        if extra and m == micro - 1:
            z_qk = parts[heads - 1]
            z_v = v[:, (heads - 1) * 64 : heads * 64]
        for h in range(heads):
            pair = m * heads + h
            if pair >= blocks:
                continue
            kept[pair, :, :128] = parts[h]
            own_v = v[:, h * 64 : (h + 1) * 64]
            if extra:
                kept[pair, :, 128:256] = z_qk
                kept[pair, :, 256:] = jnp.concatenate([own_v, z_v], 1)
            else:
                kept[pair, :, 128:] = jnp.concatenate([own_v, jnp.zeros_like(own_v)], 1)
    for pair in range(pairs, blocks):
        kept[pair] = jnp.zeros(kept.shape[1:], BF)
    for j in range(blocks):
        outs[j][...] = kept[place_ref[1] ^ j]


def turn_tables(cos_ref, sin_ref, extra):
    cos, sin = cos_ref[...], sin_ref[...]
    lane = lax.broadcasted_iota(jnp.int32, cos.shape, 1)
    low = lane < 64
    cos_r, sin_r = pltpu.roll(cos, 64, 1), pltpu.roll(sin, 64, 1)
    tables = [(jnp.where(low, cos, cos_r), jnp.where(low, sin, sin_r))]
    if extra:
        tables.append((jnp.where(low, cos_r, cos), jnp.where(low, sin_r, sin)))
    return tables


def turn(x, table):
    lane = lax.broadcasted_iota(jnp.int32, x.shape, 1)
    swapped = jnp.where(lane % 64 < 32, pltpu.roll(x, 96, 1), pltpu.roll(x, 32, 1))
    return x * table[0] + swapped * table[1]


def rotate_in_body(blocks, extra, place_ref, cos_ref, sin_ref, *refs):
    ins, outs = refs[:blocks], refs[blocks : 2 * blocks - blocks + (6 if extra else 3)]
    kept = refs[-1]
    rows = ins[0].shape[0]
    for j in range(blocks):
        at = pl.multiple_of((place_ref[1] ^ j) * rows, rows)
        kept[pl.ds(at, rows), :] = ins[j][...]
    tables = turn_tables(cos_ref, sin_ref, extra)
    x0 = turn(kept[:, :128].astype(F32), tables[0])
    outs[0][...] = (x0[:, :64] * 0.125).astype(BF)
    outs[1][...] = x0[:, 64:].astype(BF)
    if extra:
        outs[2][...] = kept[:, 256:320]
        x1 = turn(kept[:, 128:256].astype(F32), tables[1])
        outs[3][...] = (x1[:, :64] * 0.125).astype(BF)
        outs[4][...] = x1[:, 64:].astype(BF)
        outs[5][...] = kept[:, 320:]
    else:
        outs[2][...] = kept[:, 128:192]


def rotate_out_body(blocks, extra, place_ref, cos_ref, sin_ref, *refs):
    count = 6 if extra else 3
    ins, outs, kept = refs[:count], refs[count:-1], refs[-1]
    rows = outs[0].shape[0]
    parts = [ref[...].astype(F32) for ref in ins]
    tables = [(c, -s) for c, s in turn_tables(cos_ref, sin_ref, extra)]
    kept[:, :128] = turn(jnp.concatenate(parts[:2], 1), tables[0]).astype(BF)
    if extra:
        kept[:, 128:256] = turn(jnp.concatenate(parts[3:5], 1), tables[1]).astype(BF)
        kept[:, 256:] = jnp.concatenate([parts[2], parts[5]], 1).astype(BF)
    else:
        kept[:, 128:] = jnp.concatenate([parts[2], jnp.zeros_like(parts[2])], 1).astype(BF)
    for j in range(blocks):
        at = pl.multiple_of((place_ref[1] ^ j) * rows, rows)
        outs[j][...] = kept[pl.ds(at, rows), :]


def project_back_body(blocks, pairs, heads, extra, place_ref, c_ref, shift_ref, w_ref, *refs):
    kept = refs[-1]
    groups = (len(refs) - blocks - 4) // 2
    tokens, ins = refs[:groups], refs[groups : groups + blocks]
    outs = refs[groups + blocks : 2 * groups + blocks]
    grad_ref, sum_ref, dot_ref = refs[2 * groups + blocks : -1]
    micro, rows, width = tokens[0].shape
    count = groups * rows
    for j in range(blocks):
        kept[place_ref[1] ^ j] = ins[j][...]
    last = None
    if extra:
        last = jnp.zeros((count, 256), F32)
        for j in range(blocks):
            last = last + kept[j, :, 128:].astype(F32)
        last = last.astype(BF)
    all_a, all_g = [], []
    for m in range(micro):
        n = jnp.concatenate([x[m] for x in tokens], 0).astype(F32)
        a = (n * c_ref[m][None] + shift_ref[m][None]).astype(BF)
        qk, v = [], []
        for h in range(heads):
            pair = m * heads + h
            if pair < blocks:
                qk.append(kept[pair, :, :128])
                at = 256 if extra else 128
                v.append(kept[pair, :, at : at + 64])
            else:
                qk.append(last[:, :128])
                v.append(last[:, 192:])
        g = jnp.concatenate(qk + v, 1)
        da = lax.dot_general(g, w_ref[...], (((1,), (1,)), ((), ())), preferred_element_type=F32)
        for k in range(groups):
            outs[k][m] = da[k * rows : (k + 1) * rows].astype(BF)
        sum_ref[m : m + 1] = jnp.sum(da, 0, keepdims=True)
        dot_ref[m : m + 1] = jnp.sum(da * n, 0, keepdims=True)
        all_a.append(a)
        all_g.append(g)
    grad_ref[...] = lax.dot_general(
        jnp.concatenate(all_a, 0), jnp.concatenate(all_g, 0), (((0,), (0,)), ((), ())),
        preferred_element_type=F32,
    ).astype(BF)


def norm(values):
    centered = values - jnp.mean(values, -1, keepdims=True)
    inverse = lax.rsqrt(jnp.mean(centered * centered, -1, keepdims=True) + 1e-05)
    return centered * inverse, inverse


def by_micro(ref, rows):
    return jnp.concatenate(
        [jnp.broadcast_to(ref[m][None], (rows, ref.shape[1])) for m in range(ref.shape[0])], 0
    )


def middle_body(
    groups, blocks, heads, micro, rows, stripe,
    came_ref, out_ref, x_ref, gate_ref, c_ref, shift_ref,
    merged_ref, attn_ref, middle_ref, second_ref,
):
    width = x_ref.shape[1]
    for u in range(groups):
        for m in range(micro):
            for h in range(heads):
                pair = m * heads + h
                lanes = slice((u * heads + h) * 64, (u * heads + h + 1) * 64)
                if pair < blocks:
                    merged_ref[m * rows : (m + 1) * rows, lanes] = came_ref[u * blocks + pair, :rows]
                else:
                    for b in range(blocks):
                        at = m * rows + b * stripe
                        merged_ref[at : at + stripe, lanes] = came_ref[u * blocks + b, rows:]
    attn = jnp.dot(merged_ref[...], out_ref[...].reshape(width, width), preferred_element_type=F32)
    attn_ref[...] = attn
    middle = x_ref[...].astype(F32) + by_micro(gate_ref, rows) * attn
    middle_ref[...] = middle
    normed, _ = norm(middle)
    second_ref[...] = (normed * by_micro(c_ref, rows) + by_micro(shift_ref, rows)).astype(BF)


def gelu_pair(u):
    t = jnp.tanh(0.7978845608028654 * (u + 0.044715 * u * u * u))
    value = 0.5 * u * (1.0 + t)
    slope = 0.5 * (1.0 + t) + 0.5 * u * (1.0 - t * t) * (
        0.7978845608028654 * (1.0 + 0.134145 * u * u)
    )
    return value, slope


NT = (((1,), (1,)), ((), ()))
TN = (((0,), (0,)), ((), ()))


def feed_body(
    groups, blocks, heads, micro, rows, stripe,
    ex_ref, re_ref, out_w_ref, ex_bias_ref, re_bias_ref, second_ref, middle_ref, attn_ref, dy_ref,
    gate1_ref, gate2_ref, c_ref,
    layer_ref, grad_ref, dattn_ref, do_ref, sums_ref,
    branch_sum, back_sum, dm_sum, do_sum,
):
    step = pl.program_id(0)
    width = middle_ref.shape[1]

    @pl.when(step == 0)
    def _():
        branch_sum[...] = jnp.zeros_like(branch_sum)
        back_sum[...] = jnp.zeros_like(back_sum)
        dm_sum[...] = (by_micro(gate2_ref, rows) * dy_ref[...].astype(F32)).astype(BF)

    expand = ex_ref[...].reshape(width, width)
    reduce = re_ref[...].reshape(width, width)
    u = jnp.dot(second_ref[...], expand, preferred_element_type=F32) + ex_bias_ref[0]
    g, slope = gelu_pair(u)
    branch_sum[...] += jnp.dot(g.astype(BF), reduce, preferred_element_type=F32)
    dg = lax.dot_general(dm_sum[...], reduce, NT, preferred_element_type=F32)
    du = (dg * slope).astype(BF)
    back_sum[...] += lax.dot_general(du, expand, NT, preferred_element_type=F32)

    @pl.when(step == pl.num_programs(0) - 1)
    def _():
        def total(at, x):
            for m in range(micro):
                sums_ref[at * micro + m : at * micro + m + 1] = jnp.sum(
                    x[m * rows : (m + 1) * rows], 0, keepdims=True
                )

        branch = branch_sum[...] + re_bias_ref[...]
        middle = middle_ref[...]
        dy = dy_ref[...].astype(F32)
        layer_ref[...] = (middle + by_micro(gate2_ref, rows) * branch).astype(BF)
        total(0, dy * branch)
        normed, inverse = norm(middle)
        db = back_sum[...]
        total(1, db)
        total(2, db * normed)
        e = db * by_micro(c_ref, rows)
        grad = dy + inverse * (
            e
            - jnp.mean(e, -1, keepdims=True)
            - normed * jnp.mean(e * normed, -1, keepdims=True)
        )
        grad_ref[...] = grad
        total(3, grad * attn_ref[...])
        total(4, dm_sum[...].astype(F32))
        dattn = (by_micro(gate1_ref, rows) * grad).astype(BF)
        dattn_ref[...] = dattn
        do_sum[...] = lax.dot_general(
            dattn, out_w_ref[...].reshape(width, width), NT, preferred_element_type=F32
        ).astype(BF)
        for at in range(groups):
            for m in range(micro):
                for h in range(heads):
                    pair = m * heads + h
                    lanes = slice((at * heads + h) * 64, (at * heads + h + 1) * 64)
                    if pair < blocks:
                        do_ref[at * blocks + pair, :rows] = do_sum[m * rows : (m + 1) * rows, lanes]
                    else:
                        for b in range(blocks):
                            top = m * rows + b * stripe
                            do_ref[at * blocks + b, rows:] = do_sum[top : top + stripe, lanes]
            for b in range(micro * heads, blocks):
                do_ref[at * blocks + b, :rows] = jnp.zeros((rows, 64), BF)


def feed_weights_body(rows, place_ref, ex_ref, re_ref, bias_ref, gate_ref, *refs):
    groups = (len(refs) - 3) // 2
    reduce_ref, expand_ref, sum_ref = refs[2 * groups :]
    width = refs[0].shape[-1]
    second = jnp.concatenate([x[...] for x in refs[:groups]], 0)
    gate = by_micro(gate_ref, rows)
    dm = jnp.concatenate(
        [(gate * x[...].astype(F32)).astype(BF) for x in refs[groups : 2 * groups]], 0
    )
    expand = ex_ref[...].reshape(width, width)
    reduce = re_ref[...].reshape(width, width)
    u = jnp.dot(second, expand, preferred_element_type=F32) + bias_ref[0]
    g, slope = gelu_pair(u)
    du = lax.dot_general(dm, reduce, NT, preferred_element_type=F32) * slope
    du = du.astype(BF)
    sum_ref[...] = jnp.sum(du.astype(F32), 0, keepdims=True)
    reduce_ref[...] = lax.dot_general(g.astype(BF), dm, TN, preferred_element_type=F32).astype(BF)
    expand_ref[...] = lax.dot_general(second, du, TN, preferred_element_type=F32).astype(BF)


def attend_body(block, range_ref, q_ref, sq_ref, k_ref, v_ref, sk_ref, o_ref, lse_ref):
    i = pl.program_id(0)
    q, sq = q_ref[...], sq_ref[0]
    count, width = q.shape

    def step(j, carry):
        high, total, acc = carry
        at = pl.ds(pl.multiple_of(j * block, block), block)
        k, v, sk = k_ref[at, :], v_ref[at, :], sk_ref[at, :]
        s = lax.dot_general(k, q, (((1,), (1,)), ((), ())), preferred_element_type=F32)
        s = jnp.where(sk == sq, s, NEG)
        new = jnp.maximum(high, jnp.max(s, 0, keepdims=True))
        p = jnp.exp(s - new)
        fix = jnp.exp(high - new)
        total = total * fix + jnp.sum(p, 0, keepdims=True)
        acc = acc * fix + lax.dot_general(
            v, p.astype(BF), (((0,), (0,)), ((), ())), preferred_element_type=F32
        )
        return new, total, acc

    first = (
        jnp.full((1, count), NEG, F32),
        jnp.zeros((1, count), F32),
        jnp.zeros((width, count), F32),
    )
    high, total, acc = lax.fori_loop(range_ref[2 * i], range_ref[2 * i + 1], step, first)
    o_ref[...] = (acc / total).T.astype(BF)
    lse_ref[0] = high + jnp.log(total)


def attend_back_body(
    block, range_ref, q_ref, sq_ref, lse_ref, o_ref, do_ref, k_ref, v_ref, sk_ref,
    dq_ref, dk_ref, dv_ref, dk_sum, dv_sum,
):
    i = pl.program_id(0)

    @pl.when(i == 0)
    def _():
        dk_sum[...] = jnp.zeros_like(dk_sum)
        dv_sum[...] = jnp.zeros_like(dv_sum)

    q, sq, lse, do = q_ref[...], sq_ref[0], lse_ref[0], do_ref[...]
    count, width = q.shape
    delta = jnp.sum((do.astype(F32) * o_ref[...].astype(F32)).T, 0, keepdims=True)

    def step(j, dq):
        at = pl.ds(pl.multiple_of(j * block, block), block)
        k, v, sk = k_ref[at, :], v_ref[at, :], sk_ref[at, :]
        s = lax.dot_general(k, q, (((1,), (1,)), ((), ())), preferred_element_type=F32)
        p = jnp.where(sk == sq, jnp.exp(s - lse), 0.0)
        dp = lax.dot_general(v, do, (((1,), (1,)), ((), ())), preferred_element_type=F32)
        ds = (p * (dp - delta)).astype(BF)
        dv_sum[at, :] += jnp.dot(p.astype(BF), do, preferred_element_type=F32)
        dk_sum[at, :] += jnp.dot(ds, q, preferred_element_type=F32)
        return dq + lax.dot_general(
            k, ds, (((0,), (0,)), ((), ())), preferred_element_type=F32
        )

    dq = lax.fori_loop(
        range_ref[2 * i], range_ref[2 * i + 1], step, jnp.zeros((width, count), F32)
    )
    dq_ref[...] = (dq * 0.125).T.astype(BF)

    @pl.when(i == pl.num_programs(0) - 1)
    def _():
        dk_ref[...] = dk_sum[...].astype(BF)
        dv_ref[...] = dv_sum[...].astype(BF)


def attend(ranges, q, sq, k, v, sk, rows, block):
    count, width = q.shape
    steps = count // rows
    size = k.shape[0]
    by_row = pl.BlockSpec((rows, width), lambda i, r: (i, 0))
    as_row = pl.BlockSpec((1, 1, rows), lambda i, r: (i, 0, 0))
    return pl.pallas_call(
        functools.partial(attend_body, block),
        grid_spec=pltpu.PrefetchScalarGridSpec(
            num_scalar_prefetch=1,
            grid=(steps,),
            in_specs=[by_row, as_row, whole_vmem(), whole_vmem(), whole_vmem()],
            out_specs=[by_row, as_row],
        ),
        out_shape=[
            jax.ShapeDtypeStruct((count, width), BF),
            jax.ShapeDtypeStruct((steps, 1, rows), F32),
        ],
        cost_estimate=pl.CostEstimate(
            flops=count * size * width, transcendentals=count * size // 4, bytes_accessed=4 * size * width
        ),
        name="attend",
    )(ranges, q, sq.reshape(steps, 1, rows), k, v, sk)


def attend_back(ranges, q, sq, lse, o, do, k, v, sk, rows, block):
    count, width = q.shape
    steps = count // rows
    size = k.shape[0]
    by_row = pl.BlockSpec((rows, width), lambda i, r: (i, 0))
    as_row = pl.BlockSpec((1, 1, rows), lambda i, r: (i, 0, 0))
    return pl.pallas_call(
        functools.partial(attend_back_body, block),
        grid_spec=pltpu.PrefetchScalarGridSpec(
            num_scalar_prefetch=1,
            grid=(steps,),
            in_specs=[by_row, as_row, as_row, by_row, by_row, whole_vmem(), whole_vmem(), whole_vmem()],
            out_specs=[by_row, whole_vmem(), whole_vmem()],
            scratch_shapes=[pltpu.VMEM((size, width), F32)] * 2,
        ),
        out_shape=[
            jax.ShapeDtypeStruct((count, width), BF),
            jax.ShapeDtypeStruct((size, width), BF),
            jax.ShapeDtypeStruct((size, width), BF),
        ],
        cost_estimate=pl.CostEstimate(
            flops=3 * count * size * width, transcendentals=count * size // 4, bytes_accessed=8 * size * width
        ),
        name="attend_back",
    )(ranges, q, sq.reshape(steps, 1, rows), lse, o, do, k, v, sk)


def on_device(
    tokens,
    cotangent,
    lengths,
    time_step,
    modulate_weight,
    modulate_bias,
    attend_gain,
    input_weight,
    output_weight,
    feed_gain,
    expand_weight,
    expand_bias,
    reduce_weight,
    reduce_bias,
):
    groups, blocks = lax.axis_size("ulysses"), lax.axis_size("blk")
    group_id, block_id = lax.axis_index("ulysses"), lax.axis_index("blk")
    devices = groups * blocks
    micro, rows, width = tokens.shape
    own = micro * rows
    size = devices * rows
    head_width = width // HEADS
    heads = HEADS // groups
    pairs = micro * heads
    extra = pairs > blocks
    lanes = 384 if extra else 256
    stripe = rows // blocks if extra else 0
    mod_rows = modulate_weight.shape[0]
    gain_rows = attend_gain.shape[0]
    ff_rows = expand_bias.shape[0]
    ff = ff_rows * devices
    folds = ff // width
    assert pairs <= blocks + 1 and head_width == 64 and folds == groups and heads == 3
    place = jnp.stack([group_id, block_id]).astype(jnp.int32)
    pair_micro = jnp.minimum(block_id // heads, micro - 1)

    values = tokens.astype(F32)
    n1, r1 = norm(values)
    n1_b = n1.astype(BF)
    n1_group = swap([n1_b] * groups, "ulysses")
    gathered = lax.all_gather(
        jnp.concatenate(
            [
                reduce_weight,
                output_weight,
                expand_weight.reshape(gain_rows, folds, width).transpose(1, 0, 2).reshape(-1, width),
            ],
            0,
        ),
        ALL,
        axis=0,
        tiled=False,
    )
    unit = gain_rows
    while unit % 8:
        unit *= 2
    units = width // unit
    if unit != gain_rows:
        gathered = jnp.concatenate(
            [gathered[:, :ff_rows].reshape(units, -1, width)]
            + [
                gathered[:, at : at + gain_rows].reshape(units, unit, width)
                for at in range(ff_rows, ff_rows + (folds + 1) * gain_rows, gain_rows)
            ],
            1,
        )
    wide = unit * folds

    in_split = input_weight.reshape(gain_rows, 3, groups, heads, head_width)
    in_split = jnp.concatenate(
        [
            in_split[:, :2].transpose(2, 0, 3, 1, 4).reshape(groups, 1, gain_rows, -1),
            in_split[:, 2].transpose(1, 0, 2, 3).reshape(groups, 1, gain_rows, -1),
        ],
        3,
    )
    in_own = exchange(
        jnp.broadcast_to(in_split, (groups, blocks) + in_split.shape[2:]).reshape(
            (devices,) + in_split.shape[2:]
        )
    ).reshape(width, heads * 3 * head_width)

    condition = time_features(time_step, modulate_weight.shape[1] // 2)
    mod_own = jnp.einsum(
        "mc,fc->mf", condition, modulate_weight, preferred_element_type=F32
    ) + modulate_bias.astype(F32)
    small = jnp.concatenate(
        [
            mod_own.reshape(-1),
            attend_gain.astype(F32),
            feed_gain.astype(F32),
            reduce_bias.astype(F32),
            expand_bias.astype(F32),
        ]
    )
    small_size = -(-small.shape[0] // 1024) * 1024
    small = jnp.pad(small, (0, small_size - small.shape[0])).reshape(1, -1, 128)
    small_all = exchange(jnp.broadcast_to(small, (devices,) + small.shape[1:])).reshape(devices, -1)
    at = micro * mod_rows
    mods = small_all[:, :at].reshape(devices, micro, mod_rows).transpose(1, 0, 2).reshape(micro, -1)
    gain1 = small_all[:, at : at + gain_rows].reshape(-1)
    at += gain_rows
    gain2 = small_all[:, at : at + gain_rows].reshape(-1)
    at += gain_rows
    reduce_bias_f = small_all[:, at : at + gain_rows].reshape(1, -1)
    at += gain_rows
    expand_bias_f = small_all[:, at : at + ff_rows].reshape(folds, 1, width)
    shift1, scale1, gate1, shift2, scale2, gate2 = jnp.split(mods, 6, 1)
    c1 = gain1 * (1.0 + scale1)
    c2 = gain2 * (1.0 + scale2)

    index = jnp.arange(size, dtype=jnp.int32)
    pair_lengths = lax.dynamic_index_in_dim(lengths, pair_micro, 0, keepdims=False)
    segment, position = doc_layout(index, pair_lengths)
    last_lengths = lengths[micro - 1]
    last_segment, last_position = doc_layout(index, last_lengths)
    half = head_width // 2
    freqs = jnp.exp(-math.log(10000.0) * jnp.arange(half, dtype=F32) / half)
    lane = jnp.arange(128)
    angles = jnp.where(
        (lane < 64)[None, :], position.astype(F32)[:, None], last_position.astype(F32)[:, None]
    ) * jnp.tile(freqs, 4)[None, :]
    cos_table = jnp.cos(angles)
    sin_table = jnp.where((lane % 64 < 32)[None, :], -1.0, 1.0) * jnp.sin(angles)
    query_rows = math.gcd(size, 256)
    key_block = math.gcd(size, 256)
    first = jnp.arange(size // query_rows, dtype=jnp.int32) * query_rows
    ranges = key_ranges(first, first + query_rows - 1, pair_lengths, key_block)
    segment_column = segment[:, None]

    count = groups * rows
    smem = pl.BlockSpec(memory_space=pltpu.SMEM)
    outgoing = pl.pallas_call(
        functools.partial(project_body, blocks, pairs, heads, extra),
        out_shape=[jax.ShapeDtypeStruct((count, lanes), BF)] * blocks,
        in_specs=[smem] + [whole_vmem()] * (3 + groups),
        out_specs=[whole_vmem()] * blocks,
        scratch_shapes=[pltpu.VMEM((blocks, count, lanes), BF)],
        cost_estimate=pl.CostEstimate(
            flops=2 * micro * count * width * 3 * 64 * heads, transcendentals=0, bytes_accessed=8 * own * width
        ),
        name="project",
    )(place, c1, shift1, in_own, *n1_group)
    incoming = swap(outgoing, "blk")

    span = blocks * rows
    by_span = pl.BlockSpec((span, 64), lambda i, p: (i ^ p[0], 0))
    table_spec = pl.BlockSpec((span, 128), lambda i, p: (i ^ p[0], 0))
    by_rows = pl.BlockSpec((rows, lanes), lambda i, p: (i, 0))
    parts = 6 if extra else 3
    turned = pl.pallas_call(
        functools.partial(rotate_in_body, blocks, extra),
        grid_spec=pltpu.PrefetchScalarGridSpec(
            num_scalar_prefetch=1,
            grid=(groups,),
            in_specs=[table_spec, table_spec] + [by_rows] * blocks,
            out_specs=[by_span] * parts,
            scratch_shapes=[pltpu.VMEM((span, lanes), BF)],
        ),
        out_shape=[jax.ShapeDtypeStruct((size, 64), BF)] * parts,
        name="rotate_in",
    )(place, cos_table, sin_table, *incoming)
    query, key, value = turned[:3]
    attended, lse = attend(
        ranges, query, segment, key, value, segment_column, query_rows, key_block
    )
    message = attended.reshape(devices, rows, head_width)
    if extra:
        striped = lambda x: lax.dynamic_slice_in_dim(
            x.reshape((devices, rows) + x.shape[1:]), block_id * stripe, stripe, 1
        ).reshape((devices * stripe,) + x.shape[1:])
        last_key, last_value = turned[4:]
        last_query = striped(turned[3])
        last_query_segment = striped(last_segment)
        last_rows = math.gcd(devices * stripe, 128)
        chunk = last_rows // stripe
        last_first = jnp.arange(devices // chunk, dtype=jnp.int32) * (chunk * rows) + block_id * stripe
        last_ranges = key_ranges(
            last_first, last_first + (chunk - 1) * rows + stripe - 1, last_lengths, key_block
        )
        last_column = last_segment[:, None]
        last_attended, last_lse = attend(
            last_ranges, last_query, last_query_segment, last_key, last_value, last_column, last_rows, key_block
        )
        message = jnp.concatenate(
            [message, last_attended.reshape(devices, stripe, head_width)], 1
        )
    came = exchange(message)

    ex_spec = lambda f: pl.BlockSpec((units, unit, width), f)
    flat = pl.BlockSpec((own, width), lambda i: (0, 0))
    vec = lambda n: pl.BlockSpec((n, width), lambda i: (0, 0))
    message_spec = pl.BlockSpec((devices, rows + stripe, head_width), lambda i: (0, 0, 0))
    sizes = (groups, blocks, heads, micro, rows, stripe)
    own_f32 = jax.ShapeDtypeStruct((own, width), F32)
    own_bf = jax.ShapeDtypeStruct((own, width), BF)
    merged, attn, middle, second = pl.pallas_call(
        functools.partial(middle_body, *sizes),
        grid=(1,),
        in_specs=[message_spec, ex_spec(lambda i: (0, folds, 0)), flat, vec(micro), vec(micro), vec(micro)],
        out_specs=[flat] * 4,
        out_shape=[own_bf, own_f32, own_f32, own_bf],
        name="middle",
    )(came, gathered, tokens.reshape(own, width), gate1, c2, shift2)
    second_group = swap([second] * groups, "ulysses")
    dy = cotangent.reshape(own, width)
    dy_group = swap([dy] * groups, "ulysses")

    per = width // wide
    layer_output, grad_middle, grad_attn, do_message, sums = pl.pallas_call(
        functools.partial(feed_body, *sizes),
        grid=(folds,),
        in_specs=[
            ex_spec(lambda i: (0, folds + 1 + i, 0)),
            pl.BlockSpec((per, wide, width), lambda i: (i, 0, 0)),
            ex_spec(lambda i: (0, folds, 0)),
            pl.BlockSpec((1, 1, width), lambda i: (i, 0, 0)),
            vec(1),
            flat, flat, flat, flat,
            vec(micro), vec(micro), vec(micro),
        ],
        out_specs=[flat, flat, flat, message_spec, vec(5 * micro)],
        out_shape=[
            own_bf, own_f32, own_bf,
            jax.ShapeDtypeStruct((devices, rows + stripe, head_width), BF),
            jax.ShapeDtypeStruct((5 * micro, width), F32),
        ],
        scratch_shapes=[
            pltpu.VMEM((own, width), F32), pltpu.VMEM((own, width), F32),
            pltpu.VMEM((own, width), BF), pltpu.VMEM((own, width), BF),
        ],
        cost_estimate=pl.CostEstimate(
            flops=8 * own * width * ff, transcendentals=own * ff, bytes_accessed=4 * width * ff
        ),
        name="feed",
    )(gathered, gathered, gathered, expand_bias_f, reduce_bias_f, second, middle, attn, dy, gate1, gate2, c2)
    do_came = exchange(do_message)
    d_gate2, d_shift2, p2, d_gate1, dm_sums = [
        sums[i * micro : (i + 1) * micro] for i in range(5)
    ]

    flat_p = pl.BlockSpec((own, width), lambda i, p: (0, 0))
    square = pl.BlockSpec((width, width), lambda i, p: (0, 0))
    reduce_part, expand_part, bias_part = pl.pallas_call(
        functools.partial(feed_weights_body, rows),
        grid_spec=pltpu.PrefetchScalarGridSpec(
            num_scalar_prefetch=1,
            grid=(1,),
            in_specs=[
                pl.BlockSpec((units, unit, width), lambda i, p: (0, folds + 1 + p[0], 0)),
                pl.BlockSpec((per, wide, width), lambda i, p: (p[0], 0, 0)),
                pl.BlockSpec((1, 1, width), lambda i, p: (p[0], 0, 0)),
                pl.BlockSpec((micro, width), lambda i, p: (0, 0)),
            ]
            + [flat_p] * (2 * groups),
            out_specs=[square, square, pl.BlockSpec((1, width), lambda i, p: (0, 0))],
        ),
        out_shape=[
            jax.ShapeDtypeStruct((width, width), BF),
            jax.ShapeDtypeStruct((width, width), BF),
            jax.ShapeDtypeStruct((1, width), F32),
        ],
        cost_estimate=pl.CostEstimate(
            flops=10 * own * groups * width * width, transcendentals=own * ff, bytes_accessed=16 * width * width
        ),
        name="feed_weights",
    )(place, gathered, gathered, expand_bias_f, gate2, *second_group, *dy_group)
    feed_part = jnp.concatenate(
        [
            reduce_part.reshape(blocks, ff_rows, width),
            expand_part.reshape(groups, blocks, gain_rows, width)
            .transpose(1, 0, 2, 3)
            .reshape(blocks, groups * gain_rows, width),
        ],
        1,
    )
    feed_sum = lax.psum_scatter(feed_part, "blk", scatter_dimension=0, tiled=True)[0]
    reduce_grad = feed_sum[:ff_rows].astype(F32)
    expand_rows = feed_sum[ff_rows:].reshape(groups, gain_rows, width)
    expand_came = jnp.stack(
        swap(
            [
                lax.dynamic_index_in_dim(expand_rows, group_id ^ k, 0, keepdims=False)
                for k in range(groups)
            ],
            "ulysses",
        )
    )
    expand_grad = jnp.concatenate(
        [
            lax.dynamic_index_in_dim(expand_came, group_id ^ k, 0, keepdims=False)
            for k in range(groups)
        ],
        1,
    ).astype(F32)

    output_part = lax.dot_general(merged, grad_attn, TN, preferred_element_type=F32).astype(BF)
    output_part = output_part.reshape(groups, width // groups, width)
    output_part = sum(
        x.astype(F32)
        for x in swap(
            [
                lax.dynamic_index_in_dim(output_part, group_id ^ k, 0, keepdims=False)
                for k in range(groups)
            ],
            "ulysses",
        )
    )
    output_part = output_part.astype(BF).reshape(blocks, gain_rows, width)
    output_grad = sum(
        x.astype(F32)
        for x in swap(
            [
                lax.dynamic_index_in_dim(output_part, block_id ^ k, 0, keepdims=False)
                for k in range(blocks)
            ],
            "blk",
        )
    )

    do_pair = do_came[:, :rows].reshape(size, head_width)
    grads = list(
        attend_back(
            ranges, query, segment, lse, attended, do_pair, key, value, segment_column, query_rows, key_block
        )
    )
    if extra:
        dq_last, dk_last, dv_last = attend_back(
            last_ranges, last_query, last_query_segment, last_lse, last_attended,
            do_came[:, rows:].reshape(devices * stripe, head_width),
            last_key, last_value, last_column, last_rows, key_block,
        )
        dq_last = lax.dynamic_update_slice_in_dim(
            jnp.zeros((devices, rows, head_width), BF),
            dq_last.reshape(devices, stripe, head_width),
            block_id * stripe,
            1,
        ).reshape(size, head_width)
        grads += [dq_last, dk_last, dv_last]
    leaving = pl.pallas_call(
        functools.partial(rotate_out_body, blocks, extra),
        grid_spec=pltpu.PrefetchScalarGridSpec(
            num_scalar_prefetch=1,
            grid=(groups,),
            in_specs=[table_spec, table_spec] + [by_span] * parts,
            out_specs=[by_rows] * blocks,
            scratch_shapes=[pltpu.VMEM((span, lanes), BF)],
        ),
        out_shape=[jax.ShapeDtypeStruct((count, lanes), BF)] * blocks,
        name="rotate_out",
    )(place, cos_table, sin_table, *grads)
    back = swap(leaving, "blk")

    returned = pl.pallas_call(
        functools.partial(project_back_body, blocks, pairs, heads, extra),
        out_shape=[jax.ShapeDtypeStruct((micro, rows, width), BF)] * groups
        + [
            jax.ShapeDtypeStruct((width, heads * 3 * head_width), BF),
            jax.ShapeDtypeStruct((micro, width), F32),
            jax.ShapeDtypeStruct((micro, width), F32),
        ],
        in_specs=[smem] + [whole_vmem()] * (3 + groups + blocks),
        out_specs=[whole_vmem()] * (groups + 3),
        scratch_shapes=[pltpu.VMEM((blocks, count, lanes), BF)],
        cost_estimate=pl.CostEstimate(
            flops=4 * micro * count * width * 3 * 64 * heads, transcendentals=0, bytes_accessed=8 * own * width
        ),
        name="project_back",
    )(place, c1, shift1, in_own, *n1_group, *back)
    input_part, d_shift1, p1 = returned[groups:]
    grad_first = sum(x.astype(F32) for x in swap(returned[:groups], "ulysses"))
    e = grad_first * c1[:, None]
    tokens_grad = (
        grad_middle.reshape(micro, rows, width)
        + r1
        * (
            e
            - jnp.mean(e, -1, keepdims=True)
            - n1 * jnp.mean(e * n1, -1, keepdims=True)
        )
    ).astype(BF)

    grad_mods = jnp.concatenate(
        [d_shift1, p1 * gain1, d_gate1, d_shift2, p2 * gain2, d_gate2], 1
    )
    gain1_part = jnp.sum((1.0 + scale1) * p1, 0)
    gain2_part = jnp.sum((1.0 + scale2) * p2, 0)
    own_units = jnp.where(
        (jnp.arange(groups) == group_id)[:, None], bias_part.reshape(1, width), 0.0
    )
    small_parts = jnp.concatenate(
        [grad_mods.reshape(micro, devices, mod_rows).transpose(1, 0, 2).reshape(devices, -1)]
        + [
            x.reshape(devices, -1)
            for x in (gain1_part, gain2_part, jnp.sum(dm_sums, 0), own_units)
        ],
        1,
    ).astype(BF)
    in_lanes = heads * 3 * head_width
    taken = small_parts.shape[1]
    small_rows = 8 * -(-taken // (8 * in_lanes))
    small_parts = jnp.pad(small_parts, ((0, 0), (0, small_rows * in_lanes - taken)))
    final = exchange(
        jnp.concatenate(
            [
                input_part.reshape(devices, gain_rows, in_lanes),
                small_parts.reshape(devices, small_rows, in_lanes),
            ],
            1,
        )
    )
    small_sum = jnp.sum(final[:, gain_rows:].astype(F32), 0).reshape(-1)
    input_sum = jnp.sum(
        final[:, :gain_rows].astype(F32).reshape(groups, blocks, gain_rows, in_lanes), 1
    )
    two = heads * 2 * head_width
    input_grad = jnp.concatenate(
        [
            input_sum[:, :, :two]
            .reshape(groups, gain_rows, heads, 2, head_width)
            .transpose(1, 3, 0, 2, 4)
            .reshape(gain_rows, 2 * width),
            input_sum[:, :, two:].transpose(1, 0, 2).reshape(gain_rows, width),
        ],
        1,
    )
    at = micro * mod_rows
    mod_sum = small_sum[:at].reshape(micro, mod_rows)
    modulate_weight_grad = jnp.sum(
        mod_sum[:, :, None] * condition.astype(F32)[:, None, :], 0
    )
    cuts = []
    for length in (gain_rows, gain_rows, gain_rows, ff_rows):
        cuts.append(small_sum[at : at + length])
        at += length
    return (
        layer_output.reshape(micro, rows, width),
        tokens_grad,
        modulate_weight_grad,
        jnp.sum(mod_sum, 0),
        cuts[0],
        input_grad,
        output_grad,
        cuts[1],
        expand_grad,
        cuts[3],
        reduce_grad,
        cuts[2],
    )


def solution(mesh):
    both = P(("ulysses", "blk"))
    tall = P(("ulysses", "blk"), None)
    seq = P(None, ("ulysses", "blk"), None)
    in_specs = (
        seq, seq, P(), P(), tall, both, both, tall, tall, both, tall, both, tall, both,
    )
    out_specs = (seq, seq, tall, both, both, tall, tall, both, tall, both, tall, both)
    return jax.shard_map(
        on_device, mesh=mesh, in_specs=in_specs, out_specs=out_specs, check_vma=False
    )
```

```python
import functools
import math

import jax
import jax.numpy as jnp
from jax import lax
from jax.experimental import pallas as pl
from jax.experimental.pallas import tpu as pltpu
from jax.sharding import PartitionSpec as P

HEADS = 12
ALL = ("ulysses", "blk")
BF = jnp.bfloat16
F32 = jnp.float32
NEG = -1e30


def exchange(x):
    return lax.all_to_all(x, ALL, split_axis=0, concat_axis=0, tiled=True)


def time_features(time_step, half):
    freqs = jnp.exp(-math.log(10000.0) * jnp.arange(half, dtype=F32) / half)
    angles = time_step.astype(F32)[:, None] * freqs[None, :]
    return jax.nn.silu(jnp.concatenate([jnp.cos(angles), jnp.sin(angles)], 1)).astype(BF)


def doc_layout(index, lengths_row):
    ends = jnp.cumsum(lengths_row)
    over = index[:, None] >= ends[None, :]
    segment = jnp.sum(over.astype(jnp.int32), 1)
    place = index - jnp.sum(jnp.where(over, lengths_row[None, :], 0), 1)
    return segment, place


def key_ranges(first, last, lengths_row, block):
    ends = jnp.cumsum(lengths_row)
    start = jnp.sum(jnp.where(first[:, None] >= ends[None, :], lengths_row[None, :], 0), 1)
    stop = jnp.min(jnp.where(ends[None, :] > last[:, None], ends[None, :], 1 << 30), 1)
    return jnp.stack([start // block, (stop + block - 1) // block], 1).reshape(-1)


def whole_vmem():
    return pl.BlockSpec(memory_space=pltpu.VMEM)


def swap(blocks, axis):
    size = lax.axis_size(axis)
    return [
        x if k == 0 else lax.ppermute(x, axis, [(i, i ^ k) for i in range(size)])
        for k, x in enumerate(blocks)
    ]


def unscramble(x, index, axis):
    count, bit = x.shape[axis], 1
    while bit < count:
        shape = x.shape
        y = x.reshape(shape[:axis] + (count // (2 * bit), 2, bit) + shape[axis + 1 :])
        flipped = jnp.flip(y, axis + 1)
        x = jnp.where((index & bit) != 0, flipped, y).reshape(shape)
        bit *= 2
    return x


def project_body(blocks, pairs, heads, extra, place_ref, c_ref, shift_ref, w_ref, *refs):
    groups = len(refs) - blocks - 1
    tokens, outs, kept = refs[:groups], refs[groups:-1], refs[-1]
    micro, rows, width = tokens[0].shape
    end = 192 * heads
    weights = [w_ref[:, c : min(c + 128, end)] for c in range(0, end, 128)]
    order = list(range(micro))[::-1]
    z_qk = z_v = None
    for m in order:
        a = jnp.concatenate(
            [(x[m].astype(F32) * c_ref[m][None] + shift_ref[m][None]).astype(BF) for x in tokens], 0
        )
        parts = [jnp.dot(a, w, preferred_element_type=F32).astype(BF) for w in weights]
        v = jnp.concatenate(parts[heads:], 1)
        if extra and m == micro - 1:
            z_qk = parts[heads - 1]
            z_v = v[:, (heads - 1) * 64 : heads * 64]
        for h in range(heads):
            pair = m * heads + h
            if pair >= blocks:
                continue
            kept[pair, :, :128] = parts[h]
            own_v = v[:, h * 64 : (h + 1) * 64]
            if extra:
                kept[pair, :, 128:256] = z_qk
                kept[pair, :, 256:] = jnp.concatenate([own_v, z_v], 1)
            else:
                kept[pair, :, 128:] = jnp.concatenate([own_v, jnp.zeros_like(own_v)], 1)
    for pair in range(pairs, blocks):
        kept[pair] = jnp.zeros(kept.shape[1:], BF)
    for j in range(blocks):
        outs[j][...] = kept[place_ref[1] ^ j]


def turn_tables(cos, sin, extra):
    lane = lax.broadcasted_iota(jnp.int32, cos.shape, 1)
    low = lane < 64
    cos_r, sin_r = pltpu.roll(cos, 64, 1), pltpu.roll(sin, 64, 1)
    tables = [(jnp.where(low, cos, cos_r), jnp.where(low, sin, sin_r))]
    if extra:
        tables.append((jnp.where(low, cos_r, cos), jnp.where(low, sin_r, sin)))
    return tables


def turn(x, table):
    lane = lax.broadcasted_iota(jnp.int32, x.shape, 1)
    swapped = jnp.where(lane % 64 < 32, pltpu.roll(x, 96, 1), pltpu.roll(x, 32, 1))
    return x * table[0] + swapped * table[1]


def rotate_in_body(blocks, extra, place_ref, cos_ref, sin_ref, *refs):
    ins, outs = refs[:blocks], refs[blocks : 2 * blocks - blocks + (6 if extra else 3)]
    kept = refs[-1]
    rows = ins[0].shape[0]
    for j in range(blocks):
        at = pl.multiple_of((place_ref[1] ^ j) * rows, rows)
        kept[pl.ds(at, rows), :] = ins[j][...]
    tables = turn_tables(cos_ref[...], sin_ref[...], extra)
    x0 = turn(kept[:, :128].astype(F32), tables[0])
    outs[0][...] = (x0[:, :64] * 0.125).astype(BF)
    outs[1][...] = x0[:, 64:].astype(BF)
    if extra:
        outs[2][...] = kept[:, 256:320]
        x1 = turn(kept[:, 128:256].astype(F32), tables[1])
        outs[3][...] = (x1[:, :64] * 0.125).astype(BF)
        outs[4][...] = x1[:, 64:].astype(BF)
        outs[5][...] = kept[:, 320:]
    else:
        outs[2][...] = kept[:, 128:192]


def rotate_out_body(blocks, extra, place_ref, cos_ref, sin_ref, *refs):
    count = 6 if extra else 3
    ins, outs, kept = refs[:count], refs[count:-1], refs[-1]
    rows = outs[0].shape[0]
    parts = [ref[...].astype(F32) for ref in ins]
    tables = [(c, -s) for c, s in turn_tables(cos_ref[...], sin_ref[...], extra)]
    kept[:, :128] = turn(jnp.concatenate(parts[:2], 1), tables[0]).astype(BF)
    if extra:
        kept[:, 128:256] = turn(jnp.concatenate(parts[3:5], 1), tables[1]).astype(BF)
        kept[:, 256:] = jnp.concatenate([parts[2], parts[5]], 1).astype(BF)
    else:
        kept[:, 128:] = jnp.concatenate([parts[2], jnp.zeros_like(parts[2])], 1).astype(BF)
    for j in range(blocks):
        at = pl.multiple_of((place_ref[1] ^ j) * rows, rows)
        outs[j][...] = kept[pl.ds(at, rows), :]


def project_back_body(blocks, pairs, heads, extra, place_ref, c_ref, shift_ref, w_ref, *refs):
    kept = refs[-1]
    groups = (len(refs) - blocks - 4) // 2
    tokens, ins = refs[:groups], refs[groups : groups + blocks]
    outs = refs[groups + blocks : 2 * groups + blocks]
    grad_ref, sum_ref, dot_ref = refs[2 * groups + blocks : -1]
    micro, rows, width = tokens[0].shape
    count = groups * rows
    for j in range(blocks):
        kept[place_ref[1] ^ j] = ins[j][...]
    last = None
    if extra:
        last = jnp.zeros((count, 256), F32)
        for j in range(blocks):
            last = last + kept[j, :, 128:].astype(F32)
        last = last.astype(BF)
    all_a, all_g = [], []
    for m in range(micro):
        n = jnp.concatenate([x[m] for x in tokens], 0).astype(F32)
        a = (n * c_ref[m][None] + shift_ref[m][None]).astype(BF)
        qk, v = [], []
        for h in range(heads):
            pair = m * heads + h
            if pair < blocks:
                qk.append(kept[pair, :, :128])
                at = 256 if extra else 128
                v.append(kept[pair, :, at : at + 64])
            else:
                qk.append(last[:, :128])
                v.append(last[:, 192:])
        g = jnp.concatenate(qk + v, 1)
        da = lax.dot_general(g, w_ref[:, : 192 * heads], (((1,), (1,)), ((), ())), preferred_element_type=F32)
        for k in range(groups):
            outs[k][m] = da[k * rows : (k + 1) * rows].astype(BF)
        sum_ref[m : m + 1] = jnp.sum(da, 0, keepdims=True)
        dot_ref[m : m + 1] = jnp.sum(da * n, 0, keepdims=True)
        all_a.append(a)
        all_g.append(g)
    grad_ref[...] = lax.dot_general(
        jnp.concatenate(all_a, 0), jnp.concatenate(all_g, 0), (((0,), (0,)), ((), ())),
        preferred_element_type=F32,
    ).astype(BF)


def norm(values):
    centered = values - jnp.mean(values, -1, keepdims=True)
    inverse = lax.rsqrt(jnp.mean(centered * centered, -1, keepdims=True) + 1e-05)
    return centered * inverse, inverse


def by_micro(ref, rows):
    return jnp.concatenate(
        [jnp.broadcast_to(ref[m][None], (rows, ref.shape[1])) for m in range(ref.shape[0])], 0
    )


def middle_body(
    groups, blocks, heads, micro, rows, stripe,
    came_ref, out_ref, x_ref, gate_ref, c_ref, shift_ref,
    merged_ref, attn_ref, middle_ref, second_ref,
):
    width = x_ref.shape[1]
    for u in range(groups):
        for m in range(micro):
            for h in range(heads):
                pair = m * heads + h
                lanes = slice((u * heads + h) * 64, (u * heads + h + 1) * 64)
                half = rows // 2
                if pair < blocks and stripe:
                    at = m * rows
                    merged_ref[at : at + half, lanes] = came_ref[u * blocks + pair, :half, :64]
                    merged_ref[at + half : at + rows, lanes] = came_ref[u * blocks + pair, :half, 64:]
                elif pair < blocks:
                    merged_ref[m * rows : (m + 1) * rows, lanes] = came_ref[u * blocks + pair]
                else:
                    for b in range(blocks):
                        at = m * rows + b * stripe
                        merged_ref[at : at + stripe, lanes] = came_ref[u * blocks + b, half:, :64]
    attn = jnp.dot(merged_ref[...], out_ref[...].reshape(width, width), preferred_element_type=F32)
    attn_ref[...] = attn
    middle = x_ref[...].astype(F32) + by_micro(gate_ref, rows) * attn
    middle_ref[...] = middle
    normed, _ = norm(middle)
    second_ref[...] = (normed * by_micro(c_ref, rows) + by_micro(shift_ref, rows)).astype(BF)


def gelu_pair(u):
    t = jnp.tanh(0.7978845608028654 * (u + 0.044715 * u * u * u))
    value = 0.5 * u * (1.0 + t)
    slope = 0.5 * (1.0 + t) + 0.5 * u * (1.0 - t * t) * (
        0.7978845608028654 * (1.0 + 0.134145 * u * u)
    )
    return value, slope


NT = (((1,), (1,)), ((), ()))
TN = (((0,), (0,)), ((), ()))


def feed_body(
    groups, blocks, heads, micro, rows, stripe,
    ex_ref, re_ref, out_w_ref, ex_bias_ref, re_bias_ref, second_ref, middle_ref, attn_ref, dy_ref,
    gate1_ref, gate2_ref, c_ref,
    layer_ref, grad_ref, dattn_ref, do_ref, sums_ref,
    branch_sum, back_sum, dm_sum, do_sum,
):
    step = pl.program_id(0)
    width = middle_ref.shape[1]

    @pl.when(step == 0)
    def _():
        branch_sum[...] = jnp.zeros_like(branch_sum)
        back_sum[...] = jnp.zeros_like(back_sum)
        dm_sum[...] = (by_micro(gate2_ref, rows) * dy_ref[...].astype(F32)).astype(BF)

    expand = ex_ref[...].reshape(width, width)
    reduce = re_ref[...].reshape(width, width)
    u = jnp.dot(second_ref[...], expand, preferred_element_type=F32) + ex_bias_ref[0]
    g, slope = gelu_pair(u)
    branch_sum[...] += jnp.dot(g.astype(BF), reduce, preferred_element_type=F32)
    dg = lax.dot_general(dm_sum[...], reduce, NT, preferred_element_type=F32)
    du = (dg * slope).astype(BF)
    back_sum[...] += lax.dot_general(du, expand, NT, preferred_element_type=F32)

    @pl.when(step == pl.num_programs(0) - 1)
    def _():
        def total(at, x):
            for m in range(micro):
                sums_ref[at * micro + m : at * micro + m + 1] = jnp.sum(
                    x[m * rows : (m + 1) * rows], 0, keepdims=True
                )

        branch = branch_sum[...] + re_bias_ref[...]
        middle = middle_ref[...]
        dy = dy_ref[...].astype(F32)
        layer_ref[...] = (middle + by_micro(gate2_ref, rows) * branch).astype(BF)
        total(0, dy * branch)
        normed, inverse = norm(middle)
        db = back_sum[...]
        total(1, db)
        total(2, db * normed)
        e = db * by_micro(c_ref, rows)
        grad = dy + inverse * (
            e
            - jnp.mean(e, -1, keepdims=True)
            - normed * jnp.mean(e * normed, -1, keepdims=True)
        )
        grad_ref[...] = grad
        total(3, grad * attn_ref[...])
        total(4, dm_sum[...].astype(F32))
        dattn = (by_micro(gate1_ref, rows) * grad).astype(BF)
        dattn_ref[...] = dattn
        do_sum[...] = lax.dot_general(
            dattn, out_w_ref[...].reshape(width, width), NT, preferred_element_type=F32
        ).astype(BF)
        for at in range(groups):
            for m in range(micro):
                for h in range(heads):
                    pair = m * heads + h
                    lanes = slice((at * heads + h) * 64, (at * heads + h + 1) * 64)
                    half, top = rows // 2, m * rows
                    if pair < blocks and stripe:
                        do_ref[at * blocks + pair, :half, :64] = do_sum[top : top + half, lanes]
                        do_ref[at * blocks + pair, :half, 64:] = do_sum[top + half : top + rows, lanes]
                    elif pair < blocks:
                        do_ref[at * blocks + pair] = do_sum[top : top + rows, lanes]
                    else:
                        for b in range(blocks):
                            do_ref[at * blocks + b, half:, :64] = do_sum[top : top + stripe, lanes]
                            do_ref[at * blocks + b, half:, 64:] = jnp.zeros((stripe, 64), BF)
                            top += stripe
            for b in range(micro * heads, blocks):
                do_ref[at * blocks + b] = jnp.zeros((rows, 64), BF)


def feed_weights_body(rows, place_ref, ex_ref, re_ref, bias_ref, gate_ref, *refs):
    groups = (len(refs) - 3) // 2
    reduce_ref, expand_ref, sum_ref = refs[2 * groups :]
    width = refs[0].shape[-1]
    second = jnp.concatenate([x[...] for x in refs[:groups]], 0)
    gate = by_micro(gate_ref, rows)
    dm = jnp.concatenate(
        [(gate * x[...].astype(F32)).astype(BF) for x in refs[groups : 2 * groups]], 0
    )
    expand = ex_ref[...].reshape(width, width)
    reduce = re_ref[...].reshape(width, width)
    u = jnp.dot(second, expand, preferred_element_type=F32) + bias_ref[0]
    g, slope = gelu_pair(u)
    du = lax.dot_general(dm, reduce, NT, preferred_element_type=F32) * slope
    du = du.astype(BF)
    sum_ref[...] = jnp.sum(du.astype(F32), 0, keepdims=True)
    reduce_ref[...] = lax.dot_general(g.astype(BF), dm, TN, preferred_element_type=F32).astype(BF)
    expand_ref[...] = lax.dot_general(second, du, TN, preferred_element_type=F32).astype(BF)


def attend_body(block, range_ref, q_ref, sq_ref, k_ref, v_ref, sk_ref, o_ref, lse_ref):
    i = pl.program_id(0)
    q, sq = q_ref[...], sq_ref[0]
    count, width = q.shape

    def step(j, carry):
        high, total, acc = carry
        at = pl.ds(pl.multiple_of(j * block, block), block)
        k, v, sk = k_ref[at, :], v_ref[at, :], sk_ref[at, :]
        s = lax.dot_general(k, q, (((1,), (1,)), ((), ())), preferred_element_type=F32)
        s = jnp.where(sk == sq, s, NEG)
        new = jnp.maximum(high, jnp.max(s, 0, keepdims=True))
        p = jnp.exp(s - new)
        fix = jnp.exp(high - new)
        total = total * fix + jnp.sum(p, 0, keepdims=True)
        acc = acc * fix + lax.dot_general(
            v, p.astype(BF), (((0,), (0,)), ((), ())), preferred_element_type=F32
        )
        return new, total, acc

    first = (
        jnp.full((1, count), NEG, F32),
        jnp.zeros((1, count), F32),
        jnp.zeros((width, count), F32),
    )
    high, total, acc = lax.fori_loop(range_ref[2 * i], range_ref[2 * i + 1], step, first)
    o_ref[...] = (acc / total).T.astype(BF)
    lse_ref[0] = high + jnp.log(total)


def attend_back_body(
    block, range_ref, q_ref, sq_ref, lse_ref, o_ref, do_ref, k_ref, v_ref, sk_ref,
    dq_ref, dk_ref, dv_ref, dk_sum, dv_sum,
):
    i = pl.program_id(0)

    @pl.when(i == 0)
    def _():
        dk_sum[...] = jnp.zeros_like(dk_sum)
        dv_sum[...] = jnp.zeros_like(dv_sum)

    q, sq, lse, do = q_ref[...], sq_ref[0], lse_ref[0], do_ref[...]
    count, width = q.shape
    delta = jnp.sum((do.astype(F32) * o_ref[...].astype(F32)).T, 0, keepdims=True)

    def step(j, dq):
        at = pl.ds(pl.multiple_of(j * block, block), block)
        k, v, sk = k_ref[at, :], v_ref[at, :], sk_ref[at, :]
        s = lax.dot_general(k, q, (((1,), (1,)), ((), ())), preferred_element_type=F32)
        p = jnp.where(sk == sq, jnp.exp(s - lse), 0.0)
        dp = lax.dot_general(v, do, (((1,), (1,)), ((), ())), preferred_element_type=F32)
        ds = (p * (dp - delta)).astype(BF)
        dv_sum[at, :] += jnp.dot(p.astype(BF), do, preferred_element_type=F32)
        dk_sum[at, :] += jnp.dot(ds, q, preferred_element_type=F32)
        return dq + lax.dot_general(
            k, ds, (((0,), (0,)), ((), ())), preferred_element_type=F32
        )

    dq = lax.fori_loop(
        range_ref[2 * i], range_ref[2 * i + 1], step, jnp.zeros((width, count), F32)
    )
    dq_ref[...] = (dq * 0.125).T.astype(BF)

    @pl.when(i == pl.num_programs(0) - 1)
    def _():
        dk_ref[...] = dk_sum[...].astype(BF)
        dv_ref[...] = dv_sum[...].astype(BF)


def attend(ranges, q, sq, k, v, sk, rows, block):
    count, width = q.shape
    steps = count // rows
    size = k.shape[0]
    by_row = pl.BlockSpec((rows, width), lambda i, r: (i, 0))
    as_row = pl.BlockSpec((1, 1, rows), lambda i, r: (i, 0, 0))
    return pl.pallas_call(
        functools.partial(attend_body, block),
        grid_spec=pltpu.PrefetchScalarGridSpec(
            num_scalar_prefetch=1,
            grid=(steps,),
            in_specs=[by_row, as_row, whole_vmem(), whole_vmem(), whole_vmem()],
            out_specs=[by_row, as_row],
        ),
        out_shape=[
            jax.ShapeDtypeStruct((count, width), BF),
            jax.ShapeDtypeStruct((steps, 1, rows), F32),
        ],
        cost_estimate=pl.CostEstimate(
            flops=count * size * width, transcendentals=count * size // 4, bytes_accessed=4 * size * width
        ),
        name="attend",
    )(ranges, q, sq.reshape(steps, 1, rows), k, v, sk)


def attend_back(ranges, q, sq, lse, o, do, k, v, sk, rows, block):
    count, width = q.shape
    steps = count // rows
    size = k.shape[0]
    by_row = pl.BlockSpec((rows, width), lambda i, r: (i, 0))
    as_row = pl.BlockSpec((1, 1, rows), lambda i, r: (i, 0, 0))
    return pl.pallas_call(
        functools.partial(attend_back_body, block),
        grid_spec=pltpu.PrefetchScalarGridSpec(
            num_scalar_prefetch=1,
            grid=(steps,),
            in_specs=[by_row, as_row, as_row, by_row, by_row, whole_vmem(), whole_vmem(), whole_vmem()],
            out_specs=[by_row, whole_vmem(), whole_vmem()],
            scratch_shapes=[pltpu.VMEM((size, width), F32)] * 2,
        ),
        out_shape=[
            jax.ShapeDtypeStruct((count, width), BF),
            jax.ShapeDtypeStruct((size, width), BF),
            jax.ShapeDtypeStruct((size, width), BF),
        ],
        cost_estimate=pl.CostEstimate(
            flops=3 * count * size * width, transcendentals=count * size // 4, bytes_accessed=8 * size * width
        ),
        name="attend_back",
    )(ranges, q, sq.reshape(steps, 1, rows), lse, o, do, k, v, sk)


def spread(ref, at, rows):
    return ref[pl.ds(pl.multiple_of(at, rows), rows), :]


def keys_mask(low, high, at, count):
    position = at + lax.broadcasted_iota(jnp.int32, (count, low.shape[1]), 0)
    return (position >= low) & (position < high)


QB, KB = 256, 512


def attend_all_body(
    blocks, groups, rows, stripe,
    place_ref, range_ref, last_range_ref, low_ref, high_ref, last_low_ref, last_high_ref, cos_ref, sin_ref, *refs,
):
    ins = refs[:blocks]
    message, q_ref, k_ref, v_ref, zq_ref, zk_ref, zv_ref, o_ref, zo_ref, lse_ref, zlse_ref = refs[blocks : blocks + 11]
    kept, wide, scores = refs[blocks + 11 :]
    span = blocks * rows
    size = groups * span
    me_u, me_b = place_ref[0], place_ref[1]
    for g in range(groups):
        for j in range(blocks):
            kept[pl.ds(pl.multiple_of((me_b ^ j) * rows, rows), rows), :] = spread(ins[j], (me_u ^ g) * rows, rows)
        at = slice(g * span, (g + 1) * span)
        cos, sin = cos_ref[at], sin_ref[at]
        tables = turn_tables(cos, sin, True)
        x = turn(kept[:, :128].astype(F32), tables[0])
        q_ref[at] = (x[:, :64] * 0.125).astype(BF)
        k_ref[at] = x[:, 64:].astype(BF)
        v_ref[at] = kept[:, 256:320]
        x = turn(kept[:, 128:256].astype(F32), tables[1])
        wide[at] = x[:, :64] * 0.125
        zk_ref[at] = x[:, 64:].astype(BF)
        zv_ref[at] = kept[:, 320:]
    tail = slice(size, size + KB - QB)
    for ref in (k_ref, v_ref, zk_ref, zv_ref):
        ref[tail] = jnp.zeros((KB - QB, 64), BF)
    devices = groups * blocks
    for d in range(0, devices, 2):
        zq_ref[d * stripe : (d + 2) * stripe] = jnp.concatenate(
            [spread(wide, (d + e) * rows + me_b * stripe, stripe) for e in range(2)], 0
        ).astype(BF)

    def block(q, low, high, first, stop, keys, values):
        count = q.shape[0]

        def score(t, high_s):
            at = pl.multiple_of((first + 2 * t) * QB, QB)
            s = lax.dot_general(keys[pl.ds(at, KB), :], q, NT, preferred_element_type=F32)
            s = jnp.where(keys_mask(low, high, at, KB), s, NEG)
            scores[t, :, :count] = s
            return jnp.maximum(high_s, jnp.max(s, 0, keepdims=True))

        steps = (stop - first + 1) // 2
        top = lax.fori_loop(0, steps, score, jnp.full((1, count), NEG, F32))

        def weigh(t, carry):
            total, acc = carry
            at = pl.multiple_of((first + 2 * t) * QB, QB)
            p = jnp.exp(scores[t, :, :count] - top)
            return total + jnp.sum(p, 0, keepdims=True), acc + lax.dot_general(
                values[pl.ds(at, KB), :], p.astype(BF), TN, preferred_element_type=F32
            )

        total, acc = lax.fori_loop(
            0, steps, weigh, (jnp.zeros((1, count), F32), jnp.zeros((64, count), F32))
        )
        return (acc / total).T, top + jnp.log(total)

    half = rows // 2

    def run(i, _):
        o, lse = block(
            spread(q_ref, i * QB, QB), low_ref[i], high_ref[i], range_ref[2 * i], range_ref[2 * i + 1], k_ref, v_ref
        )
        o = o.astype(BF)
        o_ref[pl.ds(pl.multiple_of(i * QB, QB), QB), :] = o
        lse_ref[i] = lse
        for d in range(QB // rows):
            message[i * (QB // rows) + d, :half] = jnp.concatenate(
                [o[d * rows : d * rows + half], o[d * rows + half : (d + 1) * rows]], 1
            )
        return 0

    lax.fori_loop(0, size // QB, run, 0)
    few = zlse_ref.shape[2]

    def run_last(i, _):
        o, lse = block(
            spread(zq_ref, i * few, few), last_low_ref[i], last_high_ref[i],
            last_range_ref[2 * i], last_range_ref[2 * i + 1], zk_ref, zv_ref,
        )
        zo_ref[pl.ds(pl.multiple_of(i * few, few), few), :] = o.astype(BF)
        zlse_ref[i] = lse
        o = jnp.concatenate([o, jnp.zeros_like(o)], 1)
        for d in range(few // stripe):
            message[i * (few // stripe) + d, half:] = o[d * stripe : (d + 1) * stripe].astype(BF)
        return 0

    lax.fori_loop(0, zlse_ref.shape[0], run_last, 0)


def attend_all_back_body(
    blocks, groups, rows, stripe,
    place_ref, range_ref, last_range_ref, low_ref, high_ref, last_low_ref, last_high_ref, cos_ref, sin_ref,
    do_ref, q_ref, k_ref, v_ref, zq_ref, zk_ref, zv_ref, o_ref, zo_ref, lse_ref, zlse_ref, *refs,
):
    outs = refs[:blocks]
    kept, dq, dk, dv, zdq, zdk, zdv = refs[blocks:]
    span = blocks * rows
    size = groups * span
    half = rows // 2
    me_u, me_b = place_ref[0], place_ref[1]
    for ref in (dk, dv, zdq, zdk, zdv):
        ref[...] = jnp.zeros_like(ref)

    def block(q, do, o, lse, low, high, first, stop, keys, values, dk_sum, dv_sum):
        count = q.shape[0]
        delta = jnp.sum((do.astype(F32) * o.astype(F32)).T, 0, keepdims=True)

        def step(t, dq):
            at = pl.multiple_of((first + 2 * t) * QB, QB)
            here = pl.ds(at, KB)
            k, v = keys[here, :], values[here, :]
            s = lax.dot_general(k, q, NT, preferred_element_type=F32)
            dp = lax.dot_general(v, do, NT, preferred_element_type=F32)
            p = jnp.where(keys_mask(low, high, at, KB), jnp.exp(s - lse), 0.0)
            ds = (p * (dp - delta)).astype(BF)
            dv_sum[here, :] += jnp.dot(p.astype(BF), do, preferred_element_type=F32)
            dk_sum[here, :] += jnp.dot(ds, q, preferred_element_type=F32)
            return dq + lax.dot_general(k, ds, TN, preferred_element_type=F32)

        return (
            lax.fori_loop(0, (stop - first + 1) // 2, step, jnp.zeros((64, count), F32)) * 0.125
        ).T

    def run(i, _):
        came = []
        for d in range(QB // rows):
            x = do_ref[i * (QB // rows) + d]
            came += [x[:half, :64], x[:half, 64:]]
        at = pl.ds(pl.multiple_of(i * QB, QB), QB)
        dq[at, :] = block(
            q_ref[at, :], jnp.concatenate(came, 0), o_ref[at, :], lse_ref[i], low_ref[i], high_ref[i],
            range_ref[2 * i], range_ref[2 * i + 1], k_ref, v_ref, dk, dv,
        )
        return 0

    lax.fori_loop(0, size // QB, run, 0)
    few = zlse_ref.shape[2]

    def run_last(i, _):
        came = [
            do_ref[i * (few // stripe) + d].astype(F32)[half:, :64] for d in range(few // stripe)
        ]
        at = pl.ds(pl.multiple_of(i * few, few), few)
        x = block(
            zq_ref[at, :], jnp.concatenate(came, 0).astype(BF), zo_ref[at, :], zlse_ref[i],
            last_low_ref[i], last_high_ref[i], last_range_ref[2 * i], last_range_ref[2 * i + 1],
            zk_ref, zv_ref, zdk, zdv,
        )
        for d in range(few // stripe):
            to = (i * (few // stripe) + d) * rows + me_b * stripe
            zdq[pl.ds(pl.multiple_of(to, stripe), stripe), :] = x[d * stripe : (d + 1) * stripe]
        return 0

    lax.fori_loop(0, zlse_ref.shape[0], run_last, 0)
    for g in range(groups):
        at = slice(g * span, (g + 1) * span)
        tables = [(c, -s) for c, s in turn_tables(cos_ref[at], sin_ref[at], True)]
        kept[:, :128] = turn(jnp.concatenate([dq[at], dk[at]], 1), tables[0]).astype(BF)
        kept[:, 128:256] = turn(jnp.concatenate([zdq[at], zdk[at]], 1), tables[1]).astype(BF)
        kept[:, 256:] = jnp.concatenate([dv[at], zdv[at]], 1).astype(BF)
        for j in range(blocks):
            outs[j][pl.ds(pl.multiple_of((me_u ^ g) * rows, rows), rows), :] = spread(kept, (me_b ^ j) * rows, rows)


def on_device(
    tokens,
    cotangent,
    lengths,
    time_step,
    modulate_weight,
    modulate_bias,
    attend_gain,
    input_weight,
    output_weight,
    feed_gain,
    expand_weight,
    expand_bias,
    reduce_weight,
    reduce_bias,
):
    groups, blocks = lax.axis_size("ulysses"), lax.axis_size("blk")
    group_id, block_id = lax.axis_index("ulysses"), lax.axis_index("blk")
    devices = groups * blocks
    micro, rows, width = tokens.shape
    own = micro * rows
    size = devices * rows
    head_width = width // HEADS
    heads = HEADS // groups
    pairs = micro * heads
    extra = pairs > blocks
    lanes = 384 if extra else 256
    stripe = rows // blocks if extra else 0
    mod_rows = modulate_weight.shape[0]
    gain_rows = attend_gain.shape[0]
    ff_rows = expand_bias.shape[0]
    ff = ff_rows * devices
    folds = ff // width
    assert pairs <= blocks + 1 and head_width == 64 and folds == groups and heads == 3
    place = jnp.stack([group_id, block_id]).astype(jnp.int32)
    pair_micro = jnp.minimum(block_id // heads, micro - 1)

    values = tokens.astype(F32)
    n1, r1 = norm(values)
    n1_b = n1.astype(BF)
    n1_group = swap([n1_b] * groups, "ulysses")
    in_split = input_weight.reshape(gain_rows, 3, groups, heads, head_width)
    in_split = jnp.concatenate(
        [
            in_split[:, :2].transpose(2, 0, 3, 1, 4).reshape(groups, 1, gain_rows, -1),
            in_split[:, 2].transpose(1, 0, 2, 3).reshape(groups, 1, gain_rows, -1),
        ],
        3,
    )
    in_lanes = heads * 3 * head_width

    condition = time_features(time_step, modulate_weight.shape[1] // 2)
    mod_own = jnp.einsum(
        "mc,fc->mf", condition, modulate_weight, preferred_element_type=F32
    ) + modulate_bias.astype(F32)
    small = jnp.concatenate(
        [
            mod_own.reshape(-1),
            attend_gain.astype(F32),
            feed_gain.astype(F32),
            reduce_bias.astype(F32),
            expand_bias.astype(F32),
        ]
    )
    small_lanes = 64 * -(-small.shape[0] // (32 * gain_rows))
    small = jnp.pad(small, (0, small_lanes * gain_rows // 2 - small.shape[0]))
    small_high = small.astype(BF)
    small_low = (small - lax.reduce_precision(small, 8, 7)).astype(BF)
    small = jnp.concatenate([small_high, small_low]).reshape(1, 1, gain_rows, small_lanes)
    came = exchange(
        jnp.concatenate(
            [
                jnp.broadcast_to(in_split, (groups, blocks) + in_split.shape[2:]),
                jnp.broadcast_to(small, (groups, blocks) + small.shape[2:]),
            ],
            3,
        ).reshape(devices, gain_rows, in_lanes + small_lanes)
    )
    small_all = came[:, :, in_lanes:].astype(F32).reshape(devices, 2, -1)
    small_all = small_all[:, 0] + small_all[:, 1]
    in_own = came.reshape(width, in_lanes + small_lanes)

    weight_pack = jnp.concatenate(
            [
                reduce_weight,
                output_weight,
                expand_weight.reshape(gain_rows, folds, width).transpose(1, 0, 2).reshape(-1, width),
            ],
            0,
        )
    weight_pack, in_own = lax.optimization_barrier((weight_pack, in_own))
    gathered = lax.all_gather(weight_pack, ALL, axis=0, tiled=False)
    unit = gain_rows
    while unit % 8:
        unit *= 2
    units = width // unit
    if unit != gain_rows:
        gathered = jnp.concatenate(
            [gathered[:, :ff_rows].reshape(units, -1, width)]
            + [
                gathered[:, at : at + gain_rows].reshape(units, unit, width)
                for at in range(ff_rows, ff_rows + (folds + 1) * gain_rows, gain_rows)
            ],
            1,
        )
    wide = unit * folds

    at = micro * mod_rows
    mods = small_all[:, :at].reshape(devices, micro, mod_rows).transpose(1, 0, 2).reshape(micro, -1)
    gain1 = small_all[:, at : at + gain_rows].reshape(-1)
    at += gain_rows
    gain2 = small_all[:, at : at + gain_rows].reshape(-1)
    at += gain_rows
    reduce_bias_f = small_all[:, at : at + gain_rows].reshape(1, -1)
    at += gain_rows
    expand_bias_f = small_all[:, at : at + ff_rows].reshape(folds, 1, width)
    shift1, scale1, gate1, shift2, scale2, gate2 = jnp.split(mods, 6, 1)
    c1 = gain1 * (1.0 + scale1)
    c2 = gain2 * (1.0 + scale2)

    index = jnp.arange(size, dtype=jnp.int32)
    pair_lengths = lax.dynamic_index_in_dim(lengths, pair_micro, 0, keepdims=False)
    segment, position = doc_layout(index, pair_lengths)
    last_lengths = lengths[micro - 1]
    last_segment, last_position = doc_layout(index, last_lengths)
    half = head_width // 2
    freqs = jnp.exp(-math.log(10000.0) * jnp.arange(half, dtype=F32) / half)
    lane = jnp.arange(128)
    angles = jnp.where(
        (lane < 64)[None, :], position.astype(F32)[:, None], last_position.astype(F32)[:, None]
    ) * jnp.tile(freqs, 4)[None, :]
    cos_table = jnp.cos(angles)
    sin_table = jnp.where((lane % 64 < 32)[None, :], -1.0, 1.0) * jnp.sin(angles)
    query_rows = math.gcd(size, 256)
    key_block = math.gcd(size, 256)
    first = jnp.arange(size // query_rows, dtype=jnp.int32) * query_rows
    ranges = key_ranges(first, first + query_rows - 1, pair_lengths, key_block)
    small_path = extra and size % KB == 0 and rows % 16 == 0 and stripe % 8 == 0 and size <= 4096

    count = groups * rows
    striped = lambda x: lax.dynamic_slice_in_dim(
        x.reshape((devices, rows) + x.shape[1:]), block_id * stripe, stripe, 1
    ).reshape((devices * stripe,) + x.shape[1:])
    smem = pl.BlockSpec(memory_space=pltpu.SMEM)
    outgoing = pl.pallas_call(
        functools.partial(project_body, blocks, pairs, heads, extra),
        out_shape=[jax.ShapeDtypeStruct((count, lanes), BF)] * blocks,
        in_specs=[smem] + [whole_vmem()] * (3 + groups),
        out_specs=[whole_vmem()] * blocks,
        scratch_shapes=[pltpu.VMEM((blocks, count, lanes), BF)],
        cost_estimate=pl.CostEstimate(
            flops=2 * micro * count * width * 3 * 64 * heads, transcendentals=0, bytes_accessed=8 * own * width
        ),
        name="project",
    )(place, c1, shift1, in_own, *n1_group)
    incoming = swap(outgoing, "blk")

    span = blocks * rows
    by_span = pl.BlockSpec((span, 64), lambda i, p: (i ^ p[0], 0))
    table_spec = pl.BlockSpec((span, 128), lambda i, p: (i ^ p[0], 0))
    by_rows = pl.BlockSpec((rows, lanes), lambda i, p: (i, 0))
    parts = 6 if extra else 3
    if small_path:
        last_rows = 128
        chunk = last_rows // stripe
        last_first = jnp.arange(devices // chunk, dtype=jnp.int32) * (chunk * rows) + block_id * stripe
        last_ranges = key_ranges(
            last_first, last_first + (chunk - 1) * rows + stripe - 1, last_lengths, QB
        )
        bounds = []
        for where, lens, pick, lump in (
            (position, pair_lengths, lambda x: x, QB),
            (last_position, last_lengths, striped, last_rows),
        ):
            low = index - where
            ends = jnp.cumsum(lens)
            high = jnp.min(jnp.where(ends[None, :] > index[:, None], ends[None, :], 1 << 30), 1)
            bounds += [pick(low).reshape(-1, 1, lump), pick(high).reshape(-1, 1, lump)]
        whole = lambda *shape: jax.ShapeDtypeStruct(shape, BF)
        saved_shapes = [
            whole(size, 64), whole(size + KB - QB, 64), whole(size + KB - QB, 64),
            whole(devices * stripe, 64), whole(size + KB - QB, 64), whole(size + KB - QB, 64),
            whole(size, 64), whole(devices * stripe, 64),
            jax.ShapeDtypeStruct(bounds[0].shape, F32), jax.ShapeDtypeStruct(bounds[2].shape, F32),
        ]
        attend_args = (place, ranges, last_ranges, *bounds, cos_table, sin_table)
        specs = [smem] * 3 + [whole_vmem()] * 6
        message, *saved = pl.pallas_call(
            functools.partial(attend_all_body, blocks, groups, rows, stripe),
            in_specs=specs + [whole_vmem()] * blocks,
            out_specs=[whole_vmem()] * 11,
            out_shape=[whole(devices, rows // 2 + stripe, 128)] + saved_shapes,
            scratch_shapes=[
                pltpu.VMEM((span, lanes), BF),
                pltpu.VMEM((size, 64), F32),
                pltpu.VMEM((size // KB + 1, KB, QB), F32),
            ],
            cost_estimate=pl.CostEstimate(
                flops=size * size * 64, transcendentals=size * size // 2, bytes_accessed=16 * size * 128
            ),
            name="attend_all",
        )(*attend_args, *incoming)
    else:
        assert not extra
        turned = pl.pallas_call(
            functools.partial(rotate_in_body, blocks, extra),
            grid_spec=pltpu.PrefetchScalarGridSpec(
                num_scalar_prefetch=1,
                grid=(groups,),
                in_specs=[table_spec, table_spec] + [by_rows] * blocks,
                out_specs=[by_span] * parts,
                scratch_shapes=[pltpu.VMEM((span, lanes), BF)],
            ),
            out_shape=[jax.ShapeDtypeStruct((size, 64), BF)] * parts,
            name="rotate_in",
        )(place, cos_table, sin_table, *incoming)
        query, key, value = turned[:3]
        attended, lse = attend(
            ranges, query, segment, key, value, segment[:, None], query_rows, key_block
        )
        message = attended.reshape(devices, rows, head_width)
    came = exchange(message)

    ex_spec = lambda f: pl.BlockSpec((units, unit, width), f)
    flat = pl.BlockSpec((own, width), lambda i: (0, 0))
    vec = lambda n: pl.BlockSpec((n, width), lambda i: (0, 0))
    message_shape = message.shape
    message_spec = pl.BlockSpec(message_shape, lambda i: (0, 0, 0))
    sizes = (groups, blocks, heads, micro, rows, stripe)
    own_f32 = jax.ShapeDtypeStruct((own, width), F32)
    own_bf = jax.ShapeDtypeStruct((own, width), BF)
    merged, attn, middle, second = pl.pallas_call(
        functools.partial(middle_body, *sizes),
        grid=(1,),
        in_specs=[message_spec, ex_spec(lambda i: (0, folds, 0)), flat, vec(micro), vec(micro), vec(micro)],
        out_specs=[flat] * 4,
        out_shape=[own_bf, own_f32, own_f32, own_bf],
        name="middle",
    )(came, gathered, tokens.reshape(own, width), gate1, c2, shift2)
    second_group = swap([second] * groups, "ulysses")
    dy = cotangent.reshape(own, width)
    dy_group = swap([dy] * groups, "ulysses")

    per = width // wide
    layer_output, grad_middle, grad_attn, do_message, sums = pl.pallas_call(
        functools.partial(feed_body, *sizes),
        grid=(folds,),
        in_specs=[
            ex_spec(lambda i: (0, folds + 1 + i, 0)),
            pl.BlockSpec((per, wide, width), lambda i: (i, 0, 0)),
            ex_spec(lambda i: (0, folds, 0)),
            pl.BlockSpec((1, 1, width), lambda i: (i, 0, 0)),
            vec(1),
            flat, flat, flat, flat,
            vec(micro), vec(micro), vec(micro),
        ],
        out_specs=[flat, flat, flat, message_spec, vec(5 * micro)],
        out_shape=[
            own_bf, own_f32, own_bf,
            jax.ShapeDtypeStruct(message_shape, BF),
            jax.ShapeDtypeStruct((5 * micro, width), F32),
        ],
        scratch_shapes=[
            pltpu.VMEM((own, width), F32), pltpu.VMEM((own, width), F32),
            pltpu.VMEM((own, width), BF), pltpu.VMEM((own, width), BF),
        ],
        cost_estimate=pl.CostEstimate(
            flops=8 * own * width * ff, transcendentals=own * ff, bytes_accessed=4 * width * ff
        ),
        name="feed",
    )(gathered, gathered, gathered, expand_bias_f, reduce_bias_f, second, middle, attn, dy, gate1, gate2, c2)
    do_came = exchange(do_message)
    d_gate2, d_shift2, p2, d_gate1, dm_sums = [
        sums[i * micro : (i + 1) * micro] for i in range(5)
    ]

    output_part = lax.dot_general(merged, grad_attn, TN, preferred_element_type=F32).astype(BF)
    output_part = output_part.reshape(groups, width // groups, width)

    flat_p = pl.BlockSpec((own, width), lambda i, p: (0, 0))
    square = pl.BlockSpec((width, width), lambda i, p: (0, 0))
    reduce_part, expand_part, bias_part = pl.pallas_call(
        functools.partial(feed_weights_body, rows),
        grid_spec=pltpu.PrefetchScalarGridSpec(
            num_scalar_prefetch=1,
            grid=(1,),
            in_specs=[
                pl.BlockSpec((units, unit, width), lambda i, p: (0, folds + 1 + p[0], 0)),
                pl.BlockSpec((per, wide, width), lambda i, p: (p[0], 0, 0)),
                pl.BlockSpec((1, 1, width), lambda i, p: (p[0], 0, 0)),
                pl.BlockSpec((micro, width), lambda i, p: (0, 0)),
            ]
            + [flat_p] * (2 * groups),
            out_specs=[square, square, pl.BlockSpec((1, width), lambda i, p: (0, 0))],
        ),
        out_shape=[
            jax.ShapeDtypeStruct((width, width), BF),
            jax.ShapeDtypeStruct((width, width), BF),
            jax.ShapeDtypeStruct((1, width), F32),
        ],
        cost_estimate=pl.CostEstimate(
            flops=10 * own * groups * width * width, transcendentals=own * ff, bytes_accessed=16 * width * width
        ),
        name="feed_weights",
    )(place, gathered, gathered, expand_bias_f, gate2, *second_group, *dy_group)
    feed_part = jnp.concatenate(
        [
            reduce_part.reshape(blocks, ff_rows, width),
            expand_part.reshape(groups, blocks, gain_rows, width)
            .transpose(1, 0, 2, 3)
            .reshape(blocks, groups * gain_rows, width),
        ],
        1,
    )
    do_came, feed_part, output_part = lax.optimization_barrier((do_came, feed_part, output_part))
    output_part = swap(
        [
            lax.dynamic_index_in_dim(output_part, group_id ^ k, 0, keepdims=False)
            for k in range(groups)
        ],
        "ulysses",
    )

    feed_sum = lax.psum_scatter(feed_part, "blk", scatter_dimension=0, tiled=True)[0]
    output_part = sum(x.astype(F32) for x in output_part).astype(BF).reshape(blocks, gain_rows, width)
    output_part = swap(
        [
            lax.dynamic_index_in_dim(output_part, block_id ^ k, 0, keepdims=False)
            for k in range(blocks)
        ],
        "blk",
    )
    if small_path:
        leaving = pl.pallas_call(
            functools.partial(attend_all_back_body, blocks, groups, rows, stripe),
            in_specs=specs + [whole_vmem()] * 11,
            out_specs=[whole_vmem()] * blocks,
            out_shape=[whole(count, lanes)] * blocks,
            scratch_shapes=[pltpu.VMEM((span, lanes), BF), pltpu.VMEM((size, 64), F32)]
            + [pltpu.VMEM((size + KB - QB, 64), F32)] * 2
            + [pltpu.VMEM((size, 64), F32)]
            + [pltpu.VMEM((size + KB - QB, 64), F32)] * 2,
            cost_estimate=pl.CostEstimate(
                flops=2 * size * size * 64, transcendentals=size * size // 2, bytes_accessed=16 * size * 128
            ),
            name="attend_all_back",
        )(*attend_args, do_came, *saved)
    else:
        grads = attend_back(
            ranges, query, segment, lse, attended, do_came.reshape(size, head_width), key, value,
            segment[:, None], query_rows, key_block,
        )
        leaving = pl.pallas_call(
            functools.partial(rotate_out_body, blocks, extra),
            grid_spec=pltpu.PrefetchScalarGridSpec(
                num_scalar_prefetch=1,
                grid=(groups,),
                in_specs=[table_spec, table_spec] + [by_span] * parts,
                out_specs=[by_rows] * blocks,
                scratch_shapes=[pltpu.VMEM((span, lanes), BF)],
            ),
            out_shape=[jax.ShapeDtypeStruct((count, lanes), BF)] * blocks,
            name="rotate_out",
        )(place, cos_table, sin_table, *grads)
    leaving, output_part = lax.optimization_barrier((leaving, output_part))
    output_grad = sum(x.astype(F32) for x in output_part)
    back = swap(leaving, "blk")
    back, feed_sum = lax.optimization_barrier((back, feed_sum))

    reduce_grad = feed_sum[:ff_rows].astype(F32)
    expand_rows = feed_sum[ff_rows:].reshape(groups, gain_rows, width)
    expand_came = jnp.stack(
        swap(
            [
                lax.dynamic_index_in_dim(expand_rows, group_id ^ k, 0, keepdims=False)
                for k in range(groups)
            ],
            "ulysses",
        )
    )
    expand_grad = jnp.concatenate(
        [
            lax.dynamic_index_in_dim(expand_came, group_id ^ k, 0, keepdims=False)
            for k in range(groups)
        ],
        1,
    ).astype(F32)

    returned = pl.pallas_call(
        functools.partial(project_back_body, blocks, pairs, heads, extra),
        out_shape=[jax.ShapeDtypeStruct((micro, rows, width), BF)] * groups
        + [
            jax.ShapeDtypeStruct((width, heads * 3 * head_width), BF),
            jax.ShapeDtypeStruct((micro, width), F32),
            jax.ShapeDtypeStruct((micro, width), F32),
        ],
        in_specs=[smem] + [whole_vmem()] * (3 + groups + blocks),
        out_specs=[whole_vmem()] * (groups + 3),
        scratch_shapes=[pltpu.VMEM((blocks, count, lanes), BF)],
        cost_estimate=pl.CostEstimate(
            flops=4 * micro * count * width * 3 * 64 * heads, transcendentals=0, bytes_accessed=8 * own * width
        ),
        name="project_back",
    )(place, c1, shift1, in_own, *n1_group, *back)
    input_part, d_shift1, p1 = returned[groups:]
    grad_first = sum(x.astype(F32) for x in swap(returned[:groups], "ulysses"))
    e = grad_first * c1[:, None]
    tokens_grad = (
        grad_middle.reshape(micro, rows, width)
        + r1
        * (
            e
            - jnp.mean(e, -1, keepdims=True)
            - n1 * jnp.mean(e * n1, -1, keepdims=True)
        )
    ).astype(BF)

    grad_mods = jnp.concatenate(
        [d_shift1, p1 * gain1, d_gate1, d_shift2, p2 * gain2, d_gate2], 1
    )
    gain1_part = jnp.sum((1.0 + scale1) * p1, 0)
    gain2_part = jnp.sum((1.0 + scale2) * p2, 0)
    own_units = jnp.where(
        (jnp.arange(groups) == group_id)[:, None], bias_part.reshape(1, width), 0.0
    )
    small_parts = jnp.concatenate(
        [grad_mods.reshape(micro, devices, mod_rows).transpose(1, 0, 2).reshape(devices, -1)]
        + [
            x.reshape(devices, -1)
            for x in (gain1_part, gain2_part, jnp.sum(dm_sums, 0), own_units)
        ],
        1,
    ).astype(BF)
    taken = small_parts.shape[1]
    small_rows = 8 * -(-taken // (8 * in_lanes))
    small_parts = jnp.pad(small_parts, ((0, 0), (0, small_rows * in_lanes - taken)))
    final = exchange(
        jnp.concatenate(
            [
                input_part.reshape(devices, gain_rows, in_lanes),
                small_parts.reshape(devices, small_rows, in_lanes),
            ],
            1,
        )
    )
    small_sum = jnp.sum(final[:, gain_rows:].astype(F32), 0).reshape(-1)
    input_sum = jnp.sum(
        final[:, :gain_rows].astype(F32).reshape(groups, blocks, gain_rows, in_lanes), 1
    )
    two = heads * 2 * head_width
    input_grad = jnp.concatenate(
        [
            input_sum[:, :, :two]
            .reshape(groups, gain_rows, heads, 2, head_width)
            .transpose(1, 3, 0, 2, 4)
            .reshape(gain_rows, 2 * width),
            input_sum[:, :, two:].transpose(1, 0, 2).reshape(gain_rows, width),
        ],
        1,
    )
    at = micro * mod_rows
    mod_sum = small_sum[:at].reshape(micro, mod_rows)
    modulate_weight_grad = jnp.sum(
        mod_sum[:, :, None] * condition.astype(F32)[:, None, :], 0
    )
    cuts = []
    for length in (gain_rows, gain_rows, gain_rows, ff_rows):
        cuts.append(small_sum[at : at + length])
        at += length
    return (
        layer_output.reshape(micro, rows, width),
        tokens_grad,
        modulate_weight_grad,
        jnp.sum(mod_sum, 0),
        cuts[0],
        input_grad,
        output_grad,
        cuts[1],
        expand_grad,
        cuts[3],
        reduce_grad,
        cuts[2],
    )


def solution(mesh):
    both = P(("ulysses", "blk"))
    tall = P(("ulysses", "blk"), None)
    seq = P(None, ("ulysses", "blk"), None)
    in_specs = (
        seq, seq, P(), P(), tall, both, both, tall, tall, both, tall, both, tall, both,
    )
    out_specs = (seq, seq, tall, both, both, tall, tall, both, tall, both, tall, both)
    return jax.shard_map(
        on_device, mesh=mesh, in_specs=in_specs, out_specs=out_specs, check_vma=False
    )
```

```python
import functools
import math

import jax
import jax.numpy as jnp
from jax import lax
from jax.experimental import pallas as pl
from jax.experimental.pallas import tpu as pltpu
from jax.sharding import PartitionSpec as P

HEADS = 12
ALL = ("ulysses", "blk")
BF = jnp.bfloat16
F32 = jnp.float32
NEG = -1e30


def exchange(x):
    return lax.all_to_all(x, ALL, split_axis=0, concat_axis=0, tiled=True)


def time_features(time_step, half):
    freqs = jnp.exp(-math.log(10000.0) * jnp.arange(half, dtype=F32) / half)
    angles = time_step.astype(F32)[:, None] * freqs[None, :]
    return jax.nn.silu(jnp.concatenate([jnp.cos(angles), jnp.sin(angles)], 1)).astype(BF)


def doc_layout(index, lengths_row):
    ends = jnp.cumsum(lengths_row)
    over = index[:, None] >= ends[None, :]
    segment = jnp.sum(over.astype(jnp.int32), 1)
    place = index - jnp.sum(jnp.where(over, lengths_row[None, :], 0), 1)
    return segment, place


def key_ranges(first, last, lengths_row, block):
    ends = jnp.cumsum(lengths_row)
    start = jnp.sum(jnp.where(first[:, None] >= ends[None, :], lengths_row[None, :], 0), 1)
    stop = jnp.min(jnp.where(ends[None, :] > last[:, None], ends[None, :], 1 << 30), 1)
    return jnp.stack([start // block, (stop + block - 1) // block], 1).reshape(-1)


def whole_vmem():
    return pl.BlockSpec(memory_space=pltpu.VMEM)


def swap(blocks, axis):
    size = lax.axis_size(axis)
    return [
        x if k == 0 else lax.ppermute(x, axis, [(i, i ^ k) for i in range(size)])
        for k, x in enumerate(blocks)
    ]


def unscramble(x, index, axis):
    count, bit = x.shape[axis], 1
    while bit < count:
        shape = x.shape
        y = x.reshape(shape[:axis] + (count // (2 * bit), 2, bit) + shape[axis + 1 :])
        flipped = jnp.flip(y, axis + 1)
        x = jnp.where((index & bit) != 0, flipped, y).reshape(shape)
        bit *= 2
    return x


def halve(x, axis, index, bit):
    size = lax.axis_size(axis)
    y = x.reshape((-1, 2) + x.shape[1:])
    mine = (index // bit) % 2
    sent = lax.dynamic_index_in_dim(y, 1 - mine, 1, keepdims=False)
    kept = lax.dynamic_index_in_dim(y, mine, 1, keepdims=False)
    came = lax.ppermute(sent, axis, [(i, i ^ bit) for i in range(size)])
    return (kept.astype(F32) + came.astype(F32)).astype(BF)


def project_body(blocks, pairs, heads, extra, place_ref, c_ref, shift_ref, w_ref, *refs):
    groups = len(refs) - blocks - 1
    tokens, outs, kept = refs[:groups], refs[groups:-1], refs[-1]
    micro, rows, width = tokens[0].shape
    end = 192 * heads
    weights = [w_ref[:, c : min(c + 128, end)] for c in range(0, end, 128)]
    order = list(range(micro))[::-1]
    z_qk = z_v = None
    for m in order:
        a = jnp.concatenate(
            [(x[m].astype(F32) * c_ref[m][None] + shift_ref[m][None]).astype(BF) for x in tokens], 0
        )
        parts = [jnp.dot(a, w, preferred_element_type=F32).astype(BF) for w in weights]
        v = jnp.concatenate(parts[heads:], 1)
        if extra and m == micro - 1:
            z_qk = parts[heads - 1]
            z_v = v[:, (heads - 1) * 64 : heads * 64]
        for h in range(heads):
            pair = m * heads + h
            if pair >= blocks:
                continue
            kept[pair, :, :128] = parts[h]
            own_v = v[:, h * 64 : (h + 1) * 64]
            if extra:
                kept[pair, :, 128:256] = z_qk
                kept[pair, :, 256:] = jnp.concatenate([own_v, z_v], 1)
            else:
                kept[pair, :, 128:] = jnp.concatenate([own_v, jnp.zeros_like(own_v)], 1)
    for pair in range(pairs, blocks):
        kept[pair] = jnp.zeros(kept.shape[1:], BF)
    for j in range(blocks):
        outs[j][...] = kept[place_ref[1] ^ j]


def turn_tables(cos, sin, extra):
    lane = lax.broadcasted_iota(jnp.int32, cos.shape, 1)
    low = lane < 64
    cos_r, sin_r = pltpu.roll(cos, 64, 1), pltpu.roll(sin, 64, 1)
    tables = [(jnp.where(low, cos, cos_r), jnp.where(low, sin, sin_r))]
    if extra:
        tables.append((jnp.where(low, cos_r, cos), jnp.where(low, sin_r, sin)))
    return tables


def turn(x, table):
    lane = lax.broadcasted_iota(jnp.int32, x.shape, 1)
    swapped = jnp.where(lane % 64 < 32, pltpu.roll(x, 96, 1), pltpu.roll(x, 32, 1))
    return x * table[0] + swapped * table[1]


def rotate_in_body(blocks, extra, place_ref, cos_ref, sin_ref, *refs):
    ins, outs = refs[:blocks], refs[blocks : 2 * blocks - blocks + (6 if extra else 3)]
    kept = refs[-1]
    rows = ins[0].shape[0]
    for j in range(blocks):
        at = pl.multiple_of((place_ref[1] ^ j) * rows, rows)
        kept[pl.ds(at, rows), :] = ins[j][...]
    tables = turn_tables(cos_ref[...], sin_ref[...], extra)
    x0 = turn(kept[:, :128].astype(F32), tables[0])
    outs[0][...] = (x0[:, :64] * 0.125).astype(BF)
    outs[1][...] = x0[:, 64:].astype(BF)
    if extra:
        outs[2][...] = kept[:, 256:320]
        x1 = turn(kept[:, 128:256].astype(F32), tables[1])
        outs[3][...] = (x1[:, :64] * 0.125).astype(BF)
        outs[4][...] = x1[:, 64:].astype(BF)
        outs[5][...] = kept[:, 320:]
    else:
        outs[2][...] = kept[:, 128:192]


def rotate_out_body(blocks, extra, place_ref, cos_ref, sin_ref, *refs):
    count = 6 if extra else 3
    ins, outs, kept = refs[:count], refs[count:-1], refs[-1]
    rows = outs[0].shape[0]
    parts = [ref[...].astype(F32) for ref in ins]
    tables = [(c, -s) for c, s in turn_tables(cos_ref[...], sin_ref[...], extra)]
    kept[:, :128] = turn(jnp.concatenate(parts[:2], 1), tables[0]).astype(BF)
    if extra:
        kept[:, 128:256] = turn(jnp.concatenate(parts[3:5], 1), tables[1]).astype(BF)
        kept[:, 256:] = jnp.concatenate([parts[2], parts[5]], 1).astype(BF)
    else:
        kept[:, 128:] = jnp.concatenate([parts[2], jnp.zeros_like(parts[2])], 1).astype(BF)
    for j in range(blocks):
        at = pl.multiple_of((place_ref[1] ^ j) * rows, rows)
        outs[j][...] = kept[pl.ds(at, rows), :]


def project_back_body(blocks, pairs, heads, extra, place_ref, c_ref, shift_ref, w_ref, *refs):
    kept = refs[-1]
    groups = (len(refs) - blocks - 4) // 2
    tokens, ins = refs[:groups], refs[groups : groups + blocks]
    outs = refs[groups + blocks : 2 * groups + blocks]
    grad_ref, sum_ref, dot_ref = refs[2 * groups + blocks : -1]
    micro, rows, width = tokens[0].shape
    count = groups * rows
    for j in range(blocks):
        kept[place_ref[1] ^ j] = ins[j][...]
    last = None
    if extra:
        last = jnp.zeros((count, 256), F32)
        for j in range(blocks):
            last = last + kept[j, :, 128:].astype(F32)
        last = last.astype(BF)
    all_a, all_g = [], []
    for m in range(micro):
        n = jnp.concatenate([x[m] for x in tokens], 0).astype(F32)
        a = (n * c_ref[m][None] + shift_ref[m][None]).astype(BF)
        qk, v = [], []
        for h in range(heads):
            pair = m * heads + h
            if pair < blocks:
                qk.append(kept[pair, :, :128])
                at = 256 if extra else 128
                v.append(kept[pair, :, at : at + 64])
            else:
                qk.append(last[:, :128])
                v.append(last[:, 192:])
        g = jnp.concatenate(qk + v, 1)
        da = lax.dot_general(g, w_ref[:, : 192 * heads], (((1,), (1,)), ((), ())), preferred_element_type=F32)
        for k in range(groups):
            outs[k][m] = da[k * rows : (k + 1) * rows].astype(BF)
        sum_ref[m : m + 1] = jnp.sum(da, 0, keepdims=True)
        dot_ref[m : m + 1] = jnp.sum(da * n, 0, keepdims=True)
        all_a.append(a)
        all_g.append(g)
    grad_ref[...] = lax.dot_general(
        jnp.concatenate(all_a, 0), jnp.concatenate(all_g, 0), (((0,), (0,)), ((), ())),
        preferred_element_type=F32,
    ).astype(BF)


def norm(values):
    centered = values - jnp.mean(values, -1, keepdims=True)
    inverse = lax.rsqrt(jnp.mean(centered * centered, -1, keepdims=True) + 1e-05)
    return centered * inverse, inverse


def by_micro(ref, rows):
    return jnp.concatenate(
        [jnp.broadcast_to(ref[m][None], (rows, ref.shape[1])) for m in range(ref.shape[0])], 0
    )


def middle_body(
    groups, blocks, heads, micro, rows, stripe,
    came_ref, out_ref, x_ref, gate_ref, c_ref, shift_ref,
    merged_ref, attn_ref, middle_ref, second_ref,
):
    width = x_ref.shape[1]
    for u in range(groups):
        for m in range(micro):
            for h in range(heads):
                pair = m * heads + h
                lanes = slice((u * heads + h) * 64, (u * heads + h + 1) * 64)
                half = rows // 2
                if pair < blocks and stripe:
                    at = m * rows
                    merged_ref[at : at + half, lanes] = came_ref[u * blocks + pair, :half, :64]
                    merged_ref[at + half : at + rows, lanes] = came_ref[u * blocks + pair, :half, 64:]
                elif pair < blocks:
                    merged_ref[m * rows : (m + 1) * rows, lanes] = came_ref[u * blocks + pair]
                else:
                    for b in range(blocks):
                        at = m * rows + b * stripe
                        merged_ref[at : at + stripe, lanes] = came_ref[u * blocks + b, half:, :64]
    attn = jnp.dot(merged_ref[...], out_ref[...].reshape(width, width), preferred_element_type=F32)
    attn_ref[...] = attn
    middle = x_ref[...].astype(F32) + by_micro(gate_ref, rows) * attn
    middle_ref[...] = middle
    normed, _ = norm(middle)
    second_ref[...] = (normed * by_micro(c_ref, rows) + by_micro(shift_ref, rows)).astype(BF)


def gelu_pair(u):
    t = jnp.tanh(0.7978845608028654 * (u + 0.044715 * u * u * u))
    value = 0.5 * u * (1.0 + t)
    slope = 0.5 * (1.0 + t) + 0.5 * u * (1.0 - t * t) * (
        0.7978845608028654 * (1.0 + 0.134145 * u * u)
    )
    return value, slope


NT = (((1,), (1,)), ((), ()))
TN = (((0,), (0,)), ((), ()))


def feed_body(
    groups, blocks, heads, micro, rows, stripe,
    ex_ref, re_ref, out_w_ref, ex_bias_ref, re_bias_ref, second_ref, middle_ref, attn_ref, dy_ref,
    gate1_ref, gate2_ref, c_ref,
    layer_ref, grad_ref, dattn_ref, do_ref, sums_ref,
    branch_sum, back_sum, dm_sum, do_sum,
):
    step = pl.program_id(0)
    width = middle_ref.shape[1]

    @pl.when(step == 0)
    def _():
        branch_sum[...] = jnp.zeros_like(branch_sum)
        back_sum[...] = jnp.zeros_like(back_sum)
        dm_sum[...] = (by_micro(gate2_ref, rows) * dy_ref[...].astype(F32)).astype(BF)

    expand = ex_ref[...].reshape(width, width)
    reduce = re_ref[...].reshape(width, width)
    u = jnp.dot(second_ref[...], expand, preferred_element_type=F32) + ex_bias_ref[0]
    g, slope = gelu_pair(u)
    branch_sum[...] += jnp.dot(g.astype(BF), reduce, preferred_element_type=F32)
    dg = lax.dot_general(dm_sum[...], reduce, NT, preferred_element_type=F32)
    du = (dg * slope).astype(BF)
    back_sum[...] += lax.dot_general(du, expand, NT, preferred_element_type=F32)

    @pl.when(step == pl.num_programs(0) - 1)
    def _():
        def total(at, x):
            for m in range(micro):
                sums_ref[at * micro + m : at * micro + m + 1] = jnp.sum(
                    x[m * rows : (m + 1) * rows], 0, keepdims=True
                )

        branch = branch_sum[...] + re_bias_ref[...]
        middle = middle_ref[...]
        dy = dy_ref[...].astype(F32)
        layer_ref[...] = (middle + by_micro(gate2_ref, rows) * branch).astype(BF)
        total(0, dy * branch)
        normed, inverse = norm(middle)
        db = back_sum[...]
        total(1, db)
        total(2, db * normed)
        e = db * by_micro(c_ref, rows)
        grad = dy + inverse * (
            e
            - jnp.mean(e, -1, keepdims=True)
            - normed * jnp.mean(e * normed, -1, keepdims=True)
        )
        grad_ref[...] = grad
        total(3, grad * attn_ref[...])
        total(4, dm_sum[...].astype(F32))
        dattn = (by_micro(gate1_ref, rows) * grad).astype(BF)
        dattn_ref[...] = dattn
        do_sum[...] = lax.dot_general(
            dattn, out_w_ref[...].reshape(width, width), NT, preferred_element_type=F32
        ).astype(BF)
        for at in range(groups):
            for m in range(micro):
                for h in range(heads):
                    pair = m * heads + h
                    lanes = slice((at * heads + h) * 64, (at * heads + h + 1) * 64)
                    half, top = rows // 2, m * rows
                    if pair < blocks and stripe:
                        do_ref[at * blocks + pair, :half, :64] = do_sum[top : top + half, lanes]
                        do_ref[at * blocks + pair, :half, 64:] = do_sum[top + half : top + rows, lanes]
                    elif pair < blocks:
                        do_ref[at * blocks + pair] = do_sum[top : top + rows, lanes]
                    else:
                        for b in range(blocks):
                            do_ref[at * blocks + b, half:, :64] = do_sum[top : top + stripe, lanes]
                            do_ref[at * blocks + b, half:, 64:] = jnp.zeros((stripe, 64), BF)
                            top += stripe
            for b in range(micro * heads, blocks):
                do_ref[at * blocks + b] = jnp.zeros((rows, 64), BF)


def feed_weights_body(rows, place_ref, ex_ref, re_ref, bias_ref, gate_ref, *refs):
    groups = (len(refs) - 3) // 2
    reduce_ref, expand_ref, sum_ref = refs[2 * groups :]
    width = refs[0].shape[-1]
    second = jnp.concatenate([x[...] for x in refs[:groups]], 0)
    gate = by_micro(gate_ref, rows)
    dm = jnp.concatenate(
        [(gate * x[...].astype(F32)).astype(BF) for x in refs[groups : 2 * groups]], 0
    )
    expand = ex_ref[...].reshape(width, width)
    reduce = re_ref[...].reshape(width, width)
    u = jnp.dot(second, expand, preferred_element_type=F32) + bias_ref[0]
    g, slope = gelu_pair(u)
    du = lax.dot_general(dm, reduce, NT, preferred_element_type=F32) * slope
    du = du.astype(BF)
    sum_ref[...] = jnp.sum(du.astype(F32), 0, keepdims=True)
    reduce_ref[...] = lax.dot_general(g.astype(BF), dm, TN, preferred_element_type=F32).astype(BF)
    expand_ref[...] = lax.dot_general(second, du, TN, preferred_element_type=F32).astype(BF)


def attend_body(block, range_ref, q_ref, sq_ref, k_ref, v_ref, sk_ref, o_ref, lse_ref):
    i = pl.program_id(0)
    q, sq = q_ref[...], sq_ref[0]
    count, width = q.shape

    def step(j, carry):
        high, total, acc = carry
        at = pl.ds(pl.multiple_of(j * block, block), block)
        k, v, sk = k_ref[at, :], v_ref[at, :], sk_ref[at, :]
        s = lax.dot_general(k, q, (((1,), (1,)), ((), ())), preferred_element_type=F32)
        s = jnp.where(sk == sq, s, NEG)
        new = jnp.maximum(high, jnp.max(s, 0, keepdims=True))
        p = jnp.exp(s - new)
        fix = jnp.exp(high - new)
        total = total * fix + jnp.sum(p, 0, keepdims=True)
        acc = acc * fix + lax.dot_general(
            v, p.astype(BF), (((0,), (0,)), ((), ())), preferred_element_type=F32
        )
        return new, total, acc

    first = (
        jnp.full((1, count), NEG, F32),
        jnp.zeros((1, count), F32),
        jnp.zeros((width, count), F32),
    )
    high, total, acc = lax.fori_loop(range_ref[2 * i], range_ref[2 * i + 1], step, first)
    o_ref[...] = (acc / total).T.astype(BF)
    lse_ref[0] = high + jnp.log(total)


def attend_back_body(
    block, range_ref, q_ref, sq_ref, lse_ref, o_ref, do_ref, k_ref, v_ref, sk_ref,
    dq_ref, dk_ref, dv_ref, dk_sum, dv_sum,
):
    i = pl.program_id(0)

    @pl.when(i == 0)
    def _():
        dk_sum[...] = jnp.zeros_like(dk_sum)
        dv_sum[...] = jnp.zeros_like(dv_sum)

    q, sq, lse, do = q_ref[...], sq_ref[0], lse_ref[0], do_ref[...]
    count, width = q.shape
    delta = jnp.sum((do.astype(F32) * o_ref[...].astype(F32)).T, 0, keepdims=True)

    def step(j, dq):
        at = pl.ds(pl.multiple_of(j * block, block), block)
        k, v, sk = k_ref[at, :], v_ref[at, :], sk_ref[at, :]
        s = lax.dot_general(k, q, (((1,), (1,)), ((), ())), preferred_element_type=F32)
        p = jnp.where(sk == sq, jnp.exp(s - lse), 0.0)
        dp = lax.dot_general(v, do, (((1,), (1,)), ((), ())), preferred_element_type=F32)
        ds = (p * (dp - delta)).astype(BF)
        dv_sum[at, :] += jnp.dot(p.astype(BF), do, preferred_element_type=F32)
        dk_sum[at, :] += jnp.dot(ds, q, preferred_element_type=F32)
        return dq + lax.dot_general(
            k, ds, (((0,), (0,)), ((), ())), preferred_element_type=F32
        )

    dq = lax.fori_loop(
        range_ref[2 * i], range_ref[2 * i + 1], step, jnp.zeros((width, count), F32)
    )
    dq_ref[...] = (dq * 0.125).T.astype(BF)

    @pl.when(i == pl.num_programs(0) - 1)
    def _():
        dk_ref[...] = dk_sum[...].astype(BF)
        dv_ref[...] = dv_sum[...].astype(BF)


def attend(ranges, q, sq, k, v, sk, rows, block):
    count, width = q.shape
    steps = count // rows
    size = k.shape[0]
    by_row = pl.BlockSpec((rows, width), lambda i, r: (i, 0))
    as_row = pl.BlockSpec((1, 1, rows), lambda i, r: (i, 0, 0))
    return pl.pallas_call(
        functools.partial(attend_body, block),
        grid_spec=pltpu.PrefetchScalarGridSpec(
            num_scalar_prefetch=1,
            grid=(steps,),
            in_specs=[by_row, as_row, whole_vmem(), whole_vmem(), whole_vmem()],
            out_specs=[by_row, as_row],
        ),
        out_shape=[
            jax.ShapeDtypeStruct((count, width), BF),
            jax.ShapeDtypeStruct((steps, 1, rows), F32),
        ],
        cost_estimate=pl.CostEstimate(
            flops=count * size * width, transcendentals=count * size // 4, bytes_accessed=4 * size * width
        ),
        name="attend",
    )(ranges, q, sq.reshape(steps, 1, rows), k, v, sk)


def attend_back(ranges, q, sq, lse, o, do, k, v, sk, rows, block):
    count, width = q.shape
    steps = count // rows
    size = k.shape[0]
    by_row = pl.BlockSpec((rows, width), lambda i, r: (i, 0))
    as_row = pl.BlockSpec((1, 1, rows), lambda i, r: (i, 0, 0))
    return pl.pallas_call(
        functools.partial(attend_back_body, block),
        grid_spec=pltpu.PrefetchScalarGridSpec(
            num_scalar_prefetch=1,
            grid=(steps,),
            in_specs=[by_row, as_row, as_row, by_row, by_row, whole_vmem(), whole_vmem(), whole_vmem()],
            out_specs=[by_row, whole_vmem(), whole_vmem()],
            scratch_shapes=[pltpu.VMEM((size, width), F32)] * 2,
        ),
        out_shape=[
            jax.ShapeDtypeStruct((count, width), BF),
            jax.ShapeDtypeStruct((size, width), BF),
            jax.ShapeDtypeStruct((size, width), BF),
        ],
        cost_estimate=pl.CostEstimate(
            flops=3 * count * size * width, transcendentals=count * size // 4, bytes_accessed=8 * size * width
        ),
        name="attend_back",
    )(ranges, q, sq.reshape(steps, 1, rows), lse, o, do, k, v, sk)


def spread(ref, at, rows):
    return ref[pl.ds(pl.multiple_of(at, rows), rows), :]


def keys_mask(low, high, at, count):
    position = at + lax.broadcasted_iota(jnp.int32, (count, low.shape[1]), 0)
    return (position >= low) & (position < high)


QB, KB = 256, 512


def attend_all_body(
    blocks, groups, rows, stripe,
    place_ref, range_ref, last_range_ref, low_ref, high_ref, last_low_ref, last_high_ref, cos_ref, sin_ref, *refs,
):
    ins = refs[:blocks]
    message, q_ref, k_ref, v_ref, zq_ref, zk_ref, zv_ref, o_ref, zo_ref, lse_ref, zlse_ref = refs[blocks : blocks + 11]
    kept, wide, scores = refs[blocks + 11 :]
    span = blocks * rows
    size = groups * span
    me_u, me_b = place_ref[0], place_ref[1]
    for g in range(groups):
        for j in range(blocks):
            kept[pl.ds(pl.multiple_of((me_b ^ j) * rows, rows), rows), :] = spread(ins[j], (me_u ^ g) * rows, rows)
        at = slice(g * span, (g + 1) * span)
        cos, sin = cos_ref[at], sin_ref[at]
        tables = turn_tables(cos, sin, True)
        x = turn(kept[:, :128].astype(F32), tables[0])
        q_ref[at] = (x[:, :64] * 0.125).astype(BF)
        k_ref[at] = x[:, 64:].astype(BF)
        v_ref[at] = kept[:, 256:320]
        x = turn(kept[:, 128:256].astype(F32), tables[1])
        wide[at] = x[:, :64] * 0.125
        zk_ref[at] = x[:, 64:].astype(BF)
        zv_ref[at] = kept[:, 320:]
    tail = slice(size, size + KB - QB)
    for ref in (k_ref, v_ref, zk_ref, zv_ref):
        ref[tail] = jnp.zeros((KB - QB, 64), BF)
    devices = groups * blocks
    for d in range(0, devices, 2):
        zq_ref[d * stripe : (d + 2) * stripe] = jnp.concatenate(
            [spread(wide, (d + e) * rows + me_b * stripe, stripe) for e in range(2)], 0
        ).astype(BF)

    def block(q, low, high, first, stop, keys, values):
        count = q.shape[0]

        def score(t, high_s):
            at = pl.multiple_of((first + 2 * t) * QB, QB)
            s = lax.dot_general(keys[pl.ds(at, KB), :], q, NT, preferred_element_type=F32)
            s = jnp.where(keys_mask(low, high, at, KB), s, NEG)
            scores[t, :, :count] = s
            return jnp.maximum(high_s, jnp.max(s, 0, keepdims=True))

        steps = (stop - first + 1) // 2
        top = lax.fori_loop(0, steps, score, jnp.full((1, count), NEG, F32))

        def weigh(t, carry):
            total, acc = carry
            at = pl.multiple_of((first + 2 * t) * QB, QB)
            p = jnp.exp(scores[t, :, :count] - top)
            return total + jnp.sum(p, 0, keepdims=True), acc + lax.dot_general(
                values[pl.ds(at, KB), :], p.astype(BF), TN, preferred_element_type=F32
            )

        total, acc = lax.fori_loop(
            0, steps, weigh, (jnp.zeros((1, count), F32), jnp.zeros((64, count), F32))
        )
        return (acc / total).T, top + jnp.log(total)

    half = rows // 2

    def run(i, _):
        o, lse = block(
            spread(q_ref, i * QB, QB), low_ref[i], high_ref[i], range_ref[2 * i], range_ref[2 * i + 1], k_ref, v_ref
        )
        o = o.astype(BF)
        o_ref[pl.ds(pl.multiple_of(i * QB, QB), QB), :] = o
        lse_ref[i] = lse
        for d in range(QB // rows):
            message[i * (QB // rows) + d, :half] = jnp.concatenate(
                [o[d * rows : d * rows + half], o[d * rows + half : (d + 1) * rows]], 1
            )
        return 0

    lax.fori_loop(0, size // QB, run, 0)
    few = zlse_ref.shape[2]

    def run_last(i, _):
        o, lse = block(
            spread(zq_ref, i * few, few), last_low_ref[i], last_high_ref[i],
            last_range_ref[2 * i], last_range_ref[2 * i + 1], zk_ref, zv_ref,
        )
        zo_ref[pl.ds(pl.multiple_of(i * few, few), few), :] = o.astype(BF)
        zlse_ref[i] = lse
        o = jnp.concatenate([o, jnp.zeros_like(o)], 1)
        for d in range(few // stripe):
            message[i * (few // stripe) + d, half:] = o[d * stripe : (d + 1) * stripe].astype(BF)
        return 0

    lax.fori_loop(0, zlse_ref.shape[0], run_last, 0)


def attend_all_back_body(
    blocks, groups, rows, stripe,
    place_ref, range_ref, last_range_ref, low_ref, high_ref, last_low_ref, last_high_ref, cos_ref, sin_ref,
    do_ref, q_ref, k_ref, v_ref, zq_ref, zk_ref, zv_ref, o_ref, zo_ref, lse_ref, zlse_ref, *refs,
):
    outs = refs[:blocks]
    kept, dq, dk, dv, zdq, zdk, zdv = refs[blocks:]
    span = blocks * rows
    size = groups * span
    half = rows // 2
    me_u, me_b = place_ref[0], place_ref[1]
    for ref in (dk, dv, zdq, zdk, zdv):
        ref[...] = jnp.zeros_like(ref)

    def block(q, do, o, lse, low, high, first, stop, keys, values, dk_sum, dv_sum):
        count = q.shape[0]
        delta = jnp.sum((do.astype(F32) * o.astype(F32)).T, 0, keepdims=True)

        def step(t, dq):
            at = pl.multiple_of((first + 2 * t) * QB, QB)
            here = pl.ds(at, KB)
            k, v = keys[here, :], values[here, :]
            s = lax.dot_general(k, q, NT, preferred_element_type=F32)
            dp = lax.dot_general(v, do, NT, preferred_element_type=F32)
            p = jnp.where(keys_mask(low, high, at, KB), jnp.exp(s - lse), 0.0)
            ds = (p * (dp - delta)).astype(BF)
            dv_sum[here, :] += jnp.dot(p.astype(BF), do, preferred_element_type=F32)
            dk_sum[here, :] += jnp.dot(ds, q, preferred_element_type=F32)
            return dq + lax.dot_general(k, ds, TN, preferred_element_type=F32)

        return (
            lax.fori_loop(0, (stop - first + 1) // 2, step, jnp.zeros((64, count), F32)) * 0.125
        ).T

    def run(i, _):
        came = []
        for d in range(QB // rows):
            x = do_ref[i * (QB // rows) + d]
            came += [x[:half, :64], x[:half, 64:]]
        at = pl.ds(pl.multiple_of(i * QB, QB), QB)
        dq[at, :] = block(
            q_ref[at, :], jnp.concatenate(came, 0), o_ref[at, :], lse_ref[i], low_ref[i], high_ref[i],
            range_ref[2 * i], range_ref[2 * i + 1], k_ref, v_ref, dk, dv,
        )
        return 0

    lax.fori_loop(0, size // QB, run, 0)
    few = zlse_ref.shape[2]

    def run_last(i, _):
        came = [
            do_ref[i * (few // stripe) + d].astype(F32)[half:, :64] for d in range(few // stripe)
        ]
        at = pl.ds(pl.multiple_of(i * few, few), few)
        x = block(
            zq_ref[at, :], jnp.concatenate(came, 0).astype(BF), zo_ref[at, :], zlse_ref[i],
            last_low_ref[i], last_high_ref[i], last_range_ref[2 * i], last_range_ref[2 * i + 1],
            zk_ref, zv_ref, zdk, zdv,
        )
        for d in range(few // stripe):
            to = (i * (few // stripe) + d) * rows + me_b * stripe
            zdq[pl.ds(pl.multiple_of(to, stripe), stripe), :] = x[d * stripe : (d + 1) * stripe]
        return 0

    lax.fori_loop(0, zlse_ref.shape[0], run_last, 0)
    for g in range(groups):
        at = slice(g * span, (g + 1) * span)
        tables = [(c, -s) for c, s in turn_tables(cos_ref[at], sin_ref[at], True)]
        kept[:, :128] = turn(jnp.concatenate([dq[at], dk[at]], 1), tables[0]).astype(BF)
        kept[:, 128:256] = turn(jnp.concatenate([zdq[at], zdk[at]], 1), tables[1]).astype(BF)
        kept[:, 256:] = jnp.concatenate([dv[at], zdv[at]], 1).astype(BF)
        for j in range(blocks):
            outs[j][pl.ds(pl.multiple_of((me_u ^ g) * rows, rows), rows), :] = spread(kept, (me_b ^ j) * rows, rows)


def on_device(
    tokens,
    cotangent,
    lengths,
    time_step,
    modulate_weight,
    modulate_bias,
    attend_gain,
    input_weight,
    output_weight,
    feed_gain,
    expand_weight,
    expand_bias,
    reduce_weight,
    reduce_bias,
):
    groups, blocks = lax.axis_size("ulysses"), lax.axis_size("blk")
    group_id, block_id = lax.axis_index("ulysses"), lax.axis_index("blk")
    devices = groups * blocks
    micro, rows, width = tokens.shape
    own = micro * rows
    size = devices * rows
    head_width = width // HEADS
    heads = HEADS // groups
    pairs = micro * heads
    extra = pairs > blocks
    lanes = 384 if extra else 256
    stripe = rows // blocks if extra else 0
    mod_rows = modulate_weight.shape[0]
    gain_rows = attend_gain.shape[0]
    ff_rows = expand_bias.shape[0]
    ff = ff_rows * devices
    folds = ff // width
    assert pairs <= blocks + 1 and head_width == 64 and folds == groups and heads == 3
    place = jnp.stack([group_id, block_id]).astype(jnp.int32)
    pair_micro = jnp.minimum(block_id // heads, micro - 1)

    values = tokens.astype(F32)
    n1, r1 = norm(values)
    n1_b = n1.astype(BF)
    n1_group = swap([n1_b] * groups, "ulysses")
    in_split = input_weight.reshape(gain_rows, 3, groups, heads, head_width)
    in_split = jnp.concatenate(
        [
            in_split[:, :2].transpose(2, 0, 3, 1, 4).reshape(groups, 1, gain_rows, -1),
            in_split[:, 2].transpose(1, 0, 2, 3).reshape(groups, 1, gain_rows, -1),
        ],
        3,
    )
    in_lanes = heads * 3 * head_width

    condition = time_features(time_step, modulate_weight.shape[1] // 2)
    mod_own = jnp.einsum(
        "mc,fc->mf", condition, modulate_weight, preferred_element_type=F32
    ) + modulate_bias.astype(F32)
    small = jnp.concatenate(
        [
            mod_own.reshape(-1),
            attend_gain.astype(F32),
            feed_gain.astype(F32),
            reduce_bias.astype(F32),
            expand_bias.astype(F32),
        ]
    )
    small_lanes = 64 * -(-small.shape[0] // (32 * gain_rows))
    small = jnp.pad(small, (0, small_lanes * gain_rows // 2 - small.shape[0]))
    small_high = small.astype(BF)
    small_low = (small - lax.reduce_precision(small, 8, 7)).astype(BF)
    small = jnp.concatenate([small_high, small_low]).reshape(1, 1, gain_rows, small_lanes)
    came = exchange(
        jnp.concatenate(
            [
                jnp.broadcast_to(in_split, (groups, blocks) + in_split.shape[2:]),
                jnp.broadcast_to(small, (groups, blocks) + small.shape[2:]),
            ],
            3,
        ).reshape(devices, gain_rows, in_lanes + small_lanes)
    )
    small_all = came[:, :, in_lanes:].astype(F32).reshape(devices, 2, -1)
    small_all = small_all[:, 0] + small_all[:, 1]
    in_own = came.reshape(width, in_lanes + small_lanes)

    weight_pack = jnp.concatenate(
            [
                reduce_weight,
                output_weight,
                expand_weight.reshape(gain_rows, folds, width).transpose(1, 0, 2).reshape(-1, width),
            ],
            0,
        )
    weight_pack, in_own, small_all, n1_group = lax.optimization_barrier(
        (weight_pack, in_own, small_all, n1_group)
    )
    gathered = lax.all_gather(weight_pack, ALL, axis=0, tiled=False)
    unit = gain_rows
    while unit % 8:
        unit *= 2
    units = width // unit
    if unit != gain_rows:
        gathered = jnp.concatenate(
            [gathered[:, :ff_rows].reshape(units, -1, width)]
            + [
                gathered[:, at : at + gain_rows].reshape(units, unit, width)
                for at in range(ff_rows, ff_rows + (folds + 1) * gain_rows, gain_rows)
            ],
            1,
        )
    wide = unit * folds

    at = micro * mod_rows
    mods = small_all[:, :at].reshape(devices, micro, mod_rows).transpose(1, 0, 2).reshape(micro, -1)
    gain1 = small_all[:, at : at + gain_rows].reshape(-1)
    at += gain_rows
    gain2 = small_all[:, at : at + gain_rows].reshape(-1)
    at += gain_rows
    reduce_bias_f = small_all[:, at : at + gain_rows].reshape(1, -1)
    at += gain_rows
    expand_bias_f = small_all[:, at : at + ff_rows].reshape(folds, 1, width)
    shift1, scale1, gate1, shift2, scale2, gate2 = jnp.split(mods, 6, 1)
    c1 = gain1 * (1.0 + scale1)
    c2 = gain2 * (1.0 + scale2)

    index = jnp.arange(size, dtype=jnp.int32)
    pair_lengths = lax.dynamic_index_in_dim(lengths, pair_micro, 0, keepdims=False)
    segment, position = doc_layout(index, pair_lengths)
    last_lengths = lengths[micro - 1]
    last_segment, last_position = doc_layout(index, last_lengths)
    half = head_width // 2
    freqs = jnp.exp(-math.log(10000.0) * jnp.arange(half, dtype=F32) / half)
    lane = jnp.arange(128)
    angles = jnp.where(
        (lane < 64)[None, :], position.astype(F32)[:, None], last_position.astype(F32)[:, None]
    ) * jnp.tile(freqs, 4)[None, :]
    cos_table = jnp.cos(angles)
    sin_table = jnp.where((lane % 64 < 32)[None, :], -1.0, 1.0) * jnp.sin(angles)
    query_rows = math.gcd(size, 256)
    key_block = math.gcd(size, 256)
    first = jnp.arange(size // query_rows, dtype=jnp.int32) * query_rows
    ranges = key_ranges(first, first + query_rows - 1, pair_lengths, key_block)
    small_path = extra and size % KB == 0 and rows % 16 == 0 and stripe % 8 == 0 and size <= 4096

    count = groups * rows
    striped = lambda x: lax.dynamic_slice_in_dim(
        x.reshape((devices, rows) + x.shape[1:]), block_id * stripe, stripe, 1
    ).reshape((devices * stripe,) + x.shape[1:])
    smem = pl.BlockSpec(memory_space=pltpu.SMEM)
    outgoing = pl.pallas_call(
        functools.partial(project_body, blocks, pairs, heads, extra),
        out_shape=[jax.ShapeDtypeStruct((count, lanes), BF)] * blocks,
        in_specs=[smem] + [whole_vmem()] * (3 + groups),
        out_specs=[whole_vmem()] * blocks,
        scratch_shapes=[pltpu.VMEM((blocks, count, lanes), BF)],
        cost_estimate=pl.CostEstimate(
            flops=2 * micro * count * width * 3 * 64 * heads, transcendentals=0, bytes_accessed=8 * own * width
        ),
        name="project",
    )(place, c1, shift1, in_own, *n1_group)
    incoming = swap(outgoing, "blk")

    span = blocks * rows
    by_span = pl.BlockSpec((span, 64), lambda i, p: (i ^ p[0], 0))
    table_spec = pl.BlockSpec((span, 128), lambda i, p: (i ^ p[0], 0))
    by_rows = pl.BlockSpec((rows, lanes), lambda i, p: (i, 0))
    parts = 6 if extra else 3
    if small_path:
        last_rows = 128
        chunk = last_rows // stripe
        last_first = jnp.arange(devices // chunk, dtype=jnp.int32) * (chunk * rows) + block_id * stripe
        last_ranges = key_ranges(
            last_first, last_first + (chunk - 1) * rows + stripe - 1, last_lengths, QB
        )
        bounds = []
        for where, lens, pick, lump in (
            (position, pair_lengths, lambda x: x, QB),
            (last_position, last_lengths, striped, last_rows),
        ):
            low = index - where
            ends = jnp.cumsum(lens)
            high = jnp.min(jnp.where(ends[None, :] > index[:, None], ends[None, :], 1 << 30), 1)
            bounds += [pick(low).reshape(-1, 1, lump), pick(high).reshape(-1, 1, lump)]
        whole = lambda *shape: jax.ShapeDtypeStruct(shape, BF)
        saved_shapes = [
            whole(size, 64), whole(size + KB - QB, 64), whole(size + KB - QB, 64),
            whole(devices * stripe, 64), whole(size + KB - QB, 64), whole(size + KB - QB, 64),
            whole(size, 64), whole(devices * stripe, 64),
            jax.ShapeDtypeStruct(bounds[0].shape, F32), jax.ShapeDtypeStruct(bounds[2].shape, F32),
        ]
        attend_args = (place, ranges, last_ranges, *bounds, cos_table, sin_table)
        specs = [smem] * 3 + [whole_vmem()] * 6
        message, *saved = pl.pallas_call(
            functools.partial(attend_all_body, blocks, groups, rows, stripe),
            in_specs=specs + [whole_vmem()] * blocks,
            out_specs=[whole_vmem()] * 11,
            out_shape=[whole(devices, rows // 2 + stripe, 128)] + saved_shapes,
            scratch_shapes=[
                pltpu.VMEM((span, lanes), BF),
                pltpu.VMEM((size, 64), F32),
                pltpu.VMEM((size // KB + 1, KB, QB), F32),
            ],
            cost_estimate=pl.CostEstimate(
                flops=size * size * 64, transcendentals=size * size // 2, bytes_accessed=16 * size * 128
            ),
            name="attend_all",
        )(*attend_args, *incoming)
    else:
        assert not extra
        turned = pl.pallas_call(
            functools.partial(rotate_in_body, blocks, extra),
            grid_spec=pltpu.PrefetchScalarGridSpec(
                num_scalar_prefetch=1,
                grid=(groups,),
                in_specs=[table_spec, table_spec] + [by_rows] * blocks,
                out_specs=[by_span] * parts,
                scratch_shapes=[pltpu.VMEM((span, lanes), BF)],
            ),
            out_shape=[jax.ShapeDtypeStruct((size, 64), BF)] * parts,
            name="rotate_in",
        )(place, cos_table, sin_table, *incoming)
        query, key, value = turned[:3]
        attended, lse = attend(
            ranges, query, segment, key, value, segment[:, None], query_rows, key_block
        )
        message = attended.reshape(devices, rows, head_width)
    came = exchange(message)

    ex_spec = lambda f: pl.BlockSpec((units, unit, width), f)
    flat = pl.BlockSpec((own, width), lambda i: (0, 0))
    vec = lambda n: pl.BlockSpec((n, width), lambda i: (0, 0))
    message_shape = message.shape
    message_spec = pl.BlockSpec(message_shape, lambda i: (0, 0, 0))
    sizes = (groups, blocks, heads, micro, rows, stripe)
    own_f32 = jax.ShapeDtypeStruct((own, width), F32)
    own_bf = jax.ShapeDtypeStruct((own, width), BF)
    merged, attn, middle, second = pl.pallas_call(
        functools.partial(middle_body, *sizes),
        grid=(1,),
        in_specs=[message_spec, ex_spec(lambda i: (0, folds, 0)), flat, vec(micro), vec(micro), vec(micro)],
        out_specs=[flat] * 4,
        out_shape=[own_bf, own_f32, own_f32, own_bf],
        name="middle",
    )(came, gathered, tokens.reshape(own, width), gate1, c2, shift2)
    second_group = swap([second] * groups, "ulysses")
    dy = cotangent.reshape(own, width)
    dy_group = swap([dy] * groups, "ulysses")

    per = width // wide
    layer_output, grad_middle, grad_attn, do_message, sums = pl.pallas_call(
        functools.partial(feed_body, *sizes),
        grid=(folds,),
        in_specs=[
            ex_spec(lambda i: (0, folds + 1 + i, 0)),
            pl.BlockSpec((per, wide, width), lambda i: (i, 0, 0)),
            ex_spec(lambda i: (0, folds, 0)),
            pl.BlockSpec((1, 1, width), lambda i: (i, 0, 0)),
            vec(1),
            flat, flat, flat, flat,
            vec(micro), vec(micro), vec(micro),
        ],
        out_specs=[flat, flat, flat, message_spec, vec(5 * micro)],
        out_shape=[
            own_bf, own_f32, own_bf,
            jax.ShapeDtypeStruct(message_shape, BF),
            jax.ShapeDtypeStruct((5 * micro, width), F32),
        ],
        scratch_shapes=[
            pltpu.VMEM((own, width), F32), pltpu.VMEM((own, width), F32),
            pltpu.VMEM((own, width), BF), pltpu.VMEM((own, width), BF),
        ],
        cost_estimate=pl.CostEstimate(
            flops=8 * own * width * ff, transcendentals=own * ff, bytes_accessed=4 * width * ff
        ),
        name="feed",
    )(gathered, gathered, gathered, expand_bias_f, reduce_bias_f, second, middle, attn, dy, gate1, gate2, c2)
    do_came = exchange(do_message)
    d_gate2, d_shift2, p2, d_gate1, dm_sums = [
        sums[i * micro : (i + 1) * micro] for i in range(5)
    ]

    output_part = lax.dot_general(merged, grad_attn, TN, preferred_element_type=F32).astype(BF)
    output_part = output_part.reshape(groups, width // groups, width)

    flat_p = pl.BlockSpec((own, width), lambda i, p: (0, 0))
    square = pl.BlockSpec((width, width), lambda i, p: (0, 0))
    reduce_part, expand_part, bias_part = pl.pallas_call(
        functools.partial(feed_weights_body, rows),
        grid_spec=pltpu.PrefetchScalarGridSpec(
            num_scalar_prefetch=1,
            grid=(1,),
            in_specs=[
                pl.BlockSpec((units, unit, width), lambda i, p: (0, folds + 1 + p[0], 0)),
                pl.BlockSpec((per, wide, width), lambda i, p: (p[0], 0, 0)),
                pl.BlockSpec((1, 1, width), lambda i, p: (p[0], 0, 0)),
                pl.BlockSpec((micro, width), lambda i, p: (0, 0)),
            ]
            + [flat_p] * (2 * groups),
            out_specs=[square, square, pl.BlockSpec((1, width), lambda i, p: (0, 0))],
        ),
        out_shape=[
            jax.ShapeDtypeStruct((width, width), BF),
            jax.ShapeDtypeStruct((width, width), BF),
            jax.ShapeDtypeStruct((1, width), F32),
        ],
        cost_estimate=pl.CostEstimate(
            flops=10 * own * groups * width * width, transcendentals=own * ff, bytes_accessed=16 * width * width
        ),
        name="feed_weights",
    )(place, gathered, gathered, expand_bias_f, gate2, *second_group, *dy_group)
    feed_part = jnp.concatenate(
        [
            reduce_part.reshape(blocks, ff_rows, width),
            expand_part.reshape(groups, blocks, gain_rows, width)
            .transpose(1, 0, 2, 3)
            .reshape(blocks, groups * gain_rows, width),
        ],
        1,
    )
    do_came, feed_part, output_part = lax.optimization_barrier((do_came, feed_part, output_part))
    output_part = swap(
        [
            lax.dynamic_index_in_dim(output_part, group_id ^ k, 0, keepdims=False)
            for k in range(groups)
        ],
        "ulysses",
    )

    feed_half = halve(feed_part, "blk", block_id, 1)

    if small_path:
        leaving = pl.pallas_call(
            functools.partial(attend_all_back_body, blocks, groups, rows, stripe),
            in_specs=specs + [whole_vmem()] * 11,
            out_specs=[whole_vmem()] * blocks,
            out_shape=[whole(count, lanes)] * blocks,
            scratch_shapes=[pltpu.VMEM((span, lanes), BF), pltpu.VMEM((size, 64), F32)]
            + [pltpu.VMEM((size + KB - QB, 64), F32)] * 2
            + [pltpu.VMEM((size, 64), F32)]
            + [pltpu.VMEM((size + KB - QB, 64), F32)] * 2,
            cost_estimate=pl.CostEstimate(
                flops=2 * size * size * 64, transcendentals=size * size // 2, bytes_accessed=16 * size * 128
            ),
            name="attend_all_back",
        )(*attend_args, do_came, *saved)
    else:
        grads = attend_back(
            ranges, query, segment, lse, attended, do_came.reshape(size, head_width), key, value,
            segment[:, None], query_rows, key_block,
        )
        leaving = pl.pallas_call(
            functools.partial(rotate_out_body, blocks, extra),
            grid_spec=pltpu.PrefetchScalarGridSpec(
                num_scalar_prefetch=1,
                grid=(groups,),
                in_specs=[table_spec, table_spec] + [by_span] * parts,
                out_specs=[by_rows] * blocks,
                scratch_shapes=[pltpu.VMEM((span, lanes), BF)],
            ),
            out_shape=[jax.ShapeDtypeStruct((count, lanes), BF)] * blocks,
            name="rotate_out",
        )(place, cos_table, sin_table, *grads)
    leaving, output_part = lax.optimization_barrier((leaving, output_part))
    back = swap(leaving, "blk")
    output_part = sum(x.astype(F32) for x in output_part).astype(BF).reshape(blocks, gain_rows, width)
    output_part = halve(output_part, "blk", block_id, 1)
    back, feed_half, output_part = lax.optimization_barrier((back, feed_half, output_part))

    returned = pl.pallas_call(
        functools.partial(project_back_body, blocks, pairs, heads, extra),
        out_shape=[jax.ShapeDtypeStruct((micro, rows, width), BF)] * groups
        + [
            jax.ShapeDtypeStruct((width, heads * 3 * head_width), BF),
            jax.ShapeDtypeStruct((micro, width), F32),
            jax.ShapeDtypeStruct((micro, width), F32),
        ],
        in_specs=[smem] + [whole_vmem()] * (3 + groups + blocks),
        out_specs=[whole_vmem()] * (groups + 3),
        scratch_shapes=[pltpu.VMEM((blocks, count, lanes), BF)],
        cost_estimate=pl.CostEstimate(
            flops=4 * micro * count * width * 3 * 64 * heads, transcendentals=0, bytes_accessed=8 * own * width
        ),
        name="project_back",
    )(place, c1, shift1, in_own, *n1_group, *back)
    input_part, d_shift1, p1 = returned[groups:]
    grad_first = sum(x.astype(F32) for x in swap(returned[:groups], "ulysses"))
    e = grad_first * c1[:, None]
    tokens_grad = (
        grad_middle.reshape(micro, rows, width)
        + r1
        * (
            e
            - jnp.mean(e, -1, keepdims=True)
            - n1 * jnp.mean(e * n1, -1, keepdims=True)
        )
    ).astype(BF)

    grad_mods = jnp.concatenate(
        [d_shift1, p1 * gain1, d_gate1, d_shift2, p2 * gain2, d_gate2], 1
    )
    gain1_part = jnp.sum((1.0 + scale1) * p1, 0)
    gain2_part = jnp.sum((1.0 + scale2) * p2, 0)
    own_units = jnp.where(
        (jnp.arange(groups) == group_id)[:, None], bias_part.reshape(1, width), 0.0
    )
    small_parts = jnp.concatenate(
        [grad_mods.reshape(micro, devices, mod_rows).transpose(1, 0, 2).reshape(devices, -1)]
        + [
            x.reshape(devices, -1)
            for x in (gain1_part, gain2_part, jnp.sum(dm_sums, 0), own_units)
        ],
        1,
    ).astype(BF)
    taken = small_parts.shape[1]
    small_rows = 8 * -(-taken // (8 * in_lanes))
    small_parts = jnp.pad(small_parts, ((0, 0), (0, small_rows * in_lanes - taken)))
    input_part = jnp.concatenate(
        [
            input_part.reshape(groups, blocks, gain_rows, in_lanes),
            small_parts.reshape(groups, blocks, small_rows, in_lanes),
        ],
        2,
    ).transpose(1, 0, 2, 3)
    input_sum = halve(input_part, "blk", block_id, 1)
    weight_sum, bit = jnp.concatenate([feed_half, output_part], 1), 2
    while bit < blocks:
        weight_sum = halve(weight_sum, "blk", block_id, bit)
        input_sum = halve(input_sum, "blk", block_id, bit)
        bit *= 2
    weight_sum, input_sum = weight_sum[0], input_sum[0]
    final = jnp.stack(
        swap(
            [
                lax.dynamic_index_in_dim(input_sum, group_id ^ k, 0, keepdims=False)
                for k in range(groups)
            ],
            "ulysses",
        )
    )
    small_sum = jnp.sum(final[:, gain_rows:].astype(F32), 0).reshape(-1)
    input_sum = unscramble(final[:, :gain_rows], group_id, 0).astype(F32)
    reduce_grad = weight_sum[:ff_rows].astype(F32)
    output_grad = weight_sum[-gain_rows:].astype(F32)
    expand_rows = weight_sum[ff_rows:-gain_rows].reshape(groups, gain_rows, width)
    expand_came = jnp.stack(
        swap(
            [
                lax.dynamic_index_in_dim(expand_rows, group_id ^ k, 0, keepdims=False)
                for k in range(groups)
            ],
            "ulysses",
        )
    )
    expand_grad = jnp.concatenate(
        [
            lax.dynamic_index_in_dim(expand_came, group_id ^ k, 0, keepdims=False)
            for k in range(groups)
        ],
        1,
    ).astype(F32)

    two = heads * 2 * head_width
    input_grad = jnp.concatenate(
        [
            input_sum[:, :, :two]
            .reshape(groups, gain_rows, heads, 2, head_width)
            .transpose(1, 3, 0, 2, 4)
            .reshape(gain_rows, 2 * width),
            input_sum[:, :, two:].transpose(1, 0, 2).reshape(gain_rows, width),
        ],
        1,
    )
    at = micro * mod_rows
    mod_sum = small_sum[:at].reshape(micro, mod_rows)
    modulate_weight_grad = jnp.sum(
        mod_sum[:, :, None] * condition.astype(F32)[:, None, :], 0
    )
    cuts = []
    for length in (gain_rows, gain_rows, gain_rows, ff_rows):
        cuts.append(small_sum[at : at + length])
        at += length
    return (
        layer_output.reshape(micro, rows, width),
        tokens_grad,
        modulate_weight_grad,
        jnp.sum(mod_sum, 0),
        cuts[0],
        input_grad,
        output_grad,
        cuts[1],
        expand_grad,
        cuts[3],
        reduce_grad,
        cuts[2],
    )


def solution(mesh):
    both = P(("ulysses", "blk"))
    tall = P(("ulysses", "blk"), None)
    seq = P(None, ("ulysses", "blk"), None)
    in_specs = (
        seq, seq, P(), P(), tall, both, both, tall, tall, both, tall, both, tall, both,
    )
    out_specs = (seq, seq, tall, both, both, tall, tall, both, tall, both, tall, both)
    return jax.shard_map(
        on_device, mesh=mesh, in_specs=in_specs, out_specs=out_specs, check_vma=False
    )
```

```python
import functools
import math

import jax
import jax.numpy as jnp
from jax import lax
from jax.experimental import pallas as pl
from jax.experimental.pallas import tpu as pltpu
from jax.sharding import PartitionSpec as P

HEADS = 12
ALL = ("ulysses", "blk")
BF = jnp.bfloat16
F32 = jnp.float32
NEG = -1e30


def exchange(x):
    return lax.all_to_all(x, ALL, split_axis=0, concat_axis=0, tiled=True)


def time_features(time_step, half):
    freqs = jnp.exp(-math.log(10000.0) * jnp.arange(half, dtype=F32) / half)
    angles = time_step.astype(F32)[:, None] * freqs[None, :]
    return jax.nn.silu(jnp.concatenate([jnp.cos(angles), jnp.sin(angles)], 1)).astype(BF)


def doc_layout(index, lengths_row):
    ends = jnp.cumsum(lengths_row)
    over = index[:, None] >= ends[None, :]
    segment = jnp.sum(over.astype(jnp.int32), 1)
    place = index - jnp.sum(jnp.where(over, lengths_row[None, :], 0), 1)
    return segment, place


def key_ranges(first, last, lengths_row, block):
    ends = jnp.cumsum(lengths_row)
    start = jnp.sum(jnp.where(first[:, None] >= ends[None, :], lengths_row[None, :], 0), 1)
    stop = jnp.min(jnp.where(ends[None, :] > last[:, None], ends[None, :], 1 << 30), 1)
    return jnp.stack([start // block, (stop + block - 1) // block], 1).reshape(-1)


def whole_vmem():
    return pl.BlockSpec(memory_space=pltpu.VMEM)


def swap(blocks, axis):
    size = lax.axis_size(axis)
    return [
        x if k == 0 else lax.ppermute(x, axis, [(i, i ^ k) for i in range(size)])
        for k, x in enumerate(blocks)
    ]


def unscramble(x, index, axis):
    count, bit = x.shape[axis], 1
    while bit < count:
        shape = x.shape
        y = x.reshape(shape[:axis] + (count // (2 * bit), 2, bit) + shape[axis + 1 :])
        flipped = jnp.flip(y, axis + 1)
        x = jnp.where((index & bit) != 0, flipped, y).reshape(shape)
        bit *= 2
    return x


def halve(x, axis, index, bit):
    size = lax.axis_size(axis)
    y = x.reshape((-1, 2) + x.shape[1:])
    mine = (index // bit) % 2
    sent = lax.dynamic_index_in_dim(y, 1 - mine, 1, keepdims=False)
    kept = lax.dynamic_index_in_dim(y, mine, 1, keepdims=False)
    came = lax.ppermute(sent, axis, [(i, i ^ bit) for i in range(size)])
    return (kept.astype(F32) + came.astype(F32)).astype(BF)


def project_body(blocks, pairs, heads, extra, place_ref, c_ref, shift_ref, w_ref, *refs):
    groups = len(refs) - blocks - 1
    tokens, outs, kept = refs[:groups], refs[groups:-1], refs[-1]
    micro, rows, width = tokens[0].shape
    end = 192 * heads
    weights = [w_ref[:, c : min(c + 128, end)] for c in range(0, end, 128)]
    order = list(range(micro))[::-1]
    z_qk = z_v = None
    for m in order:
        a = jnp.concatenate(
            [(x[m].astype(F32) * c_ref[m][None] + shift_ref[m][None]).astype(BF) for x in tokens], 0
        )
        parts = [jnp.dot(a, w, preferred_element_type=F32).astype(BF) for w in weights]
        v = jnp.concatenate(parts[heads:], 1)
        if extra and m == micro - 1:
            z_qk = parts[heads - 1]
            z_v = v[:, (heads - 1) * 64 : heads * 64]
        for h in range(heads):
            pair = m * heads + h
            if pair >= blocks:
                continue
            kept[pair, :, :128] = parts[h]
            own_v = v[:, h * 64 : (h + 1) * 64]
            if extra:
                kept[pair, :, 128:256] = z_qk
                kept[pair, :, 256:] = jnp.concatenate([own_v, z_v], 1)
            else:
                kept[pair, :, 128:] = jnp.concatenate([own_v, jnp.zeros_like(own_v)], 1)
    for pair in range(pairs, blocks):
        kept[pair] = jnp.zeros(kept.shape[1:], BF)
    for j in range(blocks):
        outs[j][...] = kept[place_ref[1] ^ j]


def turn_tables(cos, sin, extra):
    lane = lax.broadcasted_iota(jnp.int32, cos.shape, 1)
    low = lane < 64
    cos_r, sin_r = pltpu.roll(cos, 64, 1), pltpu.roll(sin, 64, 1)
    tables = [(jnp.where(low, cos, cos_r), jnp.where(low, sin, sin_r))]
    if extra:
        tables.append((jnp.where(low, cos_r, cos), jnp.where(low, sin_r, sin)))
    return tables


def turn(x, table):
    lane = lax.broadcasted_iota(jnp.int32, x.shape, 1)
    swapped = jnp.where(lane % 64 < 32, pltpu.roll(x, 96, 1), pltpu.roll(x, 32, 1))
    return x * table[0] + swapped * table[1]


def rotate_in_body(blocks, extra, place_ref, cos_ref, sin_ref, *refs):
    ins, outs = refs[:blocks], refs[blocks : 2 * blocks - blocks + (6 if extra else 3)]
    kept = refs[-1]
    rows = ins[0].shape[0]
    for j in range(blocks):
        at = pl.multiple_of((place_ref[1] ^ j) * rows, rows)
        kept[pl.ds(at, rows), :] = ins[j][...]
    tables = turn_tables(cos_ref[...], sin_ref[...], extra)
    x0 = turn(kept[:, :128].astype(F32), tables[0])
    outs[0][...] = (x0[:, :64] * 0.125).astype(BF)
    outs[1][...] = x0[:, 64:].astype(BF)
    if extra:
        outs[2][...] = kept[:, 256:320]
        x1 = turn(kept[:, 128:256].astype(F32), tables[1])
        outs[3][...] = (x1[:, :64] * 0.125).astype(BF)
        outs[4][...] = x1[:, 64:].astype(BF)
        outs[5][...] = kept[:, 320:]
    else:
        outs[2][...] = kept[:, 128:192]


def rotate_out_body(blocks, extra, place_ref, cos_ref, sin_ref, *refs):
    count = 6 if extra else 3
    ins, outs, kept = refs[:count], refs[count:-1], refs[-1]
    rows = outs[0].shape[0]
    parts = [ref[...].astype(F32) for ref in ins]
    tables = [(c, -s) for c, s in turn_tables(cos_ref[...], sin_ref[...], extra)]
    kept[:, :128] = turn(jnp.concatenate(parts[:2], 1), tables[0]).astype(BF)
    if extra:
        kept[:, 128:256] = turn(jnp.concatenate(parts[3:5], 1), tables[1]).astype(BF)
        kept[:, 256:] = jnp.concatenate([parts[2], parts[5]], 1).astype(BF)
    else:
        kept[:, 128:] = jnp.concatenate([parts[2], jnp.zeros_like(parts[2])], 1).astype(BF)
    for j in range(blocks):
        at = pl.multiple_of((place_ref[1] ^ j) * rows, rows)
        outs[j][...] = kept[pl.ds(at, rows), :]


def project_back_body(blocks, pairs, heads, extra, place_ref, c_ref, shift_ref, w_ref, *refs):
    kept = refs[-1]
    groups = (len(refs) - blocks - 4) // 2
    tokens, ins = refs[:groups], refs[groups : groups + blocks]
    outs = refs[groups + blocks : 2 * groups + blocks]
    grad_ref, sum_ref, dot_ref = refs[2 * groups + blocks : -1]
    micro, rows, width = tokens[0].shape
    count = groups * rows
    for j in range(blocks):
        kept[place_ref[1] ^ j] = ins[j][...]
    last = None
    if extra:
        last = jnp.zeros((count, 256), F32)
        for j in range(blocks):
            last = last + kept[j, :, 128:].astype(F32)
        last = last.astype(BF)
    all_a, all_g = [], []
    for m in range(micro):
        n = jnp.concatenate([x[m] for x in tokens], 0).astype(F32)
        a = (n * c_ref[m][None] + shift_ref[m][None]).astype(BF)
        qk, v = [], []
        for h in range(heads):
            pair = m * heads + h
            if pair < blocks:
                qk.append(kept[pair, :, :128])
                at = 256 if extra else 128
                v.append(kept[pair, :, at : at + 64])
            else:
                qk.append(last[:, :128])
                v.append(last[:, 192:])
        g = jnp.concatenate(qk + v, 1)
        da = lax.dot_general(g, w_ref[:, : 192 * heads], (((1,), (1,)), ((), ())), preferred_element_type=F32)
        for k in range(groups):
            outs[k][m] = da[k * rows : (k + 1) * rows].astype(BF)
        sum_ref[m : m + 1] = jnp.sum(da, 0, keepdims=True)
        dot_ref[m : m + 1] = jnp.sum(da * n, 0, keepdims=True)
        all_a.append(a)
        all_g.append(g)
    grad_ref[...] = lax.dot_general(
        jnp.concatenate(all_a, 0), jnp.concatenate(all_g, 0), (((0,), (0,)), ((), ())),
        preferred_element_type=F32,
    ).astype(BF)


def norm(values):
    centered = values - jnp.mean(values, -1, keepdims=True)
    inverse = lax.rsqrt(jnp.mean(centered * centered, -1, keepdims=True) + 1e-05)
    return centered * inverse, inverse


def by_micro(ref, rows):
    return jnp.concatenate(
        [jnp.broadcast_to(ref[m][None], (rows, ref.shape[1])) for m in range(ref.shape[0])], 0
    )


def middle_body(
    groups, blocks, heads, micro, rows, stripe,
    came_ref, out_ref, x_ref, gate_ref, c_ref, shift_ref,
    merged_ref, attn_ref, middle_ref, second_ref,
):
    width = x_ref.shape[1]
    for u in range(groups):
        for m in range(micro):
            for h in range(heads):
                pair = m * heads + h
                lanes = slice((u * heads + h) * 64, (u * heads + h + 1) * 64)
                half = rows // 2
                if pair < blocks and stripe:
                    at = m * rows
                    merged_ref[at : at + half, lanes] = came_ref[u * blocks + pair, :half, :64]
                    merged_ref[at + half : at + rows, lanes] = came_ref[u * blocks + pair, :half, 64:]
                elif pair < blocks:
                    merged_ref[m * rows : (m + 1) * rows, lanes] = came_ref[u * blocks + pair]
                else:
                    for b in range(blocks):
                        at = m * rows + b * stripe
                        merged_ref[at : at + stripe, lanes] = came_ref[u * blocks + b, half:, :64]
    attn = jnp.dot(merged_ref[...], out_ref[...].reshape(width, width), preferred_element_type=F32)
    attn_ref[...] = attn
    middle = x_ref[...].astype(F32) + by_micro(gate_ref, rows) * attn
    middle_ref[...] = middle
    normed, _ = norm(middle)
    second_ref[...] = (normed * by_micro(c_ref, rows) + by_micro(shift_ref, rows)).astype(BF)


def gelu_pair(u):
    t = jnp.tanh(0.7978845608028654 * (u + 0.044715 * u * u * u))
    value = 0.5 * u * (1.0 + t)
    slope = 0.5 * (1.0 + t) + 0.5 * u * (1.0 - t * t) * (
        0.7978845608028654 * (1.0 + 0.134145 * u * u)
    )
    return value, slope


NT = (((1,), (1,)), ((), ()))
TN = (((0,), (0,)), ((), ()))


def feed_body(
    groups, blocks, heads, micro, rows, stripe,
    ex_ref, re_ref, out_w_ref, ex_bias_ref, re_bias_ref, second_ref, middle_ref, attn_ref, dy_ref,
    gate1_ref, gate2_ref, c_ref,
    layer_ref, grad_ref, dattn_ref, do_ref, sums_ref,
    branch_sum, back_sum, dm_sum, do_sum,
):
    step = pl.program_id(0)
    width = middle_ref.shape[1]

    @pl.when(step == 0)
    def _():
        branch_sum[...] = jnp.zeros_like(branch_sum)
        back_sum[...] = jnp.zeros_like(back_sum)
        dm_sum[...] = (by_micro(gate2_ref, rows) * dy_ref[...].astype(F32)).astype(BF)

    expand = ex_ref[...].reshape(width, width)
    reduce = re_ref[...].reshape(width, width)
    u = jnp.dot(second_ref[...], expand, preferred_element_type=F32) + ex_bias_ref[0]
    g, slope = gelu_pair(u)
    branch_sum[...] += jnp.dot(g.astype(BF), reduce, preferred_element_type=F32)
    dg = lax.dot_general(dm_sum[...], reduce, NT, preferred_element_type=F32)
    du = (dg * slope).astype(BF)
    back_sum[...] += lax.dot_general(du, expand, NT, preferred_element_type=F32)

    @pl.when(step == pl.num_programs(0) - 1)
    def _():
        def total(at, x):
            for m in range(micro):
                sums_ref[at * micro + m : at * micro + m + 1] = jnp.sum(
                    x[m * rows : (m + 1) * rows], 0, keepdims=True
                )

        branch = branch_sum[...] + re_bias_ref[...]
        middle = middle_ref[...]
        dy = dy_ref[...].astype(F32)
        layer_ref[...] = (middle + by_micro(gate2_ref, rows) * branch).astype(BF)
        total(0, dy * branch)
        normed, inverse = norm(middle)
        db = back_sum[...]
        total(1, db)
        total(2, db * normed)
        e = db * by_micro(c_ref, rows)
        grad = dy + inverse * (
            e
            - jnp.mean(e, -1, keepdims=True)
            - normed * jnp.mean(e * normed, -1, keepdims=True)
        )
        grad_ref[...] = grad
        total(3, grad * attn_ref[...])
        total(4, dm_sum[...].astype(F32))
        dattn = (by_micro(gate1_ref, rows) * grad).astype(BF)
        dattn_ref[...] = dattn
        do_sum[...] = lax.dot_general(
            dattn, out_w_ref[...].reshape(width, width), NT, preferred_element_type=F32
        ).astype(BF)
        for at in range(groups):
            for m in range(micro):
                for h in range(heads):
                    pair = m * heads + h
                    lanes = slice((at * heads + h) * 64, (at * heads + h + 1) * 64)
                    half, top = rows // 2, m * rows
                    if pair < blocks and stripe:
                        do_ref[at * blocks + pair, :half, :64] = do_sum[top : top + half, lanes]
                        do_ref[at * blocks + pair, :half, 64:] = do_sum[top + half : top + rows, lanes]
                    elif pair < blocks:
                        do_ref[at * blocks + pair] = do_sum[top : top + rows, lanes]
                    else:
                        for b in range(blocks):
                            do_ref[at * blocks + b, half:, :64] = do_sum[top : top + stripe, lanes]
                            do_ref[at * blocks + b, half:, 64:] = jnp.zeros((stripe, 64), BF)
                            top += stripe
            for b in range(micro * heads, blocks):
                do_ref[at * blocks + b] = jnp.zeros((rows, 64), BF)


def feed_weights_body(rows, place_ref, ex_ref, re_ref, bias_ref, gate_ref, *refs):
    groups = (len(refs) - 3) // 2
    reduce_ref, expand_ref, sum_ref = refs[2 * groups :]
    width = refs[0].shape[-1]
    second = jnp.concatenate([x[...] for x in refs[:groups]], 0)
    gate = by_micro(gate_ref, rows)
    dm = jnp.concatenate(
        [(gate * x[...].astype(F32)).astype(BF) for x in refs[groups : 2 * groups]], 0
    )
    expand = ex_ref[...].reshape(width, width)
    reduce = re_ref[...].reshape(width, width)
    u = jnp.dot(second, expand, preferred_element_type=F32) + bias_ref[0]
    g, slope = gelu_pair(u)
    du = lax.dot_general(dm, reduce, NT, preferred_element_type=F32) * slope
    du = du.astype(BF)
    sum_ref[...] = jnp.sum(du.astype(F32), 0, keepdims=True)
    reduce_ref[...] = lax.dot_general(g.astype(BF), dm, TN, preferred_element_type=F32).astype(BF)
    expand_ref[...] = lax.dot_general(second, du, TN, preferred_element_type=F32).astype(BF)


def attend_body(block, range_ref, q_ref, sq_ref, k_ref, v_ref, sk_ref, o_ref, lse_ref):
    i = pl.program_id(0)
    q, sq = q_ref[...], sq_ref[0]
    count, width = q.shape

    def step(j, carry):
        high, total, acc = carry
        at = pl.ds(pl.multiple_of(j * block, block), block)
        k, v, sk = k_ref[at, :], v_ref[at, :], sk_ref[at, :]
        s = lax.dot_general(k, q, (((1,), (1,)), ((), ())), preferred_element_type=F32)
        s = jnp.where(sk == sq, s, NEG)
        new = jnp.maximum(high, jnp.max(s, 0, keepdims=True))
        p = jnp.exp(s - new)
        fix = jnp.exp(high - new)
        total = total * fix + jnp.sum(p, 0, keepdims=True)
        acc = acc * fix + lax.dot_general(
            v, p.astype(BF), (((0,), (0,)), ((), ())), preferred_element_type=F32
        )
        return new, total, acc

    first = (
        jnp.full((1, count), NEG, F32),
        jnp.zeros((1, count), F32),
        jnp.zeros((width, count), F32),
    )
    high, total, acc = lax.fori_loop(range_ref[2 * i], range_ref[2 * i + 1], step, first)
    o_ref[...] = (acc / total).T.astype(BF)
    lse_ref[0] = high + jnp.log(total)


def attend_back_body(
    block, range_ref, q_ref, sq_ref, lse_ref, o_ref, do_ref, k_ref, v_ref, sk_ref,
    dq_ref, dk_ref, dv_ref, dk_sum, dv_sum,
):
    i = pl.program_id(0)

    @pl.when(i == 0)
    def _():
        dk_sum[...] = jnp.zeros_like(dk_sum)
        dv_sum[...] = jnp.zeros_like(dv_sum)

    q, sq, lse, do = q_ref[...], sq_ref[0], lse_ref[0], do_ref[...]
    count, width = q.shape
    delta = jnp.sum((do.astype(F32) * o_ref[...].astype(F32)).T, 0, keepdims=True)

    def step(j, dq):
        at = pl.ds(pl.multiple_of(j * block, block), block)
        k, v, sk = k_ref[at, :], v_ref[at, :], sk_ref[at, :]
        s = lax.dot_general(k, q, (((1,), (1,)), ((), ())), preferred_element_type=F32)
        p = jnp.where(sk == sq, jnp.exp(s - lse), 0.0)
        dp = lax.dot_general(v, do, (((1,), (1,)), ((), ())), preferred_element_type=F32)
        ds = (p * (dp - delta)).astype(BF)
        dv_sum[at, :] += jnp.dot(p.astype(BF), do, preferred_element_type=F32)
        dk_sum[at, :] += jnp.dot(ds, q, preferred_element_type=F32)
        return dq + lax.dot_general(
            k, ds, (((0,), (0,)), ((), ())), preferred_element_type=F32
        )

    dq = lax.fori_loop(
        range_ref[2 * i], range_ref[2 * i + 1], step, jnp.zeros((width, count), F32)
    )
    dq_ref[...] = (dq * 0.125).T.astype(BF)

    @pl.when(i == pl.num_programs(0) - 1)
    def _():
        dk_ref[...] = dk_sum[...].astype(BF)
        dv_ref[...] = dv_sum[...].astype(BF)


def attend(ranges, q, sq, k, v, sk, rows, block):
    count, width = q.shape
    steps = count // rows
    size = k.shape[0]
    by_row = pl.BlockSpec((rows, width), lambda i, r: (i, 0))
    as_row = pl.BlockSpec((1, 1, rows), lambda i, r: (i, 0, 0))
    return pl.pallas_call(
        functools.partial(attend_body, block),
        grid_spec=pltpu.PrefetchScalarGridSpec(
            num_scalar_prefetch=1,
            grid=(steps,),
            in_specs=[by_row, as_row, whole_vmem(), whole_vmem(), whole_vmem()],
            out_specs=[by_row, as_row],
        ),
        out_shape=[
            jax.ShapeDtypeStruct((count, width), BF),
            jax.ShapeDtypeStruct((steps, 1, rows), F32),
        ],
        cost_estimate=pl.CostEstimate(
            flops=count * size * width, transcendentals=count * size // 4, bytes_accessed=4 * size * width
        ),
        name="attend",
    )(ranges, q, sq.reshape(steps, 1, rows), k, v, sk)


def attend_back(ranges, q, sq, lse, o, do, k, v, sk, rows, block):
    count, width = q.shape
    steps = count // rows
    size = k.shape[0]
    by_row = pl.BlockSpec((rows, width), lambda i, r: (i, 0))
    as_row = pl.BlockSpec((1, 1, rows), lambda i, r: (i, 0, 0))
    return pl.pallas_call(
        functools.partial(attend_back_body, block),
        grid_spec=pltpu.PrefetchScalarGridSpec(
            num_scalar_prefetch=1,
            grid=(steps,),
            in_specs=[by_row, as_row, as_row, by_row, by_row, whole_vmem(), whole_vmem(), whole_vmem()],
            out_specs=[by_row, whole_vmem(), whole_vmem()],
            scratch_shapes=[pltpu.VMEM((size, width), F32)] * 2,
        ),
        out_shape=[
            jax.ShapeDtypeStruct((count, width), BF),
            jax.ShapeDtypeStruct((size, width), BF),
            jax.ShapeDtypeStruct((size, width), BF),
        ],
        cost_estimate=pl.CostEstimate(
            flops=3 * count * size * width, transcendentals=count * size // 4, bytes_accessed=8 * size * width
        ),
        name="attend_back",
    )(ranges, q, sq.reshape(steps, 1, rows), lse, o, do, k, v, sk)


def spread(ref, at, rows):
    return ref[pl.ds(pl.multiple_of(at, rows), rows), :]


def keys_mask(low, high, at, count):
    position = at + lax.broadcasted_iota(jnp.int32, (count, low.shape[1]), 0)
    return (position >= low) & (position < high)


QB, KB = 256, 512


def project_small_body(blocks, heads, c_ref, shift_ref, w_ref, *refs):
    groups = len(refs) - 3
    tokens, out_ref, last_ref, wide = refs[:groups], *refs[groups:]
    micro, rows, width = tokens[0].shape
    count = groups * rows
    half, stripe = count // 2, rows // blocks
    end = 192 * heads
    weights = [w_ref[:, c : min(c + 128, end)] for c in range(0, end, 128)]
    for m in range(micro):
        a = jnp.concatenate(
            [(x[m].astype(F32) * c_ref[m][None] + shift_ref[m][None]).astype(BF) for x in tokens], 0
        )
        parts = [jnp.dot(a, w, preferred_element_type=F32) for w in weights]
        v = jnp.concatenate(parts[heads:], 1)
        for h in range(heads):
            pair = m * heads + h
            own_v = v[:, h * 64 : (h + 1) * 64]
            if pair < blocks:
                out_ref[pair, :count] = parts[h].astype(BF)
                out_ref[pair, count : count + half] = jnp.concatenate([own_v[:half], own_v[half:]], 1).astype(BF)
            else:
                wide[...] = parts[h]
                last_ref[...] = jnp.concatenate([parts[h][:, 64:], own_v], 1).astype(BF)
    for to in range(blocks):
        pieces = [
            wide[k * rows + to * stripe : k * rows + (to + 1) * stripe, :64] for k in range(groups)
        ]
        out_ref[to, count + half :] = jnp.concatenate(
            [jnp.concatenate(pieces[:2], 0), jnp.concatenate(pieces[2:], 0)], 1
        ).astype(BF)


def pick_piece(x, k):
    y = jnp.where((k & 1) != 0, x[8:], x[:8])
    return jnp.where(k >= 2, y[:, 64:], y[:, :64])


def project_back_small_body(blocks, heads, c_ref, shift_ref, w_ref, *refs):
    wide = refs[-1]
    few = blocks // 2
    groups = (len(refs) - few - 5) // 2
    tokens, in_ref, lasts = refs[:groups], refs[groups], refs[groups + 1 : groups + 1 + few]
    outs = refs[groups + 1 + few : 2 * groups + 1 + few]
    grad_ref, sum_ref, dot_ref = refs[2 * groups + 1 + few : -1]
    micro, rows, width = tokens[0].shape
    count = groups * rows
    half, stripe = count // 2, rows // blocks
    for j in range(blocks):
        x = in_ref[j, count + half :].astype(F32)
        pieces = [x[:8, :64], x[8:, :64], x[:8, 64:], x[8:, 64:]]
        for k in range(groups):
            wide[k * rows + j * stripe : k * rows + (j + 1) * stripe] = pieces[k]
    all_a, all_g = [], []
    for m in range(micro):
        n = jnp.concatenate([x[m] for x in tokens], 0).astype(F32)
        a = (n * c_ref[m][None] + shift_ref[m][None]).astype(BF)
        qk, v = [], []
        for h in range(heads):
            pair = m * heads + h
            if pair < blocks:
                qk.append(in_ref[pair, :count])
                x = in_ref[pair, count : count + half]
                v.append(jnp.concatenate([x[:, :64], x[:, 64:]], 0))
            else:
                x = sum(ref[...].astype(F32) for ref in lasts).astype(BF)
                qk.append(jnp.concatenate([wide[...].astype(BF), x[:, :64]], 1))
                v.append(x[:, 64:])
        g = jnp.concatenate(qk + v, 1)
        da = lax.dot_general(g, w_ref[:, : 192 * heads], NT, preferred_element_type=F32)
        for k in range(groups):
            outs[k][m] = da[k * rows : (k + 1) * rows].astype(BF)
        sum_ref[m : m + 1] = jnp.sum(da, 0, keepdims=True)
        dot_ref[m : m + 1] = jnp.sum(da * n, 0, keepdims=True)
        all_a.append(a)
        all_g.append(g)
    grad_ref[...] = lax.dot_general(
        jnp.concatenate(all_a, 0), jnp.concatenate(all_g, 0), TN, preferred_element_type=F32
    ).astype(BF)


def attend_block(scores, q, low, high, first, stop, keys, values):
    count = q.shape[0]

    def score(t, top):
        at = pl.multiple_of((first + 2 * t) * QB, QB)
        s = lax.dot_general(keys[pl.ds(at, KB), :], q, NT, preferred_element_type=F32)
        s = jnp.where(keys_mask(low, high, at, KB), s, NEG)
        scores[t, :, :count] = s
        return jnp.maximum(top, jnp.max(s, 0, keepdims=True))

    steps = (stop - first + 1) // 2
    top = lax.fori_loop(0, steps, score, jnp.full((1, count), NEG, F32))

    def weigh(t, carry):
        total, acc = carry
        at = pl.multiple_of((first + 2 * t) * QB, QB)
        p = jnp.exp(scores[t, :, :count] - top)
        return total + jnp.sum(p, 0, keepdims=True), acc + lax.dot_general(
            values[pl.ds(at, KB), :], p.astype(BF), TN, preferred_element_type=F32
        )

    total, acc = lax.fori_loop(
        0, steps, weigh, (jnp.zeros((1, count), F32), jnp.zeros((64, count), F32))
    )
    return (acc / total).T, top + jnp.log(total)


def attend_own_body(
    blocks, groups, rows, place_ref, range_ref, low_ref, high_ref, cos_ref, sin_ref, *refs
):
    in_ref, message, q_ref, k_ref, v_ref, o_ref, lse_ref, kept, kept_v, scores = refs
    span = blocks * rows
    size = groups * span
    count = groups * rows
    half = rows // 2
    me_u, me_b = place_ref[0], place_ref[1]
    for g in range(groups):
        k = me_u ^ g
        for j in range(blocks):
            to = slice(j * rows, (j + 1) * rows)
            kept[to, :] = in_ref[j, pl.ds(pl.multiple_of(k * rows, rows), rows), :]
            pair = in_ref[j, pl.ds(pl.multiple_of(count + (k & 1) * rows, rows), rows), :].astype(F32)
            kept_v[to, :] = jnp.where(k >= 2, pair[:, 64:], pair[:, :64]).astype(BF)
        at = slice(g * span, (g + 1) * span)
        x = turn(kept[...].astype(F32), turn_tables(cos_ref[at], sin_ref[at], False)[0])
        q_ref[at] = (x[:, :64] * 0.125).astype(BF)
        k_ref[at] = x[:, 64:].astype(BF)
        v_ref[at] = kept_v[...]
    tail = slice(size, size + KB - QB)
    for ref in (k_ref, v_ref):
        ref[tail] = jnp.zeros((KB - QB, 64), BF)

    def run(i, _):
        o, lse = attend_block(
            scores, spread(q_ref, i * QB, QB), low_ref[i], high_ref[i],
            range_ref[2 * i], range_ref[2 * i + 1], k_ref, v_ref,
        )
        o = o.astype(BF)
        o_ref[pl.ds(pl.multiple_of(i * QB, QB), QB), :] = o
        lse_ref[i] = lse
        for d in range(QB // rows):
            message[i * (QB // rows) + d] = jnp.concatenate(
                [o[d * rows : d * rows + half], o[d * rows + half : (d + 1) * rows]], 1
            )
        return 0

    lax.fori_loop(0, size // QB, run, 0)


def stripe_tables(place_ref, cos_ref, sin_ref, wide_cos, wide_sin, devices, rows, stripe):
    for d in range(devices):
        at = slice(d * stripe, (d + 1) * stripe)
        wide_cos[at] = spread(cos_ref, d * rows + place_ref[1] * stripe, stripe)
        wide_sin[at] = spread(sin_ref, d * rows + place_ref[1] * stripe, stripe)
    return turn_tables(wide_cos[...], wide_sin[...], True)[1]


def attend_last_body(
    blocks, groups, rows, stripe, place_ref, range_ref, low_ref, high_ref, cos_ref, sin_ref, *refs
):
    in_ref, last_ins, own_ref = refs[0], refs[1:3], refs[3]
    message, q_ref, k_ref, v_ref, o_ref, lse_ref, kept, wide, wide_cos, wide_sin, scores = refs[4:]
    span = blocks * rows
    size = groups * span
    devices = groups * blocks
    count = groups * rows
    half = rows // 2
    me_u, me_b = place_ref[0], place_ref[1]
    for g in range(groups):
        k = me_u ^ g
        for j in range(blocks):
            at = (g * blocks + j) * stripe
            wide[at : at + stripe, :64] = pick_piece(in_ref[j, count + count // 2 :].astype(F32), k)
            to = pl.ds(pl.multiple_of((me_b ^ j) * rows, rows), rows)
            kept[to, :] = last_ins[j & 1][j >> 1, pl.ds(pl.multiple_of(k * rows, rows), rows), :]
        at = slice(g * span, (g + 1) * span)
        x = turn(kept[...].astype(F32), turn_tables(cos_ref[at], sin_ref[at], True)[1])
        k_ref[at] = x[:, :64].astype(BF)
        v_ref[at] = kept[:, 64:]
    tail = slice(size, size + KB - QB)
    for ref in (k_ref, v_ref):
        ref[tail] = jnp.zeros((KB - QB, 64), BF)
    wide[:, 64:] = jnp.zeros((devices * stripe, 64), F32)
    x = turn(wide[...], stripe_tables(place_ref, cos_ref, sin_ref, wide_cos, wide_sin, devices, rows, stripe))
    q_ref[...] = (x[:, :64] * 0.125).astype(BF)
    message[:, :half] = own_ref[...]
    few = lse_ref.shape[2]

    def run(i, _):
        o, lse = attend_block(
            scores, spread(q_ref, i * few, few), low_ref[i], high_ref[i],
            range_ref[2 * i], range_ref[2 * i + 1], k_ref, v_ref,
        )
        o_ref[pl.ds(pl.multiple_of(i * few, few), few), :] = o.astype(BF)
        lse_ref[i] = lse
        o = jnp.concatenate([o, jnp.zeros_like(o)], 1)
        for d in range(few // stripe):
            message[i * (few // stripe) + d, half:] = o[d * stripe : (d + 1) * stripe].astype(BF)
        return 0

    lax.fori_loop(0, lse_ref.shape[0], run, 0)


def attend_block_back(q, do, o, lse, low, high, first, stop, keys, values, dk_sum, dv_sum):
    count = q.shape[0]
    delta = jnp.sum((do.astype(F32) * o.astype(F32)).T, 0, keepdims=True)

    def step(t, dq):
        at = pl.multiple_of((first + 2 * t) * QB, QB)
        here = pl.ds(at, KB)
        k, v = keys[here, :], values[here, :]
        s = lax.dot_general(k, q, NT, preferred_element_type=F32)
        dp = lax.dot_general(v, do, NT, preferred_element_type=F32)
        p = jnp.where(keys_mask(low, high, at, KB), jnp.exp(s - lse), 0.0)
        ds = (p * (dp - delta)).astype(BF)
        dv_sum[here, :] += jnp.dot(p.astype(BF), do, preferred_element_type=F32)
        dk_sum[here, :] += jnp.dot(ds, q, preferred_element_type=F32)
        return dq + lax.dot_general(k, ds, TN, preferred_element_type=F32)

    return (
        lax.fori_loop(0, (stop - first + 1) // 2, step, jnp.zeros((64, count), F32)) * 0.125
    ).T


def attend_last_back_body(
    blocks, groups, rows, stripe, place_ref, range_ref, low_ref, high_ref, cos_ref, sin_ref,
    do_ref, q_ref, k_ref, v_ref, o_ref, lse_ref, dq_ref, last_ref, kept, wide_cos, wide_sin, dk, dv,
):
    span = blocks * rows
    devices = groups * blocks
    half = rows // 2
    for ref in (dk, dv):
        ref[...] = jnp.zeros(ref.shape, F32)
    few = lse_ref.shape[2]
    dq_ref[:, 64:] = jnp.zeros((devices * stripe, 64), F32)

    def run(i, _):
        came = [
            do_ref[i * (few // stripe) + d].astype(F32)[half:, :64] for d in range(few // stripe)
        ]
        at = pl.ds(pl.multiple_of(i * few, few), few)
        dq_ref[at, :64] = attend_block_back(
            q_ref[at, :], jnp.concatenate(came, 0).astype(BF), o_ref[at, :], lse_ref[i],
            low_ref[i], high_ref[i], range_ref[2 * i], range_ref[2 * i + 1], k_ref, v_ref, dk, dv,
        )
        return 0

    lax.fori_loop(0, lse_ref.shape[0], run, 0)
    cos, sin = stripe_tables(place_ref, cos_ref, sin_ref, wide_cos, wide_sin, devices, rows, stripe)
    dq_ref[...] = turn(dq_ref[...], (cos, -sin))
    for g in range(groups):
        at = slice(g * span, (g + 1) * span)
        k = place_ref[0] ^ g
        cos, sin = turn_tables(cos_ref[at], sin_ref[at], True)[1]
        x = turn(jnp.concatenate([dk[at], jnp.zeros_like(dk[at])], 1), (cos, -sin))[:, :64]
        kept[...] = jnp.concatenate([x, dv[at]], 1).astype(BF)
        for b in range(blocks):
            last_ref[b, pl.ds(pl.multiple_of(k * rows, rows), rows), :] = kept[b * rows : (b + 1) * rows]


def attend_own_back_body(
    blocks, groups, rows, stripe, place_ref, range_ref, low_ref, high_ref, cos_ref, sin_ref,
    do_ref, q_ref, k_ref, v_ref, o_ref, lse_ref, last_dq_ref, out_ref, kept, kept_v, wide_v, dq, dk, dv,
):
    span = blocks * rows
    size = groups * span
    count = groups * rows
    half = rows // 2
    me_u, me_b = place_ref[0], place_ref[1]
    for ref in (dk, dv):
        ref[...] = jnp.zeros(ref.shape, F32)

    def run(i, _):
        came = []
        for d in range(QB // rows):
            x = do_ref[i * (QB // rows) + d]
            came += [x[:half, :64], x[:half, 64:]]
        at = pl.ds(pl.multiple_of(i * QB, QB), QB)
        dq[at, :] = attend_block_back(
            q_ref[at, :], jnp.concatenate(came, 0), o_ref[at, :], lse_ref[i], low_ref[i], high_ref[i],
            range_ref[2 * i], range_ref[2 * i + 1], k_ref, v_ref, dk, dv,
        )
        return 0

    lax.fori_loop(0, size // QB, run, 0)
    for g in range(groups):
        at = slice(g * span, (g + 1) * span)
        k = me_u ^ g
        cos, sin = turn_tables(cos_ref[at], sin_ref[at], False)[0]
        kept[...] = turn(jnp.concatenate([dq[at], dk[at]], 1), (cos, -sin)).astype(BF)
        kept_v[...] = dv[at].astype(BF)
        for b in range(blocks):
            out_ref[b, pl.ds(pl.multiple_of(k * rows, rows), rows), :] = kept[b * rows : (b + 1) * rows]
        for b in range(blocks):
            wide_v[g * blocks + b] = kept_v[b * rows : (b + 1) * rows]
    for to in range(blocks):
        v = [wide_v[(me_u ^ k) * blocks + to] for k in range(groups)]
        out_ref[to, count : count + count // 2] = jnp.concatenate(
            [jnp.concatenate(v[:2], 0), jnp.concatenate(v[2:], 0)], 1
        )
        z = [spread(last_dq_ref, ((me_u ^ k) * blocks + to) * stripe, stripe)[:, :64] for k in range(groups)]
        out_ref[to, count + count // 2 :] = jnp.concatenate(
            [jnp.concatenate(z[:2], 0), jnp.concatenate(z[2:], 0)], 1
        ).astype(BF)


def on_device(
    tokens,
    cotangent,
    lengths,
    time_step,
    modulate_weight,
    modulate_bias,
    attend_gain,
    input_weight,
    output_weight,
    feed_gain,
    expand_weight,
    expand_bias,
    reduce_weight,
    reduce_bias,
):
    groups, blocks = lax.axis_size("ulysses"), lax.axis_size("blk")
    group_id, block_id = lax.axis_index("ulysses"), lax.axis_index("blk")
    devices = groups * blocks
    micro, rows, width = tokens.shape
    own = micro * rows
    size = devices * rows
    head_width = width // HEADS
    heads = HEADS // groups
    pairs = micro * heads
    extra = pairs > blocks
    lanes = 384 if extra else 256
    stripe = rows // blocks if extra else 0
    mod_rows = modulate_weight.shape[0]
    gain_rows = attend_gain.shape[0]
    ff_rows = expand_bias.shape[0]
    ff = ff_rows * devices
    folds = ff // width
    assert pairs <= blocks + 1 and head_width == 64 and folds == groups and heads == 3
    place = jnp.stack([group_id, block_id]).astype(jnp.int32)
    pair_micro = jnp.minimum(block_id // heads, micro - 1)

    in_split = input_weight.reshape(gain_rows, 3, groups, heads, head_width)
    in_split = jnp.concatenate(
        [
            in_split[:, :2].transpose(2, 0, 3, 1, 4).reshape(groups, 1, gain_rows, -1),
            in_split[:, 2].transpose(1, 0, 2, 3).reshape(groups, 1, gain_rows, -1),
        ],
        3,
    )
    in_lanes = heads * 3 * head_width

    condition = time_features(time_step, modulate_weight.shape[1] // 2)
    mod_own = jnp.einsum(
        "mc,fc->mf", condition, modulate_weight, preferred_element_type=F32
    ) + modulate_bias.astype(F32)
    mod_lanes = 64 * -(-mod_rows // 64)
    mod_own = jnp.pad(mod_own, ((0, 0), (0, mod_lanes - mod_rows))).reshape(-1, 64)
    mod_high = lax.reduce_precision(mod_own, 8, 7)
    mod_size = mod_own.shape[0]
    vectors = jnp.pad(
        jnp.stack([attend_gain, feed_gain, reduce_bias]), ((0, 0), (0, 64 - gain_rows))
    )
    ff_lanes = 64 * -(-ff_rows // 64)
    small = jnp.concatenate(
        [
            mod_high.astype(BF),
            (mod_own - mod_high).astype(BF),
            vectors,
            jnp.pad(expand_bias, (0, ff_lanes - ff_rows)).reshape(-1, 64),
        ],
        0,
    )
    small_lanes = 64 * -(-small.shape[0] // gain_rows)
    small = jnp.pad(small, ((0, small_lanes * gain_rows // 64 - small.shape[0]), (0, 0)))
    small = small.reshape(1, 1, gain_rows, small_lanes)
    in_message = jnp.concatenate(
        [
            jnp.broadcast_to(in_split, (groups, blocks) + in_split.shape[2:]),
            jnp.broadcast_to(small, (groups, blocks) + small.shape[2:]),
        ],
        3,
    ).reshape(devices, gain_rows, in_lanes + small_lanes)
    in_message, tokens, lengths = lax.optimization_barrier((in_message, tokens, lengths))
    came = exchange(in_message)
    values = tokens.astype(F32)
    n1, r1 = norm(values)
    n1_b = n1.astype(BF)
    n1_group = swap([n1_b] * groups, "ulysses")
    small_all = came[:, :, in_lanes:].reshape(devices, -1, 64)
    in_own = came.reshape(width, in_lanes + small_lanes)

    weight_pack = jnp.concatenate(
            [
                reduce_weight,
                output_weight,
                expand_weight.reshape(gain_rows, folds, width).transpose(1, 0, 2).reshape(-1, width),
            ],
            0,
        )
    index = jnp.arange(size, dtype=jnp.int32)
    pair_lengths = lax.dynamic_index_in_dim(lengths, pair_micro, 0, keepdims=False)
    segment, position = doc_layout(index, pair_lengths)
    last_lengths = lengths[micro - 1]
    last_segment, last_position = doc_layout(index, last_lengths)
    half = head_width // 2
    freqs = jnp.exp(-math.log(10000.0) * jnp.arange(half, dtype=F32) / half)
    lane = jnp.arange(128)
    angles = jnp.where(
        (lane < 64)[None, :], position.astype(F32)[:, None], last_position.astype(F32)[:, None]
    ) * jnp.tile(freqs, 4)[None, :]
    cos_table = jnp.cos(angles)
    sin_table = jnp.where((lane % 64 < 32)[None, :], -1.0, 1.0) * jnp.sin(angles)
    query_rows = math.gcd(size, 256)
    key_block = math.gcd(size, 256)
    first = jnp.arange(size // query_rows, dtype=jnp.int32) * query_rows
    ranges = key_ranges(first, first + query_rows - 1, pair_lengths, key_block)
    small_path = extra and size % KB == 0 and rows == 64 and stripe == 8 and groups == 4 and size <= 4096

    striped = lambda x: lax.dynamic_slice_in_dim(
        x.reshape((devices, rows) + x.shape[1:]), block_id * stripe, stripe, 1
    ).reshape((devices * stripe,) + x.shape[1:])
    last_ranges = bounds = 0
    if small_path:
        last_rows = min(256, devices * stripe)
        chunk = last_rows // stripe
        last_first = jnp.arange(devices // chunk, dtype=jnp.int32) * (chunk * rows) + block_id * stripe
        last_ranges = key_ranges(
            last_first, last_first + (chunk - 1) * rows + stripe - 1, last_lengths, QB
        )
        bounds = []
        for where, lens, pick, lump in (
            (position, pair_lengths, lambda x: x, QB),
            (last_position, last_lengths, striped, last_rows),
        ):
            low = index - where
            ends = jnp.cumsum(lens)
            high = jnp.min(jnp.where(ends[None, :] > index[:, None], ends[None, :], 1 << 30), 1)
            bounds += [pick(low).reshape(-1, 1, lump), pick(high).reshape(-1, 1, lump)]
    in_own, small_all, n1_group, place, cos_table, sin_table, ranges, last_ranges, bounds = (
        lax.optimization_barrier(
            (in_own, small_all, n1_group, place, cos_table, sin_table, ranges, last_ranges, bounds)
        )
    )
    weight_pack, in_own = lax.optimization_barrier((weight_pack, in_own))
    gathered = lax.all_gather(weight_pack, ALL, axis=0, tiled=False)
    unit = gain_rows
    while unit % 8:
        unit *= 2
    units = width // unit
    if unit != gain_rows:
        gathered = jnp.concatenate(
            [gathered[:, :ff_rows].reshape(units, -1, width)]
            + [
                gathered[:, at : at + gain_rows].reshape(units, unit, width)
                for at in range(ff_rows, ff_rows + (folds + 1) * gain_rows, gain_rows)
            ],
            1,
        )
    wide = unit * folds

    mods = small_all[:, :mod_size].astype(F32) + small_all[:, mod_size : 2 * mod_size].astype(F32)
    mods = mods.reshape(devices, micro, mod_lanes)[:, :, :mod_rows].transpose(1, 0, 2).reshape(micro, -1)
    at = 2 * mod_size
    vectors = small_all[:, at : at + 3, :gain_rows].astype(F32).transpose(1, 0, 2).reshape(3, width)
    gain1, gain2, reduce_bias_f = vectors[0], vectors[1], vectors[2:]
    at += 3
    expand_bias_f = small_all[:, at : at + ff_lanes // 64].reshape(devices, ff_lanes)[:, :ff_rows]
    expand_bias_f = expand_bias_f.astype(F32).reshape(folds, 1, width)
    shift1, scale1, gate1, shift2, scale2, gate2 = jnp.split(mods, 6, 1)
    c1 = gain1 * (1.0 + scale1)
    c2 = gain2 * (1.0 + scale2)

    count = groups * rows
    smem = pl.BlockSpec(memory_space=pltpu.SMEM)
    message_rows = count + count // 2 + 16
    if small_path:
        outgoing, last_own = pl.pallas_call(
            functools.partial(project_small_body, blocks, heads),
            out_shape=[
                jax.ShapeDtypeStruct((blocks, message_rows, 128), BF), jax.ShapeDtypeStruct((count, 128), BF),
            ],
            in_specs=[whole_vmem()] * (3 + groups),
            out_specs=[whole_vmem()] * 2,
            scratch_shapes=[pltpu.VMEM((count, 128), F32)],
            cost_estimate=pl.CostEstimate(
                flops=2 * micro * count * width * 3 * 64 * heads, transcendentals=0, bytes_accessed=8 * own * width
            ),
            name="project",
        )(c1, shift1, in_own, *n1_group)
        incoming = [lax.all_to_all(outgoing, "blk", split_axis=0, concat_axis=0, tiled=True)]
        pass_on = lambda x, bit: lax.ppermute(x, "blk", [(i, i ^ bit) for i in range(blocks)])
        last_four = jnp.stack([last_own] + [pass_on(last_own, bit) for bit in range(2, blocks, 2)])
        last_keys = [last_four, pass_on(last_four, 1)]
    else:
        outgoing = pl.pallas_call(
            functools.partial(project_body, blocks, pairs, heads, extra),
            out_shape=[jax.ShapeDtypeStruct((count, lanes), BF)] * blocks,
            in_specs=[smem] + [whole_vmem()] * (3 + groups),
            out_specs=[whole_vmem()] * blocks,
            scratch_shapes=[pltpu.VMEM((blocks, count, lanes), BF)],
            name="project",
        )(place, c1, shift1, in_own, *n1_group)
        incoming = swap(outgoing, "blk")

    span = blocks * rows
    by_span = pl.BlockSpec((span, 64), lambda i, p: (i ^ p[0], 0))
    table_spec = pl.BlockSpec((span, 128), lambda i, p: (i ^ p[0], 0))
    by_rows = pl.BlockSpec((rows, lanes), lambda i, p: (i, 0))
    parts = 6 if extra else 3
    if small_path:
        whole = lambda *shape: jax.ShapeDtypeStruct(shape, BF)
        f32 = lambda *shape: jax.ShapeDtypeStruct(shape, F32)
        padded = whole(size + KB - QB, 64)
        own_args = (place, ranges, *bounds[:2], cos_table, sin_table)
        last_args = (place, last_ranges, *bounds[2:], cos_table, sin_table)
        specs = [smem] * 2 + [whole_vmem()] * 4
        own_message, *own_saved = pl.pallas_call(
            functools.partial(attend_own_body, blocks, groups, rows),
            in_specs=specs + [whole_vmem()],
            out_specs=[whole_vmem()] * 6,
            out_shape=[
                whole(devices, rows // 2, 128), whole(size, 64), padded, padded, whole(size, 64), f32(*bounds[0].shape),
            ],
            scratch_shapes=[
                pltpu.VMEM((span, 128), BF), pltpu.VMEM((span, 64), BF),
                pltpu.VMEM((size // KB + 1, KB, QB), F32),
            ],
            cost_estimate=pl.CostEstimate(
                flops=size * size * 64, transcendentals=size * size // 2, bytes_accessed=16 * size * 128
            ),
            name="attend_own",
        )(*own_args, *incoming)
        message, *last_saved = pl.pallas_call(
            functools.partial(attend_last_body, blocks, groups, rows, stripe),
            in_specs=specs + [whole_vmem()] * 4,
            out_specs=[whole_vmem()] * 6,
            out_shape=[
                whole(devices, rows // 2 + stripe, 128), whole(devices * stripe, 64), padded, padded,
                whole(devices * stripe, 64), f32(*bounds[2].shape),
            ],
            scratch_shapes=[pltpu.VMEM((span, 128), BF)]
            + [pltpu.VMEM((devices * stripe, 128), F32)] * 3
            + [pltpu.VMEM((size // KB + 1, KB, last_rows), F32)],
            cost_estimate=pl.CostEstimate(
                flops=size * size * 16, transcendentals=size * size // 8, bytes_accessed=16 * size * 64
            ),
            name="attend_last",
        )(*last_args, *incoming, *last_keys, own_message)
    else:
        assert not extra
        turned = pl.pallas_call(
            functools.partial(rotate_in_body, blocks, extra),
            grid_spec=pltpu.PrefetchScalarGridSpec(
                num_scalar_prefetch=1,
                grid=(groups,),
                in_specs=[table_spec, table_spec] + [by_rows] * blocks,
                out_specs=[by_span] * parts,
                scratch_shapes=[pltpu.VMEM((span, lanes), BF)],
            ),
            out_shape=[jax.ShapeDtypeStruct((size, 64), BF)] * parts,
            name="rotate_in",
        )(place, cos_table, sin_table, *incoming)
        query, key, value = turned[:3]
        attended, lse = attend(
            ranges, query, segment, key, value, segment[:, None], query_rows, key_block
        )
        message = attended.reshape(devices, rows, head_width)
    came = exchange(message)

    ex_spec = lambda f: pl.BlockSpec((units, unit, width), f)
    flat = pl.BlockSpec((own, width), lambda i: (0, 0))
    vec = lambda n: pl.BlockSpec((n, width), lambda i: (0, 0))
    message_shape = message.shape
    message_spec = pl.BlockSpec(message_shape, lambda i: (0, 0, 0))
    sizes = (groups, blocks, heads, micro, rows, stripe)
    own_f32 = jax.ShapeDtypeStruct((own, width), F32)
    own_bf = jax.ShapeDtypeStruct((own, width), BF)
    merged, attn, middle, second = pl.pallas_call(
        functools.partial(middle_body, *sizes),
        grid=(1,),
        in_specs=[message_spec, ex_spec(lambda i: (0, folds, 0)), flat, vec(micro), vec(micro), vec(micro)],
        out_specs=[flat] * 4,
        out_shape=[own_bf, own_f32, own_f32, own_bf],
        name="middle",
    )(came, gathered, tokens.reshape(own, width), gate1, c2, shift2)
    second_group = swap([second] * groups, "ulysses")
    dy = cotangent.reshape(own, width)
    dy_group = swap([dy] * groups, "ulysses")

    per = width // wide
    layer_output, grad_middle, grad_attn, do_message, sums = pl.pallas_call(
        functools.partial(feed_body, *sizes),
        grid=(folds,),
        in_specs=[
            ex_spec(lambda i: (0, folds + 1 + i, 0)),
            pl.BlockSpec((per, wide, width), lambda i: (i, 0, 0)),
            ex_spec(lambda i: (0, folds, 0)),
            pl.BlockSpec((1, 1, width), lambda i: (i, 0, 0)),
            vec(1),
            flat, flat, flat, flat,
            vec(micro), vec(micro), vec(micro),
        ],
        out_specs=[flat, flat, flat, message_spec, vec(5 * micro)],
        out_shape=[
            own_bf, own_f32, own_bf,
            jax.ShapeDtypeStruct(message_shape, BF),
            jax.ShapeDtypeStruct((5 * micro, width), F32),
        ],
        scratch_shapes=[
            pltpu.VMEM((own, width), F32), pltpu.VMEM((own, width), F32),
            pltpu.VMEM((own, width), BF), pltpu.VMEM((own, width), BF),
        ],
        cost_estimate=pl.CostEstimate(
            flops=8 * own * width * ff, transcendentals=own * ff, bytes_accessed=4 * width * ff
        ),
        name="feed",
    )(gathered, gathered, gathered, expand_bias_f, reduce_bias_f, second, middle, attn, dy, gate1, gate2, c2)
    do_came = exchange(do_message)
    d_gate2, d_shift2, p2, d_gate1, dm_sums = [
        sums[i * micro : (i + 1) * micro] for i in range(5)
    ]

    output_part = lax.dot_general(merged, grad_attn, TN, preferred_element_type=F32).astype(BF)
    output_part = output_part.reshape(groups, width // groups, width)

    flat_p = pl.BlockSpec((own, width), lambda i, p: (0, 0))
    square = pl.BlockSpec((width, width), lambda i, p: (0, 0))
    reduce_part, expand_part, bias_part = pl.pallas_call(
        functools.partial(feed_weights_body, rows),
        grid_spec=pltpu.PrefetchScalarGridSpec(
            num_scalar_prefetch=1,
            grid=(1,),
            in_specs=[
                pl.BlockSpec((units, unit, width), lambda i, p: (0, folds + 1 + p[0], 0)),
                pl.BlockSpec((per, wide, width), lambda i, p: (p[0], 0, 0)),
                pl.BlockSpec((1, 1, width), lambda i, p: (p[0], 0, 0)),
                pl.BlockSpec((micro, width), lambda i, p: (0, 0)),
            ]
            + [flat_p] * (2 * groups),
            out_specs=[square, square, pl.BlockSpec((1, width), lambda i, p: (0, 0))],
        ),
        out_shape=[
            jax.ShapeDtypeStruct((width, width), BF),
            jax.ShapeDtypeStruct((width, width), BF),
            jax.ShapeDtypeStruct((1, width), F32),
        ],
        cost_estimate=pl.CostEstimate(
            flops=10 * own * groups * width * width, transcendentals=own * ff, bytes_accessed=16 * width * width
        ),
        name="feed_weights",
    )(place, gathered, gathered, expand_bias_f, gate2, *second_group, *dy_group)
    feed_part = jnp.concatenate(
        [
            reduce_part.reshape(blocks, ff_rows, width),
            expand_part.reshape(groups, blocks, gain_rows, width)
            .transpose(1, 0, 2, 3)
            .reshape(blocks, groups * gain_rows, width),
        ],
        1,
    )
    do_came, feed_part, output_part = lax.optimization_barrier((do_came, feed_part, output_part))
    output_part = swap(
        [
            lax.dynamic_index_in_dim(output_part, group_id ^ k, 0, keepdims=False)
            for k in range(groups)
        ],
        "ulysses",
    )

    feed_half = halve(feed_part, "blk", block_id, 1)

    if small_path:
        last_dq, last_leaving = pl.pallas_call(
            functools.partial(attend_last_back_body, blocks, groups, rows, stripe),
            in_specs=specs + [whole_vmem()] * 6,
            out_specs=[whole_vmem()] * 2,
            out_shape=[f32(devices * stripe, 128), whole(blocks, count, 128)],
            scratch_shapes=[pltpu.VMEM((span, 128), BF)]
            + [pltpu.VMEM((devices * stripe, 128), F32)] * 2
            + [pltpu.VMEM((size + KB - QB, 64), F32)] * 2,
            cost_estimate=pl.CostEstimate(
                flops=size * size * 32, transcendentals=size * size // 8, bytes_accessed=16 * size * 64
            ),
            name="attend_last_back",
        )(*last_args, do_came, *last_saved)
        last_half = halve(last_leaving, "blk", block_id, 1)
        do_came, last_dq = lax.optimization_barrier((do_came, last_dq))
        leaving = pl.pallas_call(
            functools.partial(attend_own_back_body, blocks, groups, rows, stripe),
            in_specs=specs + [whole_vmem()] * 7,
            out_specs=whole_vmem(),
            out_shape=whole(blocks, message_rows, 128),
            scratch_shapes=[
                pltpu.VMEM((span, 128), BF), pltpu.VMEM((span, 64), BF),
                pltpu.VMEM((devices, rows, 64), BF), pltpu.VMEM((size, 64), F32),
            ]
            + [pltpu.VMEM((size + KB - QB, 64), F32)] * 2,
            cost_estimate=pl.CostEstimate(
                flops=2 * size * size * 64, transcendentals=size * size // 2, bytes_accessed=16 * size * 128
            ),
            name="attend_own_back",
        )(*own_args, do_came, *own_saved, last_dq)
    else:
        grads = attend_back(
            ranges, query, segment, lse, attended, do_came.reshape(size, head_width), key, value,
            segment[:, None], query_rows, key_block,
        )
        leaving = pl.pallas_call(
            functools.partial(rotate_out_body, blocks, extra),
            grid_spec=pltpu.PrefetchScalarGridSpec(
                num_scalar_prefetch=1,
                grid=(groups,),
                in_specs=[table_spec, table_spec] + [by_span] * parts,
                out_specs=[by_rows] * blocks,
                scratch_shapes=[pltpu.VMEM((span, lanes), BF)],
            ),
            out_shape=[jax.ShapeDtypeStruct((count, lanes), BF)] * blocks,
            name="rotate_out",
        )(place, cos_table, sin_table, *grads)
    if small_path:
        leaving, last_half, output_part = lax.optimization_barrier((leaving, last_half, output_part))
        back = [lax.all_to_all(leaving, "blk", split_axis=0, concat_axis=0, tiled=True)]
        back += [
            pass_on(lax.dynamic_index_in_dim(last_half, (block_id // 2) ^ k, 0, keepdims=False), 2 * k)
            if k
            else lax.dynamic_index_in_dim(last_half, block_id // 2, 0, keepdims=False)
            for k in range(blocks // 2)
        ]
    else:
        leaving, output_part = lax.optimization_barrier((leaving, output_part))
        back = swap(leaving, "blk")
    output_part = sum(x.astype(F32) for x in output_part).astype(BF).reshape(blocks, gain_rows, width)
    output_part = halve(output_part, "blk", block_id, 1)
    weight_sum = halve(feed_half, "blk", block_id, 2)
    back, weight_sum, output_part = lax.optimization_barrier((back, weight_sum, output_part))
    output_part = halve(output_part, "blk", block_id, 2)
    weight_sum, weight_bit = jnp.concatenate([weight_sum, output_part], 1), 4

    if small_path:
        back_body = functools.partial(project_back_small_body, blocks, heads)
        back_scratch = [pltpu.VMEM((count, 64), F32)]
        back_args, back_specs = (), []
    else:
        back_args, back_specs = (place,), [smem]
        back_body = functools.partial(project_back_body, blocks, pairs, heads, extra)
        back_scratch = [pltpu.VMEM((blocks, count, lanes), BF)]
    returned = pl.pallas_call(
        back_body,
        out_shape=[jax.ShapeDtypeStruct((micro, rows, width), BF)] * groups
        + [
            jax.ShapeDtypeStruct((width, heads * 3 * head_width), BF),
            jax.ShapeDtypeStruct((micro, width), F32),
            jax.ShapeDtypeStruct((micro, width), F32),
        ],
        in_specs=back_specs + [whole_vmem()] * (3 + groups + len(back)),
        out_specs=[whole_vmem()] * (groups + 3),
        scratch_shapes=back_scratch,
        cost_estimate=pl.CostEstimate(
            flops=4 * micro * count * width * 3 * 64 * heads, transcendentals=0, bytes_accessed=8 * own * width
        ),
        name="project_back",
    )(*back_args, c1, shift1, in_own, *n1_group, *back)
    input_part, d_shift1, p1 = returned[groups:]
    grad_first = sum(x.astype(F32) for x in swap(returned[:groups], "ulysses"))
    e = grad_first * c1[:, None]
    tokens_grad = (
        grad_middle.reshape(micro, rows, width)
        + r1
        * (
            e
            - jnp.mean(e, -1, keepdims=True)
            - n1 * jnp.mean(e * n1, -1, keepdims=True)
        )
    ).astype(BF)

    grad_mods = jnp.concatenate(
        [d_shift1, p1 * gain1, d_gate1, d_shift2, p2 * gain2, d_gate2], 1
    )
    gain1_part = jnp.sum((1.0 + scale1) * p1, 0)
    gain2_part = jnp.sum((1.0 + scale2) * p2, 0)
    own_units = jnp.where(
        (jnp.arange(groups) == group_id)[:, None], bias_part.reshape(1, width), 0.0
    )
    small_parts = jnp.concatenate(
        [grad_mods.reshape(micro, devices, mod_rows).transpose(1, 0, 2).reshape(devices, -1)]
        + [
            x.reshape(devices, -1)
            for x in (gain1_part, gain2_part, jnp.sum(dm_sums, 0), own_units)
        ],
        1,
    ).astype(BF)
    taken = small_parts.shape[1]
    small_rows = 8 * -(-taken // (8 * in_lanes))
    small_parts = jnp.pad(small_parts, ((0, 0), (0, small_rows * in_lanes - taken)))
    input_sum = halve(
        input_part.reshape(groups, blocks, gain_rows, in_lanes).transpose(1, 0, 2, 3), "blk", block_id, 1
    )
    small_parts = halve(
        small_parts.reshape(groups, blocks, small_rows, in_lanes).transpose(1, 0, 2, 3), "blk", block_id, 1
    )
    input_sum = jnp.concatenate([input_sum, small_parts], 2)
    bit = 2
    while bit < blocks:
        input_sum = halve(input_sum, "blk", block_id, bit)
        bit *= 2
    while weight_bit < blocks:
        weight_sum = halve(weight_sum, "blk", block_id, weight_bit)
        weight_bit *= 2
    weight_sum, input_sum = weight_sum[0], input_sum[0]
    final = jnp.stack(
        swap(
            [
                lax.dynamic_index_in_dim(input_sum, group_id ^ k, 0, keepdims=False)
                for k in range(groups)
            ],
            "ulysses",
        )
    )
    small_sum = jnp.sum(final[:, gain_rows:].astype(F32), 0).reshape(-1)
    input_sum = unscramble(final[:, :gain_rows], group_id, 0).astype(F32)
    reduce_grad = weight_sum[:ff_rows].astype(F32)
    output_grad = weight_sum[-gain_rows:].astype(F32)
    expand_rows = weight_sum[ff_rows:-gain_rows].reshape(groups, gain_rows, width)
    expand_came = jnp.stack(
        swap(
            [
                lax.dynamic_index_in_dim(expand_rows, group_id ^ k, 0, keepdims=False)
                for k in range(groups)
            ],
            "ulysses",
        )
    )
    expand_grad = jnp.concatenate(
        [
            lax.dynamic_index_in_dim(expand_came, group_id ^ k, 0, keepdims=False)
            for k in range(groups)
        ],
        1,
    ).astype(F32)

    two = heads * 2 * head_width
    input_grad = jnp.concatenate(
        [
            input_sum[:, :, :two]
            .reshape(groups, gain_rows, heads, 2, head_width)
            .transpose(1, 3, 0, 2, 4)
            .reshape(gain_rows, 2 * width),
            input_sum[:, :, two:].transpose(1, 0, 2).reshape(gain_rows, width),
        ],
        1,
    )
    at = micro * mod_rows
    mod_sum = small_sum[:at].reshape(micro, mod_rows)
    modulate_weight_grad = jnp.sum(
        mod_sum[:, :, None] * condition.astype(F32)[:, None, :], 0
    )
    cuts = []
    for length in (gain_rows, gain_rows, gain_rows, ff_rows):
        cuts.append(small_sum[at : at + length])
        at += length
    return (
        layer_output.reshape(micro, rows, width),
        tokens_grad,
        modulate_weight_grad,
        jnp.sum(mod_sum, 0),
        cuts[0],
        input_grad,
        output_grad,
        cuts[1],
        expand_grad,
        cuts[3],
        reduce_grad,
        cuts[2],
    )


def solution(mesh):
    both = P(("ulysses", "blk"))
    tall = P(("ulysses", "blk"), None)
    seq = P(None, ("ulysses", "blk"), None)
    in_specs = (
        seq, seq, P(), P(), tall, both, both, tall, tall, both, tall, both, tall, both,
    )
    out_specs = (seq, seq, tall, both, both, tall, tall, both, tall, both, tall, both)
    return jax.shard_map(
        on_device, mesh=mesh, in_specs=in_specs, out_specs=out_specs, check_vma=False
    )
```

```python
import functools
import math

import jax
import jax.numpy as jnp
from jax import lax
from jax.experimental import pallas as pl
from jax.experimental.pallas import tpu as pltpu
from jax.sharding import PartitionSpec as P

HEADS = 12
ALL = ("ulysses", "blk")
BF = jnp.bfloat16
F32 = jnp.float32
NEG = -1e30


def exchange(x):
    return lax.all_to_all(x, ALL, split_axis=0, concat_axis=0, tiled=True)


def time_features(time_step, half):
    freqs = jnp.exp(-math.log(10000.0) * jnp.arange(half, dtype=F32) / half)
    angles = time_step.astype(F32)[:, None] * freqs[None, :]
    return jax.nn.silu(jnp.concatenate([jnp.cos(angles), jnp.sin(angles)], 1)).astype(BF)


def doc_layout(index, lengths_row):
    ends = jnp.cumsum(lengths_row)
    over = index[:, None] >= ends[None, :]
    segment = jnp.sum(over.astype(jnp.int32), 1)
    place = index - jnp.sum(jnp.where(over, lengths_row[None, :], 0), 1)
    return segment, place


def key_ranges(first, last, lengths_row, block):
    ends = jnp.cumsum(lengths_row)
    start = jnp.sum(jnp.where(first[:, None] >= ends[None, :], lengths_row[None, :], 0), 1)
    stop = jnp.min(jnp.where(ends[None, :] > last[:, None], ends[None, :], 1 << 30), 1)
    return jnp.stack([start // block, (stop + block - 1) // block], 1).reshape(-1)


def whole_vmem():
    return pl.BlockSpec(memory_space=pltpu.VMEM)


def swap(blocks, axis):
    size = lax.axis_size(axis)
    return [
        x if k == 0 else lax.ppermute(x, axis, [(i, i ^ k) for i in range(size)])
        for k, x in enumerate(blocks)
    ]


def unscramble(x, index, axis):
    count, bit = x.shape[axis], 1
    while bit < count:
        shape = x.shape
        y = x.reshape(shape[:axis] + (count // (2 * bit), 2, bit) + shape[axis + 1 :])
        flipped = jnp.flip(y, axis + 1)
        x = jnp.where((index & bit) != 0, flipped, y).reshape(shape)
        bit *= 2
    return x


def halve(x, axis, index, bit):
    size = lax.axis_size(axis)
    y = x.reshape((-1, 2) + x.shape[1:])
    mine = (index // bit) % 2
    sent = lax.dynamic_index_in_dim(y, 1 - mine, 1, keepdims=False)
    kept = lax.dynamic_index_in_dim(y, mine, 1, keepdims=False)
    came = lax.ppermute(sent, axis, [(i, i ^ bit) for i in range(size)])
    return (kept.astype(F32) + came.astype(F32)).astype(BF)


def project_body(blocks, pairs, heads, extra, place_ref, c_ref, shift_ref, w_ref, *refs):
    groups = len(refs) - blocks - 1
    tokens, outs, kept = refs[:groups], refs[groups:-1], refs[-1]
    micro, rows, width = tokens[0].shape
    end = 192 * heads
    weights = [w_ref[:, c : min(c + 128, end)] for c in range(0, end, 128)]
    order = list(range(micro))[::-1]
    z_qk = z_v = None
    for m in order:
        a = jnp.concatenate(
            [(x[m].astype(F32) * c_ref[m][None] + shift_ref[m][None]).astype(BF) for x in tokens], 0
        )
        parts = [jnp.dot(a, w, preferred_element_type=F32).astype(BF) for w in weights]
        v = jnp.concatenate(parts[heads:], 1)
        if extra and m == micro - 1:
            z_qk = parts[heads - 1]
            z_v = v[:, (heads - 1) * 64 : heads * 64]
        for h in range(heads):
            pair = m * heads + h
            if pair >= blocks:
                continue
            kept[pair, :, :128] = parts[h]
            own_v = v[:, h * 64 : (h + 1) * 64]
            if extra:
                kept[pair, :, 128:256] = z_qk
                kept[pair, :, 256:] = jnp.concatenate([own_v, z_v], 1)
            else:
                kept[pair, :, 128:] = jnp.concatenate([own_v, jnp.zeros_like(own_v)], 1)
    for pair in range(pairs, blocks):
        kept[pair] = jnp.zeros(kept.shape[1:], BF)
    for j in range(blocks):
        outs[j][...] = kept[place_ref[1] ^ j]


def turn_tables(cos, sin, extra):
    lane = lax.broadcasted_iota(jnp.int32, cos.shape, 1)
    low = lane < 64
    cos_r, sin_r = pltpu.roll(cos, 64, 1), pltpu.roll(sin, 64, 1)
    tables = [(jnp.where(low, cos, cos_r), jnp.where(low, sin, sin_r))]
    if extra:
        tables.append((jnp.where(low, cos_r, cos), jnp.where(low, sin_r, sin)))
    return tables


def turn(x, table):
    lane = lax.broadcasted_iota(jnp.int32, x.shape, 1)
    swapped = jnp.where(lane % 64 < 32, pltpu.roll(x, 96, 1), pltpu.roll(x, 32, 1))
    return x * table[0] + swapped * table[1]


def rotate_in_body(blocks, extra, place_ref, cos_ref, sin_ref, *refs):
    ins, outs = refs[:blocks], refs[blocks : 2 * blocks - blocks + (6 if extra else 3)]
    kept = refs[-1]
    rows = ins[0].shape[0]
    for j in range(blocks):
        at = pl.multiple_of((place_ref[1] ^ j) * rows, rows)
        kept[pl.ds(at, rows), :] = ins[j][...]
    tables = turn_tables(cos_ref[...], sin_ref[...], extra)
    x0 = turn(kept[:, :128].astype(F32), tables[0])
    outs[0][...] = (x0[:, :64] * 0.125).astype(BF)
    outs[1][...] = x0[:, 64:].astype(BF)
    if extra:
        outs[2][...] = kept[:, 256:320]
        x1 = turn(kept[:, 128:256].astype(F32), tables[1])
        outs[3][...] = (x1[:, :64] * 0.125).astype(BF)
        outs[4][...] = x1[:, 64:].astype(BF)
        outs[5][...] = kept[:, 320:]
    else:
        outs[2][...] = kept[:, 128:192]


def rotate_out_body(blocks, extra, place_ref, cos_ref, sin_ref, *refs):
    count = 6 if extra else 3
    ins, outs, kept = refs[:count], refs[count:-1], refs[-1]
    rows = outs[0].shape[0]
    parts = [ref[...].astype(F32) for ref in ins]
    tables = [(c, -s) for c, s in turn_tables(cos_ref[...], sin_ref[...], extra)]
    kept[:, :128] = turn(jnp.concatenate(parts[:2], 1), tables[0]).astype(BF)
    if extra:
        kept[:, 128:256] = turn(jnp.concatenate(parts[3:5], 1), tables[1]).astype(BF)
        kept[:, 256:] = jnp.concatenate([parts[2], parts[5]], 1).astype(BF)
    else:
        kept[:, 128:] = jnp.concatenate([parts[2], jnp.zeros_like(parts[2])], 1).astype(BF)
    for j in range(blocks):
        at = pl.multiple_of((place_ref[1] ^ j) * rows, rows)
        outs[j][...] = kept[pl.ds(at, rows), :]


def project_back_body(blocks, pairs, heads, extra, place_ref, c_ref, shift_ref, w_ref, *refs):
    kept = refs[-1]
    groups = (len(refs) - blocks - 4) // 2
    tokens, ins = refs[:groups], refs[groups : groups + blocks]
    outs = refs[groups + blocks : 2 * groups + blocks]
    grad_ref, sum_ref, dot_ref = refs[2 * groups + blocks : -1]
    micro, rows, width = tokens[0].shape
    count = groups * rows
    for j in range(blocks):
        kept[place_ref[1] ^ j] = ins[j][...]
    last = None
    if extra:
        last = jnp.zeros((count, 256), F32)
        for j in range(blocks):
            last = last + kept[j, :, 128:].astype(F32)
        last = last.astype(BF)
    all_a, all_g = [], []
    for m in range(micro):
        n = jnp.concatenate([x[m] for x in tokens], 0).astype(F32)
        a = (n * c_ref[m][None] + shift_ref[m][None]).astype(BF)
        qk, v = [], []
        for h in range(heads):
            pair = m * heads + h
            if pair < blocks:
                qk.append(kept[pair, :, :128])
                at = 256 if extra else 128
                v.append(kept[pair, :, at : at + 64])
            else:
                qk.append(last[:, :128])
                v.append(last[:, 192:])
        g = jnp.concatenate(qk + v, 1)
        da = lax.dot_general(g, w_ref[:, : 192 * heads], (((1,), (1,)), ((), ())), preferred_element_type=F32)
        for k in range(groups):
            outs[k][m] = da[k * rows : (k + 1) * rows].astype(BF)
        sum_ref[m : m + 1] = jnp.sum(da, 0, keepdims=True)
        dot_ref[m : m + 1] = jnp.sum(da * n, 0, keepdims=True)
        all_a.append(a)
        all_g.append(g)
    grad_ref[...] = lax.dot_general(
        jnp.concatenate(all_a, 0), jnp.concatenate(all_g, 0), (((0,), (0,)), ((), ())),
        preferred_element_type=F32,
    ).astype(BF)


def norm(values):
    centered = values - jnp.mean(values, -1, keepdims=True)
    inverse = lax.rsqrt(jnp.mean(centered * centered, -1, keepdims=True) + 1e-05)
    return centered * inverse, inverse


def by_micro(ref, rows):
    return jnp.concatenate(
        [jnp.broadcast_to(ref[m][None], (rows, ref.shape[1])) for m in range(ref.shape[0])], 0
    )


def middle_body(
    groups, blocks, heads, micro, rows, stripe,
    came_ref, out_ref, x_ref, gate_ref, c_ref, shift_ref,
    merged_ref, attn_ref, middle_ref, second_ref,
):
    width = x_ref.shape[1]
    for u in range(groups):
        for m in range(micro):
            for h in range(heads):
                pair = m * heads + h
                lanes = slice((u * heads + h) * 64, (u * heads + h + 1) * 64)
                half = rows // 2
                if pair < blocks and stripe:
                    at = m * rows
                    merged_ref[at : at + half, lanes] = came_ref[u * blocks + pair, :half, :64]
                    merged_ref[at + half : at + rows, lanes] = came_ref[u * blocks + pair, :half, 64:]
                elif pair < blocks:
                    merged_ref[m * rows : (m + 1) * rows, lanes] = came_ref[u * blocks + pair]
                else:
                    for b in range(blocks):
                        at = m * rows + b * stripe
                        merged_ref[at : at + stripe, lanes] = came_ref[u * blocks + b, half:, :64]
    attn = jnp.dot(merged_ref[...], out_ref[...].reshape(width, width), preferred_element_type=F32)
    attn_ref[...] = attn
    middle = x_ref[...].astype(F32) + by_micro(gate_ref, rows) * attn
    middle_ref[...] = middle
    normed, _ = norm(middle)
    second_ref[...] = (normed * by_micro(c_ref, rows) + by_micro(shift_ref, rows)).astype(BF)


def gelu_pair(u):
    t = jnp.tanh(0.7978845608028654 * (u + 0.044715 * u * u * u))
    value = 0.5 * u * (1.0 + t)
    slope = 0.5 * (1.0 + t) + 0.5 * u * (1.0 - t * t) * (
        0.7978845608028654 * (1.0 + 0.134145 * u * u)
    )
    return value, slope


NT = (((1,), (1,)), ((), ()))
TN = (((0,), (0,)), ((), ()))


def feed_body(
    groups, blocks, heads, micro, rows, stripe,
    ex_ref, re_ref, out_w_ref, ex_bias_ref, re_bias_ref, second_ref, middle_ref, attn_ref, dy_ref,
    gate1_ref, gate2_ref, c_ref,
    layer_ref, grad_ref, dattn_ref, do_ref, sums_ref,
    branch_sum, back_sum, dm_sum, do_sum,
):
    step = pl.program_id(0)
    width = middle_ref.shape[1]

    @pl.when(step == 0)
    def _():
        branch_sum[...] = jnp.zeros_like(branch_sum)
        back_sum[...] = jnp.zeros_like(back_sum)
        dm_sum[...] = (by_micro(gate2_ref, rows) * dy_ref[...].astype(F32)).astype(BF)

    expand = ex_ref[...].reshape(width, width)
    reduce = re_ref[...].reshape(width, width)
    u = jnp.dot(second_ref[...], expand, preferred_element_type=F32) + ex_bias_ref[0]
    g, slope = gelu_pair(u)
    branch_sum[...] += jnp.dot(g.astype(BF), reduce, preferred_element_type=F32)
    dg = lax.dot_general(dm_sum[...], reduce, NT, preferred_element_type=F32)
    du = (dg * slope).astype(BF)
    back_sum[...] += lax.dot_general(du, expand, NT, preferred_element_type=F32)

    @pl.when(step == pl.num_programs(0) - 1)
    def _():
        def total(at, x):
            for m in range(micro):
                sums_ref[at * micro + m : at * micro + m + 1] = jnp.sum(
                    x[m * rows : (m + 1) * rows], 0, keepdims=True
                )

        branch = branch_sum[...] + re_bias_ref[...]
        middle = middle_ref[...]
        dy = dy_ref[...].astype(F32)
        layer_ref[...] = (middle + by_micro(gate2_ref, rows) * branch).astype(BF)
        total(0, dy * branch)
        normed, inverse = norm(middle)
        db = back_sum[...]
        total(1, db)
        total(2, db * normed)
        e = db * by_micro(c_ref, rows)
        grad = dy + inverse * (
            e
            - jnp.mean(e, -1, keepdims=True)
            - normed * jnp.mean(e * normed, -1, keepdims=True)
        )
        grad_ref[...] = grad
        total(3, grad * attn_ref[...])
        total(4, dm_sum[...].astype(F32))
        dattn = (by_micro(gate1_ref, rows) * grad).astype(BF)
        dattn_ref[...] = dattn
        do_sum[...] = lax.dot_general(
            dattn, out_w_ref[...].reshape(width, width), NT, preferred_element_type=F32
        ).astype(BF)
        for at in range(groups):
            for m in range(micro):
                for h in range(heads):
                    pair = m * heads + h
                    lanes = slice((at * heads + h) * 64, (at * heads + h + 1) * 64)
                    half, top = rows // 2, m * rows
                    if pair < blocks and stripe:
                        do_ref[at * blocks + pair, :half, :64] = do_sum[top : top + half, lanes]
                        do_ref[at * blocks + pair, :half, 64:] = do_sum[top + half : top + rows, lanes]
                    elif pair < blocks:
                        do_ref[at * blocks + pair] = do_sum[top : top + rows, lanes]
                    else:
                        for b in range(blocks):
                            do_ref[at * blocks + b, half:, :64] = do_sum[top : top + stripe, lanes]
                            do_ref[at * blocks + b, half:, 64:] = jnp.zeros((stripe, 64), BF)
                            top += stripe
            for b in range(micro * heads, blocks):
                do_ref[at * blocks + b] = jnp.zeros((rows, 64), BF)


def feed_weights_body(rows, blocks, place_ref, ex_ref, re_ref, bias_ref, gate_ref, *refs):
    groups = (len(refs) - 2) // 2
    out_ref, sum_ref = refs[2 * groups :]
    width = refs[0].shape[-1]
    second = jnp.concatenate([x[...] for x in refs[:groups]], 0)
    gate = by_micro(gate_ref, rows)
    dm = jnp.concatenate(
        [(gate * x[...].astype(F32)).astype(BF) for x in refs[groups : 2 * groups]], 0
    )
    expand = ex_ref[...].reshape(width, width)
    reduce = re_ref[...].reshape(width, width)
    u = jnp.dot(second, expand, preferred_element_type=F32) + bias_ref[0]
    g, slope = gelu_pair(u)
    du = lax.dot_general(dm, reduce, NT, preferred_element_type=F32) * slope
    du = du.astype(BF)
    sum_ref[...] = jnp.sum(du.astype(F32), 0, keepdims=True)
    per, each = width // blocks, width // (groups * blocks)
    x = lax.dot_general(g.astype(BF), dm, TN, preferred_element_type=F32)
    for b in range(blocks):
        out_ref[b, :per] = x[b * per : (b + 1) * per].astype(BF)
    x = lax.dot_general(second, du, TN, preferred_element_type=F32)
    for k in range(groups):
        for b in range(blocks):
            at = (k * blocks + b) * each
            out_ref[b, per + k * each : per + (k + 1) * each] = x[at : at + each].astype(BF)


def attend_body(block, range_ref, q_ref, sq_ref, k_ref, v_ref, sk_ref, o_ref, lse_ref):
    i = pl.program_id(0)
    q, sq = q_ref[...], sq_ref[0]
    count, width = q.shape

    def step(j, carry):
        high, total, acc = carry
        at = pl.ds(pl.multiple_of(j * block, block), block)
        k, v, sk = k_ref[at, :], v_ref[at, :], sk_ref[at, :]
        s = lax.dot_general(k, q, (((1,), (1,)), ((), ())), preferred_element_type=F32)
        s = jnp.where(sk == sq, s, NEG)
        new = jnp.maximum(high, jnp.max(s, 0, keepdims=True))
        p = jnp.exp(s - new)
        fix = jnp.exp(high - new)
        total = total * fix + jnp.sum(p, 0, keepdims=True)
        acc = acc * fix + lax.dot_general(
            v, p.astype(BF), (((0,), (0,)), ((), ())), preferred_element_type=F32
        )
        return new, total, acc

    first = (
        jnp.full((1, count), NEG, F32),
        jnp.zeros((1, count), F32),
        jnp.zeros((width, count), F32),
    )
    high, total, acc = lax.fori_loop(range_ref[2 * i], range_ref[2 * i + 1], step, first)
    o_ref[...] = (acc / total).T.astype(BF)
    lse_ref[0] = high + jnp.log(total)


def attend_back_body(
    block, range_ref, q_ref, sq_ref, lse_ref, o_ref, do_ref, k_ref, v_ref, sk_ref,
    dq_ref, dk_ref, dv_ref, dk_sum, dv_sum,
):
    i = pl.program_id(0)

    @pl.when(i == 0)
    def _():
        dk_sum[...] = jnp.zeros_like(dk_sum)
        dv_sum[...] = jnp.zeros_like(dv_sum)

    q, sq, lse, do = q_ref[...], sq_ref[0], lse_ref[0], do_ref[...]
    count, width = q.shape
    delta = jnp.sum((do.astype(F32) * o_ref[...].astype(F32)).T, 0, keepdims=True)

    def step(j, dq):
        at = pl.ds(pl.multiple_of(j * block, block), block)
        k, v, sk = k_ref[at, :], v_ref[at, :], sk_ref[at, :]
        s = lax.dot_general(k, q, (((1,), (1,)), ((), ())), preferred_element_type=F32)
        p = jnp.where(sk == sq, jnp.exp(s - lse), 0.0)
        dp = lax.dot_general(v, do, (((1,), (1,)), ((), ())), preferred_element_type=F32)
        ds = (p * (dp - delta)).astype(BF)
        dv_sum[at, :] += jnp.dot(p.astype(BF), do, preferred_element_type=F32)
        dk_sum[at, :] += jnp.dot(ds, q, preferred_element_type=F32)
        return dq + lax.dot_general(
            k, ds, (((0,), (0,)), ((), ())), preferred_element_type=F32
        )

    dq = lax.fori_loop(
        range_ref[2 * i], range_ref[2 * i + 1], step, jnp.zeros((width, count), F32)
    )
    dq_ref[...] = (dq * 0.125).T.astype(BF)

    @pl.when(i == pl.num_programs(0) - 1)
    def _():
        dk_ref[...] = dk_sum[...].astype(BF)
        dv_ref[...] = dv_sum[...].astype(BF)


def attend(ranges, q, sq, k, v, sk, rows, block):
    count, width = q.shape
    steps = count // rows
    size = k.shape[0]
    by_row = pl.BlockSpec((rows, width), lambda i, r: (i, 0))
    as_row = pl.BlockSpec((1, 1, rows), lambda i, r: (i, 0, 0))
    return pl.pallas_call(
        functools.partial(attend_body, block),
        grid_spec=pltpu.PrefetchScalarGridSpec(
            num_scalar_prefetch=1,
            grid=(steps,),
            in_specs=[by_row, as_row, whole_vmem(), whole_vmem(), whole_vmem()],
            out_specs=[by_row, as_row],
        ),
        out_shape=[
            jax.ShapeDtypeStruct((count, width), BF),
            jax.ShapeDtypeStruct((steps, 1, rows), F32),
        ],
        cost_estimate=pl.CostEstimate(
            flops=count * size * width, transcendentals=count * size // 4, bytes_accessed=4 * size * width
        ),
        name="attend",
    )(ranges, q, sq.reshape(steps, 1, rows), k, v, sk)


def attend_back(ranges, q, sq, lse, o, do, k, v, sk, rows, block):
    count, width = q.shape
    steps = count // rows
    size = k.shape[0]
    by_row = pl.BlockSpec((rows, width), lambda i, r: (i, 0))
    as_row = pl.BlockSpec((1, 1, rows), lambda i, r: (i, 0, 0))
    return pl.pallas_call(
        functools.partial(attend_back_body, block),
        grid_spec=pltpu.PrefetchScalarGridSpec(
            num_scalar_prefetch=1,
            grid=(steps,),
            in_specs=[by_row, as_row, as_row, by_row, by_row, whole_vmem(), whole_vmem(), whole_vmem()],
            out_specs=[by_row, whole_vmem(), whole_vmem()],
            scratch_shapes=[pltpu.VMEM((size, width), F32)] * 2,
        ),
        out_shape=[
            jax.ShapeDtypeStruct((count, width), BF),
            jax.ShapeDtypeStruct((size, width), BF),
            jax.ShapeDtypeStruct((size, width), BF),
        ],
        cost_estimate=pl.CostEstimate(
            flops=3 * count * size * width, transcendentals=count * size // 4, bytes_accessed=8 * size * width
        ),
        name="attend_back",
    )(ranges, q, sq.reshape(steps, 1, rows), lse, o, do, k, v, sk)


def spread(ref, at, rows):
    return ref[pl.ds(pl.multiple_of(at, rows), rows), :]


def keys_mask(low, high, at, count):
    position = at + lax.broadcasted_iota(jnp.int32, (count, low.shape[1]), 0)
    return (position >= low) & (position < high)


QB, KB = 256, 512


def project_small_body(blocks, heads, c_ref, shift_ref, w_ref, *refs):
    groups = len(refs) - 3
    tokens, out_ref, last_ref, wide = refs[:groups], *refs[groups:]
    micro, rows, width = tokens[0].shape
    count = groups * rows
    half, stripe = count // 2, rows // blocks
    end = 192 * heads
    weights = [w_ref[:, c : min(c + 128, end)] for c in range(0, end, 128)]
    for m in range(micro):
        a = jnp.concatenate(
            [(x[m].astype(F32) * c_ref[m][None] + shift_ref[m][None]).astype(BF) for x in tokens], 0
        )
        parts = [jnp.dot(a, w, preferred_element_type=F32) for w in weights]
        v = jnp.concatenate(parts[heads:], 1)
        for h in range(heads):
            pair = m * heads + h
            own_v = v[:, h * 64 : (h + 1) * 64]
            if pair < blocks:
                out_ref[pair, :count] = parts[h].astype(BF)
                out_ref[pair, count : count + half] = jnp.concatenate([own_v[:half], own_v[half:]], 1).astype(BF)
            else:
                wide[...] = parts[h]
                last_ref[...] = jnp.concatenate([parts[h][:, 64:], own_v], 1).astype(BF)
    for to in range(blocks):
        pieces = [
            wide[k * rows + to * stripe : k * rows + (to + 1) * stripe, :64] for k in range(groups)
        ]
        out_ref[to, count + half :] = jnp.concatenate(
            [jnp.concatenate(pieces[:2], 0), jnp.concatenate(pieces[2:], 0)], 1
        ).astype(BF)


def pick_piece(x, k):
    y = jnp.where((k & 1) != 0, x[8:], x[:8])
    return jnp.where(k >= 2, y[:, 64:], y[:, :64])


def project_back_small_body(blocks, heads, c_ref, shift_ref, w_ref, *refs):
    wide = refs[-1]
    few = blocks // 2
    groups = (len(refs) - few - 5) // 2
    tokens, in_ref, lasts = refs[:groups], refs[groups], refs[groups + 1 : groups + 1 + few]
    outs = refs[groups + 1 + few : 2 * groups + 1 + few]
    grad_ref, sum_ref, dot_ref = refs[2 * groups + 1 + few : -1]
    micro, rows, width = tokens[0].shape
    count = groups * rows
    half, stripe = count // 2, rows // blocks
    for j in range(blocks):
        x = in_ref[j, count + half :].astype(F32)
        pieces = [x[:8, :64], x[8:, :64], x[:8, 64:], x[8:, 64:]]
        for k in range(groups):
            wide[k * rows + j * stripe : k * rows + (j + 1) * stripe] = pieces[k]
    all_a, all_g = [], []
    for m in range(micro):
        n = jnp.concatenate([x[m] for x in tokens], 0).astype(F32)
        a = (n * c_ref[m][None] + shift_ref[m][None]).astype(BF)
        qk, v = [], []
        for h in range(heads):
            pair = m * heads + h
            if pair < blocks:
                qk.append(in_ref[pair, :count])
                x = in_ref[pair, count : count + half]
                v.append(jnp.concatenate([x[:, :64], x[:, 64:]], 0))
            else:
                x = sum(ref[...].astype(F32) for ref in lasts).astype(BF)
                qk.append(jnp.concatenate([wide[...].astype(BF), x[:, :64]], 1))
                v.append(x[:, 64:])
        g = jnp.concatenate(qk + v, 1)
        da = lax.dot_general(g, w_ref[:, : 192 * heads], NT, preferred_element_type=F32)
        for k in range(groups):
            outs[k][m] = da[k * rows : (k + 1) * rows].astype(BF)
        sum_ref[m : m + 1] = jnp.sum(da, 0, keepdims=True)
        dot_ref[m : m + 1] = jnp.sum(da * n, 0, keepdims=True)
        all_a.append(a)
        all_g.append(g)
    grad_ref[...] = lax.dot_general(
        jnp.concatenate(all_a, 0), jnp.concatenate(all_g, 0), TN, preferred_element_type=F32
    ).astype(BF)


def attend_block(scores, q, low, high, first, stop, keys, values):
    count = q.shape[0]

    def score(t, top):
        at = pl.multiple_of((first + 2 * t) * QB, QB)
        s = lax.dot_general(keys[pl.ds(at, KB), :], q, NT, preferred_element_type=F32)
        s = jnp.where(keys_mask(low, high, at, KB), s, NEG)
        scores[t, :, :count] = s
        return jnp.maximum(top, jnp.max(s, 0, keepdims=True))

    steps = (stop - first + 1) // 2
    top = lax.fori_loop(0, steps, score, jnp.full((1, count), NEG, F32))

    def weigh(t, carry):
        total, acc = carry
        at = pl.multiple_of((first + 2 * t) * QB, QB)
        p = jnp.exp(scores[t, :, :count] - top)
        return total + jnp.sum(p, 0, keepdims=True), acc + lax.dot_general(
            values[pl.ds(at, KB), :], p.astype(BF), TN, preferred_element_type=F32
        )

    total, acc = lax.fori_loop(
        0, steps, weigh, (jnp.zeros((1, count), F32), jnp.zeros((64, count), F32))
    )
    return (acc / total).T, top + jnp.log(total)


def attend_own_body(
    blocks, groups, rows, place_ref, range_ref, low_ref, high_ref, cos_ref, sin_ref, *refs
):
    in_ref, message, q_ref, k_ref, v_ref, o_ref, lse_ref, kept, kept_v, scores = refs
    span = blocks * rows
    size = groups * span
    count = groups * rows
    half = rows // 2
    me_u, me_b = place_ref[0], place_ref[1]
    for g in range(groups):
        k = me_u ^ g
        for j in range(blocks):
            to = slice(j * rows, (j + 1) * rows)
            kept[to, :] = in_ref[j, pl.ds(pl.multiple_of(k * rows, rows), rows), :]
            pair = in_ref[j, pl.ds(pl.multiple_of(count + (k & 1) * rows, rows), rows), :].astype(F32)
            kept_v[to, :] = jnp.where(k >= 2, pair[:, 64:], pair[:, :64]).astype(BF)
        at = slice(g * span, (g + 1) * span)
        x = turn(kept[...].astype(F32), turn_tables(cos_ref[at], sin_ref[at], False)[0])
        q_ref[at] = (x[:, :64] * 0.125).astype(BF)
        k_ref[at] = x[:, 64:].astype(BF)
        v_ref[at] = kept_v[...]
    tail = slice(size, size + KB - QB)
    for ref in (k_ref, v_ref):
        ref[tail] = jnp.zeros((KB - QB, 64), BF)

    def run(i, _):
        o, lse = attend_block(
            scores, spread(q_ref, i * QB, QB), low_ref[i], high_ref[i],
            range_ref[2 * i], range_ref[2 * i + 1], k_ref, v_ref,
        )
        o = o.astype(BF)
        o_ref[pl.ds(pl.multiple_of(i * QB, QB), QB), :] = o
        lse_ref[i] = lse
        for d in range(QB // rows):
            message[i * (QB // rows) + d] = jnp.concatenate(
                [o[d * rows : d * rows + half], o[d * rows + half : (d + 1) * rows]], 1
            )
        return 0

    lax.fori_loop(0, size // QB, run, 0)


def stripe_tables(place_ref, cos_ref, sin_ref, wide_cos, wide_sin, devices, rows, stripe):
    for d in range(devices):
        at = slice(d * stripe, (d + 1) * stripe)
        wide_cos[at] = spread(cos_ref, d * rows + place_ref[1] * stripe, stripe)
        wide_sin[at] = spread(sin_ref, d * rows + place_ref[1] * stripe, stripe)
    return turn_tables(wide_cos[...], wide_sin[...], True)[1]


def attend_last_body(
    blocks, groups, rows, stripe, place_ref, range_ref, low_ref, high_ref, cos_ref, sin_ref, *refs
):
    in_ref, last_ins, own_ref = refs[0], refs[1:3], refs[3]
    message, q_ref, k_ref, v_ref, o_ref, lse_ref, kept, wide, wide_cos, wide_sin, scores = refs[4:]
    span = blocks * rows
    size = groups * span
    devices = groups * blocks
    count = groups * rows
    half = rows // 2
    me_u, me_b = place_ref[0], place_ref[1]
    for g in range(groups):
        k = me_u ^ g
        for j in range(blocks):
            at = (g * blocks + j) * stripe
            wide[at : at + stripe, :64] = pick_piece(in_ref[j, count + count // 2 :].astype(F32), k)
            to = pl.ds(pl.multiple_of((me_b ^ j) * rows, rows), rows)
            kept[to, :] = last_ins[j & 1][j >> 1, pl.ds(pl.multiple_of(k * rows, rows), rows), :]
        at = slice(g * span, (g + 1) * span)
        x = turn(kept[...].astype(F32), turn_tables(cos_ref[at], sin_ref[at], True)[1])
        k_ref[at] = x[:, :64].astype(BF)
        v_ref[at] = kept[:, 64:]
    tail = slice(size, size + KB - QB)
    for ref in (k_ref, v_ref):
        ref[tail] = jnp.zeros((KB - QB, 64), BF)
    wide[:, 64:] = jnp.zeros((devices * stripe, 64), F32)
    x = turn(wide[...], stripe_tables(place_ref, cos_ref, sin_ref, wide_cos, wide_sin, devices, rows, stripe))
    q_ref[...] = (x[:, :64] * 0.125).astype(BF)
    message[:, :half] = own_ref[...]
    few = lse_ref.shape[2]

    def run(i, _):
        o, lse = attend_block(
            scores, spread(q_ref, i * few, few), low_ref[i], high_ref[i],
            range_ref[2 * i], range_ref[2 * i + 1], k_ref, v_ref,
        )
        o_ref[pl.ds(pl.multiple_of(i * few, few), few), :] = o.astype(BF)
        lse_ref[i] = lse
        o = jnp.concatenate([o, jnp.zeros_like(o)], 1)
        for d in range(few // stripe):
            message[i * (few // stripe) + d, half:] = o[d * stripe : (d + 1) * stripe].astype(BF)
        return 0

    lax.fori_loop(0, lse_ref.shape[0], run, 0)


def attend_block_back(q, do, o, lse, low, high, first, stop, keys, values, dk_sum, dv_sum):
    count = q.shape[0]
    delta = jnp.sum((do.astype(F32) * o.astype(F32)).T, 0, keepdims=True)

    def step(t, dq):
        at = pl.multiple_of((first + 2 * t) * QB, QB)
        here = pl.ds(at, KB)
        k, v = keys[here, :], values[here, :]
        s = lax.dot_general(k, q, NT, preferred_element_type=F32)
        dp = lax.dot_general(v, do, NT, preferred_element_type=F32)
        p = jnp.where(keys_mask(low, high, at, KB), jnp.exp(s - lse), 0.0)
        ds = (p * (dp - delta)).astype(BF)
        dv_sum[here, :] += jnp.dot(p.astype(BF), do, preferred_element_type=F32)
        dk_sum[here, :] += jnp.dot(ds, q, preferred_element_type=F32)
        return dq + lax.dot_general(k, ds, TN, preferred_element_type=F32)

    return (
        lax.fori_loop(0, (stop - first + 1) // 2, step, jnp.zeros((64, count), F32)) * 0.125
    ).T


def attend_last_back_body(
    blocks, groups, rows, stripe, place_ref, range_ref, low_ref, high_ref, cos_ref, sin_ref,
    do_ref, q_ref, k_ref, v_ref, o_ref, lse_ref, dq_ref, keep_ref, send_ref, kept, wide_cos, wide_sin, dk, dv,
):
    span = blocks * rows
    devices = groups * blocks
    half = rows // 2
    for ref in (dk, dv):
        ref[...] = jnp.zeros(ref.shape, F32)
    few = lse_ref.shape[2]
    dq_ref[:, 64:] = jnp.zeros((devices * stripe, 64), F32)

    def run(i, _):
        came = [
            do_ref[i * (few // stripe) + d].astype(F32)[half:, :64] for d in range(few // stripe)
        ]
        at = pl.ds(pl.multiple_of(i * few, few), few)
        dq_ref[at, :64] = attend_block_back(
            q_ref[at, :], jnp.concatenate(came, 0).astype(BF), o_ref[at, :], lse_ref[i],
            low_ref[i], high_ref[i], range_ref[2 * i], range_ref[2 * i + 1], k_ref, v_ref, dk, dv,
        )
        return 0

    lax.fori_loop(0, lse_ref.shape[0], run, 0)
    cos, sin = stripe_tables(place_ref, cos_ref, sin_ref, wide_cos, wide_sin, devices, rows, stripe)
    dq_ref[...] = turn(dq_ref[...], (cos, -sin))
    for g in range(groups):
        at = slice(g * span, (g + 1) * span)
        k = place_ref[0] ^ g
        cos, sin = turn_tables(cos_ref[at], sin_ref[at], True)[1]
        x = turn(jnp.concatenate([dk[at], jnp.zeros_like(dk[at])], 1), (cos, -sin))[:, :64]
        kept[...] = jnp.concatenate([x, dv[at]], 1).astype(BF)
        to = pl.ds(pl.multiple_of(k * rows, rows), rows)
        for z in range(blocks // 2):
            mine = 2 * z + (place_ref[1] & 1)
            keep_ref[z, to, :] = spread(kept, mine * rows, rows)
            send_ref[z, to, :] = spread(kept, (mine ^ 1) * rows, rows)


def attend_own_back_body(
    blocks, groups, rows, stripe, place_ref, range_ref, low_ref, high_ref, cos_ref, sin_ref,
    do_ref, q_ref, k_ref, v_ref, o_ref, lse_ref, last_dq_ref, out_ref, kept, kept_v, wide_v, dq, dk, dv,
):
    span = blocks * rows
    size = groups * span
    count = groups * rows
    half = rows // 2
    me_u, me_b = place_ref[0], place_ref[1]
    for ref in (dk, dv):
        ref[...] = jnp.zeros(ref.shape, F32)

    def run(i, _):
        came = []
        for d in range(QB // rows):
            x = do_ref[i * (QB // rows) + d]
            came += [x[:half, :64], x[:half, 64:]]
        at = pl.ds(pl.multiple_of(i * QB, QB), QB)
        dq[at, :] = attend_block_back(
            q_ref[at, :], jnp.concatenate(came, 0), o_ref[at, :], lse_ref[i], low_ref[i], high_ref[i],
            range_ref[2 * i], range_ref[2 * i + 1], k_ref, v_ref, dk, dv,
        )
        return 0

    lax.fori_loop(0, size // QB, run, 0)
    for g in range(groups):
        at = slice(g * span, (g + 1) * span)
        k = me_u ^ g
        cos, sin = turn_tables(cos_ref[at], sin_ref[at], False)[0]
        kept[...] = turn(jnp.concatenate([dq[at], dk[at]], 1), (cos, -sin)).astype(BF)
        kept_v[...] = dv[at].astype(BF)
        for b in range(blocks):
            out_ref[b, pl.ds(pl.multiple_of(k * rows, rows), rows), :] = kept[b * rows : (b + 1) * rows]
        for b in range(blocks):
            wide_v[g * blocks + b] = kept_v[b * rows : (b + 1) * rows]
    for to in range(blocks):
        v = [wide_v[(me_u ^ k) * blocks + to] for k in range(groups)]
        out_ref[to, count : count + count // 2] = jnp.concatenate(
            [jnp.concatenate(v[:2], 0), jnp.concatenate(v[2:], 0)], 1
        )
        z = [spread(last_dq_ref, ((me_u ^ k) * blocks + to) * stripe, stripe)[:, :64] for k in range(groups)]
        out_ref[to, count + count // 2 :] = jnp.concatenate(
            [jnp.concatenate(z[:2], 0), jnp.concatenate(z[2:], 0)], 1
        ).astype(BF)


def on_device(
    tokens,
    cotangent,
    lengths,
    time_step,
    modulate_weight,
    modulate_bias,
    attend_gain,
    input_weight,
    output_weight,
    feed_gain,
    expand_weight,
    expand_bias,
    reduce_weight,
    reduce_bias,
):
    groups, blocks = lax.axis_size("ulysses"), lax.axis_size("blk")
    group_id, block_id = lax.axis_index("ulysses"), lax.axis_index("blk")
    devices = groups * blocks
    micro, rows, width = tokens.shape
    own = micro * rows
    size = devices * rows
    head_width = width // HEADS
    heads = HEADS // groups
    pairs = micro * heads
    extra = pairs > blocks
    lanes = 384 if extra else 256
    stripe = rows // blocks if extra else 0
    mod_rows = modulate_weight.shape[0]
    gain_rows = attend_gain.shape[0]
    ff_rows = expand_bias.shape[0]
    ff = ff_rows * devices
    folds = ff // width
    assert pairs <= blocks + 1 and head_width == 64 and folds == groups and heads == 3
    place = jnp.stack([group_id, block_id]).astype(jnp.int32)
    pair_micro = jnp.minimum(block_id // heads, micro - 1)

    in_split = input_weight.reshape(gain_rows, 3, groups, heads, head_width)
    in_split = jnp.concatenate(
        [
            in_split[:, :2].transpose(2, 0, 3, 1, 4).reshape(groups, 1, gain_rows, -1),
            in_split[:, 2].transpose(1, 0, 2, 3).reshape(groups, 1, gain_rows, -1),
        ],
        3,
    )
    in_lanes = heads * 3 * head_width

    condition = time_features(time_step, modulate_weight.shape[1] // 2)
    mod_own = jnp.einsum(
        "mc,fc->mf", condition, modulate_weight, preferred_element_type=F32
    ) + modulate_bias.astype(F32)
    mod_lanes = 64 * -(-mod_rows // 64)
    mod_own = jnp.pad(mod_own, ((0, 0), (0, mod_lanes - mod_rows))).reshape(-1, 64)
    mod_high = lax.reduce_precision(mod_own, 8, 7)
    mod_size = mod_own.shape[0]
    vectors = jnp.pad(
        jnp.stack([attend_gain, feed_gain, reduce_bias]), ((0, 0), (0, 64 - gain_rows))
    )
    ff_lanes = 64 * -(-ff_rows // 64)
    small = jnp.concatenate(
        [
            mod_high.astype(BF),
            (mod_own - mod_high).astype(BF),
            vectors,
            jnp.pad(expand_bias, (0, ff_lanes - ff_rows)).reshape(-1, 64),
        ],
        0,
    )
    small_lanes = 64 * -(-small.shape[0] // gain_rows)
    small = jnp.pad(small, ((0, small_lanes * gain_rows // 64 - small.shape[0]), (0, 0)))
    small = small.reshape(1, 1, gain_rows, small_lanes)
    in_message = jnp.concatenate(
        [
            jnp.broadcast_to(in_split, (groups, blocks) + in_split.shape[2:]),
            jnp.broadcast_to(small, (groups, blocks) + small.shape[2:]),
        ],
        3,
    ).reshape(devices, gain_rows, in_lanes + small_lanes)
    in_message, tokens, lengths = lax.optimization_barrier((in_message, tokens, lengths))
    came = exchange(in_message)
    values = tokens.astype(F32)
    n1, r1 = norm(values)
    n1_b = n1.astype(BF)
    n1_group = swap([n1_b] * groups, "ulysses")
    small_all = came[:, :, in_lanes:].reshape(devices, -1, 64)
    in_own = came.reshape(width, in_lanes + small_lanes)

    weight_pack = jnp.concatenate(
            [
                reduce_weight,
                output_weight,
                expand_weight.reshape(gain_rows, folds, width).transpose(1, 0, 2).reshape(-1, width),
            ],
            0,
        )
    index = jnp.arange(size, dtype=jnp.int32)
    pair_lengths = lax.dynamic_index_in_dim(lengths, pair_micro, 0, keepdims=False)
    segment, position = doc_layout(index, pair_lengths)
    last_lengths = lengths[micro - 1]
    last_segment, last_position = doc_layout(index, last_lengths)
    half = head_width // 2
    freqs = jnp.exp(-math.log(10000.0) * jnp.arange(half, dtype=F32) / half)
    lane = jnp.arange(128)
    angles = jnp.where(
        (lane < 64)[None, :], position.astype(F32)[:, None], last_position.astype(F32)[:, None]
    ) * jnp.tile(freqs, 4)[None, :]
    cos_table = jnp.cos(angles)
    sin_table = jnp.where((lane % 64 < 32)[None, :], -1.0, 1.0) * jnp.sin(angles)
    query_rows = math.gcd(size, 256)
    key_block = math.gcd(size, 256)
    first = jnp.arange(size // query_rows, dtype=jnp.int32) * query_rows
    ranges = key_ranges(first, first + query_rows - 1, pair_lengths, key_block)
    small_path = extra and size % KB == 0 and rows == 64 and stripe == 8 and groups == 4 and size <= 4096

    striped = lambda x: lax.dynamic_slice_in_dim(
        x.reshape((devices, rows) + x.shape[1:]), block_id * stripe, stripe, 1
    ).reshape((devices * stripe,) + x.shape[1:])
    last_ranges = bounds = 0
    if small_path:
        last_rows = min(256, devices * stripe)
        chunk = last_rows // stripe
        last_first = jnp.arange(devices // chunk, dtype=jnp.int32) * (chunk * rows) + block_id * stripe
        last_ranges = key_ranges(
            last_first, last_first + (chunk - 1) * rows + stripe - 1, last_lengths, QB
        )
        bounds = []
        for where, lens, pick, lump in (
            (position, pair_lengths, lambda x: x, QB),
            (last_position, last_lengths, striped, last_rows),
        ):
            low = index - where
            ends = jnp.cumsum(lens)
            high = jnp.min(jnp.where(ends[None, :] > index[:, None], ends[None, :], 1 << 30), 1)
            bounds += [pick(low).reshape(-1, 1, lump), pick(high).reshape(-1, 1, lump)]
    in_own, small_all, n1_group, place, cos_table, sin_table, ranges, last_ranges, bounds = (
        lax.optimization_barrier(
            (in_own, small_all, n1_group, place, cos_table, sin_table, ranges, last_ranges, bounds)
        )
    )
    weight_pack, in_own = lax.optimization_barrier((weight_pack, in_own))
    gathered = lax.all_gather(weight_pack, ALL, axis=0, tiled=False)
    unit = gain_rows
    while unit % 8:
        unit *= 2
    units = width // unit
    if unit != gain_rows:
        gathered = jnp.concatenate(
            [gathered[:, :ff_rows].reshape(units, -1, width)]
            + [
                gathered[:, at : at + gain_rows].reshape(units, unit, width)
                for at in range(ff_rows, ff_rows + (folds + 1) * gain_rows, gain_rows)
            ],
            1,
        )
    wide = unit * folds

    mods = small_all[:, :mod_size].astype(F32) + small_all[:, mod_size : 2 * mod_size].astype(F32)
    mods = mods.reshape(devices, micro, mod_lanes)[:, :, :mod_rows].transpose(1, 0, 2).reshape(micro, -1)
    at = 2 * mod_size
    vectors = small_all[:, at : at + 3, :gain_rows].astype(F32).transpose(1, 0, 2).reshape(3, width)
    gain1, gain2, reduce_bias_f = vectors[0], vectors[1], vectors[2:]
    at += 3
    expand_bias_f = small_all[:, at : at + ff_lanes // 64].reshape(devices, ff_lanes)[:, :ff_rows]
    expand_bias_f = expand_bias_f.astype(F32).reshape(folds, 1, width)
    shift1, scale1, gate1, shift2, scale2, gate2 = jnp.split(mods, 6, 1)
    c1 = gain1 * (1.0 + scale1)
    c2 = gain2 * (1.0 + scale2)

    count = groups * rows
    smem = pl.BlockSpec(memory_space=pltpu.SMEM)
    message_rows = count + count // 2 + 16
    if small_path:
        outgoing, last_own = pl.pallas_call(
            functools.partial(project_small_body, blocks, heads),
            out_shape=[
                jax.ShapeDtypeStruct((blocks, message_rows, 128), BF), jax.ShapeDtypeStruct((count, 128), BF),
            ],
            in_specs=[whole_vmem()] * (3 + groups),
            out_specs=[whole_vmem()] * 2,
            scratch_shapes=[pltpu.VMEM((count, 128), F32)],
            cost_estimate=pl.CostEstimate(
                flops=2 * micro * count * width * 3 * 64 * heads, transcendentals=0, bytes_accessed=8 * own * width
            ),
            name="project",
        )(c1, shift1, in_own, *n1_group)
        incoming = [lax.all_to_all(outgoing, "blk", split_axis=0, concat_axis=0, tiled=True)]
        pass_on = lambda x, bit: lax.ppermute(x, "blk", [(i, i ^ bit) for i in range(blocks)])
        last_four = jnp.stack([last_own] + [pass_on(last_own, bit) for bit in range(2, blocks, 2)])
        last_keys = [last_four, pass_on(last_four, 1)]
    else:
        outgoing = pl.pallas_call(
            functools.partial(project_body, blocks, pairs, heads, extra),
            out_shape=[jax.ShapeDtypeStruct((count, lanes), BF)] * blocks,
            in_specs=[smem] + [whole_vmem()] * (3 + groups),
            out_specs=[whole_vmem()] * blocks,
            scratch_shapes=[pltpu.VMEM((blocks, count, lanes), BF)],
            name="project",
        )(place, c1, shift1, in_own, *n1_group)
        incoming = swap(outgoing, "blk")

    span = blocks * rows
    by_span = pl.BlockSpec((span, 64), lambda i, p: (i ^ p[0], 0))
    table_spec = pl.BlockSpec((span, 128), lambda i, p: (i ^ p[0], 0))
    by_rows = pl.BlockSpec((rows, lanes), lambda i, p: (i, 0))
    parts = 6 if extra else 3
    if small_path:
        whole = lambda *shape: jax.ShapeDtypeStruct(shape, BF)
        f32 = lambda *shape: jax.ShapeDtypeStruct(shape, F32)
        padded = whole(size + KB - QB, 64)
        own_args = (place, ranges, *bounds[:2], cos_table, sin_table)
        last_args = (place, last_ranges, *bounds[2:], cos_table, sin_table)
        specs = [smem] * 2 + [whole_vmem()] * 4
        own_message, *own_saved = pl.pallas_call(
            functools.partial(attend_own_body, blocks, groups, rows),
            in_specs=specs + [whole_vmem()],
            out_specs=[whole_vmem()] * 6,
            out_shape=[
                whole(devices, rows // 2, 128), whole(size, 64), padded, padded, whole(size, 64), f32(*bounds[0].shape),
            ],
            scratch_shapes=[
                pltpu.VMEM((span, 128), BF), pltpu.VMEM((span, 64), BF),
                pltpu.VMEM((size // KB + 1, KB, QB), F32),
            ],
            cost_estimate=pl.CostEstimate(
                flops=size * size * 64, transcendentals=size * size // 2, bytes_accessed=16 * size * 128
            ),
            name="attend_own",
        )(*own_args, *incoming)
        message, *last_saved = pl.pallas_call(
            functools.partial(attend_last_body, blocks, groups, rows, stripe),
            in_specs=specs + [whole_vmem()] * 4,
            out_specs=[whole_vmem()] * 6,
            out_shape=[
                whole(devices, rows // 2 + stripe, 128), whole(devices * stripe, 64), padded, padded,
                whole(devices * stripe, 64), f32(*bounds[2].shape),
            ],
            scratch_shapes=[pltpu.VMEM((span, 128), BF)]
            + [pltpu.VMEM((devices * stripe, 128), F32)] * 3
            + [pltpu.VMEM((size // KB + 1, KB, last_rows), F32)],
            cost_estimate=pl.CostEstimate(
                flops=size * size * 16, transcendentals=size * size // 8, bytes_accessed=16 * size * 64
            ),
            name="attend_last",
        )(*last_args, *incoming, *last_keys, own_message)
    else:
        assert not extra
        turned = pl.pallas_call(
            functools.partial(rotate_in_body, blocks, extra),
            grid_spec=pltpu.PrefetchScalarGridSpec(
                num_scalar_prefetch=1,
                grid=(groups,),
                in_specs=[table_spec, table_spec] + [by_rows] * blocks,
                out_specs=[by_span] * parts,
                scratch_shapes=[pltpu.VMEM((span, lanes), BF)],
            ),
            out_shape=[jax.ShapeDtypeStruct((size, 64), BF)] * parts,
            name="rotate_in",
        )(place, cos_table, sin_table, *incoming)
        query, key, value = turned[:3]
        attended, lse = attend(
            ranges, query, segment, key, value, segment[:, None], query_rows, key_block
        )
        message = attended.reshape(devices, rows, head_width)
    came = exchange(message)

    ex_spec = lambda f: pl.BlockSpec((units, unit, width), f)
    flat = pl.BlockSpec((own, width), lambda i: (0, 0))
    vec = lambda n: pl.BlockSpec((n, width), lambda i: (0, 0))
    message_shape = message.shape
    message_spec = pl.BlockSpec(message_shape, lambda i: (0, 0, 0))
    sizes = (groups, blocks, heads, micro, rows, stripe)
    own_f32 = jax.ShapeDtypeStruct((own, width), F32)
    own_bf = jax.ShapeDtypeStruct((own, width), BF)
    merged, attn, middle, second = pl.pallas_call(
        functools.partial(middle_body, *sizes),
        grid=(1,),
        in_specs=[message_spec, ex_spec(lambda i: (0, folds, 0)), flat, vec(micro), vec(micro), vec(micro)],
        out_specs=[flat] * 4,
        out_shape=[own_bf, own_f32, own_f32, own_bf],
        name="middle",
    )(came, gathered, tokens.reshape(own, width), gate1, c2, shift2)
    second_group = swap([second] * groups, "ulysses")
    dy = cotangent.reshape(own, width)
    dy_group = swap([dy] * groups, "ulysses")

    per = width // wide
    layer_output, grad_middle, grad_attn, do_message, sums = pl.pallas_call(
        functools.partial(feed_body, *sizes),
        grid=(folds,),
        in_specs=[
            ex_spec(lambda i: (0, folds + 1 + i, 0)),
            pl.BlockSpec((per, wide, width), lambda i: (i, 0, 0)),
            ex_spec(lambda i: (0, folds, 0)),
            pl.BlockSpec((1, 1, width), lambda i: (i, 0, 0)),
            vec(1),
            flat, flat, flat, flat,
            vec(micro), vec(micro), vec(micro),
        ],
        out_specs=[flat, flat, flat, message_spec, vec(5 * micro)],
        out_shape=[
            own_bf, own_f32, own_bf,
            jax.ShapeDtypeStruct(message_shape, BF),
            jax.ShapeDtypeStruct((5 * micro, width), F32),
        ],
        scratch_shapes=[
            pltpu.VMEM((own, width), F32), pltpu.VMEM((own, width), F32),
            pltpu.VMEM((own, width), BF), pltpu.VMEM((own, width), BF),
        ],
        cost_estimate=pl.CostEstimate(
            flops=8 * own * width * ff, transcendentals=own * ff, bytes_accessed=4 * width * ff
        ),
        name="feed",
    )(gathered, gathered, gathered, expand_bias_f, reduce_bias_f, second, middle, attn, dy, gate1, gate2, c2)
    do_came = exchange(do_message)
    d_gate2, d_shift2, p2, d_gate1, dm_sums = [
        sums[i * micro : (i + 1) * micro] for i in range(5)
    ]

    flat_p = pl.BlockSpec((own, width), lambda i, p: (0, 0))
    feed_part, bias_part = pl.pallas_call(
        functools.partial(feed_weights_body, rows, blocks),
        grid_spec=pltpu.PrefetchScalarGridSpec(
            num_scalar_prefetch=1,
            grid=(1,),
            in_specs=[
                pl.BlockSpec((units, unit, width), lambda i, p: (0, folds + 1 + p[0], 0)),
                pl.BlockSpec((per, wide, width), lambda i, p: (p[0], 0, 0)),
                pl.BlockSpec((1, 1, width), lambda i, p: (p[0], 0, 0)),
                pl.BlockSpec((micro, width), lambda i, p: (0, 0)),
            ]
            + [flat_p] * (2 * groups),
            out_specs=[
                pl.BlockSpec((blocks, ff_rows + groups * gain_rows, width), lambda i, p: (0, 0, 0)),
                pl.BlockSpec((1, width), lambda i, p: (0, 0)),
            ],
        ),
        out_shape=[
            jax.ShapeDtypeStruct((blocks, ff_rows + groups * gain_rows, width), BF),
            jax.ShapeDtypeStruct((1, width), F32),
        ],
        cost_estimate=pl.CostEstimate(
            flops=10 * own * groups * width * width, transcendentals=own * ff, bytes_accessed=16 * width * width
        ),
        name="feed_weights",
    )(place, gathered, gathered, expand_bias_f, gate2, *second_group, *dy_group)
    do_came, feed_part = lax.optimization_barrier((do_came, feed_part))
    feed_sum = lax.psum_scatter(feed_part, "blk", scatter_dimension=0, tiled=True)[0]

    if small_path:
        last_dq, last_kept, last_sent = pl.pallas_call(
            functools.partial(attend_last_back_body, blocks, groups, rows, stripe),
            in_specs=specs + [whole_vmem()] * 6,
            out_specs=[whole_vmem()] * 3,
            out_shape=[f32(devices * stripe, 128)] + [whole(blocks // 2, count, 128)] * 2,
            scratch_shapes=[pltpu.VMEM((span, 128), BF)]
            + [pltpu.VMEM((devices * stripe, 128), F32)] * 2
            + [pltpu.VMEM((size + KB - QB, 64), F32)] * 2,
            cost_estimate=pl.CostEstimate(
                flops=size * size * 32, transcendentals=size * size // 8, bytes_accessed=16 * size * 64
            ),
            name="attend_last_back",
        )(*last_args, do_came, *last_saved)
        last_half = (last_kept.astype(F32) + pass_on(last_sent, 1).astype(F32)).astype(BF)
        do_came, last_dq = lax.optimization_barrier((do_came, last_dq))
        leaving = pl.pallas_call(
            functools.partial(attend_own_back_body, blocks, groups, rows, stripe),
            in_specs=specs + [whole_vmem()] * 7,
            out_specs=whole_vmem(),
            out_shape=whole(blocks, message_rows, 128),
            scratch_shapes=[
                pltpu.VMEM((span, 128), BF), pltpu.VMEM((span, 64), BF),
                pltpu.VMEM((devices, rows, 64), BF), pltpu.VMEM((size, 64), F32),
            ]
            + [pltpu.VMEM((size + KB - QB, 64), F32)] * 2,
            cost_estimate=pl.CostEstimate(
                flops=2 * size * size * 64, transcendentals=size * size // 2, bytes_accessed=16 * size * 128
            ),
            name="attend_own_back",
        )(*own_args, do_came, *own_saved, last_dq)
    else:
        grads = attend_back(
            ranges, query, segment, lse, attended, do_came.reshape(size, head_width), key, value,
            segment[:, None], query_rows, key_block,
        )
        leaving = pl.pallas_call(
            functools.partial(rotate_out_body, blocks, extra),
            grid_spec=pltpu.PrefetchScalarGridSpec(
                num_scalar_prefetch=1,
                grid=(groups,),
                in_specs=[table_spec, table_spec] + [by_span] * parts,
                out_specs=[by_rows] * blocks,
                scratch_shapes=[pltpu.VMEM((span, lanes), BF)],
            ),
            out_shape=[jax.ShapeDtypeStruct((count, lanes), BF)] * blocks,
            name="rotate_out",
        )(place, cos_table, sin_table, *grads)
    if small_path:
        leaving, last_half = lax.optimization_barrier((leaving, last_half))
        back = [lax.all_to_all(leaving, "blk", split_axis=0, concat_axis=0, tiled=True)]
        back += [
            pass_on(lax.dynamic_index_in_dim(last_half, (block_id // 2) ^ k, 0, keepdims=False), 2 * k)
            if k
            else lax.dynamic_index_in_dim(last_half, block_id // 2, 0, keepdims=False)
            for k in range(blocks // 2)
        ]
    else:
        back = swap(leaving, "blk")
    leaving, merged, grad_attn = lax.optimization_barrier((leaving, merged, grad_attn))
    output_part = lax.dot_general(merged, grad_attn, TN, preferred_element_type=F32).astype(BF)
    output_part = output_part.reshape(groups, width // groups, width)

    output_part = swap(
        [
            lax.dynamic_index_in_dim(output_part, group_id ^ k, 0, keepdims=False)
            for k in range(groups)
        ],
        "ulysses",
    )

    output_part = sum(x.astype(F32) for x in output_part).astype(BF).reshape(blocks, gain_rows, width)

    if small_path:
        back_body = functools.partial(project_back_small_body, blocks, heads)
        back_scratch = [pltpu.VMEM((count, 64), F32)]
        back_args, back_specs = (), []
    else:
        back_args, back_specs = (place,), [smem]
        back_body = functools.partial(project_back_body, blocks, pairs, heads, extra)
        back_scratch = [pltpu.VMEM((blocks, count, lanes), BF)]
    returned = pl.pallas_call(
        back_body,
        out_shape=[jax.ShapeDtypeStruct((micro, rows, width), BF)] * groups
        + [
            jax.ShapeDtypeStruct((width, heads * 3 * head_width), BF),
            jax.ShapeDtypeStruct((micro, width), F32),
            jax.ShapeDtypeStruct((micro, width), F32),
        ],
        in_specs=back_specs + [whole_vmem()] * (3 + groups + len(back)),
        out_specs=[whole_vmem()] * (groups + 3),
        scratch_shapes=back_scratch,
        cost_estimate=pl.CostEstimate(
            flops=4 * micro * count * width * 3 * 64 * heads, transcendentals=0, bytes_accessed=8 * own * width
        ),
        name="project_back",
    )(*back_args, c1, shift1, in_own, *n1_group, *back)
    input_part, d_shift1, p1 = returned[groups:]
    grad_first = sum(x.astype(F32) for x in swap(returned[:groups], "ulysses"))
    e = grad_first * c1[:, None]
    tokens_grad = (
        grad_middle.reshape(micro, rows, width)
        + r1
        * (
            e
            - jnp.mean(e, -1, keepdims=True)
            - n1 * jnp.mean(e * n1, -1, keepdims=True)
        )
    ).astype(BF)

    grad_mods = jnp.concatenate(
        [d_shift1, p1 * gain1, d_gate1, d_shift2, p2 * gain2, d_gate2], 1
    )
    gain1_part = jnp.sum((1.0 + scale1) * p1, 0)
    gain2_part = jnp.sum((1.0 + scale2) * p2, 0)
    own_units = jnp.where(
        (jnp.arange(groups) == group_id)[:, None], bias_part.reshape(1, width), 0.0
    )
    small_parts = jnp.concatenate(
        [grad_mods.reshape(micro, devices, mod_rows).transpose(1, 0, 2).reshape(devices, -1)]
        + [
            x.reshape(devices, -1)
            for x in (gain1_part, gain2_part, jnp.sum(dm_sums, 0), own_units)
        ],
        1,
    ).astype(BF)
    taken = small_parts.shape[1]
    small_rows = 8 * -(-taken // (8 * in_lanes))
    small_parts = jnp.pad(small_parts, ((0, 0), (0, small_rows * in_lanes - taken)))
    input_sum = halve(
        input_part.reshape(groups, blocks, gain_rows, in_lanes).transpose(1, 0, 2, 3), "blk", block_id, 1
    )
    out_lanes = output_part.shape[1] * output_part.shape[2] // in_lanes
    rest = jnp.concatenate(
        [
            small_parts.reshape(groups, blocks, small_rows, in_lanes)
            .transpose(1, 0, 2, 3)
            .reshape(blocks, groups * small_rows, in_lanes),
            output_part.reshape(blocks, out_lanes, in_lanes),
        ],
        1,
    )
    rest = halve(rest, "blk", block_id, 1)
    input_sum, rest, feed_sum = lax.optimization_barrier((input_sum, rest, feed_sum))
    input_sum = jnp.concatenate(
        [input_sum.reshape(blocks // 2, groups * gain_rows, in_lanes), rest], 1
    )
    bit = 2
    while bit < blocks:
        input_sum = halve(input_sum, "blk", block_id, bit)
        bit *= 2
    input_sum = input_sum[0]
    at = groups * gain_rows
    small_sum = input_sum[at : at + groups * small_rows]
    output_grad = input_sum[at + groups * small_rows :].reshape(gain_rows, width).astype(F32)
    input_sum = jnp.concatenate(
        [input_sum[:at].reshape(groups, gain_rows, in_lanes), small_sum.reshape(groups, small_rows, in_lanes)], 1
    )
    final = jnp.stack(
        swap(
            [
                lax.dynamic_index_in_dim(input_sum, group_id ^ k, 0, keepdims=False)
                for k in range(groups)
            ],
            "ulysses",
        )
    )
    small_sum = jnp.sum(final[:, gain_rows:].astype(F32), 0).reshape(-1)
    input_sum = unscramble(final[:, :gain_rows], group_id, 0).astype(F32)
    reduce_grad = feed_sum[:ff_rows].astype(F32)
    expand_rows = feed_sum[ff_rows:].reshape(groups, gain_rows, width)
    expand_came = jnp.stack(
        swap(
            [
                lax.dynamic_index_in_dim(expand_rows, group_id ^ k, 0, keepdims=False)
                for k in range(groups)
            ],
            "ulysses",
        )
    )
    expand_grad = jnp.concatenate(
        [
            lax.dynamic_index_in_dim(expand_came, group_id ^ k, 0, keepdims=False)
            for k in range(groups)
        ],
        1,
    ).astype(F32)

    two = heads * 2 * head_width
    input_grad = jnp.concatenate(
        [
            input_sum[:, :, :two]
            .reshape(groups, gain_rows, heads, 2, head_width)
            .transpose(1, 3, 0, 2, 4)
            .reshape(gain_rows, 2 * width),
            input_sum[:, :, two:].transpose(1, 0, 2).reshape(gain_rows, width),
        ],
        1,
    )
    at = micro * mod_rows
    mod_sum = small_sum[:at].reshape(micro, mod_rows)
    modulate_weight_grad = jnp.sum(
        mod_sum[:, :, None] * condition.astype(F32)[:, None, :], 0
    )
    cuts = []
    for length in (gain_rows, gain_rows, gain_rows, ff_rows):
        cuts.append(small_sum[at : at + length])
        at += length
    return (
        layer_output.reshape(micro, rows, width),
        tokens_grad,
        modulate_weight_grad,
        jnp.sum(mod_sum, 0),
        cuts[0],
        input_grad,
        output_grad,
        cuts[1],
        expand_grad,
        cuts[3],
        reduce_grad,
        cuts[2],
    )


def solution(mesh):
    both = P(("ulysses", "blk"))
    tall = P(("ulysses", "blk"), None)
    seq = P(None, ("ulysses", "blk"), None)
    in_specs = (
        seq, seq, P(), P(), tall, both, both, tall, tall, both, tall, both, tall, both,
    )
    out_specs = (seq, seq, tall, both, both, tall, tall, both, tall, both, tall, both)
    return jax.shard_map(
        on_device, mesh=mesh, in_specs=in_specs, out_specs=out_specs, check_vma=False
    )
```

```python
import functools
import math

import jax
import jax.numpy as jnp
from jax import lax
from jax.experimental import pallas as pl
from jax.experimental.pallas import tpu as pltpu
from jax.sharding import PartitionSpec as P

HEADS = 12
ALL = ("ulysses", "blk")
BF = jnp.bfloat16
F32 = jnp.float32
NEG = -1e30


def exchange(x):
    return lax.all_to_all(x, ALL, split_axis=0, concat_axis=0, tiled=True)


def time_features(time_step, half):
    freqs = jnp.exp(-math.log(10000.0) * jnp.arange(half, dtype=F32) / half)
    angles = time_step.astype(F32)[:, None] * freqs[None, :]
    return jax.nn.silu(jnp.concatenate([jnp.cos(angles), jnp.sin(angles)], 1)).astype(BF)


def doc_layout(index, lengths_row):
    ends = jnp.cumsum(lengths_row)
    over = index[:, None] >= ends[None, :]
    segment = jnp.sum(over.astype(jnp.int32), 1)
    place = index - jnp.sum(jnp.where(over, lengths_row[None, :], 0), 1)
    return segment, place


def key_ranges(first, last, lengths_row, block):
    ends = jnp.cumsum(lengths_row)
    start = jnp.sum(jnp.where(first[:, None] >= ends[None, :], lengths_row[None, :], 0), 1)
    stop = jnp.min(jnp.where(ends[None, :] > last[:, None], ends[None, :], 1 << 30), 1)
    return jnp.stack([start // block, (stop + block - 1) // block], 1).reshape(-1)


def whole_vmem():
    return pl.BlockSpec(memory_space=pltpu.VMEM)


def swap(blocks, axis):
    size = lax.axis_size(axis)
    return [
        x if k == 0 else lax.ppermute(x, axis, [(i, i ^ k) for i in range(size)])
        for k, x in enumerate(blocks)
    ]


def unscramble(x, index, axis):
    count, bit = x.shape[axis], 1
    while bit < count:
        shape = x.shape
        y = x.reshape(shape[:axis] + (count // (2 * bit), 2, bit) + shape[axis + 1 :])
        flipped = jnp.flip(y, axis + 1)
        x = jnp.where((index & bit) != 0, flipped, y).reshape(shape)
        bit *= 2
    return x


def halve(x, axis, index, bit):
    size = lax.axis_size(axis)
    y = x.reshape((-1, 2) + x.shape[1:])
    mine = (index // bit) % 2
    sent = lax.dynamic_index_in_dim(y, 1 - mine, 1, keepdims=False)
    kept = lax.dynamic_index_in_dim(y, mine, 1, keepdims=False)
    came = lax.ppermute(sent, axis, [(i, i ^ bit) for i in range(size)])
    return (kept.astype(F32) + came.astype(F32)).astype(BF)


def project_body(blocks, pairs, heads, extra, place_ref, c_ref, shift_ref, w_ref, *refs):
    groups = len(refs) - blocks - 1
    tokens, outs, kept = refs[:groups], refs[groups:-1], refs[-1]
    micro, rows, width = tokens[0].shape
    end = 192 * heads
    weights = [w_ref[:, c : min(c + 128, end)] for c in range(0, end, 128)]
    order = list(range(micro))[::-1]
    z_qk = z_v = None
    for m in order:
        a = jnp.concatenate(
            [(x[m].astype(F32) * c_ref[m][None] + shift_ref[m][None]).astype(BF) for x in tokens], 0
        )
        parts = [jnp.dot(a, w, preferred_element_type=F32).astype(BF) for w in weights]
        v = jnp.concatenate(parts[heads:], 1)
        if extra and m == micro - 1:
            z_qk = parts[heads - 1]
            z_v = v[:, (heads - 1) * 64 : heads * 64]
        for h in range(heads):
            pair = m * heads + h
            if pair >= blocks:
                continue
            kept[pair, :, :128] = parts[h]
            own_v = v[:, h * 64 : (h + 1) * 64]
            if extra:
                kept[pair, :, 128:256] = z_qk
                kept[pair, :, 256:] = jnp.concatenate([own_v, z_v], 1)
            else:
                kept[pair, :, 128:] = jnp.concatenate([own_v, jnp.zeros_like(own_v)], 1)
    for pair in range(pairs, blocks):
        kept[pair] = jnp.zeros(kept.shape[1:], BF)
    for j in range(blocks):
        outs[j][...] = kept[place_ref[1] ^ j]


def turn_tables(cos, sin, extra):
    lane = lax.broadcasted_iota(jnp.int32, cos.shape, 1)
    low = lane < 64
    cos_r, sin_r = pltpu.roll(cos, 64, 1), pltpu.roll(sin, 64, 1)
    tables = [(jnp.where(low, cos, cos_r), jnp.where(low, sin, sin_r))]
    if extra:
        tables.append((jnp.where(low, cos_r, cos), jnp.where(low, sin_r, sin)))
    return tables


def turn(x, table):
    lane = lax.broadcasted_iota(jnp.int32, x.shape, 1)
    swapped = jnp.where(lane % 64 < 32, pltpu.roll(x, 96, 1), pltpu.roll(x, 32, 1))
    return x * table[0] + swapped * table[1]


def rotate_in_body(blocks, extra, place_ref, cos_ref, sin_ref, *refs):
    ins, outs = refs[:blocks], refs[blocks : 2 * blocks - blocks + (6 if extra else 3)]
    kept = refs[-1]
    rows = ins[0].shape[0]
    for j in range(blocks):
        at = pl.multiple_of((place_ref[1] ^ j) * rows, rows)
        kept[pl.ds(at, rows), :] = ins[j][...]
    tables = turn_tables(cos_ref[...], sin_ref[...], extra)
    x0 = turn(kept[:, :128].astype(F32), tables[0])
    outs[0][...] = (x0[:, :64] * 0.125).astype(BF)
    outs[1][...] = x0[:, 64:].astype(BF)
    if extra:
        outs[2][...] = kept[:, 256:320]
        x1 = turn(kept[:, 128:256].astype(F32), tables[1])
        outs[3][...] = (x1[:, :64] * 0.125).astype(BF)
        outs[4][...] = x1[:, 64:].astype(BF)
        outs[5][...] = kept[:, 320:]
    else:
        outs[2][...] = kept[:, 128:192]


def rotate_out_body(blocks, extra, place_ref, cos_ref, sin_ref, *refs):
    count = 6 if extra else 3
    ins, outs, kept = refs[:count], refs[count:-1], refs[-1]
    rows = outs[0].shape[0]
    parts = [ref[...].astype(F32) for ref in ins]
    tables = [(c, -s) for c, s in turn_tables(cos_ref[...], sin_ref[...], extra)]
    kept[:, :128] = turn(jnp.concatenate(parts[:2], 1), tables[0]).astype(BF)
    if extra:
        kept[:, 128:256] = turn(jnp.concatenate(parts[3:5], 1), tables[1]).astype(BF)
        kept[:, 256:] = jnp.concatenate([parts[2], parts[5]], 1).astype(BF)
    else:
        kept[:, 128:] = jnp.concatenate([parts[2], jnp.zeros_like(parts[2])], 1).astype(BF)
    for j in range(blocks):
        at = pl.multiple_of((place_ref[1] ^ j) * rows, rows)
        outs[j][...] = kept[pl.ds(at, rows), :]


def project_back_body(blocks, pairs, heads, extra, place_ref, c_ref, shift_ref, w_ref, *refs):
    kept = refs[-1]
    groups = (len(refs) - blocks - 4) // 2
    tokens, ins = refs[:groups], refs[groups : groups + blocks]
    outs = refs[groups + blocks : 2 * groups + blocks]
    grad_ref, sum_ref, dot_ref = refs[2 * groups + blocks : -1]
    micro, rows, width = tokens[0].shape
    count = groups * rows
    for j in range(blocks):
        kept[place_ref[1] ^ j] = ins[j][...]
    last = None
    if extra:
        last = jnp.zeros((count, 256), F32)
        for j in range(blocks):
            last = last + kept[j, :, 128:].astype(F32)
        last = last.astype(BF)
    all_a, all_g = [], []
    for m in range(micro):
        n = jnp.concatenate([x[m] for x in tokens], 0).astype(F32)
        a = (n * c_ref[m][None] + shift_ref[m][None]).astype(BF)
        qk, v = [], []
        for h in range(heads):
            pair = m * heads + h
            if pair < blocks:
                qk.append(kept[pair, :, :128])
                at = 256 if extra else 128
                v.append(kept[pair, :, at : at + 64])
            else:
                qk.append(last[:, :128])
                v.append(last[:, 192:])
        g = jnp.concatenate(qk + v, 1)
        da = lax.dot_general(g, w_ref[:, : 192 * heads], (((1,), (1,)), ((), ())), preferred_element_type=F32)
        for k in range(groups):
            outs[k][m] = da[k * rows : (k + 1) * rows].astype(BF)
        sum_ref[m : m + 1] = jnp.sum(da, 0, keepdims=True)
        dot_ref[m : m + 1] = jnp.sum(da * n, 0, keepdims=True)
        all_a.append(a)
        all_g.append(g)
    grad_ref[...] = lax.dot_general(
        jnp.concatenate(all_a, 0), jnp.concatenate(all_g, 0), (((0,), (0,)), ((), ())),
        preferred_element_type=F32,
    ).astype(BF)


def norm(values):
    centered = values - jnp.mean(values, -1, keepdims=True)
    inverse = lax.rsqrt(jnp.mean(centered * centered, -1, keepdims=True) + 1e-05)
    return centered * inverse, inverse


def by_micro(ref, rows):
    return jnp.concatenate(
        [jnp.broadcast_to(ref[m][None], (rows, ref.shape[1])) for m in range(ref.shape[0])], 0
    )


def middle_body(
    groups, blocks, heads, micro, rows, stripe,
    came_ref, out_ref, x_ref, gate_ref, c_ref, shift_ref,
    merged_ref, attn_ref, middle_ref, second_ref,
):
    width = x_ref.shape[1]
    for u in range(groups):
        for m in range(micro):
            for h in range(heads):
                pair = m * heads + h
                lanes = slice((u * heads + h) * 64, (u * heads + h + 1) * 64)
                half = rows // 2
                if pair < blocks and stripe:
                    at = m * rows
                    merged_ref[at : at + half, lanes] = came_ref[u * blocks + pair, :half, :64]
                    merged_ref[at + half : at + rows, lanes] = came_ref[u * blocks + pair, :half, 64:]
                elif pair < blocks:
                    merged_ref[m * rows : (m + 1) * rows, lanes] = came_ref[u * blocks + pair]
                else:
                    for b in range(blocks):
                        at = m * rows + b * stripe
                        merged_ref[at : at + stripe, lanes] = came_ref[u * blocks + b, half:, :64]
    attn = jnp.dot(merged_ref[...], out_ref[...].reshape(width, width), preferred_element_type=F32)
    attn_ref[...] = attn
    middle = x_ref[...].astype(F32) + by_micro(gate_ref, rows) * attn
    middle_ref[...] = middle
    normed, _ = norm(middle)
    second_ref[...] = (normed * by_micro(c_ref, rows) + by_micro(shift_ref, rows)).astype(BF)


def gelu_pair(u):
    t = jnp.tanh(0.7978845608028654 * (u + 0.044715 * u * u * u))
    value = 0.5 * u * (1.0 + t)
    slope = 0.5 * (1.0 + t) + 0.5 * u * (1.0 - t * t) * (
        0.7978845608028654 * (1.0 + 0.134145 * u * u)
    )
    return value, slope


NT = (((1,), (1,)), ((), ()))
TN = (((0,), (0,)), ((), ()))


def feed_body(
    groups, blocks, heads, micro, rows, stripe,
    ex_ref, re_ref, out_w_ref, ex_bias_ref, re_bias_ref, second_ref, middle_ref, attn_ref, dy_ref,
    gate1_ref, gate2_ref, c_ref,
    layer_ref, grad_ref, dattn_ref, do_ref, sums_ref,
    branch_sum, back_sum, dm_sum, do_sum,
):
    step = pl.program_id(0)
    width = middle_ref.shape[1]

    @pl.when(step == 0)
    def _():
        branch_sum[...] = jnp.zeros_like(branch_sum)
        back_sum[...] = jnp.zeros_like(back_sum)
        dm_sum[...] = (by_micro(gate2_ref, rows) * dy_ref[...].astype(F32)).astype(BF)

    expand = ex_ref[...].reshape(width, width)
    reduce = re_ref[...].reshape(width, width)
    u = jnp.dot(second_ref[...], expand, preferred_element_type=F32) + ex_bias_ref[0]
    g, slope = gelu_pair(u)
    branch_sum[...] += jnp.dot(g.astype(BF), reduce, preferred_element_type=F32)
    dg = lax.dot_general(dm_sum[...], reduce, NT, preferred_element_type=F32)
    du = (dg * slope).astype(BF)
    back_sum[...] += lax.dot_general(du, expand, NT, preferred_element_type=F32)

    @pl.when(step == pl.num_programs(0) - 1)
    def _():
        def total(at, x):
            for m in range(micro):
                sums_ref[at * micro + m : at * micro + m + 1] = jnp.sum(
                    x[m * rows : (m + 1) * rows], 0, keepdims=True
                )

        branch = branch_sum[...] + re_bias_ref[...]
        middle = middle_ref[...]
        dy = dy_ref[...].astype(F32)
        layer_ref[...] = (middle + by_micro(gate2_ref, rows) * branch).astype(BF)
        total(0, dy * branch)
        normed, inverse = norm(middle)
        db = back_sum[...]
        total(1, db)
        total(2, db * normed)
        e = db * by_micro(c_ref, rows)
        grad = dy + inverse * (
            e
            - jnp.mean(e, -1, keepdims=True)
            - normed * jnp.mean(e * normed, -1, keepdims=True)
        )
        grad_ref[...] = grad
        total(3, grad * attn_ref[...])
        total(4, dm_sum[...].astype(F32))
        dattn = (by_micro(gate1_ref, rows) * grad).astype(BF)
        dattn_ref[...] = dattn
        do_sum[...] = lax.dot_general(
            dattn, out_w_ref[...].reshape(width, width), NT, preferred_element_type=F32
        ).astype(BF)
        for at in range(groups):
            for m in range(micro):
                for h in range(heads):
                    pair = m * heads + h
                    lanes = slice((at * heads + h) * 64, (at * heads + h + 1) * 64)
                    half, top = rows // 2, m * rows
                    if pair < blocks and stripe:
                        do_ref[at * blocks + pair, :half, :64] = do_sum[top : top + half, lanes]
                        do_ref[at * blocks + pair, :half, 64:] = do_sum[top + half : top + rows, lanes]
                    elif pair < blocks:
                        do_ref[at * blocks + pair] = do_sum[top : top + rows, lanes]
                    else:
                        for b in range(blocks):
                            do_ref[at * blocks + b, half:, :64] = do_sum[top : top + stripe, lanes]
                            do_ref[at * blocks + b, half:, 64:] = jnp.zeros((stripe, 64), BF)
                            top += stripe
            for b in range(micro * heads, blocks):
                do_ref[at * blocks + b] = jnp.zeros((rows, 64), BF)


def feed_weights_body(rows, blocks, place_ref, ex_ref, re_ref, bias_ref, gate_ref, *refs):
    groups = (len(refs) - 2) // 2
    out_ref, sum_ref = refs[2 * groups :]
    width = refs[0].shape[-1]
    second = jnp.concatenate([x[...] for x in refs[:groups]], 0)
    gate = by_micro(gate_ref, rows)
    dm = jnp.concatenate(
        [(gate * x[...].astype(F32)).astype(BF) for x in refs[groups : 2 * groups]], 0
    )
    expand = ex_ref[...].reshape(width, width)
    reduce = re_ref[...].reshape(width, width)
    u = jnp.dot(second, expand, preferred_element_type=F32) + bias_ref[0]
    g, slope = gelu_pair(u)
    du = lax.dot_general(dm, reduce, NT, preferred_element_type=F32) * slope
    du = du.astype(BF)
    sum_ref[...] = jnp.sum(du.astype(F32), 0, keepdims=True)
    per, each = width // blocks, width // (groups * blocks)
    x = lax.dot_general(g.astype(BF), dm, TN, preferred_element_type=F32)
    for b in range(blocks):
        out_ref[b, :per] = x[b * per : (b + 1) * per].astype(BF)
    x = lax.dot_general(second, du, TN, preferred_element_type=F32)
    for k in range(groups):
        for b in range(blocks):
            at = (k * blocks + b) * each
            out_ref[b, per + k * each : per + (k + 1) * each] = x[at : at + each].astype(BF)


def attend_body(block, range_ref, q_ref, sq_ref, k_ref, v_ref, sk_ref, o_ref, lse_ref):
    i = pl.program_id(0)
    q, sq = q_ref[...], sq_ref[0]
    count, width = q.shape

    def step(j, carry):
        high, total, acc = carry
        at = pl.ds(pl.multiple_of(j * block, block), block)
        k, v, sk = k_ref[at, :], v_ref[at, :], sk_ref[at, :]
        s = lax.dot_general(k, q, (((1,), (1,)), ((), ())), preferred_element_type=F32)
        s = jnp.where(sk == sq, s, NEG)
        new = jnp.maximum(high, jnp.max(s, 0, keepdims=True))
        p = jnp.exp(s - new)
        fix = jnp.exp(high - new)
        total = total * fix + jnp.sum(p, 0, keepdims=True)
        acc = acc * fix + lax.dot_general(
            v, p.astype(BF), (((0,), (0,)), ((), ())), preferred_element_type=F32
        )
        return new, total, acc

    first = (
        jnp.full((1, count), NEG, F32),
        jnp.zeros((1, count), F32),
        jnp.zeros((width, count), F32),
    )
    high, total, acc = lax.fori_loop(range_ref[2 * i], range_ref[2 * i + 1], step, first)
    o_ref[...] = (acc / total).T.astype(BF)
    lse_ref[0] = high + jnp.log(total)


def attend_back_body(
    block, range_ref, q_ref, sq_ref, lse_ref, o_ref, do_ref, k_ref, v_ref, sk_ref,
    dq_ref, dk_ref, dv_ref, dk_sum, dv_sum,
):
    i = pl.program_id(0)

    @pl.when(i == 0)
    def _():
        dk_sum[...] = jnp.zeros_like(dk_sum)
        dv_sum[...] = jnp.zeros_like(dv_sum)

    q, sq, lse, do = q_ref[...], sq_ref[0], lse_ref[0], do_ref[...]
    count, width = q.shape
    delta = jnp.sum((do.astype(F32) * o_ref[...].astype(F32)).T, 0, keepdims=True)

    def step(j, dq):
        at = pl.ds(pl.multiple_of(j * block, block), block)
        k, v, sk = k_ref[at, :], v_ref[at, :], sk_ref[at, :]
        s = lax.dot_general(k, q, (((1,), (1,)), ((), ())), preferred_element_type=F32)
        p = jnp.where(sk == sq, jnp.exp(s - lse), 0.0)
        dp = lax.dot_general(v, do, (((1,), (1,)), ((), ())), preferred_element_type=F32)
        ds = (p * (dp - delta)).astype(BF)
        dv_sum[at, :] += jnp.dot(p.astype(BF), do, preferred_element_type=F32)
        dk_sum[at, :] += jnp.dot(ds, q, preferred_element_type=F32)
        return dq + lax.dot_general(
            k, ds, (((0,), (0,)), ((), ())), preferred_element_type=F32
        )

    dq = lax.fori_loop(
        range_ref[2 * i], range_ref[2 * i + 1], step, jnp.zeros((width, count), F32)
    )
    dq_ref[...] = (dq * 0.125).T.astype(BF)

    @pl.when(i == pl.num_programs(0) - 1)
    def _():
        dk_ref[...] = dk_sum[...].astype(BF)
        dv_ref[...] = dv_sum[...].astype(BF)


def attend(ranges, q, sq, k, v, sk, rows, block):
    count, width = q.shape
    steps = count // rows
    size = k.shape[0]
    by_row = pl.BlockSpec((rows, width), lambda i, r: (i, 0))
    as_row = pl.BlockSpec((1, 1, rows), lambda i, r: (i, 0, 0))
    return pl.pallas_call(
        functools.partial(attend_body, block),
        grid_spec=pltpu.PrefetchScalarGridSpec(
            num_scalar_prefetch=1,
            grid=(steps,),
            in_specs=[by_row, as_row, whole_vmem(), whole_vmem(), whole_vmem()],
            out_specs=[by_row, as_row],
        ),
        out_shape=[
            jax.ShapeDtypeStruct((count, width), BF),
            jax.ShapeDtypeStruct((steps, 1, rows), F32),
        ],
        cost_estimate=pl.CostEstimate(
            flops=count * size * width, transcendentals=count * size // 4, bytes_accessed=4 * size * width
        ),
        name="attend",
    )(ranges, q, sq.reshape(steps, 1, rows), k, v, sk)


def attend_back(ranges, q, sq, lse, o, do, k, v, sk, rows, block):
    count, width = q.shape
    steps = count // rows
    size = k.shape[0]
    by_row = pl.BlockSpec((rows, width), lambda i, r: (i, 0))
    as_row = pl.BlockSpec((1, 1, rows), lambda i, r: (i, 0, 0))
    return pl.pallas_call(
        functools.partial(attend_back_body, block),
        grid_spec=pltpu.PrefetchScalarGridSpec(
            num_scalar_prefetch=1,
            grid=(steps,),
            in_specs=[by_row, as_row, as_row, by_row, by_row, whole_vmem(), whole_vmem(), whole_vmem()],
            out_specs=[by_row, whole_vmem(), whole_vmem()],
            scratch_shapes=[pltpu.VMEM((size, width), F32)] * 2,
        ),
        out_shape=[
            jax.ShapeDtypeStruct((count, width), BF),
            jax.ShapeDtypeStruct((size, width), BF),
            jax.ShapeDtypeStruct((size, width), BF),
        ],
        cost_estimate=pl.CostEstimate(
            flops=3 * count * size * width, transcendentals=count * size // 4, bytes_accessed=8 * size * width
        ),
        name="attend_back",
    )(ranges, q, sq.reshape(steps, 1, rows), lse, o, do, k, v, sk)


def spread(ref, at, rows):
    return ref[pl.ds(pl.multiple_of(at, rows), rows), :]


def keys_mask(low, high, at, count):
    position = at + lax.broadcasted_iota(jnp.int32, (count, low.shape[1]), 0)
    return (position >= low) & (position < high)


QB, KB, STEP = 512, 512, 256


def project_small_body(blocks, heads, c_ref, shift_ref, w_ref, *refs):
    groups = len(refs) - 3
    tokens, out_ref, last_ref, wide = refs[:groups], *refs[groups:]
    micro, rows, width = tokens[0].shape
    count = groups * rows
    half, stripe = count // 2, rows // blocks
    end = 192 * heads
    weights = [w_ref[:, c : min(c + 128, end)] for c in range(0, end, 128)]
    for m in range(micro):
        a = jnp.concatenate(
            [(x[m].astype(F32) * c_ref[m][None] + shift_ref[m][None]).astype(BF) for x in tokens], 0
        )
        parts = [jnp.dot(a, w, preferred_element_type=F32) for w in weights]
        v = jnp.concatenate(parts[heads:], 1)
        for h in range(heads):
            pair = m * heads + h
            own_v = v[:, h * 64 : (h + 1) * 64]
            if pair < blocks:
                out_ref[pair, :count] = parts[h].astype(BF)
                out_ref[pair, count : count + half] = jnp.concatenate([own_v[:half], own_v[half:]], 1).astype(BF)
            else:
                wide[...] = parts[h]
                last_ref[...] = jnp.concatenate([parts[h][:, 64:], own_v], 1).astype(BF)
    for to in range(blocks):
        pieces = [
            wide[k * rows + to * stripe : k * rows + (to + 1) * stripe, :64] for k in range(groups)
        ]
        out_ref[to, count + half :] = jnp.concatenate(
            [jnp.concatenate(pieces[:2], 0), jnp.concatenate(pieces[2:], 0)], 1
        ).astype(BF)


def pick_piece(x, k):
    y = jnp.where((k & 1) != 0, x[8:], x[:8])
    return jnp.where(k >= 2, y[:, 64:], y[:, :64])


def project_back_small_body(blocks, heads, place_ref, c_ref, shift_ref, w_ref, *refs):
    wide, scattered = refs[-2:]
    few = blocks // 2
    groups = (len(refs) - few - 7) // 2
    tokens, in_ref, lasts = refs[:groups], refs[groups], refs[groups + 1 : groups + 1 + few]
    outs = refs[groups + 1 + few : 2 * groups + 1 + few]
    keep_ref, send_ref, sum_ref, dot_ref = refs[2 * groups + 1 + few : -2]
    micro, rows, width = tokens[0].shape
    count = groups * rows
    half, stripe = count // 2, rows // blocks
    for j in range(blocks):
        x = in_ref[j, count + half :].astype(F32)
        pieces = [x[:8, :64], x[8:, :64], x[:8, 64:], x[8:, 64:]]
        for k in range(groups):
            wide[k * rows + j * stripe : k * rows + (j + 1) * stripe] = pieces[k]
    all_a, all_g = [], []
    for m in range(micro):
        n = jnp.concatenate([x[m] for x in tokens], 0).astype(F32)
        a = (n * c_ref[m][None] + shift_ref[m][None]).astype(BF)
        qk, v = [], []
        for h in range(heads):
            pair = m * heads + h
            if pair < blocks:
                qk.append(in_ref[pair, :count])
                x = in_ref[pair, count : count + half]
                v.append(jnp.concatenate([x[:, :64], x[:, 64:]], 0))
            else:
                x = sum(ref[...].astype(F32) for ref in lasts).astype(BF)
                qk.append(jnp.concatenate([wide[...].astype(BF), x[:, :64]], 1))
                v.append(x[:, 64:])
        g = jnp.concatenate(qk + v, 1)
        da = lax.dot_general(g, w_ref[:, : 192 * heads], NT, preferred_element_type=F32)
        for k in range(groups):
            outs[k][m] = da[k * rows : (k + 1) * rows].astype(BF)
        sum_ref[m : m + 1] = jnp.sum(da, 0, keepdims=True)
        dot_ref[m : m + 1] = jnp.sum(da * n, 0, keepdims=True)
        all_a.append(a)
        all_g.append(g)
    x = lax.dot_general(
        jnp.concatenate(all_a, 0), jnp.concatenate(all_g, 0), TN, preferred_element_type=F32
    )
    scattered[...] = x.reshape(scattered.shape)
    mine = place_ref[1] & 1
    for z in range(few):
        for k in range(groups):
            at = k * blocks + 2 * z
            keep_ref[z, k] = scattered[at + mine].astype(BF)
            send_ref[z, k] = scattered[at + 1 - mine].astype(BF)


def attend_block(scores, q, low, high, first, stop, keys, values):
    count = q.shape[0]

    def score(t, top):
        at = pl.multiple_of((first + 2 * t) * STEP, STEP)
        s = lax.dot_general(keys[pl.ds(at, KB), :], q, NT, preferred_element_type=F32)
        s = jnp.where(keys_mask(low, high, at, KB), s, NEG)
        scores[t, :, :count] = s
        return jnp.maximum(top, jnp.max(s, 0, keepdims=True))

    steps = (stop - first + 1) // 2
    top = lax.fori_loop(0, steps, score, jnp.full((1, count), NEG, F32))

    def weigh(t, carry):
        total, acc = carry
        at = pl.multiple_of((first + 2 * t) * STEP, STEP)
        p = jnp.exp(scores[t, :, :count] - top)
        return total + jnp.sum(p, 0, keepdims=True), acc + lax.dot_general(
            values[pl.ds(at, KB), :], p.astype(BF), TN, preferred_element_type=F32
        )

    total, acc = lax.fori_loop(
        0, steps, weigh, (jnp.zeros((1, count), F32), jnp.zeros((64, count), F32))
    )
    return (acc / total).T, top + jnp.log(total)


def attend_own_body(
    blocks, groups, rows, place_ref, range_ref, low_ref, high_ref, cos_ref, sin_ref, *refs
):
    in_ref, message, q_ref, k_ref, v_ref, o_ref, lse_ref, kept, kept_v, scores = refs
    span = blocks * rows
    size = groups * span
    count = groups * rows
    half = rows // 2
    me_u, me_b = place_ref[0], place_ref[1]
    for g in range(groups):
        k = me_u ^ g
        for j in range(blocks):
            to = slice(j * rows, (j + 1) * rows)
            kept[to, :] = in_ref[j, pl.ds(pl.multiple_of(k * rows, rows), rows), :]
            pair = in_ref[j, pl.ds(pl.multiple_of(count + (k & 1) * rows, rows), rows), :].astype(F32)
            kept_v[to, :] = jnp.where(k >= 2, pair[:, 64:], pair[:, :64]).astype(BF)
        at = slice(g * span, (g + 1) * span)
        x = turn(kept[...].astype(F32), turn_tables(cos_ref[at], sin_ref[at], False)[0])
        q_ref[at] = (x[:, :64] * 0.125).astype(BF)
        k_ref[at] = x[:, 64:].astype(BF)
        v_ref[at] = kept_v[...]
    tail = slice(size, size + KB - STEP)
    for ref in (k_ref, v_ref):
        ref[tail] = jnp.zeros((KB - STEP, 64), BF)

    def run(i, _):
        o, lse = attend_block(
            scores, spread(q_ref, i * QB, QB), low_ref[i], high_ref[i],
            range_ref[2 * i], range_ref[2 * i + 1], k_ref, v_ref,
        )
        o = o.astype(BF)
        o_ref[pl.ds(pl.multiple_of(i * QB, QB), QB), :] = o
        lse_ref[i] = lse
        for d in range(QB // rows):
            message[i * (QB // rows) + d] = jnp.concatenate(
                [o[d * rows : d * rows + half], o[d * rows + half : (d + 1) * rows]], 1
            )
        return 0

    lax.fori_loop(0, size // QB, run, 0)


def stripe_tables(place_ref, cos_ref, sin_ref, wide_cos, wide_sin, devices, rows, stripe):
    for d in range(devices):
        at = slice(d * stripe, (d + 1) * stripe)
        wide_cos[at] = spread(cos_ref, d * rows + place_ref[1] * stripe, stripe)
        wide_sin[at] = spread(sin_ref, d * rows + place_ref[1] * stripe, stripe)
    return turn_tables(wide_cos[...], wide_sin[...], True)[1]


def attend_last_body(
    blocks, groups, rows, stripe, place_ref, range_ref, low_ref, high_ref, cos_ref, sin_ref, *refs
):
    in_ref, last_ins, own_ref = refs[0], refs[1:3], refs[3]
    message, q_ref, k_ref, v_ref, o_ref, lse_ref, kept, wide, wide_cos, wide_sin, scores = refs[4:]
    span = blocks * rows
    size = groups * span
    devices = groups * blocks
    count = groups * rows
    half = rows // 2
    me_u, me_b = place_ref[0], place_ref[1]
    for g in range(groups):
        k = me_u ^ g
        for j in range(blocks):
            at = (g * blocks + j) * stripe
            wide[at : at + stripe, :64] = pick_piece(in_ref[j, count + count // 2 :].astype(F32), k)
            to = pl.ds(pl.multiple_of((me_b ^ j) * rows, rows), rows)
            kept[to, :] = last_ins[j & 1][j >> 1, pl.ds(pl.multiple_of(k * rows, rows), rows), :]
        at = slice(g * span, (g + 1) * span)
        x = turn(kept[...].astype(F32), turn_tables(cos_ref[at], sin_ref[at], True)[1])
        k_ref[at] = x[:, :64].astype(BF)
        v_ref[at] = kept[:, 64:]
    tail = slice(size, size + KB - STEP)
    for ref in (k_ref, v_ref):
        ref[tail] = jnp.zeros((KB - STEP, 64), BF)
    wide[:, 64:] = jnp.zeros((devices * stripe, 64), F32)
    x = turn(wide[...], stripe_tables(place_ref, cos_ref, sin_ref, wide_cos, wide_sin, devices, rows, stripe))
    q_ref[...] = (x[:, :64] * 0.125).astype(BF)
    message[:, :half] = own_ref[...]
    few = lse_ref.shape[2]

    def run(i, _):
        o, lse = attend_block(
            scores, spread(q_ref, i * few, few), low_ref[i], high_ref[i],
            range_ref[2 * i], range_ref[2 * i + 1], k_ref, v_ref,
        )
        o_ref[pl.ds(pl.multiple_of(i * few, few), few), :] = o.astype(BF)
        lse_ref[i] = lse
        o = jnp.concatenate([o, jnp.zeros_like(o)], 1)
        for d in range(few // stripe):
            message[i * (few // stripe) + d, half:] = o[d * stripe : (d + 1) * stripe].astype(BF)
        return 0

    lax.fori_loop(0, lse_ref.shape[0], run, 0)


def attend_block_back(q, do, o, lse, low, high, first, stop, keys, values, dk_sum, dv_sum):
    count = q.shape[0]
    delta = jnp.sum((do.astype(F32) * o.astype(F32)).T, 0, keepdims=True)

    def step(t, dq):
        at = pl.multiple_of((first + 2 * t) * STEP, STEP)
        here = pl.ds(at, KB)
        k, v = keys[here, :], values[here, :]
        s = lax.dot_general(k, q, NT, preferred_element_type=F32)
        dp = lax.dot_general(v, do, NT, preferred_element_type=F32)
        p = jnp.where(keys_mask(low, high, at, KB), jnp.exp(s - lse), 0.0)
        ds = (p * (dp - delta)).astype(BF)
        dv_sum[here, :] += jnp.dot(p.astype(BF), do, preferred_element_type=F32)
        dk_sum[here, :] += jnp.dot(ds, q, preferred_element_type=F32)
        return dq + lax.dot_general(k, ds, TN, preferred_element_type=F32)

    return (
        lax.fori_loop(0, (stop - first + 1) // 2, step, jnp.zeros((64, count), F32)) * 0.125
    ).T


def attend_last_back_body(
    blocks, groups, rows, stripe, place_ref, range_ref, low_ref, high_ref, cos_ref, sin_ref,
    do_ref, q_ref, k_ref, v_ref, o_ref, lse_ref, dq_ref, keep_ref, send_ref, kept, wide_cos, wide_sin, dk, dv,
):
    span = blocks * rows
    devices = groups * blocks
    half = rows // 2
    for ref in (dk, dv):
        ref[...] = jnp.zeros(ref.shape, F32)
    few = lse_ref.shape[2]
    dq_ref[:, 64:] = jnp.zeros((devices * stripe, 64), F32)

    def run(i, _):
        came = [
            do_ref[i * (few // stripe) + d].astype(F32)[half:, :64] for d in range(few // stripe)
        ]
        at = pl.ds(pl.multiple_of(i * few, few), few)
        dq_ref[at, :64] = attend_block_back(
            q_ref[at, :], jnp.concatenate(came, 0).astype(BF), o_ref[at, :], lse_ref[i],
            low_ref[i], high_ref[i], range_ref[2 * i], range_ref[2 * i + 1], k_ref, v_ref, dk, dv,
        )
        return 0

    lax.fori_loop(0, lse_ref.shape[0], run, 0)
    cos, sin = stripe_tables(place_ref, cos_ref, sin_ref, wide_cos, wide_sin, devices, rows, stripe)
    dq_ref[...] = turn(dq_ref[...], (cos, -sin))
    for g in range(groups):
        at = slice(g * span, (g + 1) * span)
        k = place_ref[0] ^ g
        cos, sin = turn_tables(cos_ref[at], sin_ref[at], True)[1]
        x = turn(jnp.concatenate([dk[at], jnp.zeros_like(dk[at])], 1), (cos, -sin))[:, :64]
        kept[...] = jnp.concatenate([x, dv[at]], 1).astype(BF)
        to = pl.ds(pl.multiple_of(k * rows, rows), rows)
        for z in range(blocks // 2):
            mine = 2 * z + (place_ref[1] & 1)
            keep_ref[z, to, :] = spread(kept, mine * rows, rows)
            send_ref[z, to, :] = spread(kept, (mine ^ 1) * rows, rows)


def attend_own_back_body(
    blocks, groups, rows, stripe, place_ref, range_ref, low_ref, high_ref, cos_ref, sin_ref,
    do_ref, q_ref, k_ref, v_ref, o_ref, lse_ref, last_dq_ref, out_ref, kept, kept_v, wide_v, dq, dk, dv,
):
    span = blocks * rows
    size = groups * span
    count = groups * rows
    half = rows // 2
    me_u, me_b = place_ref[0], place_ref[1]
    for ref in (dk, dv):
        ref[...] = jnp.zeros(ref.shape, F32)

    def run(i, _):
        came = []
        for d in range(QB // rows):
            x = do_ref[i * (QB // rows) + d]
            came += [x[:half, :64], x[:half, 64:]]
        at = pl.ds(pl.multiple_of(i * QB, QB), QB)
        dq[at, :] = attend_block_back(
            q_ref[at, :], jnp.concatenate(came, 0), o_ref[at, :], lse_ref[i], low_ref[i], high_ref[i],
            range_ref[2 * i], range_ref[2 * i + 1], k_ref, v_ref, dk, dv,
        )
        return 0

    lax.fori_loop(0, size // QB, run, 0)
    for g in range(groups):
        at = slice(g * span, (g + 1) * span)
        k = me_u ^ g
        cos, sin = turn_tables(cos_ref[at], sin_ref[at], False)[0]
        kept[...] = turn(jnp.concatenate([dq[at], dk[at]], 1), (cos, -sin)).astype(BF)
        kept_v[...] = dv[at].astype(BF)
        for b in range(blocks):
            out_ref[b, pl.ds(pl.multiple_of(k * rows, rows), rows), :] = kept[b * rows : (b + 1) * rows]
        for b in range(blocks):
            wide_v[g * blocks + b] = kept_v[b * rows : (b + 1) * rows]
    for to in range(blocks):
        v = [wide_v[(me_u ^ k) * blocks + to] for k in range(groups)]
        out_ref[to, count : count + count // 2] = jnp.concatenate(
            [jnp.concatenate(v[:2], 0), jnp.concatenate(v[2:], 0)], 1
        )
        z = [spread(last_dq_ref, ((me_u ^ k) * blocks + to) * stripe, stripe)[:, :64] for k in range(groups)]
        out_ref[to, count + count // 2 :] = jnp.concatenate(
            [jnp.concatenate(z[:2], 0), jnp.concatenate(z[2:], 0)], 1
        ).astype(BF)


def on_device(
    tokens,
    cotangent,
    lengths,
    time_step,
    modulate_weight,
    modulate_bias,
    attend_gain,
    input_weight,
    output_weight,
    feed_gain,
    expand_weight,
    expand_bias,
    reduce_weight,
    reduce_bias,
):
    groups, blocks = lax.axis_size("ulysses"), lax.axis_size("blk")
    group_id, block_id = lax.axis_index("ulysses"), lax.axis_index("blk")
    devices = groups * blocks
    micro, rows, width = tokens.shape
    own = micro * rows
    size = devices * rows
    head_width = width // HEADS
    heads = HEADS // groups
    pairs = micro * heads
    extra = pairs > blocks
    lanes = 384 if extra else 256
    stripe = rows // blocks if extra else 0
    mod_rows = modulate_weight.shape[0]
    gain_rows = attend_gain.shape[0]
    ff_rows = expand_bias.shape[0]
    ff = ff_rows * devices
    folds = ff // width
    assert pairs <= blocks + 1 and head_width == 64 and folds == groups and heads == 3
    place = jnp.stack([group_id, block_id]).astype(jnp.int32)
    pair_micro = jnp.minimum(block_id // heads, micro - 1)

    in_split = input_weight.reshape(gain_rows, 3, groups, heads, head_width)
    in_split = jnp.concatenate(
        [
            in_split[:, :2].transpose(2, 0, 3, 1, 4).reshape(groups, 1, gain_rows, -1),
            in_split[:, 2].transpose(1, 0, 2, 3).reshape(groups, 1, gain_rows, -1),
        ],
        3,
    )
    in_lanes = heads * 3 * head_width

    condition = time_features(time_step, modulate_weight.shape[1] // 2)
    mod_own = jnp.einsum(
        "mc,fc->mf", condition, modulate_weight, preferred_element_type=F32
    ) + modulate_bias.astype(F32)
    mod_lanes = 64 * -(-mod_rows // 64)
    mod_own = jnp.pad(mod_own, ((0, 0), (0, mod_lanes - mod_rows))).reshape(-1, 64)
    mod_high = lax.reduce_precision(mod_own, 8, 7)
    mod_size = mod_own.shape[0]
    vectors = jnp.pad(
        jnp.stack([attend_gain, feed_gain, reduce_bias]), ((0, 0), (0, 64 - gain_rows))
    )
    ff_lanes = 64 * -(-ff_rows // 64)
    small = jnp.concatenate(
        [
            mod_high.astype(BF),
            (mod_own - mod_high).astype(BF),
            vectors,
            jnp.pad(expand_bias, (0, ff_lanes - ff_rows)).reshape(-1, 64),
        ],
        0,
    )
    small_lanes = 64 * -(-small.shape[0] // gain_rows)
    small = jnp.pad(small, ((0, small_lanes * gain_rows // 64 - small.shape[0]), (0, 0)))
    small = small.reshape(1, 1, gain_rows, small_lanes)
    in_message = jnp.concatenate(
        [
            jnp.broadcast_to(in_split, (groups, blocks) + in_split.shape[2:]),
            jnp.broadcast_to(small, (groups, blocks) + small.shape[2:]),
        ],
        3,
    ).reshape(devices, gain_rows, in_lanes + small_lanes)
    in_message, tokens, lengths = lax.optimization_barrier((in_message, tokens, lengths))
    came = exchange(in_message)
    values = tokens.astype(F32)
    n1, r1 = norm(values)
    n1_b = n1.astype(BF)
    n1_group = swap([n1_b] * groups, "ulysses")
    small_all = came[:, :, in_lanes:].reshape(devices, -1, 64)
    in_own = came.reshape(width, in_lanes + small_lanes)

    weight_pack = jnp.concatenate(
            [
                reduce_weight,
                output_weight,
                expand_weight.reshape(gain_rows, folds, width).transpose(1, 0, 2).reshape(-1, width),
            ],
            0,
        )
    index = jnp.arange(size, dtype=jnp.int32)
    pair_lengths = lax.dynamic_index_in_dim(lengths, pair_micro, 0, keepdims=False)
    segment, position = doc_layout(index, pair_lengths)
    last_lengths = lengths[micro - 1]
    last_segment, last_position = doc_layout(index, last_lengths)
    half = head_width // 2
    freqs = jnp.exp(-math.log(10000.0) * jnp.arange(half, dtype=F32) / half)
    lane = jnp.arange(128)
    angles = jnp.where(
        (lane < 64)[None, :], position.astype(F32)[:, None], last_position.astype(F32)[:, None]
    ) * jnp.tile(freqs, 4)[None, :]
    cos_table = jnp.cos(angles)
    sin_table = jnp.where((lane % 64 < 32)[None, :], -1.0, 1.0) * jnp.sin(angles)
    query_rows = math.gcd(size, QB)
    key_block = math.gcd(size, 256)
    first = jnp.arange(size // query_rows, dtype=jnp.int32) * query_rows
    ranges = key_ranges(first, first + query_rows - 1, pair_lengths, key_block)
    small_path = extra and size % KB == 0 and rows == 64 and stripe == 8 and groups == 4 and size <= 4096

    striped = lambda x: lax.dynamic_slice_in_dim(
        x.reshape((devices, rows) + x.shape[1:]), block_id * stripe, stripe, 1
    ).reshape((devices * stripe,) + x.shape[1:])
    last_ranges = bounds = 0
    if small_path:
        last_rows = min(256, devices * stripe)
        chunk = last_rows // stripe
        last_first = jnp.arange(devices // chunk, dtype=jnp.int32) * (chunk * rows) + block_id * stripe
        last_ranges = key_ranges(
            last_first, last_first + (chunk - 1) * rows + stripe - 1, last_lengths, STEP
        )
        bounds = []
        for where, lens, pick, lump in (
            (position, pair_lengths, lambda x: x, QB),
            (last_position, last_lengths, striped, last_rows),
        ):
            low = index - where
            ends = jnp.cumsum(lens)
            high = jnp.min(jnp.where(ends[None, :] > index[:, None], ends[None, :], 1 << 30), 1)
            bounds += [pick(low).reshape(-1, 1, lump), pick(high).reshape(-1, 1, lump)]
    in_own, small_all, n1_group, place, cos_table, sin_table, ranges, last_ranges, bounds = (
        lax.optimization_barrier(
            (in_own, small_all, n1_group, place, cos_table, sin_table, ranges, last_ranges, bounds)
        )
    )
    weight_pack, in_own = lax.optimization_barrier((weight_pack, in_own))
    gathered = lax.all_gather(weight_pack, ALL, axis=0, tiled=False)
    unit = gain_rows
    while unit % 8:
        unit *= 2
    units = width // unit
    if unit != gain_rows:
        gathered = jnp.concatenate(
            [gathered[:, :ff_rows].reshape(units, -1, width)]
            + [
                gathered[:, at : at + gain_rows].reshape(units, unit, width)
                for at in range(ff_rows, ff_rows + (folds + 1) * gain_rows, gain_rows)
            ],
            1,
        )
    wide = unit * folds

    mods = small_all[:, :mod_size].astype(F32) + small_all[:, mod_size : 2 * mod_size].astype(F32)
    mods = mods.reshape(devices, micro, mod_lanes)[:, :, :mod_rows].transpose(1, 0, 2).reshape(micro, -1)
    at = 2 * mod_size
    vectors = small_all[:, at : at + 3, :gain_rows].astype(F32).transpose(1, 0, 2).reshape(3, width)
    gain1, gain2, reduce_bias_f = vectors[0], vectors[1], vectors[2:]
    at += 3
    expand_bias_f = small_all[:, at : at + ff_lanes // 64].reshape(devices, ff_lanes)[:, :ff_rows]
    expand_bias_f = expand_bias_f.astype(F32).reshape(folds, 1, width)
    shift1, scale1, gate1, shift2, scale2, gate2 = jnp.split(mods, 6, 1)
    c1 = gain1 * (1.0 + scale1)
    c2 = gain2 * (1.0 + scale2)

    count = groups * rows
    smem = pl.BlockSpec(memory_space=pltpu.SMEM)
    message_rows = count + count // 2 + 16
    if small_path:
        outgoing, last_own = pl.pallas_call(
            functools.partial(project_small_body, blocks, heads),
            out_shape=[
                jax.ShapeDtypeStruct((blocks, message_rows, 128), BF), jax.ShapeDtypeStruct((count, 128), BF),
            ],
            in_specs=[whole_vmem()] * (3 + groups),
            out_specs=[whole_vmem()] * 2,
            scratch_shapes=[pltpu.VMEM((count, 128), F32)],
            cost_estimate=pl.CostEstimate(
                flops=2 * micro * count * width * 3 * 64 * heads, transcendentals=0, bytes_accessed=8 * own * width
            ),
            name="project",
        )(c1, shift1, in_own, *n1_group)
        incoming = [lax.all_to_all(outgoing, "blk", split_axis=0, concat_axis=0, tiled=True)]
        pass_on = lambda x, bit: lax.ppermute(x, "blk", [(i, i ^ bit) for i in range(blocks)])
        last_four = jnp.stack([last_own] + [pass_on(last_own, bit) for bit in range(2, blocks, 2)])
        last_keys = [last_four, pass_on(last_four, 1)]
    else:
        outgoing = pl.pallas_call(
            functools.partial(project_body, blocks, pairs, heads, extra),
            out_shape=[jax.ShapeDtypeStruct((count, lanes), BF)] * blocks,
            in_specs=[smem] + [whole_vmem()] * (3 + groups),
            out_specs=[whole_vmem()] * blocks,
            scratch_shapes=[pltpu.VMEM((blocks, count, lanes), BF)],
            name="project",
        )(place, c1, shift1, in_own, *n1_group)
        incoming = swap(outgoing, "blk")

    span = blocks * rows
    by_span = pl.BlockSpec((span, 64), lambda i, p: (i ^ p[0], 0))
    table_spec = pl.BlockSpec((span, 128), lambda i, p: (i ^ p[0], 0))
    by_rows = pl.BlockSpec((rows, lanes), lambda i, p: (i, 0))
    parts = 6 if extra else 3
    if small_path:
        whole = lambda *shape: jax.ShapeDtypeStruct(shape, BF)
        f32 = lambda *shape: jax.ShapeDtypeStruct(shape, F32)
        padded = whole(size + KB - STEP, 64)
        own_args = (place, ranges, *bounds[:2], cos_table, sin_table)
        last_args = (place, last_ranges, *bounds[2:], cos_table, sin_table)
        specs = [smem] * 2 + [whole_vmem()] * 4
        own_message, *own_saved = pl.pallas_call(
            functools.partial(attend_own_body, blocks, groups, rows),
            in_specs=specs + [whole_vmem()],
            out_specs=[whole_vmem()] * 6,
            out_shape=[
                whole(devices, rows // 2, 128), whole(size, 64), padded, padded, whole(size, 64), f32(*bounds[0].shape),
            ],
            scratch_shapes=[
                pltpu.VMEM((span, 128), BF), pltpu.VMEM((span, 64), BF),
                pltpu.VMEM((size // KB + 1, KB, QB), F32),
            ],
            cost_estimate=pl.CostEstimate(
                flops=size * size * 64, transcendentals=size * size // 2, bytes_accessed=16 * size * 128
            ),
            name="attend_own",
        )(*own_args, *incoming)
        message, *last_saved = pl.pallas_call(
            functools.partial(attend_last_body, blocks, groups, rows, stripe),
            in_specs=specs + [whole_vmem()] * 4,
            out_specs=[whole_vmem()] * 6,
            out_shape=[
                whole(devices, rows // 2 + stripe, 128), whole(devices * stripe, 64), padded, padded,
                whole(devices * stripe, 64), f32(*bounds[2].shape),
            ],
            scratch_shapes=[pltpu.VMEM((span, 128), BF)]
            + [pltpu.VMEM((devices * stripe, 128), F32)] * 3
            + [pltpu.VMEM((size // KB + 1, KB, last_rows), F32)],
            cost_estimate=pl.CostEstimate(
                flops=size * size * 16, transcendentals=size * size // 8, bytes_accessed=16 * size * 64
            ),
            name="attend_last",
        )(*last_args, *incoming, *last_keys, own_message)
    else:
        assert not extra
        turned = pl.pallas_call(
            functools.partial(rotate_in_body, blocks, extra),
            grid_spec=pltpu.PrefetchScalarGridSpec(
                num_scalar_prefetch=1,
                grid=(groups,),
                in_specs=[table_spec, table_spec] + [by_rows] * blocks,
                out_specs=[by_span] * parts,
                scratch_shapes=[pltpu.VMEM((span, lanes), BF)],
            ),
            out_shape=[jax.ShapeDtypeStruct((size, 64), BF)] * parts,
            name="rotate_in",
        )(place, cos_table, sin_table, *incoming)
        query, key, value = turned[:3]
        attended, lse = attend(
            ranges, query, segment, key, value, segment[:, None], query_rows, key_block
        )
        message = attended.reshape(devices, rows, head_width)
    came = exchange(message)

    ex_spec = lambda f: pl.BlockSpec((units, unit, width), f)
    flat = pl.BlockSpec((own, width), lambda i: (0, 0))
    vec = lambda n: pl.BlockSpec((n, width), lambda i: (0, 0))
    message_shape = message.shape
    message_spec = pl.BlockSpec(message_shape, lambda i: (0, 0, 0))
    sizes = (groups, blocks, heads, micro, rows, stripe)
    own_f32 = jax.ShapeDtypeStruct((own, width), F32)
    own_bf = jax.ShapeDtypeStruct((own, width), BF)
    merged, attn, middle, second = pl.pallas_call(
        functools.partial(middle_body, *sizes),
        grid=(1,),
        in_specs=[message_spec, ex_spec(lambda i: (0, folds, 0)), flat, vec(micro), vec(micro), vec(micro)],
        out_specs=[flat] * 4,
        out_shape=[own_bf, own_f32, own_f32, own_bf],
        name="middle",
    )(came, gathered, tokens.reshape(own, width), gate1, c2, shift2)
    second_group = swap([second] * groups, "ulysses")
    dy = cotangent.reshape(own, width)
    dy_group = swap([dy] * groups, "ulysses")

    per = width // wide
    layer_output, grad_middle, grad_attn, do_message, sums = pl.pallas_call(
        functools.partial(feed_body, *sizes),
        grid=(folds,),
        in_specs=[
            ex_spec(lambda i: (0, folds + 1 + i, 0)),
            pl.BlockSpec((per, wide, width), lambda i: (i, 0, 0)),
            ex_spec(lambda i: (0, folds, 0)),
            pl.BlockSpec((1, 1, width), lambda i: (i, 0, 0)),
            vec(1),
            flat, flat, flat, flat,
            vec(micro), vec(micro), vec(micro),
        ],
        out_specs=[flat, flat, flat, message_spec, vec(5 * micro)],
        out_shape=[
            own_bf, own_f32, own_bf,
            jax.ShapeDtypeStruct(message_shape, BF),
            jax.ShapeDtypeStruct((5 * micro, width), F32),
        ],
        scratch_shapes=[
            pltpu.VMEM((own, width), F32), pltpu.VMEM((own, width), F32),
            pltpu.VMEM((own, width), BF), pltpu.VMEM((own, width), BF),
        ],
        cost_estimate=pl.CostEstimate(
            flops=8 * own * width * ff, transcendentals=own * ff, bytes_accessed=4 * width * ff
        ),
        name="feed",
    )(gathered, gathered, gathered, expand_bias_f, reduce_bias_f, second, middle, attn, dy, gate1, gate2, c2)
    do_came = exchange(do_message)
    d_gate2, d_shift2, p2, d_gate1, dm_sums = [
        sums[i * micro : (i + 1) * micro] for i in range(5)
    ]

    flat_p = pl.BlockSpec((own, width), lambda i, p: (0, 0))
    feed_part, bias_part = pl.pallas_call(
        functools.partial(feed_weights_body, rows, blocks),
        grid_spec=pltpu.PrefetchScalarGridSpec(
            num_scalar_prefetch=1,
            grid=(1,),
            in_specs=[
                pl.BlockSpec((units, unit, width), lambda i, p: (0, folds + 1 + p[0], 0)),
                pl.BlockSpec((per, wide, width), lambda i, p: (p[0], 0, 0)),
                pl.BlockSpec((1, 1, width), lambda i, p: (p[0], 0, 0)),
                pl.BlockSpec((micro, width), lambda i, p: (0, 0)),
            ]
            + [flat_p] * (2 * groups),
            out_specs=[
                pl.BlockSpec((blocks, ff_rows + groups * gain_rows, width), lambda i, p: (0, 0, 0)),
                pl.BlockSpec((1, width), lambda i, p: (0, 0)),
            ],
        ),
        out_shape=[
            jax.ShapeDtypeStruct((blocks, ff_rows + groups * gain_rows, width), BF),
            jax.ShapeDtypeStruct((1, width), F32),
        ],
        cost_estimate=pl.CostEstimate(
            flops=10 * own * groups * width * width, transcendentals=own * ff, bytes_accessed=16 * width * width
        ),
        name="feed_weights",
    )(place, gathered, gathered, expand_bias_f, gate2, *second_group, *dy_group)
    do_came, feed_part = lax.optimization_barrier((do_came, feed_part))
    feed_sum = lax.psum_scatter(feed_part, "blk", scatter_dimension=0, tiled=True)[0]

    if small_path:
        last_dq, last_kept, last_sent = pl.pallas_call(
            functools.partial(attend_last_back_body, blocks, groups, rows, stripe),
            in_specs=specs + [whole_vmem()] * 6,
            out_specs=[whole_vmem()] * 3,
            out_shape=[f32(devices * stripe, 128)] + [whole(blocks // 2, count, 128)] * 2,
            scratch_shapes=[pltpu.VMEM((span, 128), BF)]
            + [pltpu.VMEM((devices * stripe, 128), F32)] * 2
            + [pltpu.VMEM((size + KB - STEP, 64), F32)] * 2,
            cost_estimate=pl.CostEstimate(
                flops=size * size * 32, transcendentals=size * size // 8, bytes_accessed=16 * size * 64
            ),
            name="attend_last_back",
        )(*last_args, do_came, *last_saved)
        last_half = (last_kept.astype(F32) + pass_on(last_sent, 1).astype(F32)).astype(BF)
        do_came, last_dq = lax.optimization_barrier((do_came, last_dq))
        leaving = pl.pallas_call(
            functools.partial(attend_own_back_body, blocks, groups, rows, stripe),
            in_specs=specs + [whole_vmem()] * 7,
            out_specs=whole_vmem(),
            out_shape=whole(blocks, message_rows, 128),
            scratch_shapes=[
                pltpu.VMEM((span, 128), BF), pltpu.VMEM((span, 64), BF),
                pltpu.VMEM((devices, rows, 64), BF), pltpu.VMEM((size, 64), F32),
            ]
            + [pltpu.VMEM((size + KB - STEP, 64), F32)] * 2,
            cost_estimate=pl.CostEstimate(
                flops=2 * size * size * 64, transcendentals=size * size // 2, bytes_accessed=16 * size * 128
            ),
            name="attend_own_back",
        )(*own_args, do_came, *own_saved, last_dq)
    else:
        grads = attend_back(
            ranges, query, segment, lse, attended, do_came.reshape(size, head_width), key, value,
            segment[:, None], query_rows, key_block,
        )
        leaving = pl.pallas_call(
            functools.partial(rotate_out_body, blocks, extra),
            grid_spec=pltpu.PrefetchScalarGridSpec(
                num_scalar_prefetch=1,
                grid=(groups,),
                in_specs=[table_spec, table_spec] + [by_span] * parts,
                out_specs=[by_rows] * blocks,
                scratch_shapes=[pltpu.VMEM((span, lanes), BF)],
            ),
            out_shape=[jax.ShapeDtypeStruct((count, lanes), BF)] * blocks,
            name="rotate_out",
        )(place, cos_table, sin_table, *grads)
    if small_path:
        leaving, last_half = lax.optimization_barrier((leaving, last_half))
        back = [lax.all_to_all(leaving, "blk", split_axis=0, concat_axis=0, tiled=True)]
        back += [
            pass_on(lax.dynamic_index_in_dim(last_half, (block_id // 2) ^ k, 0, keepdims=False), 2 * k)
            if k
            else lax.dynamic_index_in_dim(last_half, block_id // 2, 0, keepdims=False)
            for k in range(blocks // 2)
        ]
    else:
        back = swap(leaving, "blk")
    leaving, merged, grad_attn = lax.optimization_barrier((leaving, merged, grad_attn))
    output_part = lax.dot_general(merged, grad_attn, TN, preferred_element_type=F32).astype(BF)
    output_part = output_part.reshape(groups, width // groups, width)

    output_part = swap(
        [
            lax.dynamic_index_in_dim(output_part, group_id ^ k, 0, keepdims=False)
            for k in range(groups)
        ],
        "ulysses",
    )

    output_part = sum(x.astype(F32) for x in output_part).astype(BF).reshape(blocks, gain_rows, width)

    if small_path:
        back_body = functools.partial(project_back_small_body, blocks, heads)
        back_scratch = [
            pltpu.VMEM((count, 64), F32), pltpu.VMEM((devices, gain_rows, heads * 3 * head_width), F32),
        ]
        back_args, back_specs = (place,), [smem]
        back_grads = [jax.ShapeDtypeStruct((blocks // 2, groups, gain_rows, heads * 3 * head_width), BF)] * 2
    else:
        back_args, back_specs = (place,), [smem]
        back_body = functools.partial(project_back_body, blocks, pairs, heads, extra)
        back_scratch = [pltpu.VMEM((blocks, count, lanes), BF)]
        back_grads = [jax.ShapeDtypeStruct((width, heads * 3 * head_width), BF)]
    returned = pl.pallas_call(
        back_body,
        out_shape=[jax.ShapeDtypeStruct((micro, rows, width), BF)] * groups
        + back_grads
        + [jax.ShapeDtypeStruct((micro, width), F32)] * 2,
        in_specs=back_specs + [whole_vmem()] * (3 + groups + len(back)),
        out_specs=[whole_vmem()] * (groups + 2 + len(back_grads)),
        scratch_shapes=back_scratch,
        cost_estimate=pl.CostEstimate(
            flops=4 * micro * count * width * 3 * 64 * heads, transcendentals=0, bytes_accessed=8 * own * width
        ),
        name="project_back",
    )(*back_args, c1, shift1, in_own, *n1_group, *back)
    *input_part, d_shift1, p1 = returned[groups:]
    grad_mods = jnp.concatenate(
        [d_shift1, p1 * gain1, d_gate1, d_shift2, p2 * gain2, d_gate2], 1
    )
    gain1_part = jnp.sum((1.0 + scale1) * p1, 0)
    gain2_part = jnp.sum((1.0 + scale2) * p2, 0)
    own_units = jnp.where(
        (jnp.arange(groups) == group_id)[:, None], bias_part.reshape(1, width), 0.0
    )
    small_parts = jnp.concatenate(
        [grad_mods.reshape(micro, devices, mod_rows).transpose(1, 0, 2).reshape(devices, -1)]
        + [
            x.reshape(devices, -1)
            for x in (gain1_part, gain2_part, jnp.sum(dm_sums, 0), own_units)
        ],
        1,
    ).astype(BF)
    taken = small_parts.shape[1]
    small_rows = 8 * -(-taken // (8 * in_lanes))
    small_parts = jnp.pad(small_parts, ((0, 0), (0, small_rows * in_lanes - taken)))
    if small_path:
        kept, sent = input_part
    else:
        halves = (
            input_part[0]
            .reshape(groups, blocks, gain_rows, in_lanes)
            .transpose(1, 0, 2, 3)
            .reshape(blocks // 2, 2, groups, gain_rows, in_lanes)
        )
        sent = lax.dynamic_index_in_dim(halves, 1 - block_id % 2, 1, keepdims=False)
        kept = lax.dynamic_index_in_dim(halves, block_id % 2, 1, keepdims=False)
    sent, token_parts = lax.optimization_barrier((sent, returned[:groups]))
    came = lax.ppermute(sent, "blk", [(i, i ^ 1) for i in range(blocks)])
    input_sum = (kept.astype(F32) + came.astype(F32)).astype(BF)
    token_parts = swap(token_parts, "ulysses")
    out_lanes = output_part.shape[1] * output_part.shape[2] // in_lanes
    rest = jnp.concatenate(
        [
            small_parts.reshape(groups, blocks, small_rows, in_lanes)
            .transpose(1, 0, 2, 3)
            .reshape(blocks, groups * small_rows, in_lanes),
            output_part.reshape(blocks, out_lanes, in_lanes),
        ],
        1,
    )
    rest = halve(rest, "blk", block_id, 1)
    input_sum, rest, feed_sum, token_parts = lax.optimization_barrier((input_sum, rest, feed_sum, token_parts))
    grad_first = sum(x.astype(F32) for x in token_parts)
    e = grad_first * c1[:, None]
    tokens_grad = (
        grad_middle.reshape(micro, rows, width)
        + r1
        * (
            e
            - jnp.mean(e, -1, keepdims=True)
            - n1 * jnp.mean(e * n1, -1, keepdims=True)
        )
    ).astype(BF)

    input_sum = jnp.concatenate(
        [input_sum.reshape(blocks // 2, groups * gain_rows, in_lanes), rest], 1
    )
    bit = 2
    while bit < blocks:
        input_sum = halve(input_sum, "blk", block_id, bit)
        if bit == 2:
            input_sum, feed_sum = lax.optimization_barrier((input_sum, feed_sum))
        bit *= 2
    input_sum = input_sum[0]
    at = groups * gain_rows
    small_sum = input_sum[at : at + groups * small_rows]
    output_grad = input_sum[at + groups * small_rows :].reshape(gain_rows, width).astype(F32)
    input_sum = jnp.concatenate(
        [input_sum[:at].reshape(groups, gain_rows, in_lanes), small_sum.reshape(groups, small_rows, in_lanes)], 1
    )
    final = jnp.stack(
        swap(
            [
                lax.dynamic_index_in_dim(input_sum, group_id ^ k, 0, keepdims=False)
                for k in range(groups)
            ],
            "ulysses",
        )
    )
    small_sum = jnp.sum(final[:, gain_rows:].astype(F32), 0).reshape(-1)
    input_sum = unscramble(final[:, :gain_rows], group_id, 0).astype(F32)
    reduce_grad = feed_sum[:ff_rows].astype(F32)
    expand_rows = feed_sum[ff_rows:].reshape(groups, gain_rows, width)
    expand_came = jnp.stack(
        swap(
            [
                lax.dynamic_index_in_dim(expand_rows, group_id ^ k, 0, keepdims=False)
                for k in range(groups)
            ],
            "ulysses",
        )
    )
    expand_grad = jnp.concatenate(
        [
            lax.dynamic_index_in_dim(expand_came, group_id ^ k, 0, keepdims=False)
            for k in range(groups)
        ],
        1,
    ).astype(F32)

    two = heads * 2 * head_width
    input_grad = jnp.concatenate(
        [
            input_sum[:, :, :two]
            .reshape(groups, gain_rows, heads, 2, head_width)
            .transpose(1, 3, 0, 2, 4)
            .reshape(gain_rows, 2 * width),
            input_sum[:, :, two:].transpose(1, 0, 2).reshape(gain_rows, width),
        ],
        1,
    )
    at = micro * mod_rows
    mod_sum = small_sum[:at].reshape(micro, mod_rows)
    modulate_weight_grad = jnp.sum(
        mod_sum[:, :, None] * condition.astype(F32)[:, None, :], 0
    )
    cuts = []
    for length in (gain_rows, gain_rows, gain_rows, ff_rows):
        cuts.append(small_sum[at : at + length])
        at += length
    return (
        layer_output.reshape(micro, rows, width),
        tokens_grad,
        modulate_weight_grad,
        jnp.sum(mod_sum, 0),
        cuts[0],
        input_grad,
        output_grad,
        cuts[1],
        expand_grad,
        cuts[3],
        reduce_grad,
        cuts[2],
    )


def solution(mesh):
    both = P(("ulysses", "blk"))
    tall = P(("ulysses", "blk"), None)
    seq = P(None, ("ulysses", "blk"), None)
    in_specs = (
        seq, seq, P(), P(), tall, both, both, tall, tall, both, tall, both, tall, both,
    )
    out_specs = (seq, seq, tall, both, both, tall, tall, both, tall, both, tall, both)
    return jax.shard_map(
        on_device, mesh=mesh, in_specs=in_specs, out_specs=out_specs, check_vma=False
    )
```

```python
import functools
import math

import jax
import jax.numpy as jnp
from jax import lax
from jax.experimental import pallas as pl
from jax.experimental.pallas import tpu as pltpu
from jax.sharding import PartitionSpec as P

HEADS = 12
BLK = ("far", "near")
ALL = ("ulysses", "far", "near")
BF = jnp.bfloat16
F32 = jnp.float32
NEG = -1e30


def axis_count(axis):
    return math.prod(lax.axis_size(name) for name in ((axis,) if isinstance(axis, str) else axis))


def exchange(x):
    return lax.all_to_all(x, ALL, split_axis=0, concat_axis=0, tiled=True)


def time_features(time_step, half):
    freqs = jnp.exp(-math.log(10000.0) * jnp.arange(half, dtype=F32) / half)
    angles = time_step.astype(F32)[:, None] * freqs[None, :]
    return jax.nn.silu(jnp.concatenate([jnp.cos(angles), jnp.sin(angles)], 1)).astype(BF)


def doc_layout(index, lengths_row):
    ends = jnp.cumsum(lengths_row)
    over = index[:, None] >= ends[None, :]
    segment = jnp.sum(over.astype(jnp.int32), 1)
    place = index - jnp.sum(jnp.where(over, lengths_row[None, :], 0), 1)
    return segment, place


def key_ranges(first, last, lengths_row, block):
    ends = jnp.cumsum(lengths_row)
    start = jnp.sum(jnp.where(first[:, None] >= ends[None, :], lengths_row[None, :], 0), 1)
    stop = jnp.min(jnp.where(ends[None, :] > last[:, None], ends[None, :], 1 << 30), 1)
    return jnp.stack([start // block, (stop + block - 1) // block], 1).reshape(-1)


def whole_vmem():
    return pl.BlockSpec(memory_space=pltpu.VMEM)


def swap(blocks, axis):
    size = axis_count(axis)
    return [
        x if k == 0 else lax.ppermute(x, axis, [(i, i ^ k) for i in range(size)])
        for k, x in enumerate(blocks)
    ]


def unscramble(x, index, axis):
    count, bit = x.shape[axis], 1
    while bit < count:
        shape = x.shape
        y = x.reshape(shape[:axis] + (count // (2 * bit), 2, bit) + shape[axis + 1 :])
        flipped = jnp.flip(y, axis + 1)
        x = jnp.where((index & bit) != 0, flipped, y).reshape(shape)
        bit *= 2
    return x


def halve(x, axis, index, bit):
    size = axis_count(axis)
    y = x.reshape((-1, 2) + x.shape[1:])
    mine = (index // bit) % 2
    sent = lax.dynamic_index_in_dim(y, 1 - mine, 1, keepdims=False)
    kept = lax.dynamic_index_in_dim(y, mine, 1, keepdims=False)
    came = lax.ppermute(sent, axis, [(i, i ^ bit) for i in range(size)])
    return (kept.astype(F32) + came.astype(F32)).astype(BF)


def project_body(blocks, pairs, heads, extra, place_ref, c_ref, shift_ref, w_ref, *refs):
    groups = len(refs) - blocks - 1
    tokens, outs, kept = refs[:groups], refs[groups:-1], refs[-1]
    micro, rows, width = tokens[0].shape
    end = 192 * heads
    weights = [w_ref[:, c : min(c + 128, end)] for c in range(0, end, 128)]
    order = list(range(micro))[::-1]
    z_qk = z_v = None
    for m in order:
        a = jnp.concatenate(
            [(x[m].astype(F32) * c_ref[m][None] + shift_ref[m][None]).astype(BF) for x in tokens], 0
        )
        parts = [jnp.dot(a, w, preferred_element_type=F32).astype(BF) for w in weights]
        v = jnp.concatenate(parts[heads:], 1)
        if extra and m == micro - 1:
            z_qk = parts[heads - 1]
            z_v = v[:, (heads - 1) * 64 : heads * 64]
        for h in range(heads):
            pair = m * heads + h
            if pair >= blocks:
                continue
            kept[pair, :, :128] = parts[h]
            own_v = v[:, h * 64 : (h + 1) * 64]
            if extra:
                kept[pair, :, 128:256] = z_qk
                kept[pair, :, 256:] = jnp.concatenate([own_v, z_v], 1)
            else:
                kept[pair, :, 128:] = jnp.concatenate([own_v, jnp.zeros_like(own_v)], 1)
    for pair in range(pairs, blocks):
        kept[pair] = jnp.zeros(kept.shape[1:], BF)
    for j in range(blocks):
        outs[j][...] = kept[place_ref[1] ^ j]


def turn_tables(cos, sin, extra):
    lane = lax.broadcasted_iota(jnp.int32, cos.shape, 1)
    low = lane < 64
    cos_r, sin_r = pltpu.roll(cos, 64, 1), pltpu.roll(sin, 64, 1)
    tables = [(jnp.where(low, cos, cos_r), jnp.where(low, sin, sin_r))]
    if extra:
        tables.append((jnp.where(low, cos_r, cos), jnp.where(low, sin_r, sin)))
    return tables


def turn(x, table):
    lane = lax.broadcasted_iota(jnp.int32, x.shape, 1)
    swapped = jnp.where(lane % 64 < 32, pltpu.roll(x, 96, 1), pltpu.roll(x, 32, 1))
    return x * table[0] + swapped * table[1]


def rotate_in_body(blocks, extra, place_ref, cos_ref, sin_ref, *refs):
    ins, outs = refs[:blocks], refs[blocks : 2 * blocks - blocks + (6 if extra else 3)]
    kept = refs[-1]
    rows = ins[0].shape[0]
    for j in range(blocks):
        at = pl.multiple_of((place_ref[1] ^ j) * rows, rows)
        kept[pl.ds(at, rows), :] = ins[j][...]
    tables = turn_tables(cos_ref[...], sin_ref[...], extra)
    x0 = turn(kept[:, :128].astype(F32), tables[0])
    outs[0][...] = (x0[:, :64] * 0.125).astype(BF)
    outs[1][...] = x0[:, 64:].astype(BF)
    if extra:
        outs[2][...] = kept[:, 256:320]
        x1 = turn(kept[:, 128:256].astype(F32), tables[1])
        outs[3][...] = (x1[:, :64] * 0.125).astype(BF)
        outs[4][...] = x1[:, 64:].astype(BF)
        outs[5][...] = kept[:, 320:]
    else:
        outs[2][...] = kept[:, 128:192]


def rotate_out_body(blocks, extra, place_ref, cos_ref, sin_ref, *refs):
    count = 6 if extra else 3
    ins, outs, kept = refs[:count], refs[count:-1], refs[-1]
    rows = outs[0].shape[0]
    parts = [ref[...].astype(F32) for ref in ins]
    tables = [(c, -s) for c, s in turn_tables(cos_ref[...], sin_ref[...], extra)]
    kept[:, :128] = turn(jnp.concatenate(parts[:2], 1), tables[0]).astype(BF)
    if extra:
        kept[:, 128:256] = turn(jnp.concatenate(parts[3:5], 1), tables[1]).astype(BF)
        kept[:, 256:] = jnp.concatenate([parts[2], parts[5]], 1).astype(BF)
    else:
        kept[:, 128:] = jnp.concatenate([parts[2], jnp.zeros_like(parts[2])], 1).astype(BF)
    for j in range(blocks):
        at = pl.multiple_of((place_ref[1] ^ j) * rows, rows)
        outs[j][...] = kept[pl.ds(at, rows), :]


def project_back_body(blocks, pairs, heads, extra, place_ref, c_ref, shift_ref, w_ref, *refs):
    kept = refs[-1]
    groups = (len(refs) - blocks - 4) // 2
    tokens, ins = refs[:groups], refs[groups : groups + blocks]
    outs = refs[groups + blocks : 2 * groups + blocks]
    grad_ref, sum_ref, dot_ref = refs[2 * groups + blocks : -1]
    micro, rows, width = tokens[0].shape
    count = groups * rows
    for j in range(blocks):
        kept[place_ref[1] ^ j] = ins[j][...]
    last = None
    if extra:
        last = jnp.zeros((count, 256), F32)
        for j in range(blocks):
            last = last + kept[j, :, 128:].astype(F32)
        last = last.astype(BF)
    all_a, all_g = [], []
    for m in range(micro):
        n = jnp.concatenate([x[m] for x in tokens], 0).astype(F32)
        a = (n * c_ref[m][None] + shift_ref[m][None]).astype(BF)
        qk, v = [], []
        for h in range(heads):
            pair = m * heads + h
            if pair < blocks:
                qk.append(kept[pair, :, :128])
                at = 256 if extra else 128
                v.append(kept[pair, :, at : at + 64])
            else:
                qk.append(last[:, :128])
                v.append(last[:, 192:])
        g = jnp.concatenate(qk + v, 1)
        da = lax.dot_general(g, w_ref[:, : 192 * heads], (((1,), (1,)), ((), ())), preferred_element_type=F32)
        for k in range(groups):
            outs[k][m] = da[k * rows : (k + 1) * rows].astype(BF)
        sum_ref[m : m + 1] = jnp.sum(da, 0, keepdims=True)
        dot_ref[m : m + 1] = jnp.sum(da * n, 0, keepdims=True)
        all_a.append(a)
        all_g.append(g)
    grad_ref[...] = lax.dot_general(
        jnp.concatenate(all_a, 0), jnp.concatenate(all_g, 0), (((0,), (0,)), ((), ())),
        preferred_element_type=F32,
    ).astype(BF)


def norm(values):
    centered = values - jnp.mean(values, -1, keepdims=True)
    inverse = lax.rsqrt(jnp.mean(centered * centered, -1, keepdims=True) + 1e-05)
    return centered * inverse, inverse


def by_micro(ref, rows):
    return jnp.concatenate(
        [jnp.broadcast_to(ref[m][None], (rows, ref.shape[1])) for m in range(ref.shape[0])], 0
    )


def middle_body(
    groups, blocks, heads, micro, rows, stripe,
    came_ref, out_ref, x_ref, gate_ref, c_ref, shift_ref,
    merged_ref, attn_ref, middle_ref, second_ref,
):
    width = x_ref.shape[1]
    for u in range(groups):
        for m in range(micro):
            for h in range(heads):
                pair = m * heads + h
                lanes = slice((u * heads + h) * 64, (u * heads + h + 1) * 64)
                half = rows // 2
                if pair < blocks and stripe:
                    at = m * rows
                    merged_ref[at : at + half, lanes] = came_ref[u * blocks + pair, :half, :64]
                    merged_ref[at + half : at + rows, lanes] = came_ref[u * blocks + pair, :half, 64:]
                elif pair < blocks:
                    merged_ref[m * rows : (m + 1) * rows, lanes] = came_ref[u * blocks + pair]
                else:
                    for b in range(blocks):
                        at = m * rows + b * stripe
                        merged_ref[at : at + stripe, lanes] = came_ref[u * blocks + b, half:, :64]
    attn = jnp.dot(merged_ref[...], out_ref[...].reshape(width, width), preferred_element_type=F32)
    attn_ref[...] = attn
    middle = x_ref[...].astype(F32) + by_micro(gate_ref, rows) * attn
    middle_ref[...] = middle
    normed, _ = norm(middle)
    second_ref[...] = (normed * by_micro(c_ref, rows) + by_micro(shift_ref, rows)).astype(BF)


def gelu_pair(u):
    t = jnp.tanh(0.7978845608028654 * (u + 0.044715 * u * u * u))
    value = 0.5 * u * (1.0 + t)
    slope = 0.5 * (1.0 + t) + 0.5 * u * (1.0 - t * t) * (
        0.7978845608028654 * (1.0 + 0.134145 * u * u)
    )
    return value, slope


NT = (((1,), (1,)), ((), ()))
TN = (((0,), (0,)), ((), ()))


def feed_body(
    groups, blocks, heads, micro, rows, stripe,
    ex_ref, re_ref, out_w_ref, ex_bias_ref, re_bias_ref, second_ref, middle_ref, attn_ref, dy_ref,
    gate1_ref, gate2_ref, c_ref,
    layer_ref, grad_ref, dattn_ref, do_ref, sums_ref,
    branch_sum, back_sum, dm_sum, do_sum,
):
    step = pl.program_id(0)
    width = middle_ref.shape[1]

    @pl.when(step == 0)
    def _():
        branch_sum[...] = jnp.zeros_like(branch_sum)
        back_sum[...] = jnp.zeros_like(back_sum)
        dm_sum[...] = (by_micro(gate2_ref, rows) * dy_ref[...].astype(F32)).astype(BF)

    expand = ex_ref[...].reshape(width, width)
    reduce = re_ref[...].reshape(width, width)
    u = jnp.dot(second_ref[...], expand, preferred_element_type=F32) + ex_bias_ref[0]
    g, slope = gelu_pair(u)
    branch_sum[...] += jnp.dot(g.astype(BF), reduce, preferred_element_type=F32)
    dg = lax.dot_general(dm_sum[...], reduce, NT, preferred_element_type=F32)
    du = (dg * slope).astype(BF)
    back_sum[...] += lax.dot_general(du, expand, NT, preferred_element_type=F32)

    @pl.when(step == pl.num_programs(0) - 1)
    def _():
        def total(at, x):
            for m in range(micro):
                sums_ref[at * micro + m : at * micro + m + 1] = jnp.sum(
                    x[m * rows : (m + 1) * rows], 0, keepdims=True
                )

        branch = branch_sum[...] + re_bias_ref[...]
        middle = middle_ref[...]
        dy = dy_ref[...].astype(F32)
        layer_ref[...] = (middle + by_micro(gate2_ref, rows) * branch).astype(BF)
        total(0, dy * branch)
        normed, inverse = norm(middle)
        db = back_sum[...]
        total(1, db)
        total(2, db * normed)
        e = db * by_micro(c_ref, rows)
        grad = dy + inverse * (
            e
            - jnp.mean(e, -1, keepdims=True)
            - normed * jnp.mean(e * normed, -1, keepdims=True)
        )
        grad_ref[...] = grad
        total(3, grad * attn_ref[...])
        total(4, dm_sum[...].astype(F32))
        dattn = (by_micro(gate1_ref, rows) * grad).astype(BF)
        dattn_ref[...] = dattn
        do_sum[...] = lax.dot_general(
            dattn, out_w_ref[...].reshape(width, width), NT, preferred_element_type=F32
        ).astype(BF)
        for at in range(groups):
            for m in range(micro):
                for h in range(heads):
                    pair = m * heads + h
                    lanes = slice((at * heads + h) * 64, (at * heads + h + 1) * 64)
                    half, top = rows // 2, m * rows
                    if pair < blocks and stripe:
                        do_ref[at * blocks + pair, :half, :64] = do_sum[top : top + half, lanes]
                        do_ref[at * blocks + pair, :half, 64:] = do_sum[top + half : top + rows, lanes]
                    elif pair < blocks:
                        do_ref[at * blocks + pair] = do_sum[top : top + rows, lanes]
                    else:
                        for b in range(blocks):
                            do_ref[at * blocks + b, half:, :64] = do_sum[top : top + stripe, lanes]
                            do_ref[at * blocks + b, half:, 64:] = jnp.zeros((stripe, 64), BF)
                            top += stripe
            for b in range(micro * heads, blocks):
                do_ref[at * blocks + b] = jnp.zeros((rows, 64), BF)


def feed_weights_body(rows, blocks, place_ref, ex_ref, re_ref, bias_ref, gate_ref, *refs):
    groups = (len(refs) - 2) // 2
    out_ref, sum_ref = refs[2 * groups :]
    width = refs[0].shape[-1]
    second = jnp.concatenate([x[...] for x in refs[:groups]], 0)
    gate = by_micro(gate_ref, rows)
    dm = jnp.concatenate(
        [(gate * x[...].astype(F32)).astype(BF) for x in refs[groups : 2 * groups]], 0
    )
    expand = ex_ref[...].reshape(width, width)
    reduce = re_ref[...].reshape(width, width)
    u = jnp.dot(second, expand, preferred_element_type=F32) + bias_ref[0]
    g, slope = gelu_pair(u)
    du = lax.dot_general(dm, reduce, NT, preferred_element_type=F32) * slope
    du = du.astype(BF)
    sum_ref[...] = jnp.sum(du.astype(F32), 0, keepdims=True)
    per, each = width // blocks, width // (groups * blocks)
    x = lax.dot_general(g.astype(BF), dm, TN, preferred_element_type=F32)
    for b in range(blocks):
        out_ref[b, :per] = x[b * per : (b + 1) * per].astype(BF)
    x = lax.dot_general(second, du, TN, preferred_element_type=F32)
    for k in range(groups):
        for b in range(blocks):
            at = (k * blocks + b) * each
            out_ref[b, per + k * each : per + (k + 1) * each] = x[at : at + each].astype(BF)


def attend_body(block, range_ref, q_ref, sq_ref, k_ref, v_ref, sk_ref, o_ref, lse_ref):
    i = pl.program_id(0)
    q, sq = q_ref[...], sq_ref[0]
    count, width = q.shape

    def step(j, carry):
        high, total, acc = carry
        at = pl.ds(pl.multiple_of(j * block, block), block)
        k, v, sk = k_ref[at, :], v_ref[at, :], sk_ref[at, :]
        s = lax.dot_general(k, q, (((1,), (1,)), ((), ())), preferred_element_type=F32)
        s = jnp.where(sk == sq, s, NEG)
        new = jnp.maximum(high, jnp.max(s, 0, keepdims=True))
        p = jnp.exp(s - new)
        fix = jnp.exp(high - new)
        total = total * fix + jnp.sum(p, 0, keepdims=True)
        acc = acc * fix + lax.dot_general(
            v, p.astype(BF), (((0,), (0,)), ((), ())), preferred_element_type=F32
        )
        return new, total, acc

    first = (
        jnp.full((1, count), NEG, F32),
        jnp.zeros((1, count), F32),
        jnp.zeros((width, count), F32),
    )
    high, total, acc = lax.fori_loop(range_ref[2 * i], range_ref[2 * i + 1], step, first)
    o_ref[...] = (acc / total).T.astype(BF)
    lse_ref[0] = high + jnp.log(total)


def attend_back_body(
    block, range_ref, q_ref, sq_ref, lse_ref, o_ref, do_ref, k_ref, v_ref, sk_ref,
    dq_ref, dk_ref, dv_ref, dk_sum, dv_sum,
):
    i = pl.program_id(0)

    @pl.when(i == 0)
    def _():
        dk_sum[...] = jnp.zeros_like(dk_sum)
        dv_sum[...] = jnp.zeros_like(dv_sum)

    q, sq, lse, do = q_ref[...], sq_ref[0], lse_ref[0], do_ref[...]
    count, width = q.shape
    delta = jnp.sum((do.astype(F32) * o_ref[...].astype(F32)).T, 0, keepdims=True)

    def step(j, dq):
        at = pl.ds(pl.multiple_of(j * block, block), block)
        k, v, sk = k_ref[at, :], v_ref[at, :], sk_ref[at, :]
        s = lax.dot_general(k, q, (((1,), (1,)), ((), ())), preferred_element_type=F32)
        p = jnp.where(sk == sq, jnp.exp(s - lse), 0.0)
        dp = lax.dot_general(v, do, (((1,), (1,)), ((), ())), preferred_element_type=F32)
        ds = (p * (dp - delta)).astype(BF)
        dv_sum[at, :] += jnp.dot(p.astype(BF), do, preferred_element_type=F32)
        dk_sum[at, :] += jnp.dot(ds, q, preferred_element_type=F32)
        return dq + lax.dot_general(
            k, ds, (((0,), (0,)), ((), ())), preferred_element_type=F32
        )

    dq = lax.fori_loop(
        range_ref[2 * i], range_ref[2 * i + 1], step, jnp.zeros((width, count), F32)
    )
    dq_ref[...] = (dq * 0.125).T.astype(BF)

    @pl.when(i == pl.num_programs(0) - 1)
    def _():
        dk_ref[...] = dk_sum[...].astype(BF)
        dv_ref[...] = dv_sum[...].astype(BF)


def attend(ranges, q, sq, k, v, sk, rows, block):
    count, width = q.shape
    steps = count // rows
    size = k.shape[0]
    by_row = pl.BlockSpec((rows, width), lambda i, r: (i, 0))
    as_row = pl.BlockSpec((1, 1, rows), lambda i, r: (i, 0, 0))
    return pl.pallas_call(
        functools.partial(attend_body, block),
        grid_spec=pltpu.PrefetchScalarGridSpec(
            num_scalar_prefetch=1,
            grid=(steps,),
            in_specs=[by_row, as_row, whole_vmem(), whole_vmem(), whole_vmem()],
            out_specs=[by_row, as_row],
        ),
        out_shape=[
            jax.ShapeDtypeStruct((count, width), BF),
            jax.ShapeDtypeStruct((steps, 1, rows), F32),
        ],
        cost_estimate=pl.CostEstimate(
            flops=count * size * width, transcendentals=count * size // 4, bytes_accessed=4 * size * width
        ),
        name="attend",
    )(ranges, q, sq.reshape(steps, 1, rows), k, v, sk)


def attend_back(ranges, q, sq, lse, o, do, k, v, sk, rows, block):
    count, width = q.shape
    steps = count // rows
    size = k.shape[0]
    by_row = pl.BlockSpec((rows, width), lambda i, r: (i, 0))
    as_row = pl.BlockSpec((1, 1, rows), lambda i, r: (i, 0, 0))
    return pl.pallas_call(
        functools.partial(attend_back_body, block),
        grid_spec=pltpu.PrefetchScalarGridSpec(
            num_scalar_prefetch=1,
            grid=(steps,),
            in_specs=[by_row, as_row, as_row, by_row, by_row, whole_vmem(), whole_vmem(), whole_vmem()],
            out_specs=[by_row, whole_vmem(), whole_vmem()],
            scratch_shapes=[pltpu.VMEM((size, width), F32)] * 2,
        ),
        out_shape=[
            jax.ShapeDtypeStruct((count, width), BF),
            jax.ShapeDtypeStruct((size, width), BF),
            jax.ShapeDtypeStruct((size, width), BF),
        ],
        cost_estimate=pl.CostEstimate(
            flops=3 * count * size * width, transcendentals=count * size // 4, bytes_accessed=8 * size * width
        ),
        name="attend_back",
    )(ranges, q, sq.reshape(steps, 1, rows), lse, o, do, k, v, sk)


def spread(ref, at, rows):
    return ref[pl.ds(pl.multiple_of(at, rows), rows), :]


def keys_mask(low, high, at, count):
    position = at + lax.broadcasted_iota(jnp.int32, (count, low.shape[1]), 0)
    return (position >= low) & (position < high)


QB, KB, STEP = 512, 512, 256


def project_small_body(blocks, heads, c_ref, shift_ref, w_ref, *refs):
    groups = len(refs) - 3
    tokens, out_ref, last_ref, wide = refs[:groups], *refs[groups:]
    micro, rows, width = tokens[0].shape
    count = groups * rows
    half, stripe = count // 2, rows // blocks
    end = 192 * heads
    weights = [w_ref[:, c : min(c + 128, end)] for c in range(0, end, 128)]
    for m in range(micro):
        a = jnp.concatenate(
            [(x[m].astype(F32) * c_ref[m][None] + shift_ref[m][None]).astype(BF) for x in tokens], 0
        )
        parts = [jnp.dot(a, w, preferred_element_type=F32) for w in weights]
        v = jnp.concatenate(parts[heads:], 1)
        for h in range(heads):
            pair = m * heads + h
            own_v = v[:, h * 64 : (h + 1) * 64]
            if pair < blocks:
                out_ref[pair, :count] = parts[h].astype(BF)
                out_ref[pair, count : count + half] = jnp.concatenate([own_v[:half], own_v[half:]], 1).astype(BF)
            else:
                wide[...] = parts[h]
                last_ref[...] = jnp.concatenate([parts[h][:, 64:], own_v], 1).astype(BF)
    for to in range(blocks):
        pieces = [
            wide[k * rows + to * stripe : k * rows + (to + 1) * stripe, :64] for k in range(groups)
        ]
        out_ref[to, count + half :] = jnp.concatenate(
            [jnp.concatenate(pieces[:2], 0), jnp.concatenate(pieces[2:], 0)], 1
        ).astype(BF)


def pick_piece(x, k):
    y = jnp.where((k & 1) != 0, x[8:], x[:8])
    return jnp.where(k >= 2, y[:, 64:], y[:, :64])


def project_back_small_body(blocks, heads, place_ref, c_ref, shift_ref, w_ref, *refs):
    wide, scattered = refs[-2:]
    few = blocks // 2
    groups = (len(refs) - few - 7) // 2
    tokens, in_ref, lasts = refs[:groups], refs[groups], refs[groups + 1 : groups + 1 + few]
    outs = refs[groups + 1 + few : 2 * groups + 1 + few]
    keep_ref, send_ref, sum_ref, dot_ref = refs[2 * groups + 1 + few : -2]
    micro, rows, width = tokens[0].shape
    count = groups * rows
    half, stripe = count // 2, rows // blocks
    for j in range(blocks):
        x = in_ref[j, count + half :].astype(F32)
        pieces = [x[:8, :64], x[8:, :64], x[:8, 64:], x[8:, 64:]]
        for k in range(groups):
            wide[k * rows + j * stripe : k * rows + (j + 1) * stripe] = pieces[k]
    all_a, all_g = [], []
    for m in range(micro):
        n = jnp.concatenate([x[m] for x in tokens], 0).astype(F32)
        a = (n * c_ref[m][None] + shift_ref[m][None]).astype(BF)
        qk, v = [], []
        for h in range(heads):
            pair = m * heads + h
            if pair < blocks:
                qk.append(in_ref[pair, :count])
                x = in_ref[pair, count : count + half]
                v.append(jnp.concatenate([x[:, :64], x[:, 64:]], 0))
            else:
                x = sum(ref[...].astype(F32) for ref in lasts).astype(BF)
                qk.append(jnp.concatenate([wide[...].astype(BF), x[:, :64]], 1))
                v.append(x[:, 64:])
        g = jnp.concatenate(qk + v, 1)
        da = lax.dot_general(g, w_ref[:, : 192 * heads], NT, preferred_element_type=F32)
        for k in range(groups):
            outs[k][m] = da[k * rows : (k + 1) * rows].astype(BF)
        sum_ref[m : m + 1] = jnp.sum(da, 0, keepdims=True)
        dot_ref[m : m + 1] = jnp.sum(da * n, 0, keepdims=True)
        all_a.append(a)
        all_g.append(g)
    x = lax.dot_general(
        jnp.concatenate(all_a, 0), jnp.concatenate(all_g, 0), TN, preferred_element_type=F32
    )
    scattered[...] = x.reshape(scattered.shape)
    mine = place_ref[1] & 1
    for z in range(few):
        for k in range(groups):
            at = k * blocks + 2 * z
            keep_ref[z, k] = scattered[at + mine].astype(BF)
            send_ref[z, k] = scattered[at + 1 - mine].astype(BF)


def attend_block(scores, q, low, high, first, stop, keys, values):
    count = q.shape[0]

    def score(t, top):
        at = pl.multiple_of((first + 2 * t) * STEP, STEP)
        s = lax.dot_general(keys[pl.ds(at, KB), :], q, NT, preferred_element_type=F32)
        s = jnp.where(keys_mask(low, high, at, KB), s, NEG)
        scores[t, :, :count] = s
        return jnp.maximum(top, jnp.max(s, 0, keepdims=True))

    steps = (stop - first + 1) // 2
    top = lax.fori_loop(0, steps, score, jnp.full((1, count), NEG, F32))

    def weigh(t, carry):
        total, acc = carry
        at = pl.multiple_of((first + 2 * t) * STEP, STEP)
        p = jnp.exp(scores[t, :, :count] - top)
        return total + jnp.sum(p, 0, keepdims=True), acc + lax.dot_general(
            values[pl.ds(at, KB), :], p.astype(BF), TN, preferred_element_type=F32
        )

    total, acc = lax.fori_loop(
        0, steps, weigh, (jnp.zeros((1, count), F32), jnp.zeros((64, count), F32))
    )
    return (acc / total).T, top + jnp.log(total)


def attend_own_body(
    blocks, groups, rows, place_ref, range_ref, low_ref, high_ref, cos_ref, sin_ref, *refs
):
    in_ref, message, q_ref, k_ref, v_ref, o_ref, lse_ref, kept, kept_v, scores = refs
    span = blocks * rows
    size = groups * span
    count = groups * rows
    half = rows // 2
    me_u, me_b = place_ref[0], place_ref[1]
    for g in range(groups):
        k = me_u ^ g
        for j in range(blocks):
            to = slice(j * rows, (j + 1) * rows)
            kept[to, :] = in_ref[j, pl.ds(pl.multiple_of(k * rows, rows), rows), :]
            pair = in_ref[j, pl.ds(pl.multiple_of(count + (k & 1) * rows, rows), rows), :].astype(F32)
            kept_v[to, :] = jnp.where(k >= 2, pair[:, 64:], pair[:, :64]).astype(BF)
        at = slice(g * span, (g + 1) * span)
        x = turn(kept[...].astype(F32), turn_tables(cos_ref[at], sin_ref[at], False)[0])
        q_ref[at] = (x[:, :64] * 0.125).astype(BF)
        k_ref[at] = x[:, 64:].astype(BF)
        v_ref[at] = kept_v[...]
    tail = slice(size, size + KB - STEP)
    for ref in (k_ref, v_ref):
        ref[tail] = jnp.zeros((KB - STEP, 64), BF)

    def run(i, _):
        o, lse = attend_block(
            scores, spread(q_ref, i * QB, QB), low_ref[i], high_ref[i],
            range_ref[2 * i], range_ref[2 * i + 1], k_ref, v_ref,
        )
        o = o.astype(BF)
        o_ref[pl.ds(pl.multiple_of(i * QB, QB), QB), :] = o
        lse_ref[i] = lse
        for d in range(QB // rows):
            message[i * (QB // rows) + d] = jnp.concatenate(
                [o[d * rows : d * rows + half], o[d * rows + half : (d + 1) * rows]], 1
            )
        return 0

    lax.fori_loop(0, size // QB, run, 0)


def stripe_tables(place_ref, cos_ref, sin_ref, wide_cos, wide_sin, devices, rows, stripe):
    for d in range(devices):
        at = slice(d * stripe, (d + 1) * stripe)
        wide_cos[at] = spread(cos_ref, d * rows + place_ref[1] * stripe, stripe)
        wide_sin[at] = spread(sin_ref, d * rows + place_ref[1] * stripe, stripe)
    return turn_tables(wide_cos[...], wide_sin[...], True)[1]


def attend_last_body(
    blocks, groups, rows, stripe, place_ref, range_ref, low_ref, high_ref, cos_ref, sin_ref, *refs
):
    in_ref, last_ins, own_ref = refs[0], refs[1:3], refs[3]
    message, q_ref, k_ref, v_ref, o_ref, lse_ref, kept, wide, wide_cos, wide_sin, scores = refs[4:]
    span = blocks * rows
    size = groups * span
    devices = groups * blocks
    count = groups * rows
    half = rows // 2
    me_u, me_b = place_ref[0], place_ref[1]
    for g in range(groups):
        k = me_u ^ g
        for j in range(blocks):
            at = (g * blocks + j) * stripe
            wide[at : at + stripe, :64] = pick_piece(in_ref[j, count + count // 2 :].astype(F32), k)
            to = pl.ds(pl.multiple_of((me_b ^ j) * rows, rows), rows)
            kept[to, :] = last_ins[j & 1][j >> 1, pl.ds(pl.multiple_of(k * rows, rows), rows), :]
        at = slice(g * span, (g + 1) * span)
        x = turn(kept[...].astype(F32), turn_tables(cos_ref[at], sin_ref[at], True)[1])
        k_ref[at] = x[:, :64].astype(BF)
        v_ref[at] = kept[:, 64:]
    tail = slice(size, size + KB - STEP)
    for ref in (k_ref, v_ref):
        ref[tail] = jnp.zeros((KB - STEP, 64), BF)
    wide[:, 64:] = jnp.zeros((devices * stripe, 64), F32)
    x = turn(wide[...], stripe_tables(place_ref, cos_ref, sin_ref, wide_cos, wide_sin, devices, rows, stripe))
    q_ref[...] = (x[:, :64] * 0.125).astype(BF)
    message[:, :half] = own_ref[...]
    few = lse_ref.shape[2]

    def run(i, _):
        o, lse = attend_block(
            scores, spread(q_ref, i * few, few), low_ref[i], high_ref[i],
            range_ref[2 * i], range_ref[2 * i + 1], k_ref, v_ref,
        )
        o_ref[pl.ds(pl.multiple_of(i * few, few), few), :] = o.astype(BF)
        lse_ref[i] = lse
        o = jnp.concatenate([o, jnp.zeros_like(o)], 1)
        for d in range(few // stripe):
            message[i * (few // stripe) + d, half:] = o[d * stripe : (d + 1) * stripe].astype(BF)
        return 0

    lax.fori_loop(0, lse_ref.shape[0], run, 0)


def attend_block_back(q, do, o, lse, low, high, first, stop, keys, values, dk_sum, dv_sum):
    count = q.shape[0]
    delta = jnp.sum((do.astype(F32) * o.astype(F32)).T, 0, keepdims=True)

    def step(t, dq):
        at = pl.multiple_of((first + 2 * t) * STEP, STEP)
        here = pl.ds(at, KB)
        k, v = keys[here, :], values[here, :]
        s = lax.dot_general(k, q, NT, preferred_element_type=F32)
        dp = lax.dot_general(v, do, NT, preferred_element_type=F32)
        p = jnp.where(keys_mask(low, high, at, KB), jnp.exp(s - lse), 0.0)
        ds = (p * (dp - delta)).astype(BF)
        dv_sum[here, :] += jnp.dot(p.astype(BF), do, preferred_element_type=F32)
        dk_sum[here, :] += jnp.dot(ds, q, preferred_element_type=F32)
        return dq + lax.dot_general(k, ds, TN, preferred_element_type=F32)

    return (
        lax.fori_loop(0, (stop - first + 1) // 2, step, jnp.zeros((64, count), F32)) * 0.125
    ).T


def attend_last_back_body(
    blocks, groups, rows, stripe, place_ref, range_ref, low_ref, high_ref, cos_ref, sin_ref,
    do_ref, q_ref, k_ref, v_ref, o_ref, lse_ref, dq_ref, keep_ref, send_ref, kept, wide_cos, wide_sin, dk, dv,
):
    span = blocks * rows
    devices = groups * blocks
    half = rows // 2
    for ref in (dk, dv):
        ref[...] = jnp.zeros(ref.shape, F32)
    few = lse_ref.shape[2]
    dq_ref[:, 64:] = jnp.zeros((devices * stripe, 64), F32)

    def run(i, _):
        came = [
            do_ref[i * (few // stripe) + d].astype(F32)[half:, :64] for d in range(few // stripe)
        ]
        at = pl.ds(pl.multiple_of(i * few, few), few)
        dq_ref[at, :64] = attend_block_back(
            q_ref[at, :], jnp.concatenate(came, 0).astype(BF), o_ref[at, :], lse_ref[i],
            low_ref[i], high_ref[i], range_ref[2 * i], range_ref[2 * i + 1], k_ref, v_ref, dk, dv,
        )
        return 0

    lax.fori_loop(0, lse_ref.shape[0], run, 0)
    cos, sin = stripe_tables(place_ref, cos_ref, sin_ref, wide_cos, wide_sin, devices, rows, stripe)
    dq_ref[...] = turn(dq_ref[...], (cos, -sin))
    for g in range(groups):
        at = slice(g * span, (g + 1) * span)
        k = place_ref[0] ^ g
        cos, sin = turn_tables(cos_ref[at], sin_ref[at], True)[1]
        x = turn(jnp.concatenate([dk[at], jnp.zeros_like(dk[at])], 1), (cos, -sin))[:, :64]
        kept[...] = jnp.concatenate([x, dv[at]], 1).astype(BF)
        to = pl.ds(pl.multiple_of(k * rows, rows), rows)
        for z in range(blocks // 2):
            mine = 2 * z + (place_ref[1] & 1)
            keep_ref[z, to, :] = spread(kept, mine * rows, rows)
            send_ref[z, to, :] = spread(kept, (mine ^ 1) * rows, rows)


def attend_own_back_body(
    blocks, groups, rows, stripe, place_ref, range_ref, low_ref, high_ref, cos_ref, sin_ref,
    do_ref, q_ref, k_ref, v_ref, o_ref, lse_ref, last_dq_ref, out_ref, kept, kept_v, wide_v, dq, dk, dv,
):
    span = blocks * rows
    size = groups * span
    count = groups * rows
    half = rows // 2
    me_u, me_b = place_ref[0], place_ref[1]
    for ref in (dk, dv):
        ref[...] = jnp.zeros(ref.shape, F32)

    def run(i, _):
        came = []
        for d in range(QB // rows):
            x = do_ref[i * (QB // rows) + d]
            came += [x[:half, :64], x[:half, 64:]]
        at = pl.ds(pl.multiple_of(i * QB, QB), QB)
        dq[at, :] = attend_block_back(
            q_ref[at, :], jnp.concatenate(came, 0), o_ref[at, :], lse_ref[i], low_ref[i], high_ref[i],
            range_ref[2 * i], range_ref[2 * i + 1], k_ref, v_ref, dk, dv,
        )
        return 0

    lax.fori_loop(0, size // QB, run, 0)
    for g in range(groups):
        at = slice(g * span, (g + 1) * span)
        k = me_u ^ g
        cos, sin = turn_tables(cos_ref[at], sin_ref[at], False)[0]
        kept[...] = turn(jnp.concatenate([dq[at], dk[at]], 1), (cos, -sin)).astype(BF)
        kept_v[...] = dv[at].astype(BF)
        for b in range(blocks):
            out_ref[b, pl.ds(pl.multiple_of(k * rows, rows), rows), :] = kept[b * rows : (b + 1) * rows]
        for b in range(blocks):
            wide_v[g * blocks + b] = kept_v[b * rows : (b + 1) * rows]
    for to in range(blocks):
        v = [wide_v[(me_u ^ k) * blocks + to] for k in range(groups)]
        out_ref[to, count : count + count // 2] = jnp.concatenate(
            [jnp.concatenate(v[:2], 0), jnp.concatenate(v[2:], 0)], 1
        )
        z = [spread(last_dq_ref, ((me_u ^ k) * blocks + to) * stripe, stripe)[:, :64] for k in range(groups)]
        out_ref[to, count + count // 2 :] = jnp.concatenate(
            [jnp.concatenate(z[:2], 0), jnp.concatenate(z[2:], 0)], 1
        ).astype(BF)


def on_device(
    tokens,
    cotangent,
    lengths,
    time_step,
    modulate_weight,
    modulate_bias,
    attend_gain,
    input_weight,
    output_weight,
    feed_gain,
    expand_weight,
    expand_bias,
    reduce_weight,
    reduce_bias,
):
    groups, blocks = axis_count("ulysses"), axis_count(BLK)
    group_id, block_id = lax.axis_index("ulysses"), lax.axis_index(BLK)
    devices = groups * blocks
    micro, rows, width = tokens.shape
    own = micro * rows
    size = devices * rows
    head_width = width // HEADS
    heads = HEADS // groups
    pairs = micro * heads
    extra = pairs > blocks
    lanes = 384 if extra else 256
    stripe = rows // blocks if extra else 0
    mod_rows = modulate_weight.shape[0]
    gain_rows = attend_gain.shape[0]
    ff_rows = expand_bias.shape[0]
    ff = ff_rows * devices
    folds = ff // width
    assert pairs <= blocks + 1 and head_width == 64 and folds == groups and heads == 3
    place = jnp.stack([group_id, block_id]).astype(jnp.int32)
    pair_micro = jnp.minimum(block_id // heads, micro - 1)

    in_split = input_weight.reshape(gain_rows, 3, groups, heads, head_width)
    in_split = jnp.concatenate(
        [
            in_split[:, :2].transpose(2, 0, 3, 1, 4).reshape(groups, 1, gain_rows, -1),
            in_split[:, 2].transpose(1, 0, 2, 3).reshape(groups, 1, gain_rows, -1),
        ],
        3,
    )
    in_lanes = heads * 3 * head_width

    condition = time_features(time_step, modulate_weight.shape[1] // 2)
    mod_own = jnp.einsum(
        "mc,fc->mf", condition, modulate_weight, preferred_element_type=F32
    ) + modulate_bias.astype(F32)
    mod_lanes = 64 * -(-mod_rows // 64)
    mod_own = jnp.pad(mod_own, ((0, 0), (0, mod_lanes - mod_rows))).reshape(-1, 64)
    mod_high = lax.reduce_precision(mod_own, 8, 7)
    mod_size = mod_own.shape[0]
    vectors = jnp.pad(
        jnp.stack([attend_gain, feed_gain, reduce_bias]), ((0, 0), (0, 64 - gain_rows))
    )
    ff_lanes = 64 * -(-ff_rows // 64)
    small = jnp.concatenate(
        [
            mod_high.astype(BF),
            (mod_own - mod_high).astype(BF),
            vectors,
            jnp.pad(expand_bias, (0, ff_lanes - ff_rows)).reshape(-1, 64),
        ],
        0,
    )
    small_lanes = 64 * -(-small.shape[0] // gain_rows)
    small = jnp.pad(small, ((0, small_lanes * gain_rows // 64 - small.shape[0]), (0, 0)))
    small = small.reshape(1, 1, gain_rows, small_lanes)
    in_message = jnp.concatenate(
        [
            jnp.broadcast_to(in_split, (groups, blocks) + in_split.shape[2:]),
            jnp.broadcast_to(small, (groups, blocks) + small.shape[2:]),
        ],
        3,
    ).reshape(devices, gain_rows, in_lanes + small_lanes)
    in_message, tokens, lengths = lax.optimization_barrier((in_message, tokens, lengths))
    came = exchange(in_message)
    values = tokens.astype(F32)
    n1, r1 = norm(values)
    n1_b = n1.astype(BF)
    n1_group = swap([n1_b] * groups, "ulysses")
    small_all = came[:, :, in_lanes:].reshape(devices, -1, 64)
    in_own = came.reshape(width, in_lanes + small_lanes)

    weight_pack = jnp.concatenate(
            [
                reduce_weight,
                output_weight,
                expand_weight.reshape(gain_rows, folds, width).transpose(1, 0, 2).reshape(-1, width),
            ],
            0,
        )
    index = jnp.arange(size, dtype=jnp.int32)
    pair_lengths = lax.dynamic_index_in_dim(lengths, pair_micro, 0, keepdims=False)
    segment, position = doc_layout(index, pair_lengths)
    last_lengths = lengths[micro - 1]
    last_segment, last_position = doc_layout(index, last_lengths)
    half = head_width // 2
    freqs = jnp.exp(-math.log(10000.0) * jnp.arange(half, dtype=F32) / half)
    lane = jnp.arange(128)
    angles = jnp.where(
        (lane < 64)[None, :], position.astype(F32)[:, None], last_position.astype(F32)[:, None]
    ) * jnp.tile(freqs, 4)[None, :]
    cos_table = jnp.cos(angles)
    sin_table = jnp.where((lane % 64 < 32)[None, :], -1.0, 1.0) * jnp.sin(angles)
    query_rows = math.gcd(size, QB)
    key_block = math.gcd(size, 256)
    first = jnp.arange(size // query_rows, dtype=jnp.int32) * query_rows
    ranges = key_ranges(first, first + query_rows - 1, pair_lengths, key_block)
    small_path = extra and size % KB == 0 and rows == 64 and stripe == 8 and groups == 4 and size <= 4096

    striped = lambda x: lax.dynamic_slice_in_dim(
        x.reshape((devices, rows) + x.shape[1:]), block_id * stripe, stripe, 1
    ).reshape((devices * stripe,) + x.shape[1:])
    last_ranges = bounds = 0
    if small_path:
        last_rows = min(256, devices * stripe)
        chunk = last_rows // stripe
        last_first = jnp.arange(devices // chunk, dtype=jnp.int32) * (chunk * rows) + block_id * stripe
        last_ranges = key_ranges(
            last_first, last_first + (chunk - 1) * rows + stripe - 1, last_lengths, STEP
        )
        bounds = []
        for where, lens, pick, lump in (
            (position, pair_lengths, lambda x: x, QB),
            (last_position, last_lengths, striped, last_rows),
        ):
            low = index - where
            ends = jnp.cumsum(lens)
            high = jnp.min(jnp.where(ends[None, :] > index[:, None], ends[None, :], 1 << 30), 1)
            bounds += [pick(low).reshape(-1, 1, lump), pick(high).reshape(-1, 1, lump)]
    in_own, small_all, n1_group, place, cos_table, sin_table, ranges, last_ranges, bounds = (
        lax.optimization_barrier(
            (in_own, small_all, n1_group, place, cos_table, sin_table, ranges, last_ranges, bounds)
        )
    )
    weight_pack, in_own = lax.optimization_barrier((weight_pack, in_own))
    gathered = lax.all_gather(weight_pack, ALL, axis=0, tiled=False)
    unit = gain_rows
    while unit % 8:
        unit *= 2
    units = width // unit
    if unit != gain_rows:
        gathered = jnp.concatenate(
            [gathered[:, :ff_rows].reshape(units, -1, width)]
            + [
                gathered[:, at : at + gain_rows].reshape(units, unit, width)
                for at in range(ff_rows, ff_rows + (folds + 1) * gain_rows, gain_rows)
            ],
            1,
        )
    wide = unit * folds

    mods = small_all[:, :mod_size].astype(F32) + small_all[:, mod_size : 2 * mod_size].astype(F32)
    mods = mods.reshape(devices, micro, mod_lanes)[:, :, :mod_rows].transpose(1, 0, 2).reshape(micro, -1)
    at = 2 * mod_size
    vectors = small_all[:, at : at + 3, :gain_rows].astype(F32).transpose(1, 0, 2).reshape(3, width)
    gain1, gain2, reduce_bias_f = vectors[0], vectors[1], vectors[2:]
    at += 3
    expand_bias_f = small_all[:, at : at + ff_lanes // 64].reshape(devices, ff_lanes)[:, :ff_rows]
    expand_bias_f = expand_bias_f.astype(F32).reshape(folds, 1, width)
    shift1, scale1, gate1, shift2, scale2, gate2 = jnp.split(mods, 6, 1)
    c1 = gain1 * (1.0 + scale1)
    c2 = gain2 * (1.0 + scale2)

    count = groups * rows
    smem = pl.BlockSpec(memory_space=pltpu.SMEM)
    message_rows = count + count // 2 + 16
    if small_path:
        outgoing, last_own = pl.pallas_call(
            functools.partial(project_small_body, blocks, heads),
            out_shape=[
                jax.ShapeDtypeStruct((blocks, message_rows, 128), BF), jax.ShapeDtypeStruct((count, 128), BF),
            ],
            in_specs=[whole_vmem()] * (3 + groups),
            out_specs=[whole_vmem()] * 2,
            scratch_shapes=[pltpu.VMEM((count, 128), F32)],
            cost_estimate=pl.CostEstimate(
                flops=2 * micro * count * width * 3 * 64 * heads, transcendentals=0, bytes_accessed=8 * own * width
            ),
            name="project",
        )(c1, shift1, in_own, *n1_group)
        incoming = [lax.all_to_all(outgoing, BLK, split_axis=0, concat_axis=0, tiled=True)]
        pass_on = lambda x, bit: lax.ppermute(x, BLK, [(i, i ^ bit) for i in range(blocks)])
        last_four = jnp.stack([last_own] + [pass_on(last_own, bit) for bit in range(2, blocks, 2)])
        last_keys = [last_four, pass_on(last_four, 1)]
    else:
        outgoing = pl.pallas_call(
            functools.partial(project_body, blocks, pairs, heads, extra),
            out_shape=[jax.ShapeDtypeStruct((count, lanes), BF)] * blocks,
            in_specs=[smem] + [whole_vmem()] * (3 + groups),
            out_specs=[whole_vmem()] * blocks,
            scratch_shapes=[pltpu.VMEM((blocks, count, lanes), BF)],
            name="project",
        )(place, c1, shift1, in_own, *n1_group)
        incoming = swap(outgoing, BLK)

    span = blocks * rows
    by_span = pl.BlockSpec((span, 64), lambda i, p: (i ^ p[0], 0))
    table_spec = pl.BlockSpec((span, 128), lambda i, p: (i ^ p[0], 0))
    by_rows = pl.BlockSpec((rows, lanes), lambda i, p: (i, 0))
    parts = 6 if extra else 3
    if small_path:
        whole = lambda *shape: jax.ShapeDtypeStruct(shape, BF)
        f32 = lambda *shape: jax.ShapeDtypeStruct(shape, F32)
        padded = whole(size + KB - STEP, 64)
        own_args = (place, ranges, *bounds[:2], cos_table, sin_table)
        last_args = (place, last_ranges, *bounds[2:], cos_table, sin_table)
        specs = [smem] * 2 + [whole_vmem()] * 4
        own_message, *own_saved = pl.pallas_call(
            functools.partial(attend_own_body, blocks, groups, rows),
            in_specs=specs + [whole_vmem()],
            out_specs=[whole_vmem()] * 6,
            out_shape=[
                whole(devices, rows // 2, 128), whole(size, 64), padded, padded, whole(size, 64), f32(*bounds[0].shape),
            ],
            scratch_shapes=[
                pltpu.VMEM((span, 128), BF), pltpu.VMEM((span, 64), BF),
                pltpu.VMEM((size // KB + 1, KB, QB), F32),
            ],
            cost_estimate=pl.CostEstimate(
                flops=size * size * 64, transcendentals=size * size // 2, bytes_accessed=16 * size * 128
            ),
            name="attend_own",
        )(*own_args, *incoming)
        message, *last_saved = pl.pallas_call(
            functools.partial(attend_last_body, blocks, groups, rows, stripe),
            in_specs=specs + [whole_vmem()] * 4,
            out_specs=[whole_vmem()] * 6,
            out_shape=[
                whole(devices, rows // 2 + stripe, 128), whole(devices * stripe, 64), padded, padded,
                whole(devices * stripe, 64), f32(*bounds[2].shape),
            ],
            scratch_shapes=[pltpu.VMEM((span, 128), BF)]
            + [pltpu.VMEM((devices * stripe, 128), F32)] * 3
            + [pltpu.VMEM((size // KB + 1, KB, last_rows), F32)],
            cost_estimate=pl.CostEstimate(
                flops=size * size * 16, transcendentals=size * size // 8, bytes_accessed=16 * size * 64
            ),
            name="attend_last",
        )(*last_args, *incoming, *last_keys, own_message)
    else:
        assert not extra
        turned = pl.pallas_call(
            functools.partial(rotate_in_body, blocks, extra),
            grid_spec=pltpu.PrefetchScalarGridSpec(
                num_scalar_prefetch=1,
                grid=(groups,),
                in_specs=[table_spec, table_spec] + [by_rows] * blocks,
                out_specs=[by_span] * parts,
                scratch_shapes=[pltpu.VMEM((span, lanes), BF)],
            ),
            out_shape=[jax.ShapeDtypeStruct((size, 64), BF)] * parts,
            name="rotate_in",
        )(place, cos_table, sin_table, *incoming)
        query, key, value = turned[:3]
        attended, lse = attend(
            ranges, query, segment, key, value, segment[:, None], query_rows, key_block
        )
        message = attended.reshape(devices, rows, head_width)
    came = exchange(message)

    ex_spec = lambda f: pl.BlockSpec((units, unit, width), f)
    flat = pl.BlockSpec((own, width), lambda i: (0, 0))
    vec = lambda n: pl.BlockSpec((n, width), lambda i: (0, 0))
    message_shape = message.shape
    message_spec = pl.BlockSpec(message_shape, lambda i: (0, 0, 0))
    sizes = (groups, blocks, heads, micro, rows, stripe)
    own_f32 = jax.ShapeDtypeStruct((own, width), F32)
    own_bf = jax.ShapeDtypeStruct((own, width), BF)
    merged, attn, middle, second = pl.pallas_call(
        functools.partial(middle_body, *sizes),
        grid=(1,),
        in_specs=[message_spec, ex_spec(lambda i: (0, folds, 0)), flat, vec(micro), vec(micro), vec(micro)],
        out_specs=[flat] * 4,
        out_shape=[own_bf, own_f32, own_f32, own_bf],
        name="middle",
    )(came, gathered, tokens.reshape(own, width), gate1, c2, shift2)
    second_group = swap([second] * groups, "ulysses")
    dy = cotangent.reshape(own, width)
    dy_group = swap([dy] * groups, "ulysses")

    per = width // wide
    layer_output, grad_middle, grad_attn, do_message, sums = pl.pallas_call(
        functools.partial(feed_body, *sizes),
        grid=(folds,),
        in_specs=[
            ex_spec(lambda i: (0, folds + 1 + i, 0)),
            pl.BlockSpec((per, wide, width), lambda i: (i, 0, 0)),
            ex_spec(lambda i: (0, folds, 0)),
            pl.BlockSpec((1, 1, width), lambda i: (i, 0, 0)),
            vec(1),
            flat, flat, flat, flat,
            vec(micro), vec(micro), vec(micro),
        ],
        out_specs=[flat, flat, flat, message_spec, vec(5 * micro)],
        out_shape=[
            own_bf, own_f32, own_bf,
            jax.ShapeDtypeStruct(message_shape, BF),
            jax.ShapeDtypeStruct((5 * micro, width), F32),
        ],
        scratch_shapes=[
            pltpu.VMEM((own, width), F32), pltpu.VMEM((own, width), F32),
            pltpu.VMEM((own, width), BF), pltpu.VMEM((own, width), BF),
        ],
        cost_estimate=pl.CostEstimate(
            flops=8 * own * width * ff, transcendentals=own * ff, bytes_accessed=4 * width * ff
        ),
        name="feed",
    )(gathered, gathered, gathered, expand_bias_f, reduce_bias_f, second, middle, attn, dy, gate1, gate2, c2)
    do_came = exchange(do_message)
    d_gate2, d_shift2, p2, d_gate1, dm_sums = [
        sums[i * micro : (i + 1) * micro] for i in range(5)
    ]

    flat_p = pl.BlockSpec((own, width), lambda i, p: (0, 0))
    feed_part, bias_part = pl.pallas_call(
        functools.partial(feed_weights_body, rows, blocks),
        grid_spec=pltpu.PrefetchScalarGridSpec(
            num_scalar_prefetch=1,
            grid=(1,),
            in_specs=[
                pl.BlockSpec((units, unit, width), lambda i, p: (0, folds + 1 + p[0], 0)),
                pl.BlockSpec((per, wide, width), lambda i, p: (p[0], 0, 0)),
                pl.BlockSpec((1, 1, width), lambda i, p: (p[0], 0, 0)),
                pl.BlockSpec((micro, width), lambda i, p: (0, 0)),
            ]
            + [flat_p] * (2 * groups),
            out_specs=[
                pl.BlockSpec((blocks, ff_rows + groups * gain_rows, width), lambda i, p: (0, 0, 0)),
                pl.BlockSpec((1, width), lambda i, p: (0, 0)),
            ],
        ),
        out_shape=[
            jax.ShapeDtypeStruct((blocks, ff_rows + groups * gain_rows, width), BF),
            jax.ShapeDtypeStruct((1, width), F32),
        ],
        cost_estimate=pl.CostEstimate(
            flops=10 * own * groups * width * width, transcendentals=own * ff, bytes_accessed=16 * width * width
        ),
        name="feed_weights",
    )(place, gathered, gathered, expand_bias_f, gate2, *second_group, *dy_group)
    do_came, feed_part = lax.optimization_barrier((do_came, feed_part))
    feed_half = halve(feed_part, BLK, block_id, 1)
    feed_sum = lax.psum_scatter(feed_half, "far", scatter_dimension=0, tiled=True)[0]

    if small_path:
        last_dq, last_kept, last_sent = pl.pallas_call(
            functools.partial(attend_last_back_body, blocks, groups, rows, stripe),
            in_specs=specs + [whole_vmem()] * 6,
            out_specs=[whole_vmem()] * 3,
            out_shape=[f32(devices * stripe, 128)] + [whole(blocks // 2, count, 128)] * 2,
            scratch_shapes=[pltpu.VMEM((span, 128), BF)]
            + [pltpu.VMEM((devices * stripe, 128), F32)] * 2
            + [pltpu.VMEM((size + KB - STEP, 64), F32)] * 2,
            cost_estimate=pl.CostEstimate(
                flops=size * size * 32, transcendentals=size * size // 8, bytes_accessed=16 * size * 64
            ),
            name="attend_last_back",
        )(*last_args, do_came, *last_saved)
        last_half = (last_kept.astype(F32) + pass_on(last_sent, 1).astype(F32)).astype(BF)
        do_came, last_dq = lax.optimization_barrier((do_came, last_dq))
        leaving = pl.pallas_call(
            functools.partial(attend_own_back_body, blocks, groups, rows, stripe),
            in_specs=specs + [whole_vmem()] * 7,
            out_specs=whole_vmem(),
            out_shape=whole(blocks, message_rows, 128),
            scratch_shapes=[
                pltpu.VMEM((span, 128), BF), pltpu.VMEM((span, 64), BF),
                pltpu.VMEM((devices, rows, 64), BF), pltpu.VMEM((size, 64), F32),
            ]
            + [pltpu.VMEM((size + KB - STEP, 64), F32)] * 2,
            cost_estimate=pl.CostEstimate(
                flops=2 * size * size * 64, transcendentals=size * size // 2, bytes_accessed=16 * size * 128
            ),
            name="attend_own_back",
        )(*own_args, do_came, *own_saved, last_dq)
    else:
        grads = attend_back(
            ranges, query, segment, lse, attended, do_came.reshape(size, head_width), key, value,
            segment[:, None], query_rows, key_block,
        )
        leaving = pl.pallas_call(
            functools.partial(rotate_out_body, blocks, extra),
            grid_spec=pltpu.PrefetchScalarGridSpec(
                num_scalar_prefetch=1,
                grid=(groups,),
                in_specs=[table_spec, table_spec] + [by_span] * parts,
                out_specs=[by_rows] * blocks,
                scratch_shapes=[pltpu.VMEM((span, lanes), BF)],
            ),
            out_shape=[jax.ShapeDtypeStruct((count, lanes), BF)] * blocks,
            name="rotate_out",
        )(place, cos_table, sin_table, *grads)
    if small_path:
        leaving, last_half = lax.optimization_barrier((leaving, last_half))
        back = [lax.all_to_all(leaving, BLK, split_axis=0, concat_axis=0, tiled=True)]
        back += [
            pass_on(lax.dynamic_index_in_dim(last_half, (block_id // 2) ^ k, 0, keepdims=False), 2 * k)
            if k
            else lax.dynamic_index_in_dim(last_half, block_id // 2, 0, keepdims=False)
            for k in range(blocks // 2)
        ]
    else:
        back = swap(leaving, BLK)
    leaving, merged, grad_attn = lax.optimization_barrier((leaving, merged, grad_attn))
    output_part = lax.dot_general(merged, grad_attn, TN, preferred_element_type=F32).astype(BF)
    output_part = output_part.reshape(groups, width // groups, width)

    output_part = swap(
        [
            lax.dynamic_index_in_dim(output_part, group_id ^ k, 0, keepdims=False)
            for k in range(groups)
        ],
        "ulysses",
    )

    output_part = sum(x.astype(F32) for x in output_part).astype(BF).reshape(blocks, gain_rows, width)

    if small_path:
        back_body = functools.partial(project_back_small_body, blocks, heads)
        back_scratch = [
            pltpu.VMEM((count, 64), F32), pltpu.VMEM((devices, gain_rows, heads * 3 * head_width), F32),
        ]
        back_args, back_specs = (place,), [smem]
        back_grads = [jax.ShapeDtypeStruct((blocks // 2, groups, gain_rows, heads * 3 * head_width), BF)] * 2
    else:
        back_args, back_specs = (place,), [smem]
        back_body = functools.partial(project_back_body, blocks, pairs, heads, extra)
        back_scratch = [pltpu.VMEM((blocks, count, lanes), BF)]
        back_grads = [jax.ShapeDtypeStruct((width, heads * 3 * head_width), BF)]
    returned = pl.pallas_call(
        back_body,
        out_shape=[jax.ShapeDtypeStruct((micro, rows, width), BF)] * groups
        + back_grads
        + [jax.ShapeDtypeStruct((micro, width), F32)] * 2,
        in_specs=back_specs + [whole_vmem()] * (3 + groups + len(back)),
        out_specs=[whole_vmem()] * (groups + 2 + len(back_grads)),
        scratch_shapes=back_scratch,
        cost_estimate=pl.CostEstimate(
            flops=4 * micro * count * width * 3 * 64 * heads, transcendentals=0, bytes_accessed=8 * own * width
        ),
        name="project_back",
    )(*back_args, c1, shift1, in_own, *n1_group, *back)
    *input_part, d_shift1, p1 = returned[groups:]
    grad_mods = jnp.concatenate(
        [d_shift1, p1 * gain1, d_gate1, d_shift2, p2 * gain2, d_gate2], 1
    )
    gain1_part = jnp.sum((1.0 + scale1) * p1, 0)
    gain2_part = jnp.sum((1.0 + scale2) * p2, 0)
    own_units = jnp.where(
        (jnp.arange(groups) == group_id)[:, None], bias_part.reshape(1, width), 0.0
    )
    small_parts = jnp.concatenate(
        [grad_mods.reshape(micro, devices, mod_rows).transpose(1, 0, 2).reshape(devices, -1)]
        + [
            x.reshape(devices, -1)
            for x in (gain1_part, gain2_part, jnp.sum(dm_sums, 0), own_units)
        ],
        1,
    ).astype(BF)
    taken = small_parts.shape[1]
    small_rows = 8 * -(-taken // (8 * in_lanes))
    small_parts = jnp.pad(small_parts, ((0, 0), (0, small_rows * in_lanes - taken)))
    if small_path:
        kept, sent = input_part
    else:
        halves = (
            input_part[0]
            .reshape(groups, blocks, gain_rows, in_lanes)
            .transpose(1, 0, 2, 3)
            .reshape(blocks // 2, 2, groups, gain_rows, in_lanes)
        )
        sent = lax.dynamic_index_in_dim(halves, 1 - block_id % 2, 1, keepdims=False)
        kept = lax.dynamic_index_in_dim(halves, block_id % 2, 1, keepdims=False)
    sent, token_parts = lax.optimization_barrier((sent, returned[:groups]))
    came = lax.ppermute(sent, BLK, [(i, i ^ 1) for i in range(blocks)])
    input_sum = (kept.astype(F32) + came.astype(F32)).astype(BF)
    token_parts = swap(token_parts, "ulysses")
    out_lanes = output_part.shape[1] * output_part.shape[2] // in_lanes
    rest = jnp.concatenate(
        [
            small_parts.reshape(groups, blocks, small_rows, in_lanes)
            .transpose(1, 0, 2, 3)
            .reshape(blocks, groups * small_rows, in_lanes),
            output_part.reshape(blocks, out_lanes, in_lanes),
        ],
        1,
    )
    rest = halve(rest, BLK, block_id, 1)
    input_sum, rest, feed_sum, token_parts = lax.optimization_barrier((input_sum, rest, feed_sum, token_parts))
    grad_first = sum(x.astype(F32) for x in token_parts)
    e = grad_first * c1[:, None]
    tokens_grad = (
        grad_middle.reshape(micro, rows, width)
        + r1
        * (
            e
            - jnp.mean(e, -1, keepdims=True)
            - n1 * jnp.mean(e * n1, -1, keepdims=True)
        )
    ).astype(BF)

    input_sum = jnp.concatenate(
        [input_sum.reshape(blocks // 2, groups * gain_rows, in_lanes), rest], 1
    )
    bit = 2
    while bit < blocks:
        input_sum = halve(input_sum, BLK, block_id, bit)
        if bit == 2:
            input_sum, feed_sum = lax.optimization_barrier((input_sum, feed_sum))
        bit *= 2
    input_sum = input_sum[0]
    at = groups * gain_rows
    small_sum = input_sum[at : at + groups * small_rows]
    output_grad = input_sum[at + groups * small_rows :].reshape(gain_rows, width).astype(F32)
    input_sum = jnp.concatenate(
        [input_sum[:at].reshape(groups, gain_rows, in_lanes), small_sum.reshape(groups, small_rows, in_lanes)], 1
    )
    final = jnp.stack(
        swap(
            [
                lax.dynamic_index_in_dim(input_sum, group_id ^ k, 0, keepdims=False)
                for k in range(groups)
            ],
            "ulysses",
        )
    )
    small_sum = jnp.sum(final[:, gain_rows:].astype(F32), 0).reshape(-1)
    input_sum = unscramble(final[:, :gain_rows], group_id, 0).astype(F32)
    reduce_grad = feed_sum[:ff_rows].astype(F32)
    expand_rows = feed_sum[ff_rows:].reshape(groups, gain_rows, width)
    expand_came = jnp.stack(
        swap(
            [
                lax.dynamic_index_in_dim(expand_rows, group_id ^ k, 0, keepdims=False)
                for k in range(groups)
            ],
            "ulysses",
        )
    )
    expand_grad = jnp.concatenate(
        [
            lax.dynamic_index_in_dim(expand_came, group_id ^ k, 0, keepdims=False)
            for k in range(groups)
        ],
        1,
    ).astype(F32)

    two = heads * 2 * head_width
    input_grad = jnp.concatenate(
        [
            input_sum[:, :, :two]
            .reshape(groups, gain_rows, heads, 2, head_width)
            .transpose(1, 3, 0, 2, 4)
            .reshape(gain_rows, 2 * width),
            input_sum[:, :, two:].transpose(1, 0, 2).reshape(gain_rows, width),
        ],
        1,
    )
    at = micro * mod_rows
    mod_sum = small_sum[:at].reshape(micro, mod_rows)
    modulate_weight_grad = jnp.sum(
        mod_sum[:, :, None] * condition.astype(F32)[:, None, :], 0
    )
    cuts = []
    for length in (gain_rows, gain_rows, gain_rows, ff_rows):
        cuts.append(small_sum[at : at + length])
        at += length
    return (
        layer_output.reshape(micro, rows, width),
        tokens_grad,
        modulate_weight_grad,
        jnp.sum(mod_sum, 0),
        cuts[0],
        input_grad,
        output_grad,
        cuts[1],
        expand_grad,
        cuts[3],
        reduce_grad,
        cuts[2],
    )


def solution(mesh):
    groups, blocks = mesh.devices.shape
    split = jax.sharding.Mesh(mesh.devices.reshape(groups, blocks // 2, 2), ALL)
    both = P(ALL)
    tall = P(ALL, None)
    seq = P(None, ALL, None)
    in_specs = (
        seq, seq, P(), P(), tall, both, both, tall, tall, both, tall, both, tall, both,
    )
    out_specs = (seq, seq, tall, both, both, tall, tall, both, tall, both, tall, both)
    return jax.shard_map(
        on_device, mesh=split, in_specs=in_specs, out_specs=out_specs, check_vma=False
    )
```

```python
import functools
import math

import jax
import jax.numpy as jnp
from jax import lax
from jax.experimental import pallas as pl
from jax.experimental.pallas import tpu as pltpu
from jax.sharding import PartitionSpec as P

HEADS = 12
BLK = ("far", "near")
ALL = ("ulysses", "far", "near")
BF = jnp.bfloat16
F32 = jnp.float32
NEG = -1e30


def axis_count(axis):
    return math.prod(lax.axis_size(name) for name in ((axis,) if isinstance(axis, str) else axis))


def exchange(x):
    return lax.all_to_all(x, ALL, split_axis=0, concat_axis=0, tiled=True)


def time_features(time_step, half):
    freqs = jnp.exp(-math.log(10000.0) * jnp.arange(half, dtype=F32) / half)
    angles = time_step.astype(F32)[:, None] * freqs[None, :]
    return jax.nn.silu(jnp.concatenate([jnp.cos(angles), jnp.sin(angles)], 1)).astype(BF)


def doc_layout(index, lengths_row):
    ends = jnp.cumsum(lengths_row)
    over = index[:, None] >= ends[None, :]
    segment = jnp.sum(over.astype(jnp.int32), 1)
    place = index - jnp.sum(jnp.where(over, lengths_row[None, :], 0), 1)
    return segment, place


def key_ranges(first, last, lengths_row, block):
    ends = jnp.cumsum(lengths_row)
    start = jnp.sum(jnp.where(first[:, None] >= ends[None, :], lengths_row[None, :], 0), 1)
    stop = jnp.min(jnp.where(ends[None, :] > last[:, None], ends[None, :], 1 << 30), 1)
    return jnp.stack([start // block, (stop + block - 1) // block], 1).reshape(-1)


def whole_vmem():
    return pl.BlockSpec(memory_space=pltpu.VMEM)


def swap(blocks, axis):
    size = axis_count(axis)
    return [
        x if k == 0 else lax.ppermute(x, axis, [(i, i ^ k) for i in range(size)])
        for k, x in enumerate(blocks)
    ]


def unscramble(x, index, axis):
    count, bit = x.shape[axis], 1
    while bit < count:
        shape = x.shape
        y = x.reshape(shape[:axis] + (count // (2 * bit), 2, bit) + shape[axis + 1 :])
        flipped = jnp.flip(y, axis + 1)
        x = jnp.where((index & bit) != 0, flipped, y).reshape(shape)
        bit *= 2
    return x


def halve(x, axis, index, bit):
    size = axis_count(axis)
    y = x.reshape((-1, 2) + x.shape[1:])
    mine = (index // bit) % 2
    sent = lax.dynamic_index_in_dim(y, 1 - mine, 1, keepdims=False)
    kept = lax.dynamic_index_in_dim(y, mine, 1, keepdims=False)
    came = lax.ppermute(sent, axis, [(i, i ^ bit) for i in range(size)])
    return (kept.astype(F32) + came.astype(F32)).astype(BF)


def project_body(blocks, pairs, heads, extra, place_ref, c_ref, shift_ref, w_ref, *refs):
    groups = len(refs) - blocks - 1
    tokens, outs, kept = refs[:groups], refs[groups:-1], refs[-1]
    micro, rows, width = tokens[0].shape
    end = 192 * heads
    weights = [w_ref[:, c : min(c + 128, end)] for c in range(0, end, 128)]
    order = list(range(micro))[::-1]
    z_qk = z_v = None
    for m in order:
        a = jnp.concatenate(
            [(x[m].astype(F32) * c_ref[m][None] + shift_ref[m][None]).astype(BF) for x in tokens], 0
        )
        parts = [jnp.dot(a, w, preferred_element_type=F32).astype(BF) for w in weights]
        v = jnp.concatenate(parts[heads:], 1)
        if extra and m == micro - 1:
            z_qk = parts[heads - 1]
            z_v = v[:, (heads - 1) * 64 : heads * 64]
        for h in range(heads):
            pair = m * heads + h
            if pair >= blocks:
                continue
            kept[pair, :, :128] = parts[h]
            own_v = v[:, h * 64 : (h + 1) * 64]
            if extra:
                kept[pair, :, 128:256] = z_qk
                kept[pair, :, 256:] = jnp.concatenate([own_v, z_v], 1)
            else:
                kept[pair, :, 128:] = jnp.concatenate([own_v, jnp.zeros_like(own_v)], 1)
    for pair in range(pairs, blocks):
        kept[pair] = jnp.zeros(kept.shape[1:], BF)
    for j in range(blocks):
        outs[j][...] = kept[place_ref[1] ^ j]


def turn_tables(cos, sin, extra):
    lane = lax.broadcasted_iota(jnp.int32, cos.shape, 1)
    low = lane < 64
    cos_r, sin_r = pltpu.roll(cos, 64, 1), pltpu.roll(sin, 64, 1)
    tables = [(jnp.where(low, cos, cos_r), jnp.where(low, sin, sin_r))]
    if extra:
        tables.append((jnp.where(low, cos_r, cos), jnp.where(low, sin_r, sin)))
    return tables


def turn(x, table):
    lane = lax.broadcasted_iota(jnp.int32, x.shape, 1)
    swapped = jnp.where(lane % 64 < 32, pltpu.roll(x, 96, 1), pltpu.roll(x, 32, 1))
    return x * table[0] + swapped * table[1]


def rotate_in_body(blocks, extra, place_ref, cos_ref, sin_ref, *refs):
    ins, outs = refs[:blocks], refs[blocks : 2 * blocks - blocks + (6 if extra else 3)]
    kept = refs[-1]
    rows = ins[0].shape[0]
    for j in range(blocks):
        at = pl.multiple_of((place_ref[1] ^ j) * rows, rows)
        kept[pl.ds(at, rows), :] = ins[j][...]
    tables = turn_tables(cos_ref[...], sin_ref[...], extra)
    x0 = turn(kept[:, :128].astype(F32), tables[0])
    outs[0][...] = (x0[:, :64] * 0.125).astype(BF)
    outs[1][...] = x0[:, 64:].astype(BF)
    if extra:
        outs[2][...] = kept[:, 256:320]
        x1 = turn(kept[:, 128:256].astype(F32), tables[1])
        outs[3][...] = (x1[:, :64] * 0.125).astype(BF)
        outs[4][...] = x1[:, 64:].astype(BF)
        outs[5][...] = kept[:, 320:]
    else:
        outs[2][...] = kept[:, 128:192]


def rotate_out_body(blocks, extra, place_ref, cos_ref, sin_ref, *refs):
    count = 6 if extra else 3
    ins, outs, kept = refs[:count], refs[count:-1], refs[-1]
    rows = outs[0].shape[0]
    parts = [ref[...].astype(F32) for ref in ins]
    tables = [(c, -s) for c, s in turn_tables(cos_ref[...], sin_ref[...], extra)]
    kept[:, :128] = turn(jnp.concatenate(parts[:2], 1), tables[0]).astype(BF)
    if extra:
        kept[:, 128:256] = turn(jnp.concatenate(parts[3:5], 1), tables[1]).astype(BF)
        kept[:, 256:] = jnp.concatenate([parts[2], parts[5]], 1).astype(BF)
    else:
        kept[:, 128:] = jnp.concatenate([parts[2], jnp.zeros_like(parts[2])], 1).astype(BF)
    for j in range(blocks):
        at = pl.multiple_of((place_ref[1] ^ j) * rows, rows)
        outs[j][...] = kept[pl.ds(at, rows), :]


def project_back_body(blocks, pairs, heads, extra, place_ref, c_ref, shift_ref, w_ref, *refs):
    kept = refs[-1]
    groups = (len(refs) - blocks - 4) // 2
    tokens, ins = refs[:groups], refs[groups : groups + blocks]
    outs = refs[groups + blocks : 2 * groups + blocks]
    grad_ref, sum_ref, dot_ref = refs[2 * groups + blocks : -1]
    micro, rows, width = tokens[0].shape
    count = groups * rows
    for j in range(blocks):
        kept[place_ref[1] ^ j] = ins[j][...]
    last = None
    if extra:
        last = jnp.zeros((count, 256), F32)
        for j in range(blocks):
            last = last + kept[j, :, 128:].astype(F32)
        last = last.astype(BF)
    all_a, all_g = [], []
    for m in range(micro):
        n = jnp.concatenate([x[m] for x in tokens], 0).astype(F32)
        a = (n * c_ref[m][None] + shift_ref[m][None]).astype(BF)
        qk, v = [], []
        for h in range(heads):
            pair = m * heads + h
            if pair < blocks:
                qk.append(kept[pair, :, :128])
                at = 256 if extra else 128
                v.append(kept[pair, :, at : at + 64])
            else:
                qk.append(last[:, :128])
                v.append(last[:, 192:])
        g = jnp.concatenate(qk + v, 1)
        da = lax.dot_general(g, w_ref[:, : 192 * heads], (((1,), (1,)), ((), ())), preferred_element_type=F32)
        for k in range(groups):
            outs[k][m] = da[k * rows : (k + 1) * rows].astype(BF)
        sum_ref[m : m + 1] = jnp.sum(da, 0, keepdims=True)
        dot_ref[m : m + 1] = jnp.sum(da * n, 0, keepdims=True)
        all_a.append(a)
        all_g.append(g)
    grad_ref[...] = lax.dot_general(
        jnp.concatenate(all_a, 0), jnp.concatenate(all_g, 0), (((0,), (0,)), ((), ())),
        preferred_element_type=F32,
    ).astype(BF)


def norm(values):
    centered = values - jnp.mean(values, -1, keepdims=True)
    inverse = lax.rsqrt(jnp.mean(centered * centered, -1, keepdims=True) + 1e-05)
    return centered * inverse, inverse


def by_micro(ref, rows):
    return jnp.concatenate(
        [jnp.broadcast_to(ref[m][None], (rows, ref.shape[1])) for m in range(ref.shape[0])], 0
    )


def middle_body(
    groups, blocks, heads, micro, rows, stripe,
    came_ref, out_ref, x_ref, gate_ref, c_ref, shift_ref,
    merged_ref, attn_ref, middle_ref, second_ref,
):
    width = x_ref.shape[1]
    for u in range(groups):
        for m in range(micro):
            for h in range(heads):
                pair = m * heads + h
                lanes = slice((u * heads + h) * 64, (u * heads + h + 1) * 64)
                half = rows // 2
                if pair < blocks and stripe:
                    at = m * rows
                    merged_ref[at : at + half, lanes] = came_ref[u * blocks + pair, :half, :64]
                    merged_ref[at + half : at + rows, lanes] = came_ref[u * blocks + pair, :half, 64:]
                elif pair < blocks:
                    merged_ref[m * rows : (m + 1) * rows, lanes] = came_ref[u * blocks + pair]
                else:
                    for b in range(blocks):
                        at = m * rows + b * stripe
                        merged_ref[at : at + stripe, lanes] = came_ref[u * blocks + b, half:, :64]
    attn = jnp.dot(merged_ref[...], out_ref[...].reshape(width, width), preferred_element_type=F32)
    attn_ref[...] = attn
    middle = x_ref[...].astype(F32) + by_micro(gate_ref, rows) * attn
    middle_ref[...] = middle
    normed, _ = norm(middle)
    second_ref[...] = (normed * by_micro(c_ref, rows) + by_micro(shift_ref, rows)).astype(BF)


def gelu_pair(u):
    t = jnp.tanh(0.7978845608028654 * (u + 0.044715 * u * u * u))
    value = 0.5 * u * (1.0 + t)
    slope = 0.5 * (1.0 + t) + 0.5 * u * (1.0 - t * t) * (
        0.7978845608028654 * (1.0 + 0.134145 * u * u)
    )
    return value, slope


NT = (((1,), (1,)), ((), ()))
TN = (((0,), (0,)), ((), ()))


def feed_body(
    groups, blocks, heads, micro, rows, stripe,
    ex_ref, re_ref, out_w_ref, ex_bias_ref, re_bias_ref, second_ref, middle_ref, attn_ref, dy_ref,
    gate1_ref, gate2_ref, c_ref,
    layer_ref, grad_ref, dattn_ref, do_ref, sums_ref,
    branch_sum, back_sum, dm_sum, do_sum,
):
    step = pl.program_id(0)
    width = middle_ref.shape[1]

    @pl.when(step == 0)
    def _():
        branch_sum[...] = jnp.zeros_like(branch_sum)
        back_sum[...] = jnp.zeros_like(back_sum)
        dm_sum[...] = (by_micro(gate2_ref, rows) * dy_ref[...].astype(F32)).astype(BF)

    expand = ex_ref[...].reshape(width, width)
    reduce = re_ref[...].reshape(width, width)
    u = jnp.dot(second_ref[...], expand, preferred_element_type=F32) + ex_bias_ref[0]
    g, slope = gelu_pair(u)
    branch_sum[...] += jnp.dot(g.astype(BF), reduce, preferred_element_type=F32)
    dg = lax.dot_general(dm_sum[...], reduce, NT, preferred_element_type=F32)
    du = (dg * slope).astype(BF)
    back_sum[...] += lax.dot_general(du, expand, NT, preferred_element_type=F32)

    @pl.when(step == pl.num_programs(0) - 1)
    def _():
        def total(at, x):
            for m in range(micro):
                sums_ref[at * micro + m : at * micro + m + 1] = jnp.sum(
                    x[m * rows : (m + 1) * rows], 0, keepdims=True
                )

        branch = branch_sum[...] + re_bias_ref[...]
        middle = middle_ref[...]
        dy = dy_ref[...].astype(F32)
        layer_ref[...] = (middle + by_micro(gate2_ref, rows) * branch).astype(BF)
        total(0, dy * branch)
        normed, inverse = norm(middle)
        db = back_sum[...]
        total(1, db)
        total(2, db * normed)
        e = db * by_micro(c_ref, rows)
        grad = dy + inverse * (
            e
            - jnp.mean(e, -1, keepdims=True)
            - normed * jnp.mean(e * normed, -1, keepdims=True)
        )
        grad_ref[...] = grad
        total(3, grad * attn_ref[...])
        total(4, dm_sum[...].astype(F32))
        dattn = (by_micro(gate1_ref, rows) * grad).astype(BF)
        dattn_ref[...] = dattn
        do_sum[...] = lax.dot_general(
            dattn, out_w_ref[...].reshape(width, width), NT, preferred_element_type=F32
        ).astype(BF)
        for at in range(groups):
            for m in range(micro):
                for h in range(heads):
                    pair = m * heads + h
                    lanes = slice((at * heads + h) * 64, (at * heads + h + 1) * 64)
                    half, top = rows // 2, m * rows
                    if pair < blocks and stripe:
                        do_ref[at * blocks + pair, :half, :64] = do_sum[top : top + half, lanes]
                        do_ref[at * blocks + pair, :half, 64:] = do_sum[top + half : top + rows, lanes]
                    elif pair < blocks:
                        do_ref[at * blocks + pair] = do_sum[top : top + rows, lanes]
                    else:
                        for b in range(blocks):
                            do_ref[at * blocks + b, half:, :64] = do_sum[top : top + stripe, lanes]
                            do_ref[at * blocks + b, half:, 64:] = jnp.zeros((stripe, 64), BF)
                            top += stripe
            for b in range(micro * heads, blocks):
                do_ref[at * blocks + b] = jnp.zeros((rows, 64), BF)


def feed_weights_body(rows, blocks, place_ref, ex_ref, re_ref, bias_ref, gate_ref, *refs):
    groups = (len(refs) - 4) // 2
    keep_ref, send_ref, sum_ref, out_ref = refs[2 * groups :]
    width = refs[0].shape[-1]
    second = jnp.concatenate([x[...] for x in refs[:groups]], 0)
    gate = by_micro(gate_ref, rows)
    dm = jnp.concatenate(
        [(gate * x[...].astype(F32)).astype(BF) for x in refs[groups : 2 * groups]], 0
    )
    expand = ex_ref[...].reshape(width, width)
    reduce = re_ref[...].reshape(width, width)
    u = jnp.dot(second, expand, preferred_element_type=F32) + bias_ref[0]
    g, slope = gelu_pair(u)
    du = lax.dot_general(dm, reduce, NT, preferred_element_type=F32) * slope
    du = du.astype(BF)
    sum_ref[...] = jnp.sum(du.astype(F32), 0, keepdims=True)
    per, each = width // blocks, width // (groups * blocks)
    x = lax.dot_general(g.astype(BF), dm, TN, preferred_element_type=F32)
    for b in range(blocks):
        out_ref[b, :per] = x[b * per : (b + 1) * per].astype(BF)
    x = lax.dot_general(second, du, TN, preferred_element_type=F32)
    for k in range(groups):
        for b in range(blocks):
            at = (k * blocks + b) * each
            out_ref[b, per + k * each : per + (k + 1) * each] = x[at : at + each].astype(BF)
    mine = place_ref[1] & 1
    for z in range(blocks // 2):
        keep_ref[z] = out_ref[2 * z + mine]
        send_ref[z] = out_ref[2 * z + 1 - mine]


def attend_body(block, range_ref, q_ref, sq_ref, k_ref, v_ref, sk_ref, o_ref, lse_ref):
    i = pl.program_id(0)
    q, sq = q_ref[...], sq_ref[0]
    count, width = q.shape

    def step(j, carry):
        high, total, acc = carry
        at = pl.ds(pl.multiple_of(j * block, block), block)
        k, v, sk = k_ref[at, :], v_ref[at, :], sk_ref[at, :]
        s = lax.dot_general(k, q, (((1,), (1,)), ((), ())), preferred_element_type=F32)
        s = jnp.where(sk == sq, s, NEG)
        new = jnp.maximum(high, jnp.max(s, 0, keepdims=True))
        p = jnp.exp(s - new)
        fix = jnp.exp(high - new)
        total = total * fix + jnp.sum(p, 0, keepdims=True)
        acc = acc * fix + lax.dot_general(
            v, p.astype(BF), (((0,), (0,)), ((), ())), preferred_element_type=F32
        )
        return new, total, acc

    first = (
        jnp.full((1, count), NEG, F32),
        jnp.zeros((1, count), F32),
        jnp.zeros((width, count), F32),
    )
    high, total, acc = lax.fori_loop(range_ref[2 * i], range_ref[2 * i + 1], step, first)
    o_ref[...] = (acc / total).T.astype(BF)
    lse_ref[0] = high + jnp.log(total)


def attend_back_body(
    block, range_ref, q_ref, sq_ref, lse_ref, o_ref, do_ref, k_ref, v_ref, sk_ref,
    dq_ref, dk_ref, dv_ref, dk_sum, dv_sum,
):
    i = pl.program_id(0)

    @pl.when(i == 0)
    def _():
        dk_sum[...] = jnp.zeros_like(dk_sum)
        dv_sum[...] = jnp.zeros_like(dv_sum)

    q, sq, lse, do = q_ref[...], sq_ref[0], lse_ref[0], do_ref[...]
    count, width = q.shape
    delta = jnp.sum((do.astype(F32) * o_ref[...].astype(F32)).T, 0, keepdims=True)

    def step(j, dq):
        at = pl.ds(pl.multiple_of(j * block, block), block)
        k, v, sk = k_ref[at, :], v_ref[at, :], sk_ref[at, :]
        s = lax.dot_general(k, q, (((1,), (1,)), ((), ())), preferred_element_type=F32)
        p = jnp.where(sk == sq, jnp.exp(s - lse), 0.0)
        dp = lax.dot_general(v, do, (((1,), (1,)), ((), ())), preferred_element_type=F32)
        ds = (p * (dp - delta)).astype(BF)
        dv_sum[at, :] += jnp.dot(p.astype(BF), do, preferred_element_type=F32)
        dk_sum[at, :] += jnp.dot(ds, q, preferred_element_type=F32)
        return dq + lax.dot_general(
            k, ds, (((0,), (0,)), ((), ())), preferred_element_type=F32
        )

    dq = lax.fori_loop(
        range_ref[2 * i], range_ref[2 * i + 1], step, jnp.zeros((width, count), F32)
    )
    dq_ref[...] = (dq * 0.125).T.astype(BF)

    @pl.when(i == pl.num_programs(0) - 1)
    def _():
        dk_ref[...] = dk_sum[...].astype(BF)
        dv_ref[...] = dv_sum[...].astype(BF)


def attend(ranges, q, sq, k, v, sk, rows, block):
    count, width = q.shape
    steps = count // rows
    size = k.shape[0]
    by_row = pl.BlockSpec((rows, width), lambda i, r: (i, 0))
    as_row = pl.BlockSpec((1, 1, rows), lambda i, r: (i, 0, 0))
    return pl.pallas_call(
        functools.partial(attend_body, block),
        grid_spec=pltpu.PrefetchScalarGridSpec(
            num_scalar_prefetch=1,
            grid=(steps,),
            in_specs=[by_row, as_row, whole_vmem(), whole_vmem(), whole_vmem()],
            out_specs=[by_row, as_row],
        ),
        out_shape=[
            jax.ShapeDtypeStruct((count, width), BF),
            jax.ShapeDtypeStruct((steps, 1, rows), F32),
        ],
        cost_estimate=pl.CostEstimate(
            flops=count * size * width, transcendentals=count * size // 4, bytes_accessed=4 * size * width
        ),
        name="attend",
    )(ranges, q, sq.reshape(steps, 1, rows), k, v, sk)


def attend_back(ranges, q, sq, lse, o, do, k, v, sk, rows, block):
    count, width = q.shape
    steps = count // rows
    size = k.shape[0]
    by_row = pl.BlockSpec((rows, width), lambda i, r: (i, 0))
    as_row = pl.BlockSpec((1, 1, rows), lambda i, r: (i, 0, 0))
    return pl.pallas_call(
        functools.partial(attend_back_body, block),
        grid_spec=pltpu.PrefetchScalarGridSpec(
            num_scalar_prefetch=1,
            grid=(steps,),
            in_specs=[by_row, as_row, as_row, by_row, by_row, whole_vmem(), whole_vmem(), whole_vmem()],
            out_specs=[by_row, whole_vmem(), whole_vmem()],
            scratch_shapes=[pltpu.VMEM((size, width), F32)] * 2,
        ),
        out_shape=[
            jax.ShapeDtypeStruct((count, width), BF),
            jax.ShapeDtypeStruct((size, width), BF),
            jax.ShapeDtypeStruct((size, width), BF),
        ],
        cost_estimate=pl.CostEstimate(
            flops=3 * count * size * width, transcendentals=count * size // 4, bytes_accessed=8 * size * width
        ),
        name="attend_back",
    )(ranges, q, sq.reshape(steps, 1, rows), lse, o, do, k, v, sk)


def spread(ref, at, rows):
    return ref[pl.ds(pl.multiple_of(at, rows), rows), :]


def keys_mask(low, high, at, count):
    position = at + lax.broadcasted_iota(jnp.int32, (count, low.shape[1]), 0)
    return (position >= low) & (position < high)


QB, KB, STEP = 512, 512, 256


def project_small_body(blocks, heads, c_ref, shift_ref, w_ref, *refs):
    groups = len(refs) - 3
    tokens, out_ref, last_ref, wide = refs[:groups], *refs[groups:]
    micro, rows, width = tokens[0].shape
    count = groups * rows
    half, stripe = count // 2, rows // blocks
    end = 192 * heads
    weights = [w_ref[:, c : min(c + 128, end)] for c in range(0, end, 128)]
    for m in range(micro):
        a = jnp.concatenate(
            [(x[m].astype(F32) * c_ref[m][None] + shift_ref[m][None]).astype(BF) for x in tokens], 0
        )
        parts = [jnp.dot(a, w, preferred_element_type=F32) for w in weights]
        v = jnp.concatenate(parts[heads:], 1)
        for h in range(heads):
            pair = m * heads + h
            own_v = v[:, h * 64 : (h + 1) * 64]
            if pair < blocks:
                out_ref[pair, :count] = parts[h].astype(BF)
                out_ref[pair, count : count + half] = jnp.concatenate([own_v[:half], own_v[half:]], 1).astype(BF)
            else:
                wide[...] = parts[h]
                last_ref[...] = jnp.concatenate([parts[h][:, 64:], own_v], 1).astype(BF)
    for to in range(blocks):
        pieces = [
            wide[k * rows + to * stripe : k * rows + (to + 1) * stripe, :64] for k in range(groups)
        ]
        out_ref[to, count + half :] = jnp.concatenate(
            [jnp.concatenate(pieces[:2], 0), jnp.concatenate(pieces[2:], 0)], 1
        ).astype(BF)


def pick_piece(x, k):
    y = jnp.where((k & 1) != 0, x[8:], x[:8])
    return jnp.where(k >= 2, y[:, 64:], y[:, :64])


def project_back_small_body(blocks, heads, place_ref, c_ref, shift_ref, w_ref, *refs):
    wide, scattered = refs[-2:]
    few = blocks // 2
    groups = (len(refs) - few - 7) // 2
    tokens, in_ref, lasts = refs[:groups], refs[groups], refs[groups + 1 : groups + 1 + few]
    outs = refs[groups + 1 + few : 2 * groups + 1 + few]
    keep_ref, send_ref, sum_ref, dot_ref = refs[2 * groups + 1 + few : -2]
    micro, rows, width = tokens[0].shape
    count = groups * rows
    half, stripe = count // 2, rows // blocks
    for j in range(blocks):
        x = in_ref[j, count + half :].astype(F32)
        pieces = [x[:8, :64], x[8:, :64], x[:8, 64:], x[8:, 64:]]
        for k in range(groups):
            wide[k * rows + j * stripe : k * rows + (j + 1) * stripe] = pieces[k]
    all_a, all_g = [], []
    for m in range(micro):
        n = jnp.concatenate([x[m] for x in tokens], 0).astype(F32)
        a = (n * c_ref[m][None] + shift_ref[m][None]).astype(BF)
        qk, v = [], []
        for h in range(heads):
            pair = m * heads + h
            if pair < blocks:
                qk.append(in_ref[pair, :count])
                x = in_ref[pair, count : count + half]
                v.append(jnp.concatenate([x[:, :64], x[:, 64:]], 0))
            else:
                x = sum(ref[...].astype(F32) for ref in lasts).astype(BF)
                qk.append(jnp.concatenate([wide[...].astype(BF), x[:, :64]], 1))
                v.append(x[:, 64:])
        g = jnp.concatenate(qk + v, 1)
        da = lax.dot_general(g, w_ref[:, : 192 * heads], NT, preferred_element_type=F32)
        for k in range(groups):
            outs[k][m] = da[k * rows : (k + 1) * rows].astype(BF)
        sum_ref[m : m + 1] = jnp.sum(da, 0, keepdims=True)
        dot_ref[m : m + 1] = jnp.sum(da * n, 0, keepdims=True)
        all_a.append(a)
        all_g.append(g)
    x = lax.dot_general(
        jnp.concatenate(all_a, 0), jnp.concatenate(all_g, 0), TN, preferred_element_type=F32
    )
    scattered[...] = x.reshape(scattered.shape)
    mine = place_ref[1] & 1
    for z in range(few):
        for k in range(groups):
            at = k * blocks + 2 * z
            keep_ref[z, k] = scattered[at + mine].astype(BF)
            send_ref[z, k] = scattered[at + 1 - mine].astype(BF)


def attend_block(scores, q, low, high, first, stop, keys, values):
    count = q.shape[0]

    def score(t, top):
        at = pl.multiple_of((first + 2 * t) * STEP, STEP)
        s = lax.dot_general(keys[pl.ds(at, KB), :], q, NT, preferred_element_type=F32)
        s = jnp.where(keys_mask(low, high, at, KB), s, NEG)
        scores[t, :, :count] = s
        return jnp.maximum(top, jnp.max(s, 0, keepdims=True))

    steps = (stop - first + 1) // 2
    top = lax.fori_loop(0, steps, score, jnp.full((1, count), NEG, F32))

    def weigh(t, carry):
        total, acc = carry
        at = pl.multiple_of((first + 2 * t) * STEP, STEP)
        p = jnp.exp(scores[t, :, :count] - top)
        return total + jnp.sum(p, 0, keepdims=True), acc + lax.dot_general(
            values[pl.ds(at, KB), :], p.astype(BF), TN, preferred_element_type=F32
        )

    total, acc = lax.fori_loop(
        0, steps, weigh, (jnp.zeros((1, count), F32), jnp.zeros((64, count), F32))
    )
    return (acc / total).T, top + jnp.log(total)


def attend_own_body(
    blocks, groups, rows, place_ref, range_ref, low_ref, high_ref, cos_ref, sin_ref, *refs
):
    in_ref, message, q_ref, k_ref, v_ref, o_ref, lse_ref, kept, kept_v, scores = refs
    span = blocks * rows
    size = groups * span
    count = groups * rows
    half = rows // 2
    me_u, me_b = place_ref[0], place_ref[1]
    for g in range(groups):
        k = me_u ^ g
        for j in range(blocks):
            to = slice(j * rows, (j + 1) * rows)
            kept[to, :] = in_ref[j, pl.ds(pl.multiple_of(k * rows, rows), rows), :]
            pair = in_ref[j, pl.ds(pl.multiple_of(count + (k & 1) * rows, rows), rows), :].astype(F32)
            kept_v[to, :] = jnp.where(k >= 2, pair[:, 64:], pair[:, :64]).astype(BF)
        at = slice(g * span, (g + 1) * span)
        x = turn(kept[...].astype(F32), turn_tables(cos_ref[at], sin_ref[at], False)[0])
        q_ref[at] = (x[:, :64] * 0.125).astype(BF)
        k_ref[at] = x[:, 64:].astype(BF)
        v_ref[at] = kept_v[...]
    tail = slice(size, size + KB - STEP)
    for ref in (k_ref, v_ref):
        ref[tail] = jnp.zeros((KB - STEP, 64), BF)

    def run(i, _):
        o, lse = attend_block(
            scores, spread(q_ref, i * QB, QB), low_ref[i], high_ref[i],
            range_ref[2 * i], range_ref[2 * i + 1], k_ref, v_ref,
        )
        o = o.astype(BF)
        o_ref[pl.ds(pl.multiple_of(i * QB, QB), QB), :] = o
        lse_ref[i] = lse
        for d in range(QB // rows):
            message[i * (QB // rows) + d] = jnp.concatenate(
                [o[d * rows : d * rows + half], o[d * rows + half : (d + 1) * rows]], 1
            )
        return 0

    lax.fori_loop(0, size // QB, run, 0)


def stripe_tables(place_ref, cos_ref, sin_ref, wide_cos, wide_sin, devices, rows, stripe):
    for d in range(devices):
        at = slice(d * stripe, (d + 1) * stripe)
        wide_cos[at] = spread(cos_ref, d * rows + place_ref[1] * stripe, stripe)
        wide_sin[at] = spread(sin_ref, d * rows + place_ref[1] * stripe, stripe)
    return turn_tables(wide_cos[...], wide_sin[...], True)[1]


def attend_last_body(
    blocks, groups, rows, stripe, place_ref, range_ref, low_ref, high_ref, cos_ref, sin_ref, *refs
):
    in_ref, last_ins, own_ref = refs[0], refs[1:3], refs[3]
    message, q_ref, k_ref, v_ref, o_ref, lse_ref, kept, wide, wide_cos, wide_sin, scores = refs[4:]
    span = blocks * rows
    size = groups * span
    devices = groups * blocks
    count = groups * rows
    half = rows // 2
    me_u, me_b = place_ref[0], place_ref[1]
    for g in range(groups):
        k = me_u ^ g
        for j in range(blocks):
            at = (g * blocks + j) * stripe
            wide[at : at + stripe, :64] = pick_piece(in_ref[j, count + count // 2 :].astype(F32), k)
            to = pl.ds(pl.multiple_of((me_b ^ j) * rows, rows), rows)
            kept[to, :] = last_ins[j & 1][j >> 1, pl.ds(pl.multiple_of(k * rows, rows), rows), :]
        at = slice(g * span, (g + 1) * span)
        x = turn(kept[...].astype(F32), turn_tables(cos_ref[at], sin_ref[at], True)[1])
        k_ref[at] = x[:, :64].astype(BF)
        v_ref[at] = kept[:, 64:]
    tail = slice(size, size + KB - STEP)
    for ref in (k_ref, v_ref):
        ref[tail] = jnp.zeros((KB - STEP, 64), BF)
    wide[:, 64:] = jnp.zeros((devices * stripe, 64), F32)
    x = turn(wide[...], stripe_tables(place_ref, cos_ref, sin_ref, wide_cos, wide_sin, devices, rows, stripe))
    q_ref[...] = (x[:, :64] * 0.125).astype(BF)
    message[:, :half] = own_ref[...]
    few = lse_ref.shape[2]

    def run(i, _):
        o, lse = attend_block(
            scores, spread(q_ref, i * few, few), low_ref[i], high_ref[i],
            range_ref[2 * i], range_ref[2 * i + 1], k_ref, v_ref,
        )
        o_ref[pl.ds(pl.multiple_of(i * few, few), few), :] = o.astype(BF)
        lse_ref[i] = lse
        o = jnp.concatenate([o, jnp.zeros_like(o)], 1)
        for d in range(few // stripe):
            message[i * (few // stripe) + d, half:] = o[d * stripe : (d + 1) * stripe].astype(BF)
        return 0

    lax.fori_loop(0, lse_ref.shape[0], run, 0)


def attend_block_back(q, do, o, lse, low, high, first, stop, keys, values, dk_sum, dv_sum):
    count = q.shape[0]
    delta = jnp.sum((do.astype(F32) * o.astype(F32)).T, 0, keepdims=True)

    def step(t, dq):
        at = pl.multiple_of((first + 2 * t) * STEP, STEP)
        here = pl.ds(at, KB)
        k, v = keys[here, :], values[here, :]
        s = lax.dot_general(k, q, NT, preferred_element_type=F32)
        dp = lax.dot_general(v, do, NT, preferred_element_type=F32)
        p = jnp.where(keys_mask(low, high, at, KB), jnp.exp(s - lse), 0.0)
        ds = (p * (dp - delta)).astype(BF)
        dv_sum[here, :] += jnp.dot(p.astype(BF), do, preferred_element_type=F32)
        dk_sum[here, :] += jnp.dot(ds, q, preferred_element_type=F32)
        return dq + lax.dot_general(k, ds, TN, preferred_element_type=F32)

    return (
        lax.fori_loop(0, (stop - first + 1) // 2, step, jnp.zeros((64, count), F32)) * 0.125
    ).T


def attend_last_back_body(
    blocks, groups, rows, stripe, place_ref, range_ref, low_ref, high_ref, cos_ref, sin_ref,
    do_ref, q_ref, k_ref, v_ref, o_ref, lse_ref, dq_ref, keep_ref, send_ref, kept, wide_cos, wide_sin, dk, dv,
):
    span = blocks * rows
    devices = groups * blocks
    half = rows // 2
    for ref in (dk, dv):
        ref[...] = jnp.zeros(ref.shape, F32)
    few = lse_ref.shape[2]
    dq_ref[:, 64:] = jnp.zeros((devices * stripe, 64), F32)

    def run(i, _):
        came = [
            do_ref[i * (few // stripe) + d].astype(F32)[half:, :64] for d in range(few // stripe)
        ]
        at = pl.ds(pl.multiple_of(i * few, few), few)
        dq_ref[at, :64] = attend_block_back(
            q_ref[at, :], jnp.concatenate(came, 0).astype(BF), o_ref[at, :], lse_ref[i],
            low_ref[i], high_ref[i], range_ref[2 * i], range_ref[2 * i + 1], k_ref, v_ref, dk, dv,
        )
        return 0

    lax.fori_loop(0, lse_ref.shape[0], run, 0)
    cos, sin = stripe_tables(place_ref, cos_ref, sin_ref, wide_cos, wide_sin, devices, rows, stripe)
    dq_ref[...] = turn(dq_ref[...], (cos, -sin))
    for g in range(groups):
        at = slice(g * span, (g + 1) * span)
        k = place_ref[0] ^ g
        cos, sin = turn_tables(cos_ref[at], sin_ref[at], True)[1]
        x = turn(jnp.concatenate([dk[at], jnp.zeros_like(dk[at])], 1), (cos, -sin))[:, :64]
        kept[...] = jnp.concatenate([x, dv[at]], 1).astype(BF)
        to = pl.ds(pl.multiple_of(k * rows, rows), rows)
        for z in range(blocks // 2):
            mine = 2 * z + (place_ref[1] & 1)
            keep_ref[z, to, :] = spread(kept, mine * rows, rows)
            send_ref[z, to, :] = spread(kept, (mine ^ 1) * rows, rows)


def attend_own_back_body(
    blocks, groups, rows, stripe, place_ref, range_ref, low_ref, high_ref, cos_ref, sin_ref,
    do_ref, q_ref, k_ref, v_ref, o_ref, lse_ref, last_dq_ref, out_ref, kept, kept_v, wide_v, dq, dk, dv,
):
    span = blocks * rows
    size = groups * span
    count = groups * rows
    half = rows // 2
    me_u, me_b = place_ref[0], place_ref[1]
    for ref in (dk, dv):
        ref[...] = jnp.zeros(ref.shape, F32)

    def run(i, _):
        came = []
        for d in range(QB // rows):
            x = do_ref[i * (QB // rows) + d]
            came += [x[:half, :64], x[:half, 64:]]
        at = pl.ds(pl.multiple_of(i * QB, QB), QB)
        dq[at, :] = attend_block_back(
            q_ref[at, :], jnp.concatenate(came, 0), o_ref[at, :], lse_ref[i], low_ref[i], high_ref[i],
            range_ref[2 * i], range_ref[2 * i + 1], k_ref, v_ref, dk, dv,
        )
        return 0

    lax.fori_loop(0, size // QB, run, 0)
    for g in range(groups):
        at = slice(g * span, (g + 1) * span)
        k = me_u ^ g
        cos, sin = turn_tables(cos_ref[at], sin_ref[at], False)[0]
        kept[...] = turn(jnp.concatenate([dq[at], dk[at]], 1), (cos, -sin)).astype(BF)
        kept_v[...] = dv[at].astype(BF)
        for b in range(blocks):
            out_ref[b, pl.ds(pl.multiple_of(k * rows, rows), rows), :] = kept[b * rows : (b + 1) * rows]
        for b in range(blocks):
            wide_v[g * blocks + b] = kept_v[b * rows : (b + 1) * rows]
    for to in range(blocks):
        v = [wide_v[(me_u ^ k) * blocks + to] for k in range(groups)]
        out_ref[to, count : count + count // 2] = jnp.concatenate(
            [jnp.concatenate(v[:2], 0), jnp.concatenate(v[2:], 0)], 1
        )
        z = [spread(last_dq_ref, ((me_u ^ k) * blocks + to) * stripe, stripe)[:, :64] for k in range(groups)]
        out_ref[to, count + count // 2 :] = jnp.concatenate(
            [jnp.concatenate(z[:2], 0), jnp.concatenate(z[2:], 0)], 1
        ).astype(BF)


def on_device(
    tokens,
    cotangent,
    lengths,
    time_step,
    modulate_weight,
    modulate_bias,
    attend_gain,
    input_weight,
    output_weight,
    feed_gain,
    expand_weight,
    expand_bias,
    reduce_weight,
    reduce_bias,
):
    groups, blocks = axis_count("ulysses"), axis_count(BLK)
    group_id, block_id = lax.axis_index("ulysses"), lax.axis_index(BLK)
    devices = groups * blocks
    micro, rows, width = tokens.shape
    own = micro * rows
    size = devices * rows
    head_width = width // HEADS
    heads = HEADS // groups
    pairs = micro * heads
    extra = pairs > blocks
    lanes = 384 if extra else 256
    stripe = rows // blocks if extra else 0
    mod_rows = modulate_weight.shape[0]
    gain_rows = attend_gain.shape[0]
    ff_rows = expand_bias.shape[0]
    ff = ff_rows * devices
    folds = ff // width
    assert pairs <= blocks + 1 and head_width == 64 and folds == groups and heads == 3
    place = jnp.stack([group_id, block_id]).astype(jnp.int32)
    pair_micro = jnp.minimum(block_id // heads, micro - 1)

    in_split = input_weight.reshape(gain_rows, 3, groups, heads, head_width)
    in_split = jnp.concatenate(
        [
            in_split[:, :2].transpose(2, 0, 3, 1, 4).reshape(groups, 1, gain_rows, -1),
            in_split[:, 2].transpose(1, 0, 2, 3).reshape(groups, 1, gain_rows, -1),
        ],
        3,
    )
    in_lanes = heads * 3 * head_width

    condition = time_features(time_step, modulate_weight.shape[1] // 2)
    mod_own = jnp.einsum(
        "mc,fc->mf", condition, modulate_weight, preferred_element_type=F32
    ) + modulate_bias.astype(F32)
    mod_lanes = 64 * -(-mod_rows // 64)
    mod_own = jnp.pad(mod_own, ((0, 0), (0, mod_lanes - mod_rows))).reshape(-1, 64)
    mod_high = lax.reduce_precision(mod_own, 8, 7)
    mod_size = mod_own.shape[0]
    vectors = jnp.pad(
        jnp.stack([attend_gain, feed_gain, reduce_bias]), ((0, 0), (0, 64 - gain_rows))
    )
    ff_lanes = 64 * -(-ff_rows // 64)
    small = jnp.concatenate(
        [
            mod_high.astype(BF),
            (mod_own - mod_high).astype(BF),
            vectors,
            jnp.pad(expand_bias, (0, ff_lanes - ff_rows)).reshape(-1, 64),
        ],
        0,
    )
    small_lanes = 64 * -(-small.shape[0] // gain_rows)
    small = jnp.pad(small, ((0, small_lanes * gain_rows // 64 - small.shape[0]), (0, 0)))
    small = small.reshape(1, 1, gain_rows, small_lanes)
    in_message = jnp.concatenate(
        [
            jnp.broadcast_to(in_split, (groups, blocks) + in_split.shape[2:]),
            jnp.broadcast_to(small, (groups, blocks) + small.shape[2:]),
        ],
        3,
    ).reshape(devices, gain_rows, in_lanes + small_lanes)
    in_message, tokens, lengths = lax.optimization_barrier((in_message, tokens, lengths))
    came = exchange(in_message)
    values = tokens.astype(F32)
    n1, r1 = norm(values)
    n1_b = n1.astype(BF)
    n1_group = swap([n1_b] * groups, "ulysses")
    small_all = came[:, :, in_lanes:].reshape(devices, -1, 64)
    in_own = came.reshape(width, in_lanes + small_lanes)

    weight_pack = jnp.concatenate(
            [
                reduce_weight,
                output_weight,
                expand_weight.reshape(gain_rows, folds, width).transpose(1, 0, 2).reshape(-1, width),
            ],
            0,
        )
    index = jnp.arange(size, dtype=jnp.int32)
    pair_lengths = lax.dynamic_index_in_dim(lengths, pair_micro, 0, keepdims=False)
    segment, position = doc_layout(index, pair_lengths)
    last_lengths = lengths[micro - 1]
    last_segment, last_position = doc_layout(index, last_lengths)
    half = head_width // 2
    freqs = jnp.exp(-math.log(10000.0) * jnp.arange(half, dtype=F32) / half)
    lane = jnp.arange(128)
    angles = jnp.where(
        (lane < 64)[None, :], position.astype(F32)[:, None], last_position.astype(F32)[:, None]
    ) * jnp.tile(freqs, 4)[None, :]
    cos_table = jnp.cos(angles)
    sin_table = jnp.where((lane % 64 < 32)[None, :], -1.0, 1.0) * jnp.sin(angles)
    query_rows = math.gcd(size, QB)
    key_block = math.gcd(size, 256)
    first = jnp.arange(size // query_rows, dtype=jnp.int32) * query_rows
    ranges = key_ranges(first, first + query_rows - 1, pair_lengths, key_block)
    small_path = extra and size % KB == 0 and rows == 64 and stripe == 8 and groups == 4 and size <= 4096

    striped = lambda x: lax.dynamic_slice_in_dim(
        x.reshape((devices, rows) + x.shape[1:]), block_id * stripe, stripe, 1
    ).reshape((devices * stripe,) + x.shape[1:])
    last_ranges = bounds = 0
    if small_path:
        last_rows = min(256, devices * stripe)
        chunk = last_rows // stripe
        last_first = jnp.arange(devices // chunk, dtype=jnp.int32) * (chunk * rows) + block_id * stripe
        last_ranges = key_ranges(
            last_first, last_first + (chunk - 1) * rows + stripe - 1, last_lengths, STEP
        )
        bounds = []
        for where, lens, pick, lump in (
            (position, pair_lengths, lambda x: x, QB),
            (last_position, last_lengths, striped, last_rows),
        ):
            low = index - where
            ends = jnp.cumsum(lens)
            high = jnp.min(jnp.where(ends[None, :] > index[:, None], ends[None, :], 1 << 30), 1)
            bounds += [pick(low).reshape(-1, 1, lump), pick(high).reshape(-1, 1, lump)]
    in_own, small_all, n1_group, place, cos_table, sin_table, ranges, last_ranges, bounds = (
        lax.optimization_barrier(
            (in_own, small_all, n1_group, place, cos_table, sin_table, ranges, last_ranges, bounds)
        )
    )
    weight_pack, in_own = lax.optimization_barrier((weight_pack, in_own))
    gathered = lax.all_gather(weight_pack, ALL, axis=0, tiled=False)
    unit = gain_rows
    while unit % 8:
        unit *= 2
    units = width // unit
    if unit != gain_rows:
        gathered = jnp.concatenate(
            [gathered[:, :ff_rows].reshape(units, -1, width)]
            + [
                gathered[:, at : at + gain_rows].reshape(units, unit, width)
                for at in range(ff_rows, ff_rows + (folds + 1) * gain_rows, gain_rows)
            ],
            1,
        )
    wide = unit * folds

    mods = small_all[:, :mod_size].astype(F32) + small_all[:, mod_size : 2 * mod_size].astype(F32)
    mods = mods.reshape(devices, micro, mod_lanes)[:, :, :mod_rows].transpose(1, 0, 2).reshape(micro, -1)
    at = 2 * mod_size
    vectors = small_all[:, at : at + 3, :gain_rows].astype(F32).transpose(1, 0, 2).reshape(3, width)
    gain1, gain2, reduce_bias_f = vectors[0], vectors[1], vectors[2:]
    at += 3
    expand_bias_f = small_all[:, at : at + ff_lanes // 64].reshape(devices, ff_lanes)[:, :ff_rows]
    expand_bias_f = expand_bias_f.astype(F32).reshape(folds, 1, width)
    shift1, scale1, gate1, shift2, scale2, gate2 = jnp.split(mods, 6, 1)
    c1 = gain1 * (1.0 + scale1)
    c2 = gain2 * (1.0 + scale2)

    count = groups * rows
    smem = pl.BlockSpec(memory_space=pltpu.SMEM)
    message_rows = count + count // 2 + 16
    if small_path:
        outgoing, last_own = pl.pallas_call(
            functools.partial(project_small_body, blocks, heads),
            out_shape=[
                jax.ShapeDtypeStruct((blocks, message_rows, 128), BF), jax.ShapeDtypeStruct((count, 128), BF),
            ],
            in_specs=[whole_vmem()] * (3 + groups),
            out_specs=[whole_vmem()] * 2,
            scratch_shapes=[pltpu.VMEM((count, 128), F32)],
            cost_estimate=pl.CostEstimate(
                flops=2 * micro * count * width * 3 * 64 * heads, transcendentals=0, bytes_accessed=8 * own * width
            ),
            name="project",
        )(c1, shift1, in_own, *n1_group)
        incoming = [lax.all_to_all(outgoing, BLK, split_axis=0, concat_axis=0, tiled=True)]
        pass_on = lambda x, bit: lax.ppermute(x, BLK, [(i, i ^ bit) for i in range(blocks)])
        last_four = jnp.stack([last_own] + [pass_on(last_own, bit) for bit in range(2, blocks, 2)])
        last_keys = [last_four, pass_on(last_four, 1)]
    else:
        outgoing = pl.pallas_call(
            functools.partial(project_body, blocks, pairs, heads, extra),
            out_shape=[jax.ShapeDtypeStruct((count, lanes), BF)] * blocks,
            in_specs=[smem] + [whole_vmem()] * (3 + groups),
            out_specs=[whole_vmem()] * blocks,
            scratch_shapes=[pltpu.VMEM((blocks, count, lanes), BF)],
            name="project",
        )(place, c1, shift1, in_own, *n1_group)
        incoming = swap(outgoing, BLK)

    span = blocks * rows
    by_span = pl.BlockSpec((span, 64), lambda i, p: (i ^ p[0], 0))
    table_spec = pl.BlockSpec((span, 128), lambda i, p: (i ^ p[0], 0))
    by_rows = pl.BlockSpec((rows, lanes), lambda i, p: (i, 0))
    parts = 6 if extra else 3
    if small_path:
        whole = lambda *shape: jax.ShapeDtypeStruct(shape, BF)
        f32 = lambda *shape: jax.ShapeDtypeStruct(shape, F32)
        padded = whole(size + KB - STEP, 64)
        own_args = (place, ranges, *bounds[:2], cos_table, sin_table)
        last_args = (place, last_ranges, *bounds[2:], cos_table, sin_table)
        specs = [smem] * 2 + [whole_vmem()] * 4
        own_message, *own_saved = pl.pallas_call(
            functools.partial(attend_own_body, blocks, groups, rows),
            in_specs=specs + [whole_vmem()],
            out_specs=[whole_vmem()] * 6,
            out_shape=[
                whole(devices, rows // 2, 128), whole(size, 64), padded, padded, whole(size, 64), f32(*bounds[0].shape),
            ],
            scratch_shapes=[
                pltpu.VMEM((span, 128), BF), pltpu.VMEM((span, 64), BF),
                pltpu.VMEM((size // KB + 1, KB, QB), F32),
            ],
            cost_estimate=pl.CostEstimate(
                flops=size * size * 64, transcendentals=size * size // 2, bytes_accessed=16 * size * 128
            ),
            name="attend_own",
        )(*own_args, *incoming)
        message, *last_saved = pl.pallas_call(
            functools.partial(attend_last_body, blocks, groups, rows, stripe),
            in_specs=specs + [whole_vmem()] * 4,
            out_specs=[whole_vmem()] * 6,
            out_shape=[
                whole(devices, rows // 2 + stripe, 128), whole(devices * stripe, 64), padded, padded,
                whole(devices * stripe, 64), f32(*bounds[2].shape),
            ],
            scratch_shapes=[pltpu.VMEM((span, 128), BF)]
            + [pltpu.VMEM((devices * stripe, 128), F32)] * 3
            + [pltpu.VMEM((size // KB + 1, KB, last_rows), F32)],
            cost_estimate=pl.CostEstimate(
                flops=size * size * 16, transcendentals=size * size // 8, bytes_accessed=16 * size * 64
            ),
            name="attend_last",
        )(*last_args, *incoming, *last_keys, own_message)
    else:
        assert not extra
        turned = pl.pallas_call(
            functools.partial(rotate_in_body, blocks, extra),
            grid_spec=pltpu.PrefetchScalarGridSpec(
                num_scalar_prefetch=1,
                grid=(groups,),
                in_specs=[table_spec, table_spec] + [by_rows] * blocks,
                out_specs=[by_span] * parts,
                scratch_shapes=[pltpu.VMEM((span, lanes), BF)],
            ),
            out_shape=[jax.ShapeDtypeStruct((size, 64), BF)] * parts,
            name="rotate_in",
        )(place, cos_table, sin_table, *incoming)
        query, key, value = turned[:3]
        attended, lse = attend(
            ranges, query, segment, key, value, segment[:, None], query_rows, key_block
        )
        message = attended.reshape(devices, rows, head_width)
    came = exchange(message)

    ex_spec = lambda f: pl.BlockSpec((units, unit, width), f)
    flat = pl.BlockSpec((own, width), lambda i: (0, 0))
    vec = lambda n: pl.BlockSpec((n, width), lambda i: (0, 0))
    message_shape = message.shape
    message_spec = pl.BlockSpec(message_shape, lambda i: (0, 0, 0))
    sizes = (groups, blocks, heads, micro, rows, stripe)
    own_f32 = jax.ShapeDtypeStruct((own, width), F32)
    own_bf = jax.ShapeDtypeStruct((own, width), BF)
    merged, attn, middle, second = pl.pallas_call(
        functools.partial(middle_body, *sizes),
        grid=(1,),
        in_specs=[message_spec, ex_spec(lambda i: (0, folds, 0)), flat, vec(micro), vec(micro), vec(micro)],
        out_specs=[flat] * 4,
        out_shape=[own_bf, own_f32, own_f32, own_bf],
        name="middle",
    )(came, gathered, tokens.reshape(own, width), gate1, c2, shift2)
    second_group = swap([second] * groups, "ulysses")
    dy = cotangent.reshape(own, width)
    dy_group = swap([dy] * groups, "ulysses")

    per = width // wide
    layer_output, grad_middle, grad_attn, do_message, sums = pl.pallas_call(
        functools.partial(feed_body, *sizes),
        grid=(folds,),
        in_specs=[
            ex_spec(lambda i: (0, folds + 1 + i, 0)),
            pl.BlockSpec((per, wide, width), lambda i: (i, 0, 0)),
            ex_spec(lambda i: (0, folds, 0)),
            pl.BlockSpec((1, 1, width), lambda i: (i, 0, 0)),
            vec(1),
            flat, flat, flat, flat,
            vec(micro), vec(micro), vec(micro),
        ],
        out_specs=[flat, flat, flat, message_spec, vec(5 * micro)],
        out_shape=[
            own_bf, own_f32, own_bf,
            jax.ShapeDtypeStruct(message_shape, BF),
            jax.ShapeDtypeStruct((5 * micro, width), F32),
        ],
        scratch_shapes=[
            pltpu.VMEM((own, width), F32), pltpu.VMEM((own, width), F32),
            pltpu.VMEM((own, width), BF), pltpu.VMEM((own, width), BF),
        ],
        cost_estimate=pl.CostEstimate(
            flops=8 * own * width * ff, transcendentals=own * ff, bytes_accessed=4 * width * ff
        ),
        name="feed",
    )(gathered, gathered, gathered, expand_bias_f, reduce_bias_f, second, middle, attn, dy, gate1, gate2, c2)
    do_came = exchange(do_message)
    d_gate2, d_shift2, p2, d_gate1, dm_sums = [
        sums[i * micro : (i + 1) * micro] for i in range(5)
    ]

    flat_p = pl.BlockSpec((own, width), lambda i, p: (0, 0))
    feed_kept, feed_sent, bias_part = pl.pallas_call(
        functools.partial(feed_weights_body, rows, blocks),
        grid_spec=pltpu.PrefetchScalarGridSpec(
            num_scalar_prefetch=1,
            grid=(1,),
            in_specs=[
                pl.BlockSpec((units, unit, width), lambda i, p: (0, folds + 1 + p[0], 0)),
                pl.BlockSpec((per, wide, width), lambda i, p: (p[0], 0, 0)),
                pl.BlockSpec((1, 1, width), lambda i, p: (p[0], 0, 0)),
                pl.BlockSpec((micro, width), lambda i, p: (0, 0)),
            ]
            + [flat_p] * (2 * groups),
            out_specs=[
                pl.BlockSpec((blocks // 2, ff_rows + groups * gain_rows, width), lambda i, p: (0, 0, 0)),
                pl.BlockSpec((blocks // 2, ff_rows + groups * gain_rows, width), lambda i, p: (0, 0, 0)),
                pl.BlockSpec((1, width), lambda i, p: (0, 0)),
            ],
            scratch_shapes=[pltpu.VMEM((blocks, ff_rows + groups * gain_rows, width), BF)],
        ),
        out_shape=[
            jax.ShapeDtypeStruct((blocks // 2, ff_rows + groups * gain_rows, width), BF),
            jax.ShapeDtypeStruct((blocks // 2, ff_rows + groups * gain_rows, width), BF),
            jax.ShapeDtypeStruct((1, width), F32),
        ],
        cost_estimate=pl.CostEstimate(
            flops=10 * own * groups * width * width, transcendentals=own * ff, bytes_accessed=16 * width * width
        ),
        name="feed_weights",
    )(place, gathered, gathered, expand_bias_f, gate2, *second_group, *dy_group)
    do_came, feed_kept, feed_sent = lax.optimization_barrier((do_came, feed_kept, feed_sent))
    feed_came = lax.ppermute(feed_sent, BLK, [(i, i ^ 1) for i in range(blocks)])
    feed_half = (feed_kept.astype(F32) + feed_came.astype(F32)).astype(BF)
    feed_sum = lax.psum_scatter(feed_half, "far", scatter_dimension=0, tiled=True)[0]

    if small_path:
        last_dq, last_kept, last_sent = pl.pallas_call(
            functools.partial(attend_last_back_body, blocks, groups, rows, stripe),
            in_specs=specs + [whole_vmem()] * 6,
            out_specs=[whole_vmem()] * 3,
            out_shape=[f32(devices * stripe, 128)] + [whole(blocks // 2, count, 128)] * 2,
            scratch_shapes=[pltpu.VMEM((span, 128), BF)]
            + [pltpu.VMEM((devices * stripe, 128), F32)] * 2
            + [pltpu.VMEM((size + KB - STEP, 64), F32)] * 2,
            cost_estimate=pl.CostEstimate(
                flops=size * size * 32, transcendentals=size * size // 8, bytes_accessed=16 * size * 64
            ),
            name="attend_last_back",
        )(*last_args, do_came, *last_saved)
        last_half = (last_kept.astype(F32) + pass_on(last_sent, 1).astype(F32)).astype(BF)
        do_came, last_dq = lax.optimization_barrier((do_came, last_dq))
        leaving = pl.pallas_call(
            functools.partial(attend_own_back_body, blocks, groups, rows, stripe),
            in_specs=specs + [whole_vmem()] * 7,
            out_specs=whole_vmem(),
            out_shape=whole(blocks, message_rows, 128),
            scratch_shapes=[
                pltpu.VMEM((span, 128), BF), pltpu.VMEM((span, 64), BF),
                pltpu.VMEM((devices, rows, 64), BF), pltpu.VMEM((size, 64), F32),
            ]
            + [pltpu.VMEM((size + KB - STEP, 64), F32)] * 2,
            cost_estimate=pl.CostEstimate(
                flops=2 * size * size * 64, transcendentals=size * size // 2, bytes_accessed=16 * size * 128
            ),
            name="attend_own_back",
        )(*own_args, do_came, *own_saved, last_dq)
    else:
        grads = attend_back(
            ranges, query, segment, lse, attended, do_came.reshape(size, head_width), key, value,
            segment[:, None], query_rows, key_block,
        )
        leaving = pl.pallas_call(
            functools.partial(rotate_out_body, blocks, extra),
            grid_spec=pltpu.PrefetchScalarGridSpec(
                num_scalar_prefetch=1,
                grid=(groups,),
                in_specs=[table_spec, table_spec] + [by_span] * parts,
                out_specs=[by_rows] * blocks,
                scratch_shapes=[pltpu.VMEM((span, lanes), BF)],
            ),
            out_shape=[jax.ShapeDtypeStruct((count, lanes), BF)] * blocks,
            name="rotate_out",
        )(place, cos_table, sin_table, *grads)
    if small_path:
        leaving, last_half = lax.optimization_barrier((leaving, last_half))
        back = [lax.all_to_all(leaving, BLK, split_axis=0, concat_axis=0, tiled=True)]
        back += [
            pass_on(lax.dynamic_index_in_dim(last_half, (block_id // 2) ^ k, 0, keepdims=False), 2 * k)
            if k
            else lax.dynamic_index_in_dim(last_half, block_id // 2, 0, keepdims=False)
            for k in range(blocks // 2)
        ]
    else:
        back = swap(leaving, BLK)
    leaving, merged, grad_attn = lax.optimization_barrier((leaving, merged, grad_attn))
    output_part = lax.dot_general(merged, grad_attn, TN, preferred_element_type=F32).astype(BF)
    output_part = output_part.reshape(groups, width // groups, width)

    output_part = swap(
        [
            lax.dynamic_index_in_dim(output_part, group_id ^ k, 0, keepdims=False)
            for k in range(groups)
        ],
        "ulysses",
    )

    output_part = sum(x.astype(F32) for x in output_part).astype(BF).reshape(blocks, gain_rows, width)

    if small_path:
        back_body = functools.partial(project_back_small_body, blocks, heads)
        back_scratch = [
            pltpu.VMEM((count, 64), F32), pltpu.VMEM((devices, gain_rows, heads * 3 * head_width), F32),
        ]
        back_args, back_specs = (place,), [smem]
        back_grads = [jax.ShapeDtypeStruct((blocks // 2, groups, gain_rows, heads * 3 * head_width), BF)] * 2
    else:
        back_args, back_specs = (place,), [smem]
        back_body = functools.partial(project_back_body, blocks, pairs, heads, extra)
        back_scratch = [pltpu.VMEM((blocks, count, lanes), BF)]
        back_grads = [jax.ShapeDtypeStruct((width, heads * 3 * head_width), BF)]
    returned = pl.pallas_call(
        back_body,
        out_shape=[jax.ShapeDtypeStruct((micro, rows, width), BF)] * groups
        + back_grads
        + [jax.ShapeDtypeStruct((micro, width), F32)] * 2,
        in_specs=back_specs + [whole_vmem()] * (3 + groups + len(back)),
        out_specs=[whole_vmem()] * (groups + 2 + len(back_grads)),
        scratch_shapes=back_scratch,
        cost_estimate=pl.CostEstimate(
            flops=4 * micro * count * width * 3 * 64 * heads, transcendentals=0, bytes_accessed=8 * own * width
        ),
        name="project_back",
    )(*back_args, c1, shift1, in_own, *n1_group, *back)
    *input_part, d_shift1, p1 = returned[groups:]
    grad_mods = jnp.concatenate(
        [d_shift1, p1 * gain1, d_gate1, d_shift2, p2 * gain2, d_gate2], 1
    )
    gain1_part = jnp.sum((1.0 + scale1) * p1, 0)
    gain2_part = jnp.sum((1.0 + scale2) * p2, 0)
    own_units = jnp.where(
        (jnp.arange(groups) == group_id)[:, None], bias_part.reshape(1, width), 0.0
    )
    small_parts = jnp.concatenate(
        [grad_mods.reshape(micro, devices, mod_rows).transpose(1, 0, 2).reshape(devices, -1)]
        + [
            x.reshape(devices, -1)
            for x in (gain1_part, gain2_part, jnp.sum(dm_sums, 0), own_units)
        ],
        1,
    ).astype(BF)
    taken = small_parts.shape[1]
    small_rows = 8 * -(-taken // (8 * in_lanes))
    small_parts = jnp.pad(small_parts, ((0, 0), (0, small_rows * in_lanes - taken)))
    if small_path:
        kept, sent = input_part
    else:
        halves = (
            input_part[0]
            .reshape(groups, blocks, gain_rows, in_lanes)
            .transpose(1, 0, 2, 3)
            .reshape(blocks // 2, 2, groups, gain_rows, in_lanes)
        )
        sent = lax.dynamic_index_in_dim(halves, 1 - block_id % 2, 1, keepdims=False)
        kept = lax.dynamic_index_in_dim(halves, block_id % 2, 1, keepdims=False)
    sent, token_parts = lax.optimization_barrier((sent, returned[:groups]))
    came = lax.ppermute(sent, BLK, [(i, i ^ 1) for i in range(blocks)])
    input_sum = (kept.astype(F32) + came.astype(F32)).astype(BF)
    token_parts = swap(token_parts, "ulysses")
    out_lanes = output_part.shape[1] * output_part.shape[2] // in_lanes
    rest = jnp.concatenate(
        [
            small_parts.reshape(groups, blocks, small_rows, in_lanes)
            .transpose(1, 0, 2, 3)
            .reshape(blocks, groups * small_rows, in_lanes),
            output_part.reshape(blocks, out_lanes, in_lanes),
        ],
        1,
    )
    rest = halve(rest, BLK, block_id, 1)
    input_sum, rest, feed_sum, token_parts = lax.optimization_barrier((input_sum, rest, feed_sum, token_parts))
    grad_first = sum(x.astype(F32) for x in token_parts)
    e = grad_first * c1[:, None]
    tokens_grad = (
        grad_middle.reshape(micro, rows, width)
        + r1
        * (
            e
            - jnp.mean(e, -1, keepdims=True)
            - n1 * jnp.mean(e * n1, -1, keepdims=True)
        )
    ).astype(BF)

    input_sum = jnp.concatenate(
        [input_sum.reshape(blocks // 2, groups * gain_rows, in_lanes), rest], 1
    )
    bit = 2
    while bit < blocks:
        input_sum = halve(input_sum, BLK, block_id, bit)
        if bit == 2:
            input_sum, feed_sum = lax.optimization_barrier((input_sum, feed_sum))
        bit *= 2
    input_sum = input_sum[0]
    at = groups * gain_rows
    small_sum = input_sum[at : at + groups * small_rows]
    output_grad = input_sum[at + groups * small_rows :].reshape(gain_rows, width).astype(F32)
    input_sum = jnp.concatenate(
        [input_sum[:at].reshape(groups, gain_rows, in_lanes), small_sum.reshape(groups, small_rows, in_lanes)], 1
    )
    final = jnp.stack(
        swap(
            [
                lax.dynamic_index_in_dim(input_sum, group_id ^ k, 0, keepdims=False)
                for k in range(groups)
            ],
            "ulysses",
        )
    )
    small_sum = jnp.sum(final[:, gain_rows:].astype(F32), 0).reshape(-1)
    input_sum = unscramble(final[:, :gain_rows], group_id, 0).astype(F32)
    reduce_grad = feed_sum[:ff_rows].astype(F32)
    expand_rows = feed_sum[ff_rows:].reshape(groups, gain_rows, width)
    expand_came = jnp.stack(
        swap(
            [
                lax.dynamic_index_in_dim(expand_rows, group_id ^ k, 0, keepdims=False)
                for k in range(groups)
            ],
            "ulysses",
        )
    )
    expand_grad = jnp.concatenate(
        [
            lax.dynamic_index_in_dim(expand_came, group_id ^ k, 0, keepdims=False)
            for k in range(groups)
        ],
        1,
    ).astype(F32)

    two = heads * 2 * head_width
    input_grad = jnp.concatenate(
        [
            input_sum[:, :, :two]
            .reshape(groups, gain_rows, heads, 2, head_width)
            .transpose(1, 3, 0, 2, 4)
            .reshape(gain_rows, 2 * width),
            input_sum[:, :, two:].transpose(1, 0, 2).reshape(gain_rows, width),
        ],
        1,
    )
    at = micro * mod_rows
    mod_sum = small_sum[:at].reshape(micro, mod_rows)
    modulate_weight_grad = jnp.sum(
        mod_sum[:, :, None] * condition.astype(F32)[:, None, :], 0
    )
    cuts = []
    for length in (gain_rows, gain_rows, gain_rows, ff_rows):
        cuts.append(small_sum[at : at + length])
        at += length
    return (
        layer_output.reshape(micro, rows, width),
        tokens_grad,
        modulate_weight_grad,
        jnp.sum(mod_sum, 0),
        cuts[0],
        input_grad,
        output_grad,
        cuts[1],
        expand_grad,
        cuts[3],
        reduce_grad,
        cuts[2],
    )


def solution(mesh):
    groups, blocks = mesh.devices.shape
    split = jax.sharding.Mesh(mesh.devices.reshape(groups, blocks // 2, 2), ALL)
    both = P(ALL)
    tall = P(ALL, None)
    seq = P(None, ALL, None)
    in_specs = (
        seq, seq, P(), P(), tall, both, both, tall, tall, both, tall, both, tall, both,
    )
    out_specs = (seq, seq, tall, both, both, tall, tall, both, tall, both, tall, both)
    return jax.shard_map(
        on_device, mesh=split, in_specs=in_specs, out_specs=out_specs, check_vma=False
    )
```
